32 devices in a mesh: dp: 4 (over z), tensor: 8 (over y, x, core).
Axes of the slice: x: 2, y: 2, z: 4, core: 2. Of those that a mesh axis runs over, the one named last changes fastest.
Arguments:
- hidden_input: bfloat16 [16384, 2048], P(('dp', 'tensor')), may hold values from -6 to 6
- first_gain: bfloat16 [2048], replicated, may hold values from 0.5 to 1.5
- first_shift: bfloat16 [2048], replicated, may hold values from -3 to 3
- qkv_weight: bfloat16 [2048, 6144], P('dp', 'tensor'), may hold values from -0.125 to 0.125
- query_bias: bfloat16 [2048], P('tensor'), may hold values from -3 to 3
- value_bias: bfloat16 [2048], P('tensor'), may hold values from -3 to 3
- dense_weight: bfloat16 [2048, 2048], P('tensor', 'dp'), may hold values from -0.5 to 0.5
- dense_bias: bfloat16 [2048], replicated, may hold values from -3 to 3
- second_gain: bfloat16 [2048], replicated, may hold values from 0.5 to 1.5
- second_shift: bfloat16 [2048], replicated, may hold values from -3 to 3
- up_weight: bfloat16 [2048, 8192], P('dp', 'tensor'), may hold values from -0.125 to 0.125
- up_bias: bfloat16 [8192], P('tensor'), may hold values from -3 to 3
- down_weight: bfloat16 [8192, 2048], P('tensor', 'dp'), may hold values from -0.0625 to 0.0625
- down_bias: bfloat16 [2048], replicated, may hold values from -3 to 3
- segments: int32 [16384], P('dp'), may hold values from 0 to 17, as said below
- document_lengths: int32 [16, 18], P('dp'), may hold values from 0 to 800, as said below
- cotangent: bfloat16 [16384, 2048], P(('dp', 'tensor')), may hold values from -6 to 6
Outputs:
- hidden_output: bfloat16 [16384, 2048], P(('dp', 'tensor'))
- grad_input: float32 [16384, 2048], P(('dp', 'tensor'))
- grad_first_gain: float32 [2048], replicated
- grad_first_shift: float32 [2048], replicated
- grad_qkv_weight: float32 [2048, 6144], P('dp', 'tensor')
- grad_query_bias: float32 [2048], P('tensor')
- grad_value_bias: float32 [2048], P('tensor')
- grad_dense_weight: float32 [2048, 2048], P('tensor', 'dp')
- grad_dense_bias: float32 [2048], replicated
- grad_second_gain: float32 [2048], replicated
- grad_second_shift: float32 [2048], replicated
- grad_up_weight: float32 [2048, 8192], P('dp', 'tensor')
- grad_up_bias: float32 [8192], P('tensor')
- grad_down_weight: float32 [8192, 2048], P('tensor', 'dp')
- grad_down_bias: float32 [2048], replicated
The draws below stay inside these ranges and needn't reach their ends.
Inputs may be any that keep to these rules, and one draw needn't show every extreme that they name: `segments`: within each packed sequence the numbers start at 0 and never fall, each document's run matches its entry of document_lengths, and tokens after the last document carry the next number. `document_lengths`: each row holds documents of 60 to 800 tokens first, then zeros; a row's sum is at most 1024.
All inputs are finite; a program needn't handle non-finite values.
Results may differ from the reference program's by a relative error of at most 0.02.
Values may be sent and summed in bfloat16 or wider, within the bound.
A program may use at most 256 MiB of HBM per device.

```python
import math
import jax
import jax.numpy as jnp
from jax import lax

D = 2048
HEADS = 16
HEAD_DIM = 128
FF = 8192
LEN = 1024
SEQ_GRP = 4
DOC_MIN = 60
DOC_MAX = 800
DOCS_SEQ = 18
SEQS = 16
TOKENS = 16384


def packing(key):
    inner = jax.random.fold_in(key, 31)
    first, second = jax.random.split(inner)
    drawn = jax.random.randint(first, (SEQS, DOCS_SEQ), DOC_MIN, DOC_MAX + 1)
    chosen = jax.random.randint(second, (), 0, SEQS)
    packed_row = (chosen + 1) % SEQS
    row_index = lax.broadcasted_iota(jnp.int32, (SEQS, DOCS_SEQ), 0)
    column_index = lax.broadcasted_iota(jnp.int32, (SEQS, DOCS_SEQ), 1)
    drawn = jnp.where((row_index == chosen) & (column_index == 0), DOC_MAX, drawn)
    drawn = jnp.where(row_index == packed_row, DOC_MIN, drawn).astype(jnp.int32)
    finish = jnp.cumsum(drawn, axis=1)
    inside = finish <= LEN
    lengths = jnp.where(inside, drawn, 0).astype(jnp.int32)
    bounds = jnp.where(inside, finish, LEN + 1)
    position = lax.broadcasted_iota(jnp.int32, (SEQS, LEN, DOCS_SEQ), 1)
    labels = jnp.sum((bounds[:, None, :] <= position).astype(jnp.int32), axis=2)
    return (lengths, labels.reshape(SEQS * LEN).astype(jnp.int32))


def draw_segments(key, part):
    return packing(key)[1]


def draw_document_lengths(key, part):
    return packing(key)[0]


def draw_cotangent(key, part):
    rows = lax.broadcasted_iota(jnp.float32, (TOKENS, D), 0)
    ramp = 0.5 + rows / TOKENS
    base = jnp.clip(jax.random.normal(key, (TOKENS, D), jnp.float32), -4.0, 4.0)
    return (base * ramp).astype(jnp.bfloat16)


def steps_of(rng, dims, cuts, low, high):
    gain, own = 1.0, jax.random.fold_in(rng, 6)
    for axis_at, blocks in cuts:
        draws = jnp.exp(jax.random.uniform(jax.random.fold_in(own, axis_at), (blocks,), jnp.float32, low / len(cuts), high / len(cuts)))
        gain = gain * jnp.repeat(draws, dims[axis_at] // blocks).reshape([-1 if axis == axis_at else 1 for axis in range(len(dims))])
    return gain


def centred(rng, shape, deviation, limit, cuts=(), held_as=jnp.bfloat16):
    loudness = steps_of(rng, shape, cuts, -0.22, 0.18) if cuts else 1.0
    values = jax.random.normal(rng, shape, jnp.float32) * deviation * loudness
    return jnp.minimum(jnp.maximum(values, -limit), limit).astype(held_as)


def setup_inputs(seed: int = 0) -> dict:
    key_list = jax.random.split(jax.random.key(seed), 18)
    hidden_input = centred(key_list[0], (TOKENS, D), 1.0, 6.0, ((0, 32),))
    first_gain = jnp.clip(1.0 + 0.1 * jax.random.normal(key_list[1], (D,), jnp.float32), 0.5, 1.5).astype(jnp.bfloat16)
    first_shift = centred(key_list[2], (D,), 0.3, 3.0)
    qkv_weight = centred(key_list[3], (D, 3 * D), D ** -0.5, 0.125, ((0, 4), (1, 8)))
    query_bias = centred(key_list[4], (D,), 0.5, 3.0, ((0, 8),))
    value_bias = centred(key_list[5], (D,), 0.5, 3.0, ((0, 8),))
    dense_weight = centred(key_list[6], (D, D), (D // 16) ** -0.5, 0.5, ((0, 8), (1, 4)))
    dense_bias = centred(key_list[7], (D,), 0.3, 3.0)
    second_gain = jnp.clip(1.0 + 0.1 * jax.random.normal(key_list[8], (D,), jnp.float32), 0.5, 1.5).astype(jnp.bfloat16)
    second_shift = centred(key_list[9], (D,), 0.3, 3.0)
    up_weight = centred(key_list[10], (D, FF), D ** -0.5, 0.125, ((0, 4), (1, 8)))
    up_bias = centred(key_list[11], (FF,), 0.5, 3.0, ((0, 8),))
    down_weight = centred(key_list[12], (FF, D), FF ** -0.5, 0.0625, ((0, 8), (1, 4)))
    down_bias = centred(key_list[13], (D,), 0.3, 3.0)
    segments = draw_segments(jax.random.fold_in(key_list[17], 71), 0)
    document_lengths = draw_document_lengths(jax.random.fold_in(key_list[17], 71), 0)
    cotangent = draw_cotangent(jax.random.fold_in(key_list[17], 71), 0)
    return {"hidden_input": hidden_input, "first_gain": first_gain, "first_shift": first_shift, "qkv_weight": qkv_weight, "query_bias": query_bias, "value_bias": value_bias, "dense_weight": dense_weight, "dense_bias": dense_bias, "second_gain": second_gain, "second_shift": second_shift, "up_weight": up_weight, "up_bias": up_bias, "down_weight": down_weight, "down_bias": down_bias, "segments": segments, "document_lengths": document_lengths, "cotangent": cotangent}


@jax.custom_vjp
def low(v):
    return lax.optimization_barrier(v.astype(jnp.bfloat16)).astype(jnp.float32)

@jax.custom_vjp
def low_back(v):
    return v

def low_keep(v):
    return (low(v), None)

def low_pass(kept, grad):
    return (grad,)

def back_keep(v):
    return (v, None)

def back_low(kept, grad):
    return (low(grad),)
low.defvjp(low_keep, low_pass)
low_back.defvjp(back_keep, back_low)

def gelu_tanh(value):
    return 0.5 * value * (1.0 + jnp.tanh(0.7978845608028654 * (value + 0.044715 * value * value * value)))

def layer_norm(rows):
    center = rows - lax.optimization_barrier(jnp.mean(rows, axis=1, keepdims=True))
    return center * lax.rsqrt(lax.optimization_barrier(jnp.mean(center * center, axis=1, keepdims=True)) + 1e-05)

def allowed_mask(labels, lengths):
    length = labels.shape[0]
    position = lax.broadcasted_iota(jnp.int32, (length, length), 0)
    other = lax.broadcasted_iota(jnp.int32, (length, length), 1)
    filled = jnp.sum(lengths).astype(jnp.int32)
    same = labels[:, None] == labels[None, :]
    allowed = same & (other <= position) & ((other < filled) | (other == position))
    return (allowed, (other - position).astype(jnp.float32))

def attend(item):
    queries, keys, values, labels, lengths = item
    allowed, distance = allowed_mask(labels, lengths)
    slopes = jnp.exp2(-8.0 * (jnp.arange(HEADS).astype(jnp.float32) + 1.0) / HEADS)
    raw = jnp.einsum('qhd,khd->hqk', queries, keys, precision=lax.Precision.HIGHEST) * (1.0 / math.sqrt(HEAD_DIM))
    raw = raw + slopes[:, None, None] * distance[None]
    scores = jnp.where(allowed[None], low_back(raw), -1e+30)
    top = lax.optimization_barrier(jnp.max(scores, axis=2, keepdims=True))
    expo = jnp.exp(scores - top)
    probs = low(expo / lax.optimization_barrier(jnp.sum(expo, axis=2, keepdims=True)))
    return jnp.einsum('hqk,khd->qhd', probs, values, precision=lax.Precision.HIGHEST)

def layer(params, inputs, labels, lengths):
    first_gain, first_shift, qkv_weight, query_bias, value_bias, dense_weight, dense_bias, second_gain, second_shift, up_weight, up_bias, down_weight, down_bias = params
    rows = inputs.shape[0]
    attn_input = low(layer_norm(inputs) * first_gain + first_shift)
    projected = jnp.dot(attn_input, qkv_weight, precision=lax.Precision.HIGHEST).reshape(rows, HEADS, 3, HEAD_DIM)
    queries = low(low_back(projected[:, :, 0] + query_bias.reshape(HEADS, HEAD_DIM)))
    keys = low(low_back(projected[:, :, 1]))
    values = low(low_back(projected[:, :, 2] + value_bias.reshape(HEADS, HEAD_DIM)))
    count = labels.shape[0]
    shaped = (queries.reshape(count, LEN, HEADS, HEAD_DIM), keys.reshape(count, LEN, HEADS, HEAD_DIM), values.reshape(count, LEN, HEADS, HEAD_DIM), labels, lengths)
    mixed = lax.map(jax.checkpoint(attend), shaped)
    mixed = low(low_back(mixed.reshape(rows, D)))
    attn_out = low_back(jnp.dot(mixed, dense_weight, precision=lax.Precision.HIGHEST))
    residual = inputs + attn_out + dense_bias
    mlp_input = low(layer_norm(residual) * second_gain + second_shift)
    pre_act = low_back(jnp.dot(mlp_input, up_weight, precision=lax.Precision.HIGHEST) + up_bias)
    activated = low(gelu_tanh(pre_act))
    return residual + jnp.dot(activated, down_weight, precision=lax.Precision.HIGHEST) + down_bias

def reference(hidden_input, first_gain, first_shift, qkv_weight, query_bias, value_bias, dense_weight, dense_bias, second_gain, second_shift, up_weight, up_bias, down_weight, down_bias, segments, document_lengths, cotangent):
    params = tuple((p.astype(jnp.float32) for p in (first_gain, first_shift, qkv_weight, query_bias, value_bias, dense_weight, dense_bias, second_gain, second_shift, up_weight, up_bias, down_weight, down_bias)))
    block_rows = SEQ_GRP * LEN
    blocks = TOKENS // block_rows
    items = (hidden_input.astype(jnp.float32).reshape(blocks, block_rows, D), cotangent.astype(jnp.float32).reshape(blocks, block_rows, D), segments.reshape(blocks, SEQ_GRP, LEN), document_lengths.reshape(blocks, SEQ_GRP, DOCS_SEQ))

    def step(total, item):
        inputs, grads, labels, lengths = item
        output, pull = jax.vjp(lambda pr, xx: layer(pr, xx, labels, lengths), params, inputs)
        grad_params, grad_inputs = pull(grads)
        total = jax.tree.map(jnp.add, total, grad_params)
        return (total, (output.astype(jnp.bfloat16), grad_inputs))
    start = jax.tree.map(jnp.zeros_like, params)
    total, (outputs, grad_inputs) = lax.scan(step, start, items)
    g_first_gain, g_first_shift, g_qkv, g_query, g_value, g_dense, g_dense_bias, g_second_gain, g_second_shift, g_up, g_up_bias, g_down, g_down_bias = total
    return (outputs.reshape(TOKENS, D), grad_inputs.reshape(TOKENS, D), g_first_gain, g_first_shift, g_qkv, g_query, g_value, g_dense, g_dense_bias, g_second_gain, g_second_shift, g_up, g_up_bias, g_down, g_down_bias)
```

```python
import functools
import math

import jax
import jax.numpy as jnp
from jax import lax
from jax.experimental import pallas as pl
from jax.experimental.pallas import tpu as pltpu
from jax.sharding import PartitionSpec as P

VMEM_LIMIT = 62 << 20


def flip(index, bit):
    return index + (1 - 2 * ((index // 2**bit) % 2)) * 2**bit


def chip_bits(n):
    return n.bit_length() - 2


def column_parts(width, count):
    blocks = width // 128
    edges = [128 * (blocks * i // count) for i in range(count + 1)]
    return [(a, b - a) for a, b in zip(edges[:-1], edges[1:])]


def peer(index):
    return {"tensor": index}


def greet(me, bits):
    barrier = pltpu.get_barrier_semaphore()
    for bit in range(bits + 1):
        pl.semaphore_signal(
            barrier, inc=1, device_id=peer(flip(me, bit)), device_id_type=pl.DeviceIdType.MESH
        )
    pl.semaphore_wait(barrier, bits + 1)


def remote(src, dst, send_sem, recv_sem, target):
    return pltpu.make_async_remote_copy(
        src_ref=src,
        dst_ref=dst,
        send_sem=send_sem,
        recv_sem=recv_sem,
        device_id=peer(target),
        device_id_type=pl.DeviceIdType.MESH,
    )


def gather_body(n, own_ref, out_ref, own_sem, chip_send, chip_recv, core_send, core_recv):
    me = lax.axis_index("tensor")
    bits = chip_bits(n)
    rows, width = own_ref.shape
    parts = column_parts(width, bits)
    held = 2**bits
    other_core = flip(me, 0)
    greet(me, bits)

    def slot(part, index):
        at = me
        for step in range(bits):
            if (index >> step) & 1:
                at = flip(at, 1 + (part + step) % bits)
        return at

    def block(part, index):
        start, size = parts[part]
        return out_ref.at[pl.ds(slot(part, index) * rows, rows), pl.ds(start, size)]

    sends = []
    keep = pltpu.make_async_copy(own_ref, out_ref.at[pl.ds(me * rows, rows), :], own_sem)

    def send(part, index, step):
        start, size = parts[part]
        source = own_ref.at[:, pl.ds(start, size)] if index == 0 else block(part, index)
        arrives = index + 2**step
        copy = remote(
            source,
            block(part, index),
            chip_send.at[part, arrives],
            chip_recv.at[part, arrives],
            flip(me, 1 + (part + step) % bits),
        )
        copy.start()
        sends.append(copy)

    for step in range(bits):
        for part in range(bits):
            send(part, 0, step)
    for part in range(bits):
        start, size = parts[part]
        copy = remote(
            own_ref.at[:, pl.ds(start, size)],
            block(part, 0),
            core_send.at[part, 0],
            core_recv.at[part, 0],
            other_core,
        )
        copy.start()
        sends.append(copy)
    keep.start()
    for index in range(1, held):
        for part in range(bits):
            arrived = block(part, index)
            remote(arrived, arrived, chip_send.at[part, index], chip_recv.at[part, index], other_core).wait_recv()
            for step in range(index.bit_length(), bits):
                send(part, index, step)
            copy = remote(arrived, arrived, core_send.at[part, index], core_recv.at[part, index], other_core)
            copy.start()
            sends.append(copy)
    for copy in sends:
        copy.wait_send()
    for part in range(bits):
        for index in range(held):
            arrived = block(part, index)
            remote(arrived, arrived, core_send.at[part, index], core_recv.at[part, index], other_core).wait_recv()
    keep.wait()


def gather_kernel(n, x_ref, out_ref, *sems):
    gather_body(n, x_ref, out_ref, *sems)


def gather_sems(n):
    bits = chip_bits(n)
    dma = pltpu.SemaphoreType.DMA
    return [dma(())] + [dma((bits, 2**bits))] * 4


def gather_rows(x, n, collective_id):
    rows, width = x.shape
    return pl.pallas_call(
        functools.partial(gather_kernel, n),
        out_shape=jax.ShapeDtypeStruct((n * rows, width), x.dtype),
        in_specs=[pl.BlockSpec(memory_space=pltpu.VMEM)],
        out_specs=pl.BlockSpec(memory_space=pl.ANY),
        scratch_shapes=gather_sems(n),
        compiler_params=pltpu.CompilerParams(
            collective_id=collective_id, has_side_effects=True, vmem_limit_bytes=VMEM_LIMIT
        ),
        name="gather_rows",
    )(x)


def scatter_kernel(n, chunk, transposed, a_ref, w_ref, out_ref, csend, crecv, held, recv, *sems):
    me = lax.axis_index("tensor")
    bits = chip_bits(n)
    core_send, core_recv, chip_send, chip_recv = sems
    rows, width = out_ref.shape
    chunks = rows // chunk
    parts = column_parts(width, bits)
    total = 2**bits
    other_core = flip(me, 0)
    greet(me, bits)

    def slot(part, index):
        at = me
        for step in range(bits):
            if (index >> (bits - 1 - step)) & 1:
                at = flip(at, 1 + (part + step) % bits)
        return at

    def product(at, j, part):
        start, size = parts[part]
        lhs = a_ref[pl.ds(pl.multiple_of(at * rows + j * chunk, chunk), chunk), :]
        if transposed:
            return lax.dot_general(
                lhs, w_ref[start : start + size, :], (((1,), (1,)), ((), ())), preferred_element_type=jnp.float32
            )
        return jnp.dot(lhs, w_ref[:, start : start + size], preferred_element_type=jnp.float32)

    def strip(ref, first, count, j, part):
        start, size = parts[part]
        return ref.at[pl.ds(first, count), pl.ds(pl.multiple_of(j * chunk, chunk), chunk), pl.ds(start, size)]

    def core_copy(j, part):
        return remote(
            strip(csend, 0, total, j, part),
            strip(crecv, 0, total, j, part),
            core_send.at[part, j],
            core_recv.at[part, j],
            other_core,
        )

    def chip_copy(j, part, step):
        half = total >> (step + 1)
        first = sum(total >> (s + 1) for s in range(step))
        return remote(
            strip(held, half, half, j, part),
            strip(recv, first, half, j, part),
            chip_send.at[part, step, j],
            chip_recv.at[part, step, j],
            flip(me, 1 + (part + step) % bits),
        )

    def rows_of(j):
        return pl.ds(pl.multiple_of(j * chunk, chunk), chunk)

    def stage_core(j):
        for part in range(bits):
            start, size = parts[part]
            for index in range(total):
                csend[index, rows_of(j), start : start + size] = product(
                    flip(slot(part, index), 0), j, part
                ).astype(csend.dtype)
            core_copy(j, part).start()

    def stage_first(j):
        for part in range(bits):
            start, size = parts[part]
            core_copy(j, part).wait_recv()
            for index in reversed(range(total)):
                value = product(slot(part, index), j, part) + crecv[index, rows_of(j), start : start + size].astype(
                    jnp.float32
                )
                if index:
                    held[index, rows_of(j), start : start + size] = value.astype(held.dtype)
                else:
                    out_ref[rows_of(j), start : start + size] = value
            chip_copy(j, part, 0).start()

    def stage_next(j, step):
        half = total >> (step + 1)
        first = sum(total >> (s + 1) for s in range(step))
        for part in range(bits):
            start, size = parts[part]
            chip_copy(j, part, step).wait_recv()
            for index in reversed(range(half)):
                got = recv[first + index, rows_of(j), start : start + size].astype(jnp.float32)
                if index:
                    value = held[index, rows_of(j), start : start + size].astype(jnp.float32) + got
                    held[index, rows_of(j), start : start + size] = value.astype(held.dtype)
                else:
                    out_ref[rows_of(j), start : start + size] += got
            if step + 1 < bits:
                chip_copy(j, part, step + 1).start()

    def body(u, carry):
        for stage in range(bits + 2):
            j = u - stage

            @pl.when((j >= 0) & (j < chunks))
            def _():
                if stage == 0:
                    stage_core(j)
                elif stage == 1:
                    stage_first(j)
                else:
                    stage_next(j, stage - 2)

        return carry

    lax.fori_loop(0, chunks + bits + 1, body, 0)

    def drain(j, carry):
        for part in range(bits):
            core_copy(j, part).wait_send()
            for step in range(bits):
                chip_copy(j, part, step).wait_send()
        return carry

    lax.fori_loop(0, chunks, drain, 0)


def scatter_rows(a, w, n, collective_id, transposed=False, chunks=4):
    rows = a.shape[0] // n
    width = w.shape[0] if transposed else w.shape[1]
    bits = chip_bits(n)
    total = 2**bits
    chunk = rows // chunks
    dma = pltpu.SemaphoreType.DMA
    return pl.pallas_call(
        functools.partial(scatter_kernel, n, chunk, transposed),
        out_shape=jax.ShapeDtypeStruct((rows, width), jnp.float32),
        in_specs=[pl.BlockSpec(memory_space=pltpu.VMEM)] * 2,
        out_specs=pl.BlockSpec(memory_space=pltpu.VMEM),
        scratch_shapes=[
            pltpu.VMEM((total, rows, width), jnp.bfloat16),
            pltpu.VMEM((total, rows, width), jnp.bfloat16),
            pltpu.VMEM((total, rows, width), jnp.bfloat16),
            pltpu.VMEM((total - 1, rows, width), jnp.bfloat16),
            dma((bits, chunks)),
            dma((bits, chunks)),
            dma((bits, bits, chunks)),
            dma((bits, bits, chunks)),
        ],
        compiler_params=pltpu.CompilerParams(
            collective_id=collective_id, has_side_effects=True, vmem_limit_bytes=VMEM_LIMIT
        ),
        name="scatter_rows",
    )(a, w)


HEAD_DIM = 128
LOG2E = 1.4426950408889634
SCALE = 1.0 / math.sqrt(HEAD_DIM)
BLOCK = 256
NT = (((1,), (1,)), ((), ()))
TN = (((0,), (0,)), ((), ()))


def masked_scores(slope, q, keys, query_labels, key_labels, first):
    raw = lax.dot_general(q, keys, NT, preferred_element_type=jnp.float32)
    rows, width = raw.shape
    column = lax.broadcasted_iota(jnp.int32, (1, width), 1)
    bias = column.astype(jnp.float32) * slope
    same = query_labels == key_labels
    causal = lax.broadcasted_iota(jnp.int32, (rows, width), 1) <= first + lax.broadcasted_iota(
        jnp.int32, (rows, width), 0
    )
    return jnp.where(same & causal, raw * (SCALE * LOG2E) + bias, -1e30)


def attend_kernel(slope_ref, q_ref, k_ref, v_ref, column_ref, row_ref, out_ref):
    slope = slope_ref[pl.program_id(1)]
    length = q_ref.shape[0]
    for first in range(0, length, BLOCK):
        last = first + BLOCK
        scores = masked_scores(
            slope,
            q_ref[first:last, :],
            k_ref[:last, :],
            column_ref[0, first:last, :],
            row_ref[0, :, :last],
            first,
        )
        top = jnp.max(scores, axis=1, keepdims=True)
        expo = jnp.exp2(scores - top)
        total = jnp.sum(expo, axis=1, keepdims=True)
        mixed = jnp.dot(expo.astype(jnp.bfloat16), v_ref[:last, :], preferred_element_type=jnp.float32)
        out_ref[first:last, :] = (mixed / total).astype(out_ref.dtype)


def attend(proj, slopes, labels, length):
    rows, width = proj.shape
    heads = width // (3 * HEAD_DIM)
    sequences = rows // length
    part = lambda which: pl.BlockSpec((length, HEAD_DIM), lambda s, h: (s, h * 3 + which))
    return pl.pallas_call(
        attend_kernel,
        grid=(sequences, heads),
        in_specs=[
            pl.BlockSpec(memory_space=pltpu.SMEM),
            part(0),
            part(1),
            part(2),
            pl.BlockSpec((1, length, 1), lambda s, h: (s, 0, 0)),
            pl.BlockSpec((1, 1, length), lambda s, h: (s, 0, 0)),
        ],
        out_specs=pl.BlockSpec((length, HEAD_DIM), lambda s, h: (s, h)),
        out_shape=jax.ShapeDtypeStruct((rows, heads * HEAD_DIM), jnp.bfloat16),
        name="attend",
    )(slopes, proj, proj, proj, labels[:, :, None], labels[:, None, :])


def attend_back_kernel(slope_ref, q_ref, k_ref, v_ref, g_ref, column_ref, row_ref, out_ref, dk_ref, dv_ref):
    slope = slope_ref[pl.program_id(1)]
    length = q_ref.shape[0]
    for first in reversed(range(0, length, BLOCK)):
        last = first + BLOCK
        q, g = q_ref[first:last, :], g_ref[first:last, :]
        scores = masked_scores(
            slope, q, k_ref[:last, :], column_ref[0, first:last, :], row_ref[0, :, :last], first
        )
        top = jnp.max(scores, axis=1, keepdims=True)
        expo = jnp.exp2(scores - top)
        probs = expo * (1.0 / jnp.sum(expo, axis=1, keepdims=True))
        grad_probs = lax.dot_general(g, v_ref[:last, :], NT, preferred_element_type=jnp.float32)
        product = probs * grad_probs
        grad_scores = (product - probs * jnp.sum(product, axis=1, keepdims=True)).astype(jnp.bfloat16)
        rounded = probs.astype(jnp.bfloat16)
        out_ref[first:last, :HEAD_DIM] = (
            jnp.dot(grad_scores, k_ref[:last, :], preferred_element_type=jnp.float32) * SCALE
        ).astype(out_ref.dtype)
        grad_keys = lax.dot_general(grad_scores, q, TN, preferred_element_type=jnp.float32)
        grad_values = lax.dot_general(rounded, g, TN, preferred_element_type=jnp.float32)
        if last == length:
            dk_ref[...] = grad_keys
            dv_ref[...] = grad_values
        else:
            dk_ref[:last, :] += grad_keys
            dv_ref[:last, :] += grad_values
    out_ref[:, HEAD_DIM : 2 * HEAD_DIM] = (dk_ref[...] * SCALE).astype(out_ref.dtype)
    out_ref[:, 2 * HEAD_DIM :] = dv_ref[...].astype(out_ref.dtype)


def attend_back(proj, grad_mixed, slopes, labels, length):
    rows, width = proj.shape
    heads = width // (3 * HEAD_DIM)
    sequences = rows // length
    part = lambda which: pl.BlockSpec((length, HEAD_DIM), lambda s, h: (s, h * 3 + which))
    return pl.pallas_call(
        attend_back_kernel,
        grid=(sequences, heads),
        in_specs=[
            pl.BlockSpec(memory_space=pltpu.SMEM),
            part(0),
            part(1),
            part(2),
            pl.BlockSpec((length, HEAD_DIM), lambda s, h: (s, h)),
            pl.BlockSpec((1, length, 1), lambda s, h: (s, 0, 0)),
            pl.BlockSpec((1, 1, length), lambda s, h: (s, 0, 0)),
        ],
        out_specs=pl.BlockSpec((length, 3 * HEAD_DIM), lambda s, h: (s, h)),
        out_shape=jax.ShapeDtypeStruct((rows, width), jnp.bfloat16),
        scratch_shapes=[pltpu.VMEM((length, HEAD_DIM), jnp.float32)] * 2,
        name="attend_back",
    )(slopes, proj, proj, proj, grad_mixed, labels[:, :, None], labels[:, None, :])


HEADS = 16


def gelu_tanh(value):
    return (
        0.5
        * value
        * (1.0 + jnp.tanh(0.7978845608028654 * (value + 0.044715 * value * value * value)))
    )


def normalize(rows):
    center = rows - jnp.mean(rows, axis=1, keepdims=True)
    factor = lax.rsqrt(jnp.mean(center * center, axis=1, keepdims=True) + 1e-05)
    return (center * factor, factor)


def norm_back(grad_out, normed, factor, gain):
    scaled = grad_out * gain
    return factor * (
        scaled
        - jnp.mean(scaled, axis=1, keepdims=True)
        - normed * jnp.mean(scaled * normed, axis=1, keepdims=True)
    )


def on_device(
    hidden_input,
    first_gain,
    first_shift,
    qkv_weight,
    query_bias,
    value_bias,
    dense_weight,
    dense_bias,
    second_gain,
    second_shift,
    up_weight,
    up_bias,
    down_weight,
    down_bias,
    segments,
    document_lengths,
    cotangent,
    *,
    n,
):
    heads_local = query_bias.shape[0] // HEAD_DIM
    first_gain32 = first_gain.astype(jnp.float32)
    second_gain32 = second_gain.astype(jnp.float32)
    inputs = hidden_input.astype(jnp.float32)
    normed_first, factor_first = normalize(inputs)
    attn_input = (normed_first * first_gain32 + first_shift.astype(jnp.float32)).astype(
        jnp.bfloat16
    )
    attn_rows = gather_rows(attn_input, n, 1)
    project_full, dense_full, expand_full, shrink_full = (
        lax.all_gather(qkv_weight, "dp", axis=0, tiled=True),
        lax.all_gather(dense_weight, "dp", axis=1, tiled=True),
        lax.all_gather(up_weight, "dp", axis=0, tiled=True),
        lax.all_gather(down_weight, "dp", axis=1, tiled=True),
    )
    group_rows = attn_rows.shape[0]
    sequences = document_lengths.shape[0]
    length = group_rows // sequences
    heads_index = lax.axis_index("tensor") * heads_local + lax.broadcasted_iota(
        jnp.int32, (heads_local,), 0
    )
    slopes = jnp.exp2(-8.0 * (heads_index.astype(jnp.float32) + 1.0) / HEADS) * LOG2E
    position = lax.broadcasted_iota(jnp.int32, (sequences, length), 1)
    filled = jnp.sum(document_lengths, axis=1, keepdims=True)
    labels = jnp.where(position < filled, segments.reshape(sequences, length), length + position)
    query_bias32 = query_bias.astype(jnp.float32).reshape(heads_local, HEAD_DIM)
    value_bias32 = value_bias.astype(jnp.float32).reshape(heads_local, HEAD_DIM)
    proj_bias = jnp.stack((query_bias32, jnp.zeros_like(query_bias32), value_bias32), axis=1).reshape(
        heads_local * 3 * HEAD_DIM
    )
    proj = (jnp.dot(attn_rows, project_full, preferred_element_type=jnp.float32) + proj_bias).astype(
        jnp.bfloat16
    )
    mixed = attend(proj, slopes, labels, length)
    attn_out = scatter_rows(mixed, dense_full, n, 2)
    residual = inputs + attn_out + dense_bias.astype(jnp.float32)
    normed_second, factor_second = normalize(residual)
    mlp_input = (normed_second * second_gain32 + second_shift.astype(jnp.float32)).astype(
        jnp.bfloat16
    )
    mlp_rows = gather_rows(mlp_input, n, 1)
    pre_act = jnp.dot(mlp_rows, expand_full, preferred_element_type=jnp.float32) + up_bias.astype(
        jnp.float32
    )
    activated = gelu_tanh(pre_act).astype(jnp.bfloat16)
    mlp_out = scatter_rows(activated, shrink_full, n, 3)
    hidden_output = (residual + mlp_out + down_bias.astype(jnp.float32)).astype(jnp.bfloat16)
    grad_rows = gather_rows(cotangent, n, 1)
    grad_down = jnp.einsum("tf,td->fd", activated, grad_rows, preferred_element_type=jnp.float32)
    grad_act = jnp.einsum("td,fd->tf", grad_rows, shrink_full, preferred_element_type=jnp.float32)
    grad_pre = jax.vjp(gelu_tanh, pre_act)[1](grad_act)[0].astype(jnp.bfloat16)
    grad_up = jnp.einsum("td,tf->df", mlp_rows, grad_pre, preferred_element_type=jnp.float32)
    sum_up_bias = jnp.sum(grad_pre.astype(jnp.float32), axis=0)
    grad_mlp_in = scatter_rows(grad_pre, expand_full, n, 4, transposed=True, chunks=2)
    cotangent32 = cotangent.astype(jnp.float32)
    grad_residual = cotangent32 + norm_back(
        grad_mlp_in, normed_second, factor_second, second_gain32
    )
    sum_second_gain = jnp.sum(grad_mlp_in * normed_second, axis=0)
    sum_second_shift = jnp.sum(grad_mlp_in, axis=0)
    sum_down_bias = jnp.sum(cotangent32, axis=0)
    sum_dense_bias = jnp.sum(grad_residual, axis=0)
    grad_attn_rows = gather_rows(grad_residual.astype(jnp.bfloat16), n, 1)
    grad_dense = jnp.einsum("tc,td->cd", mixed, grad_attn_rows, preferred_element_type=jnp.float32)
    grad_mixed = jnp.einsum(
        "td,cd->tc", grad_attn_rows, dense_full, preferred_element_type=jnp.float32
    ).astype(jnp.bfloat16)
    grad_proj = attend_back(proj, grad_mixed, slopes, labels, length)
    proj_sums = jnp.sum(grad_proj.astype(jnp.float32), axis=0).reshape(heads_local, 3, HEAD_DIM)
    sum_query_bias = proj_sums[:, 0].reshape(heads_local * HEAD_DIM)
    sum_value_bias = proj_sums[:, 2].reshape(heads_local * HEAD_DIM)
    grad_project = jnp.einsum("td,tc->dc", attn_rows, grad_proj, preferred_element_type=jnp.float32)
    grad_attn_in = scatter_rows(grad_proj, project_full, n, 5, transposed=True, chunks=2)
    grad_input = grad_residual + norm_back(grad_attn_in, normed_first, factor_first, first_gain32)
    sum_first_gain = jnp.sum(grad_attn_in * normed_first, axis=0)
    sum_first_shift = jnp.sum(grad_attn_in, axis=0)
    grad_qkv_weight, grad_dense_weight, grad_up_weight, grad_down_weight = (
        lax.psum_scatter(
            grad_project.astype(jnp.bfloat16), "dp", scatter_dimension=0, tiled=True
        ).astype(jnp.float32),
        lax.psum_scatter(
            grad_dense.astype(jnp.bfloat16), "dp", scatter_dimension=1, tiled=True
        ).astype(jnp.float32),
        lax.psum_scatter(
            grad_up.astype(jnp.bfloat16), "dp", scatter_dimension=0, tiled=True
        ).astype(jnp.float32),
        lax.psum_scatter(
            grad_down.astype(jnp.bfloat16), "dp", scatter_dimension=1, tiled=True
        ).astype(jnp.float32),
    )
    grad_query_bias, grad_value_bias, grad_up_bias = lax.psum(
        (sum_query_bias, sum_value_bias, sum_up_bias), "dp"
    )
    (
        grad_first_gain,
        grad_first_shift,
        grad_second_gain,
        grad_second_shift,
        grad_dense_bias,
        grad_down_bias,
    ) = lax.psum(
        (
            sum_first_gain,
            sum_first_shift,
            sum_second_gain,
            sum_second_shift,
            sum_dense_bias,
            sum_down_bias,
        ),
        ("dp", "tensor"),
    )
    return (
        hidden_output,
        grad_input,
        grad_first_gain,
        grad_first_shift,
        grad_qkv_weight,
        grad_query_bias,
        grad_value_bias,
        grad_dense_weight,
        grad_dense_bias,
        grad_second_gain,
        grad_second_shift,
        grad_up_weight,
        grad_up_bias,
        grad_down_weight,
        grad_down_bias,
    )


def solution(mesh):
    return jax.shard_map(
        functools.partial(on_device, n=mesh.shape["tensor"]),
        mesh=mesh,
        in_specs=(
            P(("dp", "tensor"), None),
            P(),
            P(),
            P("dp", "tensor"),
            P("tensor"),
            P("tensor"),
            P("tensor", "dp"),
            P(),
            P(),
            P(),
            P("dp", "tensor"),
            P("tensor"),
            P("tensor", "dp"),
            P(),
            P("dp"),
            P("dp", None),
            P(("dp", "tensor"), None),
        ),
        out_specs=(
            P(("dp", "tensor"), None),
            P(("dp", "tensor"), None),
            P(),
            P(),
            P("dp", "tensor"),
            P("tensor"),
            P("tensor"),
            P("tensor", "dp"),
            P(),
            P(),
            P(),
            P("dp", "tensor"),
            P("tensor"),
            P("tensor", "dp"),
            P(),
        ),
        check_vma=False,
    )
```

```python
import functools
import math

import jax
import jax.numpy as jnp
from jax import lax
from jax.experimental import pallas as pl
from jax.experimental.pallas import tpu as pltpu
from jax.sharding import PartitionSpec as P

VMEM_LIMIT = 62 << 20


def flip(index, bit):
    return index + (1 - 2 * ((index // 2**bit) % 2)) * 2**bit


def chip_bits(n):
    return n.bit_length() - 2


def column_parts(width, count):
    blocks = width // 128
    edges = [128 * (blocks * i // count) for i in range(count + 1)]
    return [(a, b - a) for a, b in zip(edges[:-1], edges[1:])]


def peer(index):
    return {"tensor": index}


def greet(me, bits):
    barrier = pltpu.get_barrier_semaphore()
    for bit in range(bits + 1):
        pl.semaphore_signal(
            barrier, inc=1, device_id=peer(flip(me, bit)), device_id_type=pl.DeviceIdType.MESH
        )
    pl.semaphore_wait(barrier, bits + 1)


def remote(src, dst, send_sem, recv_sem, target):
    return pltpu.make_async_remote_copy(
        src_ref=src,
        dst_ref=dst,
        send_sem=send_sem,
        recv_sem=recv_sem,
        device_id=peer(target),
        device_id_type=pl.DeviceIdType.MESH,
    )


class Gather:
    def __init__(self, n, own_ref, out_ref, sems):
        self.me = lax.axis_index("tensor")
        self.bits = chip_bits(n)
        self.rows, width = own_ref.shape
        self.parts = column_parts(width, self.bits)
        self.own, self.out = own_ref, out_ref
        self.own_sem, self.chip_send, self.chip_recv, self.core_send, self.core_recv = sems
        self.sends = []

    def slot(self, part, index):
        at = self.me
        for step in range(self.bits):
            if (index >> step) & 1:
                at = flip(at, 1 + (part + step) % self.bits)
        return at

    def place(self, mask, core):
        at = flip(self.me, 0) if core else self.me
        for bit in range(self.bits):
            if (mask >> bit) & 1:
                at = flip(at, 1 + bit)
        return at

    def index_of(self, part, mask):
        return sum(2 ** ((bit - part) % self.bits) for bit in range(self.bits) if (mask >> bit) & 1)

    def level(self, count):
        return [index for index in range(2**self.bits) if index.bit_count() == count]

    def block(self, part, index, core=0):
        start, size = self.parts[part]
        at = flip(self.slot(part, index), 0) if core else self.slot(part, index)
        return self.out.at[pl.ds(pl.multiple_of(at * self.rows, self.rows), self.rows), pl.ds(start, size)]

    def source(self, part, index):
        start, size = self.parts[part]
        return self.own.at[:, pl.ds(start, size)] if index == 0 else self.block(part, index)

    def send(self, part, index, step):
        arrives = index + 2**step
        copy = remote(
            self.source(part, index),
            self.block(part, index),
            self.chip_send.at[part, arrives],
            self.chip_recv.at[part, arrives],
            flip(self.me, 1 + (part + step) % self.bits),
        )
        copy.start()
        self.sends.append(copy)

    def hand_over(self, part, index):
        copy = remote(
            self.source(part, index),
            self.block(part, index),
            self.core_send.at[part, index],
            self.core_recv.at[part, index],
            flip(self.me, 0),
        )
        copy.start()
        self.sends.append(copy)

    def keep(self):
        rows = pl.ds(pl.multiple_of(self.me * self.rows, self.rows), self.rows)
        return pltpu.make_async_copy(self.own, self.out.at[rows, :], self.own_sem)

    def start(self):
        greet(self.me, self.bits)
        for step in range(self.bits):
            for part in range(self.bits):
                self.send(part, 0, step)
        for part in range(self.bits):
            self.hand_over(part, 0)
        self.keep().start()

    def forward(self, count):
        for index in self.level(count):
            for part in range(self.bits):
                arrived = self.block(part, index)
                remote(
                    arrived, arrived, self.chip_send.at[part, index], self.chip_recv.at[part, index], flip(self.me, 0)
                ).wait_recv()
                for step in range(index.bit_length(), self.bits):
                    self.send(part, index, step)
                self.hand_over(part, index)

    def wait_core(self, mask):
        for part in range(self.bits):
            index = self.index_of(part, mask)
            arrived = self.block(part, index, 1)
            remote(
                arrived, arrived, self.core_send.at[part, index], self.core_recv.at[part, index], flip(self.me, 0)
            ).wait_recv()

    def finish_sends(self):
        for copy in self.sends:
            copy.wait_send()


def gather_kernel(n, x_ref, out_ref, *sems):
    gather = Gather(n, x_ref, out_ref, sems)
    gather.start()
    for count in range(1, gather.bits + 1):
        gather.forward(count)
    for mask in range(2**gather.bits):
        gather.wait_core(mask)
    gather.finish_sends()
    gather.keep().wait()


def gather_sems(n):
    bits = chip_bits(n)
    dma = pltpu.SemaphoreType.DMA
    return [dma(())] + [dma((bits, 2**bits))] * 4


def gather_rows(x, n, collective_id):
    rows, width = x.shape
    return pl.pallas_call(
        functools.partial(gather_kernel, n),
        out_shape=jax.ShapeDtypeStruct((n * rows, width), x.dtype),
        in_specs=[pl.BlockSpec(memory_space=pltpu.VMEM)],
        out_specs=pl.BlockSpec(memory_space=pl.ANY),
        scratch_shapes=gather_sems(n),
        compiler_params=pltpu.CompilerParams(
            collective_id=collective_id, has_side_effects=True, vmem_limit_bytes=VMEM_LIMIT
        ),
        name="gather_rows",
    )(x)


def scatter_kernel(n, chunk, transposed, a_ref, w_ref, out_ref, csend, crecv, held, recv, *sems):
    me = lax.axis_index("tensor")
    bits = chip_bits(n)
    core_send, core_recv, chip_send, chip_recv = sems
    rows, width = out_ref.shape
    chunks = rows // chunk
    parts = column_parts(width, bits)
    total = 2**bits
    other_core = flip(me, 0)
    greet(me, bits)

    def slot(part, index):
        at = me
        for step in range(bits):
            if (index >> (bits - 1 - step)) & 1:
                at = flip(at, 1 + (part + step) % bits)
        return at

    def product(at, j, part):
        start, size = parts[part]
        lhs = a_ref[pl.ds(pl.multiple_of(at * rows + j * chunk, chunk), chunk), :]
        if transposed:
            return lax.dot_general(
                lhs, w_ref[start : start + size, :], (((1,), (1,)), ((), ())), preferred_element_type=jnp.float32
            )
        return jnp.dot(lhs, w_ref[:, start : start + size], preferred_element_type=jnp.float32)

    def strip(ref, first, count, j, part):
        start, size = parts[part]
        return ref.at[pl.ds(first, count), pl.ds(pl.multiple_of(j * chunk, chunk), chunk), pl.ds(start, size)]

    def core_copy(j, part):
        return remote(
            strip(csend, 0, total, j, part),
            strip(crecv, 0, total, j, part),
            core_send.at[part, j],
            core_recv.at[part, j],
            other_core,
        )

    def chip_copy(j, part, step):
        half = total >> (step + 1)
        first = sum(total >> (s + 1) for s in range(step))
        return remote(
            strip(held, half, half, j, part),
            strip(recv, first, half, j, part),
            chip_send.at[part, step, j],
            chip_recv.at[part, step, j],
            flip(me, 1 + (part + step) % bits),
        )

    def rows_of(j):
        return pl.ds(pl.multiple_of(j * chunk, chunk), chunk)

    def stage_core(j):
        for part in range(bits):
            start, size = parts[part]
            for index in range(total):
                csend[index, rows_of(j), start : start + size] = product(
                    flip(slot(part, index), 0), j, part
                ).astype(csend.dtype)
            core_copy(j, part).start()

    def stage_first(j):
        for part in range(bits):
            start, size = parts[part]
            core_copy(j, part).wait_recv()
            for index in reversed(range(total)):
                value = product(slot(part, index), j, part) + crecv[index, rows_of(j), start : start + size].astype(
                    jnp.float32
                )
                if index:
                    held[index, rows_of(j), start : start + size] = value.astype(held.dtype)
                else:
                    out_ref[rows_of(j), start : start + size] = value
            chip_copy(j, part, 0).start()

    def stage_next(j, step):
        half = total >> (step + 1)
        first = sum(total >> (s + 1) for s in range(step))
        for part in range(bits):
            start, size = parts[part]
            chip_copy(j, part, step).wait_recv()
            for index in reversed(range(half)):
                got = recv[first + index, rows_of(j), start : start + size].astype(jnp.float32)
                if index:
                    value = held[index, rows_of(j), start : start + size].astype(jnp.float32) + got
                    held[index, rows_of(j), start : start + size] = value.astype(held.dtype)
                else:
                    out_ref[rows_of(j), start : start + size] += got
            if step + 1 < bits:
                chip_copy(j, part, step + 1).start()

    def body(u, carry):
        for stage in range(bits + 2):
            j = u - stage

            @pl.when((j >= 0) & (j < chunks))
            def _():
                if stage == 0:
                    stage_core(j)
                elif stage == 1:
                    stage_first(j)
                else:
                    stage_next(j, stage - 2)

        return carry

    lax.fori_loop(0, chunks + bits + 1, body, 0)

    def drain(j, carry):
        for part in range(bits):
            core_copy(j, part).wait_send()
            for step in range(bits):
                chip_copy(j, part, step).wait_send()
        return carry

    lax.fori_loop(0, chunks, drain, 0)


def scatter_rows(a, w, n, collective_id, transposed=False, chunks=4):
    rows = a.shape[0] // n
    width = w.shape[0] if transposed else w.shape[1]
    bits = chip_bits(n)
    total = 2**bits
    chunk = rows // chunks
    dma = pltpu.SemaphoreType.DMA
    return pl.pallas_call(
        functools.partial(scatter_kernel, n, chunk, transposed),
        out_shape=jax.ShapeDtypeStruct((rows, width), jnp.float32),
        in_specs=[pl.BlockSpec(memory_space=pltpu.VMEM)] * 2,
        out_specs=pl.BlockSpec(memory_space=pltpu.VMEM),
        scratch_shapes=[
            pltpu.VMEM((total, rows, width), jnp.bfloat16),
            pltpu.VMEM((total, rows, width), jnp.bfloat16),
            pltpu.VMEM((total, rows, width), jnp.bfloat16),
            pltpu.VMEM((total - 1, rows, width), jnp.bfloat16),
            dma((bits, chunks)),
            dma((bits, chunks)),
            dma((bits, bits, chunks)),
            dma((bits, bits, chunks)),
        ],
        compiler_params=pltpu.CompilerParams(
            collective_id=collective_id, has_side_effects=True, vmem_limit_bytes=VMEM_LIMIT
        ),
        name="scatter_rows",
    )(a, w)


HEAD_DIM = 128
LOG2E = 1.4426950408889634
SCALE = 1.0 / math.sqrt(HEAD_DIM)
BLOCK = 256
NT = (((1,), (1,)), ((), ()))
TN = (((0,), (0,)), ((), ()))


def masked_scores(slope, q, keys, query_labels, key_labels, first):
    raw = lax.dot_general(q, keys, NT, preferred_element_type=jnp.float32)
    rows, width = raw.shape
    column = lax.broadcasted_iota(jnp.int32, (1, width), 1)
    bias = column.astype(jnp.float32) * slope
    same = query_labels == key_labels
    causal = lax.broadcasted_iota(jnp.int32, (rows, width), 1) <= first + lax.broadcasted_iota(
        jnp.int32, (rows, width), 0
    )
    return jnp.where(same & causal, raw * (SCALE * LOG2E) + bias, -1e30)


def attend_kernel(slope_ref, q_ref, k_ref, v_ref, column_ref, row_ref, out_ref):
    slope = slope_ref[pl.program_id(1)]
    length = q_ref.shape[0]
    for first in range(0, length, BLOCK):
        last = first + BLOCK
        scores = masked_scores(
            slope,
            q_ref[first:last, :],
            k_ref[:last, :],
            column_ref[0, first:last, :],
            row_ref[0, :, :last],
            first,
        )
        top = jnp.max(scores, axis=1, keepdims=True)
        expo = jnp.exp2(scores - top)
        total = jnp.sum(expo, axis=1, keepdims=True)
        mixed = jnp.dot(expo.astype(jnp.bfloat16), v_ref[:last, :], preferred_element_type=jnp.float32)
        out_ref[first:last, :] = (mixed / total).astype(out_ref.dtype)


def attend(proj, slopes, labels, length):
    rows, width = proj.shape
    heads = width // (3 * HEAD_DIM)
    sequences = rows // length
    part = lambda which: pl.BlockSpec((length, HEAD_DIM), lambda s, h: (s, h * 3 + which))
    return pl.pallas_call(
        attend_kernel,
        grid=(sequences, heads),
        in_specs=[
            pl.BlockSpec(memory_space=pltpu.SMEM),
            part(0),
            part(1),
            part(2),
            pl.BlockSpec((1, length, 1), lambda s, h: (s, 0, 0)),
            pl.BlockSpec((1, 1, length), lambda s, h: (s, 0, 0)),
        ],
        out_specs=pl.BlockSpec((length, HEAD_DIM), lambda s, h: (s, h)),
        out_shape=jax.ShapeDtypeStruct((rows, heads * HEAD_DIM), jnp.bfloat16),
        name="attend",
    )(slopes, proj, proj, proj, labels[:, :, None], labels[:, None, :])


def attend_back_kernel(slope_ref, q_ref, k_ref, v_ref, g_ref, column_ref, row_ref, out_ref, dk_ref, dv_ref):
    slope = slope_ref[pl.program_id(1)]
    length = q_ref.shape[0]
    for first in reversed(range(0, length, BLOCK)):
        last = first + BLOCK
        q, g = q_ref[first:last, :], g_ref[first:last, :]
        scores = masked_scores(
            slope, q, k_ref[:last, :], column_ref[0, first:last, :], row_ref[0, :, :last], first
        )
        top = jnp.max(scores, axis=1, keepdims=True)
        expo = jnp.exp2(scores - top)
        probs = expo * (1.0 / jnp.sum(expo, axis=1, keepdims=True))
        grad_probs = lax.dot_general(g, v_ref[:last, :], NT, preferred_element_type=jnp.float32)
        product = probs * grad_probs
        grad_scores = (product - probs * jnp.sum(product, axis=1, keepdims=True)).astype(jnp.bfloat16)
        rounded = probs.astype(jnp.bfloat16)
        out_ref[first:last, :HEAD_DIM] = (
            jnp.dot(grad_scores, k_ref[:last, :], preferred_element_type=jnp.float32) * SCALE
        ).astype(out_ref.dtype)
        grad_keys = lax.dot_general(grad_scores, q, TN, preferred_element_type=jnp.float32)
        grad_values = lax.dot_general(rounded, g, TN, preferred_element_type=jnp.float32)
        if last == length:
            dk_ref[...] = grad_keys
            dv_ref[...] = grad_values
        else:
            dk_ref[:last, :] += grad_keys
            dv_ref[:last, :] += grad_values
    out_ref[:, HEAD_DIM : 2 * HEAD_DIM] = (dk_ref[...] * SCALE).astype(out_ref.dtype)
    out_ref[:, 2 * HEAD_DIM :] = dv_ref[...].astype(out_ref.dtype)


def attend_back(proj, grad_mixed, slopes, labels, length):
    rows, width = proj.shape
    heads = width // (3 * HEAD_DIM)
    sequences = rows // length
    part = lambda which: pl.BlockSpec((length, HEAD_DIM), lambda s, h: (s, h * 3 + which))
    return pl.pallas_call(
        attend_back_kernel,
        grid=(sequences, heads),
        in_specs=[
            pl.BlockSpec(memory_space=pltpu.SMEM),
            part(0),
            part(1),
            part(2),
            pl.BlockSpec((length, HEAD_DIM), lambda s, h: (s, h)),
            pl.BlockSpec((1, length, 1), lambda s, h: (s, 0, 0)),
            pl.BlockSpec((1, 1, length), lambda s, h: (s, 0, 0)),
        ],
        out_specs=pl.BlockSpec((length, 3 * HEAD_DIM), lambda s, h: (s, h)),
        out_shape=jax.ShapeDtypeStruct((rows, width), jnp.bfloat16),
        scratch_shapes=[pltpu.VMEM((length, HEAD_DIM), jnp.float32)] * 2,
        name="attend_back",
    )(slopes, proj, proj, proj, grad_mixed, labels[:, :, None], labels[:, None, :])


def sum_kernel(n, d, flat_rows, x_ref, out_ref, pair, lines, send_sem, recv_sem, line_send, line_recv):
    me, z = lax.axis_index("tensor"), lax.axis_index("dp")
    levels = n.bit_length() - 1
    barrier = pltpu.get_barrier_semaphore()
    for level in range(levels):
        pl.semaphore_signal(
            barrier, inc=1, device_id=peer(flip(me, level)), device_id_type=pl.DeviceIdType.MESH
        )
    for ahead in range(1, d):
        pl.semaphore_signal(
            barrier, inc=1, device_id={"dp": lax.rem(z + ahead, d)}, device_id_type=pl.DeviceIdType.MESH
        )
    pl.semaphore_wait(barrier, levels + d - 1)
    pair[0] = x_ref[:flat_rows, :]
    sends = []
    for level in range(levels):
        copy = remote(
            pair.at[2 * level], pair.at[2 * level + 1], send_sem.at[level], recv_sem.at[level], flip(me, level)
        )
        copy.start()
        sends.append(copy)
        copy.wait_recv()
        pair[2 * level + 2] = pair[2 * level] + pair[2 * level + 1]
    lines[0, :flat_rows, :] = pair[2 * levels]
    lines[0, flat_rows:, :] = x_ref[flat_rows:, :]
    for ahead in range(1, d):
        copy = pltpu.make_async_remote_copy(
            src_ref=lines.at[0],
            dst_ref=lines.at[ahead],
            send_sem=line_send.at[ahead],
            recv_sem=line_recv.at[ahead],
            device_id={"dp": lax.rem(z + ahead, d)},
            device_id_type=pl.DeviceIdType.MESH,
        )
        copy.start()
        sends.append(copy)
    for copy in sends[levels:]:
        copy.wait_recv()

    total = None
    for index in range(d):
        value = lines[lax.rem(z - index + d, d)]
        total = value if total is None else total + value
    out_ref[...] = total
    for copy in sends:
        copy.wait_send()


def sum_small(x, flat_rows, n, d, collective_id):
    rows, width = x.shape
    levels = n.bit_length() - 1
    dma = pltpu.SemaphoreType.DMA
    return pl.pallas_call(
        functools.partial(sum_kernel, n, d, flat_rows),
        out_shape=jax.ShapeDtypeStruct((rows, width), jnp.float32),
        in_specs=[pl.BlockSpec(memory_space=pltpu.VMEM)],
        out_specs=pl.BlockSpec(memory_space=pltpu.VMEM),
        scratch_shapes=[
            pltpu.VMEM((2 * levels + 1, flat_rows, width), jnp.float32),
            pltpu.VMEM((d, rows, width), jnp.float32),
            dma((levels,)),
            dma((levels,)),
            dma((d,)),
            dma((d,)),
        ],
        compiler_params=pltpu.CompilerParams(collective_id=collective_id, has_side_effects=True),
        name="sum_small",
    )(x)


def tile_of(width):
    return 256 if width % 256 == 0 else width


def attend_one(slope, proj_ref, start, head, column_ref, row_ref, out_ref, length):
    at = pl.multiple_of(head * 3 * HEAD_DIM, HEAD_DIM)

    def take(which, first, size):
        return proj_ref[pl.ds(start + first, size), pl.ds(at + which * HEAD_DIM, HEAD_DIM)]

    for first in range(0, length, BLOCK):
        last = first + BLOCK
        scores = masked_scores(
            slope, take(0, first, BLOCK), take(1, 0, last), column_ref[first:last, :], row_ref[:, :last], first
        )
        top = jnp.max(scores, axis=1, keepdims=True)
        expo = jnp.exp2(scores - top)
        total = jnp.sum(expo, axis=1, keepdims=True)
        mixed = jnp.dot(expo.astype(jnp.bfloat16), take(2, 0, last), preferred_element_type=jnp.float32)
        out_ref[pl.ds(start + first, BLOCK), pl.ds(pl.multiple_of(head * HEAD_DIM, HEAD_DIM), HEAD_DIM)] = (
            mixed / total
        ).astype(out_ref.dtype)


def project_kernel(
    n, length, slope_ref, own_ref, rows_hbm, w_ref, bias_ref, column_ref, row_ref, gathered, proj_hbm, mixed_ref,
    proj, buf, load_sem, store_sem, *sems
):
    gather = Gather(n, own_ref, gathered, sems)
    rows = own_ref.shape[0]
    width = w_ref.shape[1]
    tile = tile_of(width)
    heads = width // (3 * HEAD_DIM)
    sequences = n * rows // length

    def load(i):
        at = pl.ds(pl.multiple_of(i * rows, rows), rows)
        return pltpu.make_async_copy(rows_hbm.at[at, :], buf.at[lax.rem(i, 2)], load_sem.at[lax.rem(i, 2)])

    load(0).start()
    gather.start()

    def store(i):
        at = pl.ds(pl.multiple_of(i * rows, rows), rows)
        return pltpu.make_async_copy(proj.at[at, :], proj_hbm.at[at, :], store_sem.at[i])

    def project(i, carry):
        load(i).wait()

        @pl.when(i + 1 < n)
        def _():
            load(i + 1).start()

        at = pl.ds(pl.multiple_of(i * rows, rows), rows)
        for first in range(0, width, tile):
            cols = slice(first, first + tile)
            proj[at, cols] = (
                jnp.dot(buf[lax.rem(i, 2)], w_ref[:, cols], preferred_element_type=jnp.float32) + bias_ref[:, cols]
            ).astype(proj.dtype)
        store(i).start()
        return carry

    lax.fori_loop(0, n, project, 0)
    gather.forward(1)

    def one(i, carry):
        s, head = i // heads, lax.rem(i, heads)
        attend_one(
            slope_ref[head],
            proj,
            pl.multiple_of(s * length, length),
            head,
            column_ref.at[s],
            row_ref.at[s],
            mixed_ref,
            length,
        )
        return carry

    lax.fori_loop(0, sequences * heads, one, 0)
    for count in range(2, gather.bits + 1):
        gather.forward(count)
    for i in range(n):
        store(i).wait()
    for mask in range(2**gather.bits):
        gather.wait_core(mask)
    gather.finish_sends()
    gather.keep().wait()


def project_attend(attn_rows, weight, bias, slopes, labels, own, n, collective_id):
    total, depth = attn_rows.shape
    rows, width = own.shape[0], weight.shape[1]
    heads = width // (3 * HEAD_DIM)
    vmem = pl.BlockSpec(memory_space=pltpu.VMEM)
    hbm = pl.BlockSpec(memory_space=pl.ANY)
    dma = pltpu.SemaphoreType.DMA
    return pl.pallas_call(
        functools.partial(project_kernel, n, labels.shape[1]),
        out_shape=(
            jax.ShapeDtypeStruct((total, own.shape[1]), own.dtype),
            jax.ShapeDtypeStruct((total, width), jnp.bfloat16),
            jax.ShapeDtypeStruct((total, heads * HEAD_DIM), jnp.bfloat16),
        ),
        in_specs=[pl.BlockSpec(memory_space=pltpu.SMEM), vmem, hbm, vmem, vmem, vmem, vmem],
        out_specs=(hbm, hbm, vmem),
        scratch_shapes=[
            pltpu.VMEM((total, width), jnp.bfloat16),
            pltpu.VMEM((2, rows, depth), jnp.bfloat16),
            dma((2,)),
            dma((n,)),
        ]
        + gather_sems(n),
        compiler_params=pltpu.CompilerParams(
            collective_id=collective_id, has_side_effects=True, vmem_limit_bytes=VMEM_LIMIT
        ),
        name="project_attend",
    )(slopes, own, attn_rows, weight, bias, labels[:, :, None], labels[:, None, :])


def gelu_both(value):
    c, a = 0.7978845608028654, 0.044715
    square = value * value
    half = 0.5 + 0.5 * jnp.tanh(value * (c + (c * a) * square))
    active = value * half
    slope = half + (2.0 * active) * (1.0 - half) * (c + (3.0 * c * a) * square)
    return active, slope


def expand_kernel(
    n, own_ref, grad_hbm, up_ref, down_ref, bias_ref, rows_hbm, act_hbm, pre_hbm, sum_ref,
    gathered, grads, act, pre, load_sem, act_sem, pre_sem, rows_sem, *sems
):
    gather = Gather(n, own_ref, gathered, sems)
    rows, depth = own_ref.shape
    width = up_ref.shape[1]
    tile = tile_of(width)
    order = [gather.place(mask, core) for mask in (0,) for core in (0, 1)]
    for count in range(1, gather.bits + 1):
        for core in (0, 1):
            order += [gather.place(mask, core) for mask in gather.level(count)]

    def span(at):
        return pl.ds(pl.multiple_of(at * rows, rows), rows)

    def load(i):
        return pltpu.make_async_copy(grad_hbm.at[span(order[i]), :], grads.at[i % 2], load_sem.at[i % 2])

    def store(i):
        return (
            pltpu.make_async_copy(act.at[i % 2], act_hbm.at[span(order[i]), :], act_sem.at[i % 2]),
            pltpu.make_async_copy(pre.at[i % 2], pre_hbm.at[span(order[i]), :], pre_sem.at[i % 2]),
        )

    def keep_rows(i):
        return pltpu.make_async_copy(gathered.at[span(order[i]), :], rows_hbm.at[span(order[i]), :], rows_sem.at[i])

    def work(i):
        at = order[i]
        keep_rows(i).start()
        load(i).wait()
        if i + 1 < n:
            load(i + 1).start()
        if i >= 2:
            for copy in store(i - 2):
                copy.wait()

        def columns(j, carry):
            cols = pl.ds(pl.multiple_of(j * tile, tile), tile)
            before = (
                jnp.dot(gathered[span(at), :], up_ref[:, cols], preferred_element_type=jnp.float32)
                + bias_ref[:, cols]
            )
            back = lax.dot_general(grads[i % 2], down_ref[cols, :], NT, preferred_element_type=jnp.float32)
            active, slope = gelu_both(before)
            act[i % 2, :, cols] = active.astype(act.dtype)
            rounded = (back * slope).astype(pre.dtype)
            pre[i % 2, :, cols] = rounded
            sum_ref[:, cols] += jnp.sum(rounded.astype(jnp.float32), axis=0, keepdims=True)
            return carry

        lax.fori_loop(0, width // tile, columns, 0)
        for copy in store(i):
            copy.start()

    sum_ref[...] = jnp.zeros_like(sum_ref)
    load(0).start()
    gather.start()
    gather.keep().wait()
    work(0)
    gather.wait_core(0)
    work(1)
    i = 2
    for count in range(1, gather.bits + 1):
        masks = gather.level(count)
        gather.forward(count)
        for _ in masks:
            work(i)
            i += 1
        for mask in masks:
            gather.wait_core(mask)
            work(i)
            i += 1
    for last in (n - 2, n - 1):
        for copy in store(last):
            copy.wait()
    for i in range(n):
        keep_rows(i).wait()
    gather.finish_sends()


def expand(own, grad_rows, up, down, bias, n, collective_id):
    rows, depth = own.shape
    width = up.shape[1]
    total = n * rows
    vmem = pl.BlockSpec(memory_space=pltpu.VMEM)
    hbm = pl.BlockSpec(memory_space=pl.ANY)
    dma = pltpu.SemaphoreType.DMA
    return pl.pallas_call(
        functools.partial(expand_kernel, n),
        out_shape=(
            jax.ShapeDtypeStruct((total, depth), jnp.bfloat16),
            jax.ShapeDtypeStruct((total, width), jnp.bfloat16),
            jax.ShapeDtypeStruct((total, width), jnp.bfloat16),
            jax.ShapeDtypeStruct((1, width), jnp.float32),
        ),
        in_specs=[vmem, hbm, vmem, vmem, vmem],
        out_specs=(hbm, hbm, hbm, vmem),
        scratch_shapes=[
            pltpu.VMEM((total, depth), jnp.bfloat16),
            pltpu.VMEM((2, rows, depth), jnp.bfloat16),
            pltpu.VMEM((2, rows, width), jnp.bfloat16),
            pltpu.VMEM((2, rows, width), jnp.bfloat16),
            dma((2,)),
            dma((2,)),
            dma((2,)),
            dma((n,)),
        ]
        + gather_sems(n),
        compiler_params=pltpu.CompilerParams(
            collective_id=collective_id, has_side_effects=True, vmem_limit_bytes=VMEM_LIMIT
        ),
        name="expand",
    )(own, grad_rows, up, down, bias)


HEADS = 16


def gelu_tanh(value):
    return (
        0.5
        * value
        * (1.0 + jnp.tanh(0.7978845608028654 * (value + 0.044715 * value * value * value)))
    )


def normalize(rows):
    center = rows - jnp.mean(rows, axis=1, keepdims=True)
    factor = lax.rsqrt(jnp.mean(center * center, axis=1, keepdims=True) + 1e-05)
    return (center * factor, factor)


def norm_back(grad_out, normed, factor, gain):
    scaled = grad_out * gain
    return factor * (
        scaled
        - jnp.mean(scaled, axis=1, keepdims=True)
        - normed * jnp.mean(scaled * normed, axis=1, keepdims=True)
    )


def on_device(
    hidden_input,
    first_gain,
    first_shift,
    qkv_weight,
    query_bias,
    value_bias,
    dense_weight,
    dense_bias,
    second_gain,
    second_shift,
    up_weight,
    up_bias,
    down_weight,
    down_bias,
    segments,
    document_lengths,
    cotangent,
    *,
    n,
    d,
):
    heads_local = query_bias.shape[0] // HEAD_DIM
    first_gain32 = first_gain.astype(jnp.float32)
    second_gain32 = second_gain.astype(jnp.float32)
    inputs = hidden_input.astype(jnp.float32)
    normed_first, factor_first = normalize(inputs)
    attn_input = (normed_first * first_gain32 + first_shift.astype(jnp.float32)).astype(
        jnp.bfloat16
    )
    attn_rows = gather_rows(attn_input, n, 1)
    project_full, dense_full, expand_full, shrink_full = (
        lax.all_gather(qkv_weight, "dp", axis=0, tiled=True),
        lax.all_gather(dense_weight, "dp", axis=1, tiled=True),
        lax.all_gather(up_weight, "dp", axis=0, tiled=True),
        lax.all_gather(down_weight, "dp", axis=1, tiled=True),
    )
    group_rows = attn_rows.shape[0]
    sequences = document_lengths.shape[0]
    length = group_rows // sequences
    heads_index = lax.axis_index("tensor") * heads_local + lax.broadcasted_iota(
        jnp.int32, (heads_local,), 0
    )
    slopes = jnp.exp2(-8.0 * (heads_index.astype(jnp.float32) + 1.0) / HEADS) * LOG2E
    position = lax.broadcasted_iota(jnp.int32, (sequences, length), 1)
    filled = jnp.sum(document_lengths, axis=1, keepdims=True)
    labels = jnp.where(position < filled, segments.reshape(sequences, length), length + position)
    query_bias32 = query_bias.astype(jnp.float32).reshape(heads_local, HEAD_DIM)
    value_bias32 = value_bias.astype(jnp.float32).reshape(heads_local, HEAD_DIM)
    proj_bias = jnp.stack((query_bias32, jnp.zeros_like(query_bias32), value_bias32), axis=1).reshape(
        heads_local * 3 * HEAD_DIM
    )
    grad_rows, proj, mixed = project_attend(
        attn_rows, project_full, proj_bias[None], slopes, labels, cotangent, n, 6
    )
    attn_out = scatter_rows(mixed, dense_full, n, 2)
    residual = inputs + attn_out + dense_bias.astype(jnp.float32)
    normed_second, factor_second = normalize(residual)
    mlp_input = (normed_second * second_gain32 + second_shift.astype(jnp.float32)).astype(
        jnp.bfloat16
    )
    mlp_rows, activated, grad_pre, sum_up_bias = expand(
        mlp_input, grad_rows, expand_full, shrink_full, up_bias.astype(jnp.float32)[None], n, 7
    )
    mlp_out = scatter_rows(activated, shrink_full, n, 3)
    hidden_output = (residual + mlp_out + down_bias.astype(jnp.float32)).astype(jnp.bfloat16)
    grad_down = jnp.einsum("tf,td->fd", activated, grad_rows, preferred_element_type=jnp.float32)
    grad_up = jnp.einsum("td,tf->df", mlp_rows, grad_pre, preferred_element_type=jnp.float32)
    grad_mlp_in = scatter_rows(grad_pre, expand_full, n, 4, transposed=True, chunks=2)
    cotangent32 = cotangent.astype(jnp.float32)
    grad_residual = cotangent32 + norm_back(
        grad_mlp_in, normed_second, factor_second, second_gain32
    )
    sum_second_gain = jnp.sum(grad_mlp_in * normed_second, axis=0)
    sum_second_shift = jnp.sum(grad_mlp_in, axis=0)
    sum_down_bias = jnp.sum(cotangent32, axis=0)
    sum_dense_bias = jnp.sum(grad_residual, axis=0)
    grad_attn_rows = gather_rows(grad_residual.astype(jnp.bfloat16), n, 1)
    grad_dense = jnp.einsum("tc,td->cd", mixed, grad_attn_rows, preferred_element_type=jnp.float32)
    grad_mixed = jnp.einsum(
        "td,cd->tc", grad_attn_rows, dense_full, preferred_element_type=jnp.float32
    ).astype(jnp.bfloat16)
    grad_proj = attend_back(proj, grad_mixed, slopes, labels, length)
    proj_sums = jnp.sum(grad_proj.astype(jnp.float32), axis=0).reshape(heads_local, 3, HEAD_DIM)
    sum_query_bias = proj_sums[:, 0].reshape(heads_local * HEAD_DIM)
    sum_value_bias = proj_sums[:, 2].reshape(heads_local * HEAD_DIM)
    grad_project = jnp.einsum("td,tc->dc", attn_rows, grad_proj, preferred_element_type=jnp.float32)
    grad_attn_in = scatter_rows(grad_proj, project_full, n, 5, transposed=True, chunks=2)
    grad_input = grad_residual + norm_back(grad_attn_in, normed_first, factor_first, first_gain32)
    sum_first_gain = jnp.sum(grad_attn_in * normed_first, axis=0)
    sum_first_shift = jnp.sum(grad_attn_in, axis=0)
    grad_qkv_weight, grad_dense_weight, grad_up_weight, grad_down_weight = (
        lax.psum_scatter(
            grad_project.astype(jnp.bfloat16), "dp", scatter_dimension=0, tiled=True
        ).astype(jnp.float32),
        lax.psum_scatter(
            grad_dense.astype(jnp.bfloat16), "dp", scatter_dimension=1, tiled=True
        ).astype(jnp.float32),
        lax.psum_scatter(
            grad_up.astype(jnp.bfloat16), "dp", scatter_dimension=0, tiled=True
        ).astype(jnp.float32),
        lax.psum_scatter(
            grad_down.astype(jnp.bfloat16), "dp", scatter_dimension=1, tiled=True
        ).astype(jnp.float32),
    )
    model = sum_first_gain.shape[0]
    heads_width = heads_local * HEAD_DIM
    biases = jnp.concatenate((sum_query_bias, sum_value_bias, sum_up_bias[0]))
    lines = -(-biases.shape[0] // model)
    sums = jnp.concatenate(
        (
            sum_first_gain,
            sum_first_shift,
            sum_second_gain,
            sum_second_shift,
            sum_dense_bias,
            sum_down_bias,
            jnp.zeros((2 * model,), jnp.float32),
            jnp.pad(biases, (0, -(-lines // 8) * 8 * model - biases.shape[0])),
        )
    ).reshape(-1, model)
    sums = sum_small(sums, 8, n, d, 8)
    grad_first_gain, grad_first_shift, grad_second_gain, grad_second_shift, grad_dense_bias, grad_down_bias = (
        sums[i] for i in range(6)
    )
    biases = sums[8:].reshape(-1)
    grad_query_bias = biases[:heads_width]
    grad_value_bias = biases[heads_width : 2 * heads_width]
    grad_up_bias = biases[2 * heads_width : 2 * heads_width + up_bias.shape[0]]
    return (
        hidden_output,
        grad_input,
        grad_first_gain,
        grad_first_shift,
        grad_qkv_weight,
        grad_query_bias,
        grad_value_bias,
        grad_dense_weight,
        grad_dense_bias,
        grad_second_gain,
        grad_second_shift,
        grad_up_weight,
        grad_up_bias,
        grad_down_weight,
        grad_down_bias,
    )


def solution(mesh):
    return jax.shard_map(
        functools.partial(on_device, n=mesh.shape["tensor"], d=mesh.shape["dp"]),
        mesh=mesh,
        in_specs=(
            P(("dp", "tensor"), None),
            P(),
            P(),
            P("dp", "tensor"),
            P("tensor"),
            P("tensor"),
            P("tensor", "dp"),
            P(),
            P(),
            P(),
            P("dp", "tensor"),
            P("tensor"),
            P("tensor", "dp"),
            P(),
            P("dp"),
            P("dp", None),
            P(("dp", "tensor"), None),
        ),
        out_specs=(
            P(("dp", "tensor"), None),
            P(("dp", "tensor"), None),
            P(),
            P(),
            P("dp", "tensor"),
            P("tensor"),
            P("tensor"),
            P("tensor", "dp"),
            P(),
            P(),
            P(),
            P("dp", "tensor"),
            P("tensor"),
            P("tensor", "dp"),
            P(),
        ),
        check_vma=False,
    )
```

```python
import functools
import math

import jax
import jax.numpy as jnp
from jax import lax
from jax.experimental import pallas as pl
from jax.experimental.pallas import tpu as pltpu
from jax.sharding import PartitionSpec as P

VMEM_LIMIT = 62 << 20


def flip(index, bit):
    return index + (1 - 2 * ((index // 2**bit) % 2)) * 2**bit


def chip_bits(n):
    return n.bit_length() - 2


def column_parts(width, count):
    blocks = width // 128
    edges = [128 * (blocks * i // count) for i in range(count + 1)]
    return [(a, b - a) for a, b in zip(edges[:-1], edges[1:])]


def peer(index):
    return {"tensor": index}


def greet(me, bits):
    barrier = pltpu.get_barrier_semaphore()
    for bit in range(bits + 1):
        pl.semaphore_signal(
            barrier, inc=1, device_id=peer(flip(me, bit)), device_id_type=pl.DeviceIdType.MESH
        )
    pl.semaphore_wait(barrier, bits + 1)


def remote(src, dst, send_sem, recv_sem, target):
    return pltpu.make_async_remote_copy(
        src_ref=src,
        dst_ref=dst,
        send_sem=send_sem,
        recv_sem=recv_sem,
        device_id=peer(target),
        device_id_type=pl.DeviceIdType.MESH,
    )


class Gather:
    def __init__(self, n, own_ref, out_ref, sems):
        self.me = lax.axis_index("tensor")
        self.bits = chip_bits(n)
        self.rows, width = own_ref.shape
        self.parts = column_parts(width, self.bits)
        self.own, self.out = own_ref, out_ref
        self.own_sem, self.chip_send, self.chip_recv, self.core_send, self.core_recv = sems
        self.sends = []

    def slot(self, part, index):
        at = self.me
        for step in range(self.bits):
            if (index >> step) & 1:
                at = flip(at, 1 + (part + step) % self.bits)
        return at

    def place(self, mask, core):
        at = flip(self.me, 0) if core else self.me
        for bit in range(self.bits):
            if (mask >> bit) & 1:
                at = flip(at, 1 + bit)
        return at

    def index_of(self, part, mask):
        return sum(2 ** ((bit - part) % self.bits) for bit in range(self.bits) if (mask >> bit) & 1)

    def level(self, count):
        return [index for index in range(2**self.bits) if index.bit_count() == count]

    def block(self, part, index, core=0):
        start, size = self.parts[part]
        at = flip(self.slot(part, index), 0) if core else self.slot(part, index)
        return self.out.at[pl.ds(pl.multiple_of(at * self.rows, self.rows), self.rows), pl.ds(start, size)]

    def source(self, part, index):
        start, size = self.parts[part]
        return self.own.at[:, pl.ds(start, size)] if index == 0 else self.block(part, index)

    def send(self, part, index, step):
        arrives = index + 2**step
        copy = remote(
            self.source(part, index),
            self.block(part, index),
            self.chip_send.at[part, arrives],
            self.chip_recv.at[part, arrives],
            flip(self.me, 1 + (part + step) % self.bits),
        )
        copy.start()
        self.sends.append(copy)

    def hand_over(self, part, index):
        copy = remote(
            self.source(part, index),
            self.block(part, index),
            self.core_send.at[part, index],
            self.core_recv.at[part, index],
            flip(self.me, 0),
        )
        copy.start()
        self.sends.append(copy)

    def keep(self):
        rows = pl.ds(pl.multiple_of(self.me * self.rows, self.rows), self.rows)
        return pltpu.make_async_copy(self.own, self.out.at[rows, :], self.own_sem)

    def start(self):
        greet(self.me, self.bits)
        for step in range(self.bits):
            for part in range(self.bits):
                self.send(part, 0, step)
        for part in range(self.bits):
            self.hand_over(part, 0)
        self.keep().start()

    def forward(self, count):
        for index in self.level(count):
            for part in range(self.bits):
                arrived = self.block(part, index)
                remote(
                    arrived, arrived, self.chip_send.at[part, index], self.chip_recv.at[part, index], flip(self.me, 0)
                ).wait_recv()
                for step in range(index.bit_length(), self.bits):
                    self.send(part, index, step)
                self.hand_over(part, index)

    def wait_core(self, mask):
        for part in range(self.bits):
            index = self.index_of(part, mask)
            arrived = self.block(part, index, 1)
            remote(
                arrived, arrived, self.core_send.at[part, index], self.core_recv.at[part, index], flip(self.me, 0)
            ).wait_recv()

    def finish_sends(self):
        for copy in self.sends:
            copy.wait_send()


def gather_kernel(n, x_ref, out_ref, *sems):
    gather = Gather(n, x_ref, out_ref, sems)
    gather.start()
    for count in range(1, gather.bits + 1):
        gather.forward(count)
    for mask in range(2**gather.bits):
        gather.wait_core(mask)
    gather.finish_sends()
    gather.keep().wait()


def gather_sems(n):
    bits = chip_bits(n)
    dma = pltpu.SemaphoreType.DMA
    return [dma(())] + [dma((bits, 2**bits))] * 4


def gather_rows(x, n, collective_id):
    rows, width = x.shape
    return pl.pallas_call(
        functools.partial(gather_kernel, n),
        out_shape=jax.ShapeDtypeStruct((n * rows, width), x.dtype),
        in_specs=[pl.BlockSpec(memory_space=pltpu.VMEM)],
        out_specs=pl.BlockSpec(memory_space=pl.ANY),
        scratch_shapes=gather_sems(n),
        compiler_params=pltpu.CompilerParams(
            collective_id=collective_id, has_side_effects=True, vmem_limit_bytes=VMEM_LIMIT
        ),
        name="gather_rows",
    )(x)


class Scatter:
    def __init__(self, n, transposed, a_hbm, w_ref, out_ref, scratch):
        (self.csend, self.crecv, self.recv, self.other, self.mine, self.load_sem) = scratch[:6]
        self.core_send, self.core_recv, self.chip_send, self.chip_recv = scratch[6:]
        self.me = lax.axis_index("tensor")
        self.bits = chip_bits(n)
        self.total = 2**self.bits
        self.transposed = transposed
        self.a, self.w, self.out = a_hbm, w_ref, out_ref
        self.rows, width = out_ref.shape
        self.chunk = self.csend.shape[2]
        self.chunks = self.rows // self.chunk
        self.parts = column_parts(width, self.bits)

    def index_of(self, part, mask):
        top = self.bits - 1
        return sum(2 ** (top - (bit - part) % self.bits) for bit in range(self.bits) if (mask >> bit) & 1)

    def place(self, mask, core):
        at = flip(self.me, 0) if core else self.me
        for bit in range(self.bits):
            if (mask >> bit) & 1:
                at = flip(at, 1 + bit)
        return at

    def rows_of(self, j):
        return pl.ds(pl.multiple_of(j * self.chunk, self.chunk), self.chunk)

    def loads(self, j, core):
        into = self.other if core else self.mine
        copies = []
        for mask in range(self.total):
            start = pl.multiple_of(self.place(mask, core) * self.rows + j * self.chunk, self.chunk)
            copies.append(
                pltpu.make_async_copy(
                    self.a.at[pl.ds(start, self.chunk), :],
                    into.at[lax.rem(j, 2), pl.ds(mask * self.chunk, self.chunk), :],
                    self.load_sem.at[core, lax.rem(j, 2), mask],
                )
            )
        return copies

    def core_copy(self, j, part):
        start, size = self.parts[part]
        return remote(
            self.csend.at[lax.rem(j, 2), :, :, pl.ds(start, size)],
            self.crecv.at[:, self.rows_of(j), pl.ds(start, size)],
            self.core_send.at[part, j],
            self.core_recv.at[part, j],
            flip(self.me, 0),
        )

    def chip_copy(self, j, part, step):
        half = self.total >> (step + 1)
        first = sum(self.total >> (s + 1) for s in range(step))
        start, size = self.parts[part]
        return remote(
            self.crecv.at[pl.ds(half, half), self.rows_of(j), pl.ds(start, size)],
            self.recv.at[pl.ds(first, half), self.rows_of(j), pl.ds(start, size)],
            self.chip_send.at[part, step, j],
            self.chip_recv.at[part, step, j],
            flip(self.me, 1 + (part + step) % self.bits),
        )

    def tiles(self, part, lhs, put):
        start, size = self.parts[part]
        tile = 256 if size % 256 == 0 and start % 256 == 0 else 128

        def one(i, carry):
            cols = pl.ds(pl.multiple_of(start + i * tile, tile), tile)
            if self.transposed:
                value = lax.dot_general(
                    lhs[...], self.w[cols, :], (((1,), (1,)), ((), ())), preferred_element_type=jnp.float32
                )
            else:
                value = jnp.dot(lhs[...], self.w[:, cols], preferred_element_type=jnp.float32)
            put(cols, value)
            return carry

        lax.fori_loop(0, size // tile, one, 0)

    def piece(self, value, mask):
        return value[mask * self.chunk : (mask + 1) * self.chunk, :]

    def stage_core(self, j):
        for copy in self.loads(j, 1):
            copy.wait()

        @pl.when(j >= 2)
        def _():
            for part in range(self.bits):
                self.core_copy(j - 2, part).wait_send()

        for part in range(self.bits):

            def put(cols, value):
                for mask in range(self.total):
                    self.csend[lax.rem(j, 2), self.index_of(part, mask), :, cols] = self.piece(value, mask).astype(
                        self.csend.dtype
                    )

            self.tiles(part, self.other.at[lax.rem(j, 2)], put)
            self.core_copy(j, part).start()

    def stage_first(self, j):
        for copy in self.loads(j, 0):
            copy.wait()
        for part in range(self.bits):
            self.core_copy(j, part).wait_recv()

            def put(cols, value):
                for mask in range(self.total):
                    index = self.index_of(part, mask)
                    got = self.piece(value, mask) + self.crecv[index, self.rows_of(j), cols].astype(jnp.float32)
                    if index:
                        self.crecv[index, self.rows_of(j), cols] = got.astype(self.crecv.dtype)
                    else:
                        self.out[self.rows_of(j), cols] = got

            self.tiles(part, self.mine.at[lax.rem(j, 2)], put)
            self.chip_copy(j, part, 0).start()

    def stage_next(self, j, step):
        half = self.total >> (step + 1)
        first = sum(self.total >> (s + 1) for s in range(step))
        for part in range(self.bits):
            start, size = self.parts[part]
            cols = slice(start, start + size)
            self.chip_copy(j, part, step).wait_recv()
            for index in reversed(range(half)):
                got = self.recv[first + index, self.rows_of(j), cols].astype(jnp.float32)
                if index:
                    value = self.crecv[index, self.rows_of(j), cols].astype(jnp.float32) + got
                    self.crecv[index, self.rows_of(j), cols] = value.astype(self.crecv.dtype)
                else:
                    self.out[self.rows_of(j), cols] += got
            if step + 1 < self.bits:
                self.chip_copy(j, part, step + 1).start()

    def run(self, filler=None):
        for copy in self.loads(0, 1):
            copy.start()
        greet(self.me, self.bits)

        def body(u, carry):
            @pl.when(u + 1 < self.chunks)
            def _():
                for copy in self.loads(u + 1, 1):
                    copy.start()

            @pl.when(u < self.chunks)
            def _():
                for copy in self.loads(u, 0):
                    copy.start()
                self.stage_core(u)

            @pl.when((u >= 1) & (u <= self.chunks))
            def _():
                self.stage_first(u - 1)

            for step in range(self.bits):

                @pl.when((u >= 2 + step) & (u < self.chunks + 2 + step))
                def _():
                    self.stage_next(u - 2 - step, step)

            if filler is not None:

                @pl.when((u >= 1) & (u <= self.chunks))
                def _():
                    filler(u - 1)

            return carry

        lax.fori_loop(0, self.chunks + self.bits + 1, body, 0)
        for part in range(self.bits):
            for j in range(self.chunks):
                if j >= self.chunks - 2:
                    self.core_copy(j, part).wait_send()
                for step in range(self.bits):
                    self.chip_copy(j, part, step).wait_send()


def scatter_scratch(n, rows, depth, width, chunks):
    bits = chip_bits(n)
    total = 2**bits
    chunk = rows // chunks
    dma = pltpu.SemaphoreType.DMA
    return [
        pltpu.VMEM((2, total, chunk, width), jnp.bfloat16),
        pltpu.VMEM((total, rows, width), jnp.bfloat16),
        pltpu.VMEM((total - 1, rows, width), jnp.bfloat16),
        pltpu.VMEM((2, total * chunk, depth), jnp.bfloat16),
        pltpu.VMEM((2, total * chunk, depth), jnp.bfloat16),
        dma((2, 2, total)),
        dma((bits, chunks)),
        dma((bits, chunks)),
        dma((bits, bits, chunks)),
        dma((bits, bits, chunks)),
    ]


HEAD_DIM = 128
LOG2E = 1.4426950408889634
SCALE = 1.0 / math.sqrt(HEAD_DIM)
BLOCK = 256
NT = (((1,), (1,)), ((), ()))
TN = (((0,), (0,)), ((), ()))


def masked_scores(slope, q, keys, query_labels, key_labels, first):
    raw = lax.dot_general(q, keys, NT, preferred_element_type=jnp.float32)
    rows, width = raw.shape
    column = lax.broadcasted_iota(jnp.int32, (1, width), 1)
    bias = column.astype(jnp.float32) * slope
    same = query_labels == key_labels
    causal = lax.broadcasted_iota(jnp.int32, (rows, width), 1) <= first + lax.broadcasted_iota(
        jnp.int32, (rows, width), 0
    )
    return jnp.where(same & causal, raw * (SCALE * LOG2E) + bias, -1e30)


def sum_kernel(n, d, x_ref, y_ref, out_ref, pair, lines, send_sem, recv_sem, line_send, line_recv):
    flat_rows = x_ref.shape[0]
    me, z = lax.axis_index("tensor"), lax.axis_index("dp")
    levels = n.bit_length() - 1
    barrier = pltpu.get_barrier_semaphore()
    for level in range(levels):
        pl.semaphore_signal(
            barrier, inc=1, device_id=peer(flip(me, level)), device_id_type=pl.DeviceIdType.MESH
        )
    for ahead in range(1, d):
        pl.semaphore_signal(
            barrier, inc=1, device_id={"dp": lax.rem(z + ahead, d)}, device_id_type=pl.DeviceIdType.MESH
        )
    pl.semaphore_wait(barrier, levels + d - 1)
    pair[0] = x_ref[...]
    sends = []
    for level in range(levels):
        copy = remote(
            pair.at[2 * level], pair.at[2 * level + 1], send_sem.at[level], recv_sem.at[level], flip(me, level)
        )
        copy.start()
        sends.append(copy)
        copy.wait_recv()
        pair[2 * level + 2] = pair[2 * level] + pair[2 * level + 1]
    lines[0, :flat_rows, :] = pair[2 * levels]
    lines[0, flat_rows:, :] = y_ref[...]
    for ahead in range(1, d):
        copy = pltpu.make_async_remote_copy(
            src_ref=lines.at[0],
            dst_ref=lines.at[ahead],
            send_sem=line_send.at[ahead],
            recv_sem=line_recv.at[ahead],
            device_id={"dp": lax.rem(z + ahead, d)},
            device_id_type=pl.DeviceIdType.MESH,
        )
        copy.start()
        sends.append(copy)
    for copy in sends[levels:]:
        copy.wait_recv()

    total = None
    for index in range(d):
        value = lines[lax.rem(z - index + d, d)]
        total = value if total is None else total + value
    out_ref[...] = total
    for copy in sends:
        copy.wait_send()


def sum_small(x, y, n, d, collective_id):
    flat_rows, width = x.shape
    rows = flat_rows + y.shape[0]
    levels = n.bit_length() - 1
    dma = pltpu.SemaphoreType.DMA
    return pl.pallas_call(
        functools.partial(sum_kernel, n, d),
        out_shape=jax.ShapeDtypeStruct((rows, width), jnp.float32),
        in_specs=[pl.BlockSpec(memory_space=pltpu.VMEM)] * 2,
        out_specs=pl.BlockSpec(memory_space=pltpu.VMEM),
        scratch_shapes=[
            pltpu.VMEM((2 * levels + 1, flat_rows, width), jnp.float32),
            pltpu.VMEM((d, rows, width), jnp.float32),
            dma((levels,)),
            dma((levels,)),
            dma((d,)),
            dma((d,)),
        ],
        compiler_params=pltpu.CompilerParams(collective_id=collective_id, has_side_effects=True),
        name="sum_small",
    )(x, y)


def tile_of(width):
    return 256 if width % 256 == 0 else width


def attend_one(slope, proj_ref, start, head, column_ref, row_ref, out_ref, length):
    at = pl.multiple_of(head * 3 * HEAD_DIM, HEAD_DIM)

    def take(which, first, size):
        return proj_ref[pl.ds(start + first, size), pl.ds(at + which * HEAD_DIM, HEAD_DIM)]

    for first in range(0, length, BLOCK):
        last = first + BLOCK
        scores = masked_scores(
            slope, take(0, first, BLOCK), take(1, 0, last), column_ref[first:last, :], row_ref[:, :last], first
        )
        top = jnp.max(scores, axis=1, keepdims=True)
        expo = jnp.exp2(scores - top)
        total = jnp.sum(expo, axis=1, keepdims=True)
        mixed = jnp.dot(expo.astype(jnp.bfloat16), take(2, 0, last), preferred_element_type=jnp.float32)
        out_ref[pl.ds(start + first, BLOCK), pl.ds(pl.multiple_of(head * HEAD_DIM, HEAD_DIM), HEAD_DIM)] = (
            mixed / total
        ).astype(out_ref.dtype)


def project_kernel(
    n, length, slope_ref, own_ref, rows_hbm, w_ref, bias_ref, column_ref, row_ref, gathered, proj_hbm, mixed_ref,
    proj, buf, load_sem, store_sem, *sems
):
    gather = Gather(n, own_ref, gathered, sems)
    rows = own_ref.shape[0]
    width = w_ref.shape[1]
    tile = tile_of(width)
    heads = width // (3 * HEAD_DIM)
    sequences = n * rows // length

    def load(i):
        at = pl.ds(pl.multiple_of(i * rows, rows), rows)
        return pltpu.make_async_copy(rows_hbm.at[at, :], buf.at[lax.rem(i, 2)], load_sem.at[lax.rem(i, 2)])

    load(0).start()
    gather.start()

    def store(i):
        at = pl.ds(pl.multiple_of(i * rows, rows), rows)
        return pltpu.make_async_copy(proj.at[at, :], proj_hbm.at[at, :], store_sem.at[i])

    def project(i, carry):
        load(i).wait()

        @pl.when(i + 1 < n)
        def _():
            load(i + 1).start()

        at = pl.ds(pl.multiple_of(i * rows, rows), rows)
        for first in range(0, width, tile):
            cols = slice(first, first + tile)
            proj[at, cols] = (
                jnp.dot(buf[lax.rem(i, 2)], w_ref[:, cols], preferred_element_type=jnp.float32) + bias_ref[:, cols]
            ).astype(proj.dtype)
        store(i).start()
        return carry

    lax.fori_loop(0, n, project, 0)
    gather.forward(1)

    def one(i, carry):
        s, head = i // heads, lax.rem(i, heads)
        attend_one(
            slope_ref[head],
            proj,
            pl.multiple_of(s * length, length),
            head,
            column_ref.at[s],
            row_ref.at[s],
            mixed_ref,
            length,
        )
        return carry

    lax.fori_loop(0, sequences * heads, one, 0)
    for count in range(2, gather.bits + 1):
        gather.forward(count)
    for i in range(n):
        store(i).wait()
    for mask in range(2**gather.bits):
        gather.wait_core(mask)
    gather.finish_sends()
    gather.keep().wait()


def project_attend(attn_rows, weight, bias, slopes, labels, own, n, collective_id):
    total, depth = attn_rows.shape
    rows, width = own.shape[0], weight.shape[1]
    heads = width // (3 * HEAD_DIM)
    vmem = pl.BlockSpec(memory_space=pltpu.VMEM)
    hbm = pl.BlockSpec(memory_space=pl.ANY)
    dma = pltpu.SemaphoreType.DMA
    return pl.pallas_call(
        functools.partial(project_kernel, n, labels.shape[1]),
        out_shape=(
            jax.ShapeDtypeStruct((total, own.shape[1]), own.dtype),
            jax.ShapeDtypeStruct((total, width), jnp.bfloat16),
            jax.ShapeDtypeStruct((total, heads * HEAD_DIM), jnp.bfloat16),
        ),
        in_specs=[pl.BlockSpec(memory_space=pltpu.SMEM), vmem, hbm, vmem, vmem, vmem, vmem],
        out_specs=(hbm, hbm, vmem),
        scratch_shapes=[
            pltpu.VMEM((total, width), jnp.bfloat16),
            pltpu.VMEM((2, rows, depth), jnp.bfloat16),
            dma((2,)),
            dma((n,)),
        ]
        + gather_sems(n),
        compiler_params=pltpu.CompilerParams(
            collective_id=collective_id, has_side_effects=True, vmem_limit_bytes=VMEM_LIMIT
        ),
        name="project_attend",
    )(slopes, own, attn_rows, weight, bias, labels[:, :, None], labels[:, None, :])


def gelu_both(value):
    c, a = 0.7978845608028654, 0.044715
    square = value * value
    half = 0.5 + 0.5 * jnp.tanh(value * (c + (c * a) * square))
    active = value * half
    slope = half + (2.0 * active) * (1.0 - half) * (c + (3.0 * c * a) * square)
    return active, slope


def expand_kernel(
    n, own_ref, grad_hbm, up_ref, down_ref, bias_ref, rows_hbm, act_hbm, pre_hbm, sum_ref,
    gathered, grads, act, pre, load_sem, act_sem, pre_sem, rows_sem, *sems
):
    gather = Gather(n, own_ref, gathered, sems)
    rows, depth = own_ref.shape
    width = up_ref.shape[1]
    tile = tile_of(width)
    order = [gather.place(mask, core) for mask in (0,) for core in (0, 1)]
    for count in range(1, gather.bits + 1):
        for core in (0, 1):
            order += [gather.place(mask, core) for mask in gather.level(count)]

    def span(at):
        return pl.ds(pl.multiple_of(at * rows, rows), rows)

    def load(i):
        return pltpu.make_async_copy(grad_hbm.at[span(order[i]), :], grads.at[i % 2], load_sem.at[i % 2])

    def store(i):
        return (
            pltpu.make_async_copy(act.at[i % 2], act_hbm.at[span(order[i]), :], act_sem.at[i % 2]),
            pltpu.make_async_copy(pre.at[i % 2], pre_hbm.at[span(order[i]), :], pre_sem.at[i % 2]),
        )

    def keep_rows(i):
        return pltpu.make_async_copy(gathered.at[span(order[i]), :], rows_hbm.at[span(order[i]), :], rows_sem.at[i])

    def work(i):
        at = order[i]
        keep_rows(i).start()
        load(i).wait()
        if i + 1 < n:
            load(i + 1).start()
        if i >= 2:
            for copy in store(i - 2):
                copy.wait()

        def columns(j, carry):
            cols = pl.ds(pl.multiple_of(j * tile, tile), tile)
            before = (
                jnp.dot(gathered[span(at), :], up_ref[:, cols], preferred_element_type=jnp.float32)
                + bias_ref[:, cols]
            )
            back = lax.dot_general(grads[i % 2], down_ref[cols, :], NT, preferred_element_type=jnp.float32)
            active, slope = gelu_both(before)
            act[i % 2, :, cols] = active.astype(act.dtype)
            rounded = (back * slope).astype(pre.dtype)
            pre[i % 2, :, cols] = rounded
            sum_ref[:, cols] += jnp.sum(rounded.astype(jnp.float32), axis=0, keepdims=True)
            return carry

        lax.fori_loop(0, width // tile, columns, 0)
        for copy in store(i):
            copy.start()

    sum_ref[...] = jnp.zeros_like(sum_ref)
    load(0).start()
    gather.start()
    gather.keep().wait()
    work(0)
    gather.wait_core(0)
    work(1)
    i = 2
    for count in range(1, gather.bits + 1):
        masks = gather.level(count)
        gather.forward(count)
        for _ in masks:
            work(i)
            i += 1
        for mask in masks:
            gather.wait_core(mask)
            work(i)
            i += 1
    for last in (n - 2, n - 1):
        for copy in store(last):
            copy.wait()
    for i in range(n):
        keep_rows(i).wait()
    gather.finish_sends()


def expand(own, grad_rows, up, down, bias, n, collective_id):
    rows, depth = own.shape
    width = up.shape[1]
    total = n * rows
    vmem = pl.BlockSpec(memory_space=pltpu.VMEM)
    hbm = pl.BlockSpec(memory_space=pl.ANY)
    dma = pltpu.SemaphoreType.DMA
    return pl.pallas_call(
        functools.partial(expand_kernel, n),
        out_shape=(
            jax.ShapeDtypeStruct((total, depth), jnp.bfloat16),
            jax.ShapeDtypeStruct((total, width), jnp.bfloat16),
            jax.ShapeDtypeStruct((total, width), jnp.bfloat16),
            jax.ShapeDtypeStruct((1, width), jnp.float32),
        ),
        in_specs=[vmem, hbm, vmem, vmem, vmem],
        out_specs=(hbm, hbm, hbm, vmem),
        scratch_shapes=[
            pltpu.VMEM((total, depth), jnp.bfloat16),
            pltpu.VMEM((2, rows, depth), jnp.bfloat16),
            pltpu.VMEM((2, rows, width), jnp.bfloat16),
            pltpu.VMEM((2, rows, width), jnp.bfloat16),
            dma((2,)),
            dma((2,)),
            dma((2,)),
            dma((n,)),
        ]
        + gather_sems(n),
        compiler_params=pltpu.CompilerParams(
            collective_id=collective_id, has_side_effects=True, vmem_limit_bytes=VMEM_LIMIT
        ),
        name="expand",
    )(own, grad_rows, up, down, bias)


class Product:
    def __init__(self, left, right, out, scratch):
        self.left, self.right, self.out = left, right, out
        self.lbuf, self.rbuf, self.acc, self.obuf, self.left_sem, self.right_sem, self.out_sem = scratch
        self.depth, self.tall = self.lbuf.shape[1:]
        self.wide = self.rbuf.shape[2]
        self.inner = left.shape[0] // self.depth
        self.across = right.shape[1] // self.wide
        self.steps = (left.shape[1] // self.tall) * self.across * self.inner

    def load(self, i):
        k = lax.rem(i, self.inner)
        col = lax.rem(i // self.inner, self.across)
        row = i // (self.inner * self.across)
        rows = pl.ds(pl.multiple_of(k * self.depth, self.depth), self.depth)
        slot = lax.rem(i, 2)
        return (
            pltpu.make_async_copy(
                self.left.at[rows, pl.ds(pl.multiple_of(row * self.tall, self.tall), self.tall)],
                self.lbuf.at[slot],
                self.left_sem.at[slot],
            ),
            pltpu.make_async_copy(
                self.right.at[rows, pl.ds(pl.multiple_of(col * self.wide, self.wide), self.wide)],
                self.rbuf.at[slot],
                self.right_sem.at[slot],
            ),
        )

    def store(self, tile):
        col = lax.rem(tile, self.across)
        row = tile // self.across
        return pltpu.make_async_copy(
            self.obuf,
            self.out.at[
                pl.ds(pl.multiple_of(row * self.tall, self.tall), self.tall),
                pl.ds(pl.multiple_of(col * self.wide, self.wide), self.wide),
            ],
            self.out_sem,
        )

    def start(self):
        for copy in self.load(0):
            copy.start()

    def step(self, i, carry=0):
        for copy in self.load(i):
            copy.wait()

        @pl.when(i + 1 < self.steps)
        def _():
            for copy in self.load(i + 1):
                copy.start()

        k = lax.rem(i, self.inner)
        slot = lax.rem(i, 2)
        part = min(self.wide, 512)

        @pl.when(k == 0)
        def _():
            self.acc[...] = jnp.zeros_like(self.acc)

        for first in range(0, self.wide, part):
            cols = slice(first, first + part)
            self.acc[:, cols] += lax.dot_general(
                self.lbuf[slot], self.rbuf[slot, :, cols], TN, preferred_element_type=jnp.float32
            )

        @pl.when(k == self.inner - 1)
        def _():
            tile = i // self.inner

            @pl.when(tile > 0)
            def _():
                self.store(tile - 1).wait()

            self.obuf[...] = self.acc[...].astype(self.obuf.dtype)
            self.store(tile).start()

        return carry

    def batch(self, j, batches):
        per = -(-self.steps // batches)
        first = j * per
        lax.fori_loop(first, jnp.minimum(first + per, self.steps), self.step, 0)

    def finish(self):
        self.store(self.steps // self.inner - 1).wait()


def product_scratch(rows, tall, wide):
    dma = pltpu.SemaphoreType.DMA
    depth = min(1024, rows)
    tall, wide = min(512, tall), min(1024, wide)
    return [
        pltpu.VMEM((2, depth, tall), jnp.bfloat16),
        pltpu.VMEM((2, depth, wide), jnp.bfloat16),
        pltpu.VMEM((tall, wide), jnp.float32),
        pltpu.VMEM((tall, wide), jnp.bfloat16),
        dma((2,)),
        dma((2,)),
        dma(()),
    ]


def row_blocks(rows, each, work):
    def one(i, carry):
        work(pl.ds(pl.multiple_of(i * each, each), each))
        return carry

    lax.fori_loop(0, rows // each, one, 0)


def normal_rows(value):
    center = value - jnp.mean(value, axis=1, keepdims=True)
    factor = lax.rsqrt(jnp.mean(center * center, axis=1, keepdims=True) + 1e-05)
    return center * factor, factor


def dense_kernel(
    n, a_hbm, w_ref, input_hbm, bias_ref, gain_ref, shift_ref, out_ref, next_ref, inputs, input_sem, *scratch
):
    fetch = pltpu.make_async_copy(input_hbm, inputs, input_sem)
    fetch.start()
    Scatter(n, False, a_hbm, w_ref, out_ref, scratch).run()
    fetch.wait()

    def work(at):
        residual = inputs[at, :].astype(jnp.float32) + out_ref[at, :] + bias_ref[...]
        out_ref[at, :] = residual
        normed, _ = normal_rows(residual)
        next_ref[at, :] = (normed * gain_ref[...] + shift_ref[...]).astype(next_ref.dtype)

    row_blocks(out_ref.shape[0], 32, work)


def back_rows(grad, source, gain):
    normed, factor = normal_rows(source)
    scaled = grad * gain
    product = grad * normed
    back = factor * (
        scaled
        - jnp.mean(scaled, axis=1, keepdims=True)
        - normed * jnp.mean(scaled * normed, axis=1, keepdims=True)
    )
    return back, product


def column_sum(value):
    return jnp.sum(value, axis=0, keepdims=True)


def expand_back_kernel(
    n, a_hbm, w_ref, act_hbm, rows_hbm, residual_hbm, cotangent_hbm, gain_ref,
    out_ref, next_ref, sums_ref, grad_hbm, residual, cotangent, fetch_sem, *scratch
):
    fetches = (
        pltpu.make_async_copy(residual_hbm, residual, fetch_sem.at[0]),
        pltpu.make_async_copy(cotangent_hbm, cotangent, fetch_sem.at[1]),
    )
    for fetch in fetches:
        fetch.start()
    product = Product(act_hbm, rows_hbm, grad_hbm, scratch[:7])
    scatter = Scatter(n, True, a_hbm, w_ref, out_ref, scratch[7:])
    product.start()
    scatter.run(lambda j: product.batch(j, scatter.chunks))
    product.finish()
    for fetch in fetches:
        fetch.wait()
    sums_ref[...] = jnp.zeros_like(sums_ref)

    def work(at):
        grad = out_ref[at, :]
        other = cotangent[at, :].astype(jnp.float32)
        back, terms = back_rows(grad, residual[at, :], gain_ref[...])
        result = other + back
        out_ref[at, :] = result
        next_ref[at, :] = result.astype(next_ref.dtype)
        sums_ref[0:1, :] += column_sum(terms)
        sums_ref[1:2, :] += column_sum(grad)
        sums_ref[2:3, :] += column_sum(result)
        sums_ref[3:4, :] += column_sum(other)

    row_blocks(out_ref.shape[0], 32, work)


def comm_params(collective_id):
    return pltpu.CompilerParams(collective_id=collective_id, has_side_effects=True, vmem_limit_bytes=VMEM_LIMIT)


VMEM_SPEC = pl.BlockSpec(memory_space=pltpu.VMEM)
HBM_SPEC = pl.BlockSpec(memory_space=pl.ANY)
CHUNKS = 4


def dense(mixed, weight, inputs, bias, gain, shift, n, collective_id):
    rows, width = inputs.shape
    return pl.pallas_call(
        functools.partial(dense_kernel, n),
        out_shape=(
            jax.ShapeDtypeStruct((rows, width), jnp.float32),
            jax.ShapeDtypeStruct((rows, width), jnp.bfloat16),
        ),
        in_specs=[HBM_SPEC, VMEM_SPEC, HBM_SPEC, VMEM_SPEC, VMEM_SPEC, VMEM_SPEC],
        out_specs=(VMEM_SPEC, VMEM_SPEC),
        scratch_shapes=[pltpu.VMEM((rows, width), inputs.dtype), pltpu.SemaphoreType.DMA(())]
        + scatter_scratch(n, rows, mixed.shape[1], width, CHUNKS),
        compiler_params=comm_params(collective_id),
        name="dense",
    )(mixed, weight, inputs, bias, gain, shift)


def expand_back(grad_pre, up, activated, grad_rows, residual, cotangent, gain, n, collective_id):
    rows, width = residual.shape
    units = activated.shape[1]
    return pl.pallas_call(
        functools.partial(expand_back_kernel, n),
        out_shape=(
            jax.ShapeDtypeStruct((rows, width), jnp.float32),
            jax.ShapeDtypeStruct((rows, width), jnp.bfloat16),
            jax.ShapeDtypeStruct((8, width), jnp.float32),
            jax.ShapeDtypeStruct((units, width), jnp.bfloat16),
        ),
        in_specs=[HBM_SPEC, VMEM_SPEC, HBM_SPEC, HBM_SPEC, HBM_SPEC, HBM_SPEC, VMEM_SPEC],
        out_specs=(VMEM_SPEC, VMEM_SPEC, VMEM_SPEC, HBM_SPEC),
        scratch_shapes=[
            pltpu.VMEM((rows, width), jnp.float32),
            pltpu.VMEM((rows, width), cotangent.dtype),
            pltpu.SemaphoreType.DMA((2,)),
        ]
        + product_scratch(n * rows, units, width)
        + scatter_scratch(n, rows, units, width, CHUNKS),
        compiler_params=comm_params(collective_id),
        name="expand_back",
    )(grad_pre, up, activated, grad_rows, residual, cotangent, gain)


def dense_back_kernel(
    n, own_ref, mixed_ref, w_ref, left_hbm, right_hbm, grad_mixed_ref, grad_dense_ref, grad_up_hbm, gathered, acc, *scratch
):
    product = Product(left_hbm, right_hbm, grad_up_hbm, scratch[:7])
    gather = Gather(n, own_ref, gathered, scratch[7:])
    rows = own_ref.shape[0]

    def work(at):
        span = pl.ds(pl.multiple_of(at * rows, rows), rows)
        grad_mixed_ref[span, :] = lax.dot_general(
            gathered[span, :], w_ref[...], NT, preferred_element_type=jnp.float32
        ).astype(grad_mixed_ref.dtype)
        width = acc.shape[1]
        part = min(width, 512)
        for first in range(0, width, part):
            cols = slice(first, first + part)
            acc[:, cols] += lax.dot_general(
                mixed_ref[span, :], gathered[span, cols], TN, preferred_element_type=jnp.float32
            )

    product.start()
    gather.start()
    acc[...] = jnp.zeros_like(acc)
    product.batch(0, 1)
    for count in range(1, gather.bits + 1):
        gather.forward(count)
        if count == 1:
            gather.keep().wait()
            work(gather.place(0, 0))
            gather.wait_core(0)
            work(gather.place(0, 1))
        for core in (0, 1):
            for mask in gather.level(count):
                if core:
                    gather.wait_core(mask)
                work(gather.place(mask, core))
    grad_dense_ref[...] = acc[...].astype(grad_dense_ref.dtype)
    product.finish()
    gather.finish_sends()


def dense_back(own, mixed, weight, mlp_rows, grad_pre, n, collective_id):
    rows, width = own.shape
    total, depth = mixed.shape
    return pl.pallas_call(
        functools.partial(dense_back_kernel, n),
        out_shape=(
            jax.ShapeDtypeStruct((total, depth), jnp.bfloat16),
            jax.ShapeDtypeStruct((depth, width), jnp.bfloat16),
            jax.ShapeDtypeStruct((mlp_rows.shape[1], grad_pre.shape[1]), jnp.bfloat16),
        ),
        in_specs=[VMEM_SPEC, VMEM_SPEC, VMEM_SPEC, HBM_SPEC, HBM_SPEC],
        out_specs=(VMEM_SPEC, VMEM_SPEC, HBM_SPEC),
        scratch_shapes=[pltpu.VMEM((total, width), jnp.bfloat16), pltpu.VMEM((depth, width), jnp.float32)]
        + product_scratch(total, mlp_rows.shape[1], grad_pre.shape[1])
        + gather_sems(n),
        compiler_params=comm_params(collective_id),
        name="dense_back",
    )(own, mixed, weight, mlp_rows, grad_pre)


def attend_back_one(slope, proj_ref, grad_ref, start, head, column_ref, row_ref, out_ref, dk_ref, dv_ref, sums_ref, length):
    at = pl.multiple_of(head * 3 * HEAD_DIM, HEAD_DIM)
    own = pl.ds(pl.multiple_of(head * HEAD_DIM, HEAD_DIM), HEAD_DIM)

    def cols(which):
        return pl.ds(at + which * HEAD_DIM, HEAD_DIM)

    def take(which, first, size):
        return proj_ref[pl.ds(start + first, size), cols(which)]

    sums = None
    for first in reversed(range(0, length, BLOCK)):
        last = first + BLOCK
        q, g = take(0, first, BLOCK), grad_ref[pl.ds(start + first, BLOCK), own]
        scores = masked_scores(slope, q, take(1, 0, last), column_ref[first:last, :], row_ref[:, :last], first)
        top = jnp.max(scores, axis=1, keepdims=True)
        expo = jnp.exp2(scores - top)
        probs = expo * (1.0 / jnp.sum(expo, axis=1, keepdims=True))
        grad_probs = lax.dot_general(g, take(2, 0, last), NT, preferred_element_type=jnp.float32)
        product = probs * grad_probs
        grad_scores = (product - probs * jnp.sum(product, axis=1, keepdims=True)).astype(jnp.bfloat16)
        rounded = probs.astype(jnp.bfloat16)
        grad_queries = (jnp.dot(grad_scores, take(1, 0, last), preferred_element_type=jnp.float32) * SCALE).astype(
            out_ref.dtype
        )
        out_ref[pl.ds(start + first, BLOCK), cols(0)] = grad_queries
        here = column_sum(grad_queries.astype(jnp.float32))
        sums = here if sums is None else sums + here
        grad_keys = lax.dot_general(grad_scores, q, TN, preferred_element_type=jnp.float32)
        grad_values = lax.dot_general(rounded, g, TN, preferred_element_type=jnp.float32)
        if last == length:
            dk_ref[...] = grad_keys
            dv_ref[...] = grad_values
        else:
            dk_ref[:last, :] += grad_keys
            dv_ref[:last, :] += grad_values
    span = pl.ds(start, length)
    out_ref[span, cols(1)] = (dk_ref[...] * SCALE).astype(out_ref.dtype)
    grad_values = dv_ref[...].astype(out_ref.dtype)
    out_ref[span, cols(2)] = grad_values
    sums_ref[0:1, own] += sums
    sums_ref[1:2, own] += column_sum(grad_values.astype(jnp.float32))


def shrink_kernel(
    n, length, slope_ref, a_hbm, w_ref, residual_hbm, bias_ref, proj_hbm, grad_mixed_ref, column_ref, row_ref,
    hidden_ref, grad_proj_ref, sums_ref, out, residual, proj, dk, dv, fetch_sem, *scratch
):
    fetches = (
        pltpu.make_async_copy(proj_hbm, proj, fetch_sem.at[0]),
        pltpu.make_async_copy(residual_hbm, residual, fetch_sem.at[1]),
    )
    for fetch in fetches:
        fetch.start()
    scatter = Scatter(n, False, a_hbm, w_ref, out, scratch)
    heads = grad_proj_ref.shape[1] // (3 * HEAD_DIM)
    units = grad_proj_ref.shape[0] // length * heads
    per = -(-units // scatter.chunks)
    sums_ref[...] = jnp.zeros_like(sums_ref)

    def one(i, carry):
        s, head = i // heads, lax.rem(i, heads)
        attend_back_one(
            slope_ref[head], proj, grad_mixed_ref, pl.multiple_of(s * length, length), head, column_ref.at[s],
            row_ref.at[s], grad_proj_ref, dk, dv, sums_ref, length,
        )
        return carry

    def filler(j):
        @pl.when(j == 0)
        def _():
            fetches[0].wait()

        lax.fori_loop(j * per, jnp.minimum(j * per + per, units), one, 0)

    scatter.run(filler)
    fetches[1].wait()

    def work(at):
        hidden_ref[at, :] = (residual[at, :] + out[at, :] + bias_ref[...]).astype(hidden_ref.dtype)

    row_blocks(out.shape[0], 64, work)


def shrink(activated, down, residual, bias, slopes, proj, grad_mixed, labels, n, collective_id):
    rows, width = residual.shape
    heads_width = grad_mixed.shape[1]
    length = labels.shape[1]
    return pl.pallas_call(
        functools.partial(shrink_kernel, n, length),
        out_shape=(
            jax.ShapeDtypeStruct((rows, width), jnp.bfloat16),
            jax.ShapeDtypeStruct(proj.shape, jnp.bfloat16),
            jax.ShapeDtypeStruct((8, heads_width), jnp.float32),
        ),
        in_specs=[
            pl.BlockSpec(memory_space=pltpu.SMEM), HBM_SPEC, VMEM_SPEC, HBM_SPEC, VMEM_SPEC, HBM_SPEC, VMEM_SPEC, VMEM_SPEC,
            VMEM_SPEC,
        ],
        out_specs=(VMEM_SPEC, VMEM_SPEC, VMEM_SPEC),
        scratch_shapes=[
            pltpu.VMEM((rows, width), jnp.float32),
            pltpu.VMEM((rows, width), jnp.float32),
            pltpu.VMEM(proj.shape, jnp.bfloat16),
            pltpu.VMEM((length, HEAD_DIM), jnp.float32),
            pltpu.VMEM((length, HEAD_DIM), jnp.float32),
            pltpu.SemaphoreType.DMA((2,)),
        ]
        + scatter_scratch(n, rows, activated.shape[1], width, CHUNKS),
        compiler_params=comm_params(collective_id),
        name="shrink",
    )(slopes, activated, down, residual, bias, proj, grad_mixed, labels[:, :, None], labels[:, None, :])


def project_back_kernel(
    n, a_hbm, w_ref, input_hbm, grad_hbm, gain_ref, earlier_ref, out_ref, sums_ref, inputs, grads, fetch_sem, *scratch
):
    fetches = (
        pltpu.make_async_copy(input_hbm, inputs, fetch_sem.at[0]),
        pltpu.make_async_copy(grad_hbm, grads, fetch_sem.at[1]),
    )
    for fetch in fetches:
        fetch.start()
    Scatter(n, True, a_hbm, w_ref, out_ref, scratch).run()
    for fetch in fetches:
        fetch.wait()
    sums_ref[...] = earlier_ref[...]

    def work(at):
        grad = out_ref[at, :]
        back, terms = back_rows(grad, inputs[at, :].astype(jnp.float32), gain_ref[...])
        out_ref[at, :] = grads[at, :] + back
        sums_ref[4:5, :] += column_sum(terms)
        sums_ref[5:6, :] += column_sum(grad)

    row_blocks(out_ref.shape[0], 32, work)


def project_back(grad_proj, weight, inputs, grad_residual, gain, earlier, n, collective_id):
    rows, width = inputs.shape
    return pl.pallas_call(
        functools.partial(project_back_kernel, n),
        out_shape=(jax.ShapeDtypeStruct((rows, width), jnp.float32), jax.ShapeDtypeStruct((8, width), jnp.float32)),
        in_specs=[HBM_SPEC, VMEM_SPEC, HBM_SPEC, HBM_SPEC, VMEM_SPEC, VMEM_SPEC],
        out_specs=(VMEM_SPEC, VMEM_SPEC),
        scratch_shapes=[
            pltpu.VMEM((rows, width), inputs.dtype),
            pltpu.VMEM((rows, width), jnp.float32),
            pltpu.SemaphoreType.DMA((2,)),
        ]
        + scatter_scratch(n, rows, grad_proj.shape[1], width, CHUNKS),
        compiler_params=comm_params(collective_id),
        name="project_back",
    )(grad_proj, weight, inputs, grad_residual, gain, earlier)


HEADS = 16


def normalize(rows):
    center = rows - jnp.mean(rows, axis=1, keepdims=True)
    factor = lax.rsqrt(jnp.mean(center * center, axis=1, keepdims=True) + 1e-05)
    return center * factor


def wide(vector):
    return vector.astype(jnp.float32)[None]


def share(grad, dimension):
    return lax.psum_scatter(grad, "dp", scatter_dimension=dimension, tiled=True).astype(jnp.float32)


def on_device(
    hidden_input,
    first_gain,
    first_shift,
    qkv_weight,
    query_bias,
    value_bias,
    dense_weight,
    dense_bias,
    second_gain,
    second_shift,
    up_weight,
    up_bias,
    down_weight,
    down_bias,
    segments,
    document_lengths,
    cotangent,
    *,
    n,
    d,
):
    heads_local = query_bias.shape[0] // HEAD_DIM
    normed_first = normalize(hidden_input.astype(jnp.float32))
    attn_input = (normed_first * wide(first_gain) + wide(first_shift)).astype(jnp.bfloat16)
    attn_rows = gather_rows(attn_input, n, 1)
    project_full, dense_full, expand_full, shrink_full = (
        lax.all_gather(qkv_weight, "dp", axis=0, tiled=True),
        lax.all_gather(dense_weight, "dp", axis=1, tiled=True),
        lax.all_gather(up_weight, "dp", axis=0, tiled=True),
        lax.all_gather(down_weight, "dp", axis=1, tiled=True),
    )
    group_rows = attn_rows.shape[0]
    sequences = document_lengths.shape[0]
    length = group_rows // sequences
    heads_index = lax.axis_index("tensor") * heads_local + lax.broadcasted_iota(
        jnp.int32, (heads_local,), 0
    )
    slopes = jnp.exp2(-8.0 * (heads_index.astype(jnp.float32) + 1.0) / HEADS) * LOG2E
    position = lax.broadcasted_iota(jnp.int32, (sequences, length), 1)
    filled = jnp.sum(document_lengths, axis=1, keepdims=True)
    labels = jnp.where(position < filled, segments.reshape(sequences, length), length + position)
    query_bias32 = query_bias.astype(jnp.float32).reshape(heads_local, HEAD_DIM)
    value_bias32 = value_bias.astype(jnp.float32).reshape(heads_local, HEAD_DIM)
    proj_bias = jnp.stack((query_bias32, jnp.zeros_like(query_bias32), value_bias32), axis=1).reshape(
        heads_local * 3 * HEAD_DIM
    )
    grad_rows, proj, mixed = project_attend(
        attn_rows, project_full, proj_bias[None], slopes, labels, cotangent, n, 6
    )
    residual, mlp_input = dense(
        mixed, dense_full, hidden_input, wide(dense_bias), wide(second_gain), wide(second_shift), n, 2
    )
    mlp_rows, activated, grad_pre, sum_up_bias = expand(
        mlp_input, grad_rows, expand_full, shrink_full, wide(up_bias), n, 7
    )
    grad_residual, grad_attn_out, early_sums, grad_down = expand_back(
        grad_pre, expand_full, activated, grad_rows, residual, cotangent, wide(second_gain), n, 4
    )
    grad_down_weight = share(grad_down, 1)
    grad_mixed, grad_dense, grad_up = dense_back(grad_attn_out, mixed, dense_full, mlp_rows, grad_pre, n, 9)
    grad_down_weight, activated, grad_mixed = lax.optimization_barrier((grad_down_weight, activated, grad_mixed))
    grad_up_weight = share(grad_up, 0)
    hidden_output, grad_proj, head_sums = shrink(
        activated, shrink_full, residual, wide(down_bias), slopes, proj, grad_mixed, labels, n, 3
    )
    grad_up_weight, grad_proj = lax.optimization_barrier((grad_up_weight, grad_proj))
    grad_project = jnp.einsum("td,tc->dc", attn_rows, grad_proj, preferred_element_type=jnp.float32).astype(
        jnp.bfloat16
    )
    grad_qkv_weight = share(grad_project, 0)
    grad_dense_weight = share(grad_dense, 1)
    grad_input, flat_sums = project_back(
        grad_proj, project_full, hidden_input, grad_residual, wide(first_gain), early_sums, n, 5
    )
    model = hidden_input.shape[1]
    heads_width = heads_local * HEAD_DIM
    biases = jnp.concatenate((head_sums[0], head_sums[1], sum_up_bias[0]))
    lines = -(-biases.shape[0] // (8 * model)) * 8
    biases = jnp.pad(biases, (0, lines * model - biases.shape[0])).reshape(lines, model)
    sums = sum_small(flat_sums, biases, n, d, 8)
    grad_second_gain, grad_second_shift, grad_dense_bias, grad_down_bias, grad_first_gain, grad_first_shift = (
        sums[i] for i in range(6)
    )
    biases = sums[8:].reshape(-1)
    grad_query_bias = biases[:heads_width]
    grad_value_bias = biases[heads_width : 2 * heads_width]
    grad_up_bias = biases[2 * heads_width : 2 * heads_width + up_bias.shape[0]]
    return (
        hidden_output,
        grad_input,
        grad_first_gain,
        grad_first_shift,
        grad_qkv_weight,
        grad_query_bias,
        grad_value_bias,
        grad_dense_weight,
        grad_dense_bias,
        grad_second_gain,
        grad_second_shift,
        grad_up_weight,
        grad_up_bias,
        grad_down_weight,
        grad_down_bias,
    )


def solution(mesh):
    return jax.shard_map(
        functools.partial(on_device, n=mesh.shape["tensor"], d=mesh.shape["dp"]),
        mesh=mesh,
        in_specs=(
            P(("dp", "tensor"), None),
            P(),
            P(),
            P("dp", "tensor"),
            P("tensor"),
            P("tensor"),
            P("tensor", "dp"),
            P(),
            P(),
            P(),
            P("dp", "tensor"),
            P("tensor"),
            P("tensor", "dp"),
            P(),
            P("dp"),
            P("dp", None),
            P(("dp", "tensor"), None),
        ),
        out_specs=(
            P(("dp", "tensor"), None),
            P(("dp", "tensor"), None),
            P(),
            P(),
            P("dp", "tensor"),
            P("tensor"),
            P("tensor"),
            P("tensor", "dp"),
            P(),
            P(),
            P(),
            P("dp", "tensor"),
            P("tensor"),
            P("tensor", "dp"),
            P(),
        ),
        check_vma=False,
    )
```

```python
import functools
import math

import jax
import jax.numpy as jnp
from jax import lax
from jax.experimental import pallas as pl
from jax.experimental.pallas import tpu as pltpu
from jax.sharding import PartitionSpec as P

VMEM_LIMIT = 62 << 20
LINK_COST = pl.CostEstimate(flops=0, bytes_accessed=280_000_000, transcendentals=0)


def flip(index, bit):
    return index + (1 - 2 * ((index // 2**bit) % 2)) * 2**bit


def chip_bits(n):
    return n.bit_length() - 2


def column_parts(width, count):
    blocks = width // 128
    edges = [128 * (blocks * i // count) for i in range(count + 1)]
    return [(a, b - a) for a, b in zip(edges[:-1], edges[1:])]


def peer(index):
    return {"tensor": index}


def greet(me, bits, d=1):
    barrier = pltpu.get_barrier_semaphore()
    for bit in range(bits + 1):
        pl.semaphore_signal(
            barrier, inc=1, device_id=peer(flip(me, bit)), device_id_type=pl.DeviceIdType.MESH
        )
    for ahead in range(1, d):
        pl.semaphore_signal(
            barrier, inc=1, device_id=ahead_on_dp(ahead, d), device_id_type=pl.DeviceIdType.MESH
        )
    pl.semaphore_wait(barrier, bits + d)


def ahead_on_dp(ahead, d):
    return {"dp": lax.rem(lax.axis_index("dp") + ahead, d)}


def remote(src, dst, send_sem, recv_sem, target):
    return pltpu.make_async_remote_copy(
        src_ref=src,
        dst_ref=dst,
        send_sem=send_sem,
        recv_sem=recv_sem,
        device_id=peer(target),
        device_id_type=pl.DeviceIdType.MESH,
    )


class Gather:
    def __init__(self, n, own_ref, out_ref, sems):
        self.me = lax.axis_index("tensor")
        self.bits = chip_bits(n)
        self.rows, width = own_ref.shape
        self.parts = column_parts(width, self.bits)
        self.own, self.out = own_ref, out_ref
        self.own_sem, self.chip_send, self.chip_recv, self.core_send, self.core_recv = sems
        self.sends = []

    def slot(self, part, index):
        at = self.me
        for step in range(self.bits):
            if (index >> step) & 1:
                at = flip(at, 1 + (part + step) % self.bits)
        return at

    def place(self, mask, core):
        at = flip(self.me, 0) if core else self.me
        for bit in range(self.bits):
            if (mask >> bit) & 1:
                at = flip(at, 1 + bit)
        return at

    def index_of(self, part, mask):
        return sum(2 ** ((bit - part) % self.bits) for bit in range(self.bits) if (mask >> bit) & 1)

    def level(self, count):
        return [index for index in range(2**self.bits) if index.bit_count() == count]

    def block(self, part, index, core=0):
        start, size = self.parts[part]
        at = flip(self.slot(part, index), 0) if core else self.slot(part, index)
        return self.out.at[pl.ds(pl.multiple_of(at * self.rows, self.rows), self.rows), pl.ds(start, size)]

    def source(self, part, index):
        start, size = self.parts[part]
        return self.own.at[:, pl.ds(start, size)] if index == 0 else self.block(part, index)

    def send(self, part, index, step):
        arrives = index + 2**step
        copy = remote(
            self.source(part, index),
            self.block(part, index),
            self.chip_send.at[part, arrives],
            self.chip_recv.at[part, arrives],
            flip(self.me, 1 + (part + step) % self.bits),
        )
        copy.start()
        self.sends.append(copy)

    def hand_over(self, part, index):
        copy = remote(
            self.source(part, index),
            self.block(part, index),
            self.core_send.at[part, index],
            self.core_recv.at[part, index],
            flip(self.me, 0),
        )
        copy.start()
        self.sends.append(copy)

    def keep(self):
        rows = pl.ds(pl.multiple_of(self.me * self.rows, self.rows), self.rows)
        return pltpu.make_async_copy(self.own, self.out.at[rows, :], self.own_sem)

    def start(self):
        greet(self.me, self.bits)
        for step in range(self.bits):
            for part in range(self.bits):
                self.send(part, 0, step)
        for part in range(self.bits):
            self.hand_over(part, 0)
        self.keep().start()

    def forward(self, count):
        for index in self.level(count):
            for part in range(self.bits):
                arrived = self.block(part, index)
                remote(
                    arrived, arrived, self.chip_send.at[part, index], self.chip_recv.at[part, index], flip(self.me, 0)
                ).wait_recv()
                for step in range(index.bit_length(), self.bits):
                    self.send(part, index, step)
                self.hand_over(part, index)

    def wait_core(self, mask):
        for part in range(self.bits):
            index = self.index_of(part, mask)
            arrived = self.block(part, index, 1)
            remote(
                arrived, arrived, self.core_send.at[part, index], self.core_recv.at[part, index], flip(self.me, 0)
            ).wait_recv()

    def finish_sends(self):
        for copy in self.sends:
            copy.wait_send()


def gather_kernel(n, x_ref, out_ref, *sems):
    gather = Gather(n, x_ref, out_ref, sems)
    gather.start()
    for count in range(1, gather.bits + 1):
        gather.forward(count)
    for mask in range(2**gather.bits):
        gather.wait_core(mask)
    gather.finish_sends()
    gather.keep().wait()


def gather_sems(n):
    bits = chip_bits(n)
    dma = pltpu.SemaphoreType.DMA
    return [dma(())] + [dma((bits, 2**bits))] * 4


def gather_rows(x, n, collective_id):
    rows, width = x.shape
    return pl.pallas_call(
        functools.partial(gather_kernel, n),
        out_shape=jax.ShapeDtypeStruct((n * rows, width), x.dtype),
        in_specs=[pl.BlockSpec(memory_space=pltpu.VMEM)],
        out_specs=pl.BlockSpec(memory_space=pl.ANY),
        scratch_shapes=gather_sems(n),
        compiler_params=pltpu.CompilerParams(
            collective_id=collective_id, has_side_effects=True, vmem_limit_bytes=VMEM_LIMIT
        ),
        cost_estimate=LINK_COST,
        name="gather_rows",
    )(x)


class Scatter:
    def __init__(self, n, transposed, a_hbm, w_ref, out_ref, scratch):
        (self.csend, self.crecv, self.recv, self.other, self.mine, self.load_sem) = scratch[:6]
        self.core_send, self.core_recv, self.chip_send, self.chip_recv = scratch[6:]
        self.me = lax.axis_index("tensor")
        self.bits = chip_bits(n)
        self.total = 2**self.bits
        self.transposed = transposed
        self.a, self.w, self.out = a_hbm, w_ref, out_ref
        self.rows, width = out_ref.shape
        self.chunk = self.csend.shape[2]
        self.chunks = self.rows // self.chunk
        self.parts = column_parts(width, self.bits)

    def index_of(self, part, mask):
        top = self.bits - 1
        return sum(2 ** (top - (bit - part) % self.bits) for bit in range(self.bits) if (mask >> bit) & 1)

    def place(self, mask, core):
        at = flip(self.me, 0) if core else self.me
        for bit in range(self.bits):
            if (mask >> bit) & 1:
                at = flip(at, 1 + bit)
        return at

    def rows_of(self, j):
        return pl.ds(pl.multiple_of(j * self.chunk, self.chunk), self.chunk)

    def loads(self, j, core):
        into = self.other if core else self.mine
        copies = []
        for mask in range(self.total):
            start = pl.multiple_of(self.place(mask, core) * self.rows + j * self.chunk, self.chunk)
            copies.append(
                pltpu.make_async_copy(
                    self.a.at[pl.ds(start, self.chunk), :],
                    into.at[lax.rem(j, 2), pl.ds(mask * self.chunk, self.chunk), :],
                    self.load_sem.at[core, lax.rem(j, 2), mask],
                )
            )
        return copies

    def core_copy(self, j, part):
        start, size = self.parts[part]
        return remote(
            self.csend.at[lax.rem(j, 2), :, :, pl.ds(start, size)],
            self.crecv.at[:, self.rows_of(j), pl.ds(start, size)],
            self.core_send.at[part, j],
            self.core_recv.at[part, j],
            flip(self.me, 0),
        )

    def chip_copy(self, j, part, step):
        half = self.total >> (step + 1)
        first = sum(self.total >> (s + 1) for s in range(step))
        start, size = self.parts[part]
        return remote(
            self.crecv.at[pl.ds(half, half), self.rows_of(j), pl.ds(start, size)],
            self.recv.at[pl.ds(first, half), self.rows_of(j), pl.ds(start, size)],
            self.chip_send.at[part, step, j],
            self.chip_recv.at[part, step, j],
            flip(self.me, 1 + (part + step) % self.bits),
        )

    def tiles(self, part, lhs, put):
        start, size = self.parts[part]
        tile = 256 if size % 256 == 0 and start % 256 == 0 else 128

        def one(i, carry):
            cols = pl.ds(pl.multiple_of(start + i * tile, tile), tile)
            if self.transposed:
                value = lax.dot_general(
                    lhs[...], self.w[cols, :], (((1,), (1,)), ((), ())), preferred_element_type=jnp.float32
                )
            else:
                value = jnp.dot(lhs[...], self.w[:, cols], preferred_element_type=jnp.float32)
            put(cols, value)
            return carry

        lax.fori_loop(0, size // tile, one, 0)

    def piece(self, value, mask):
        return value[mask * self.chunk : (mask + 1) * self.chunk, :]

    def stage_core(self, j):
        for copy in self.loads(j, 1):
            copy.wait()

        @pl.when(j >= 2)
        def _():
            for part in range(self.bits):
                self.core_copy(j - 2, part).wait_send()

        for part in range(self.bits):

            def put(cols, value):
                for mask in range(self.total):
                    self.csend[lax.rem(j, 2), self.index_of(part, mask), :, cols] = self.piece(value, mask).astype(
                        self.csend.dtype
                    )

            self.tiles(part, self.other.at[lax.rem(j, 2)], put)
            self.core_copy(j, part).start()

    def stage_first(self, j):
        for copy in self.loads(j, 0):
            copy.wait()
        for part in range(self.bits):
            self.core_copy(j, part).wait_recv()

            def put(cols, value):
                for mask in range(self.total):
                    index = self.index_of(part, mask)
                    got = self.piece(value, mask) + self.crecv[index, self.rows_of(j), cols].astype(jnp.float32)
                    if index:
                        self.crecv[index, self.rows_of(j), cols] = got.astype(self.crecv.dtype)
                    else:
                        self.out[self.rows_of(j), cols] = got

            self.tiles(part, self.mine.at[lax.rem(j, 2)], put)
            self.chip_copy(j, part, 0).start()

    def stage_next(self, j, step):
        half = self.total >> (step + 1)
        first = sum(self.total >> (s + 1) for s in range(step))
        for part in range(self.bits):
            start, size = self.parts[part]
            cols = slice(start, start + size)
            self.chip_copy(j, part, step).wait_recv()
            for index in reversed(range(half)):
                got = self.recv[first + index, self.rows_of(j), cols].astype(jnp.float32)
                if index:
                    value = self.crecv[index, self.rows_of(j), cols].astype(jnp.float32) + got
                    self.crecv[index, self.rows_of(j), cols] = value.astype(self.crecv.dtype)
                else:
                    self.out[self.rows_of(j), cols] += got
            if step + 1 < self.bits:
                self.chip_copy(j, part, step + 1).start()

    def run(self, filler=None, d=1):
        for copy in self.loads(0, 1):
            copy.start()
        greet(self.me, self.bits, d)

        def body(u, carry):
            @pl.when(u + 1 < self.chunks)
            def _():
                for copy in self.loads(u + 1, 1):
                    copy.start()

            @pl.when(u < self.chunks)
            def _():
                for copy in self.loads(u, 0):
                    copy.start()
                self.stage_core(u)

            @pl.when((u >= 1) & (u <= self.chunks))
            def _():
                self.stage_first(u - 1)

            for step in range(self.bits):

                @pl.when((u >= 2 + step) & (u < self.chunks + 2 + step))
                def _():
                    self.stage_next(u - 2 - step, step)

            if filler is not None:

                @pl.when((u >= 1) & (u <= self.chunks))
                def _():
                    filler(u - 1)

            return carry

        lax.fori_loop(0, self.chunks + self.bits + 1, body, 0)
        for part in range(self.bits):
            for j in range(self.chunks):
                if j >= self.chunks - 2:
                    self.core_copy(j, part).wait_send()
                for step in range(self.bits):
                    self.chip_copy(j, part, step).wait_send()


def scatter_scratch(n, rows, depth, width, chunks):
    bits = chip_bits(n)
    total = 2**bits
    chunk = rows // chunks
    dma = pltpu.SemaphoreType.DMA
    return [
        pltpu.VMEM((2, total, chunk, width), jnp.bfloat16),
        pltpu.VMEM((total, rows, width), jnp.bfloat16),
        pltpu.VMEM((total - 1, rows, width), jnp.bfloat16),
        pltpu.VMEM((2, total * chunk, depth), jnp.bfloat16),
        pltpu.VMEM((2, total * chunk, depth), jnp.bfloat16),
        dma((2, 2, total)),
        dma((bits, chunks)),
        dma((bits, chunks)),
        dma((bits, bits, chunks)),
        dma((bits, bits, chunks)),
    ]


HEAD_DIM = 128
LOG2E = 1.4426950408889634
SCALE = 1.0 / math.sqrt(HEAD_DIM)
BLOCK = 256
NT = (((1,), (1,)), ((), ()))
TN = (((0,), (0,)), ((), ()))


def masked_scores(slope, q, keys, query_labels, key_labels, first):
    raw = lax.dot_general(q, keys, NT, preferred_element_type=jnp.float32)
    rows, width = raw.shape
    column = lax.broadcasted_iota(jnp.int32, (1, width), 1)
    bias = column.astype(jnp.float32) * slope
    same = query_labels == key_labels
    causal = lax.broadcasted_iota(jnp.int32, (rows, width), 1) <= first + lax.broadcasted_iota(
        jnp.int32, (rows, width), 0
    )
    return jnp.where(same & causal, raw * (SCALE * LOG2E) + bias, -1e30)


class Total:
    def __init__(self, n, d, scratch):
        self.pair, self.lines, self.send, self.recv, self.line_send, self.line_recv = scratch
        self.me, self.d = lax.axis_index("tensor"), d
        self.levels = n.bit_length() - 1

    def level_copy(self, level):
        return remote(
            self.pair.at[2 * level],
            self.pair.at[2 * level + 1],
            self.send.at[level],
            self.recv.at[level],
            flip(self.me, level),
        )

    def line_copy(self, ahead):
        return pltpu.make_async_remote_copy(
            src_ref=self.lines.at[0],
            dst_ref=self.lines.at[ahead],
            send_sem=self.line_send.at[ahead],
            recv_sem=self.line_recv.at[ahead],
            device_id=ahead_on_dp(ahead, self.d),
            device_id_type=pl.DeviceIdType.MESH,
        )

    def spread(self):
        for ahead in range(1, self.d):
            self.line_copy(ahead).start()

    def step(self, level):
        if level:
            self.level_copy(level - 1).wait_recv()
            self.pair[2 * level] = self.pair[2 * level - 2] + self.pair[2 * level - 1]
        if level < self.levels:
            self.level_copy(level).start()
        else:
            self.lines[0] = self.pair[2 * level]
            self.spread()

    def finish(self, levels=True):
        for ahead in range(1, self.d):
            self.line_copy(ahead).wait_recv()
        z = lax.axis_index("dp")
        total = None
        for index in range(self.d):
            value = self.lines[lax.rem(z - index + self.d, self.d)]
            total = value if total is None else total + value
        for ahead in range(1, self.d):
            self.line_copy(ahead).wait_send()
        if levels:
            for level in range(self.levels):
                self.level_copy(level).wait_send()
        return total


def total_scratch(n, d, rows, width):
    levels = n.bit_length() - 1
    dma = pltpu.SemaphoreType.DMA
    return [
        pltpu.VMEM((2 * levels + 1, rows, width), jnp.float32),
        pltpu.VMEM((d, rows, width), jnp.float32),
        dma((levels,)),
        dma((levels,)),
        dma((d,)),
        dma((d,)),
    ]


def tile_of(width):
    return 256 if width % 256 == 0 else width


def attend_one(slope, proj_ref, start, head, column_ref, row_ref, out_ref, length):
    at = pl.multiple_of(head * 3 * HEAD_DIM, HEAD_DIM)

    def take(which, first, size):
        return proj_ref[pl.ds(start + first, size), pl.ds(at + which * HEAD_DIM, HEAD_DIM)]

    for first in range(0, length, BLOCK):
        last = first + BLOCK
        scores = masked_scores(
            slope, take(0, first, BLOCK), take(1, 0, last), column_ref[first:last, :], row_ref[:, :last], first
        )
        top = jnp.max(scores, axis=1, keepdims=True)
        expo = jnp.exp2(scores - top)
        total = jnp.sum(expo, axis=1, keepdims=True)
        mixed = jnp.dot(expo.astype(jnp.bfloat16), take(2, 0, last), preferred_element_type=jnp.float32)
        out_ref[pl.ds(start + first, BLOCK), pl.ds(pl.multiple_of(head * HEAD_DIM, HEAD_DIM), HEAD_DIM)] = (
            mixed / total
        ).astype(out_ref.dtype)


def project_kernel(
    n, length, slope_ref, own_ref, rows_hbm, w_ref, bias_ref, column_ref, row_ref, gathered, proj_hbm, mixed_ref,
    proj, buf, load_sem, store_sem, *sems
):
    gather = Gather(n, own_ref, gathered, sems)
    rows = own_ref.shape[0]
    width = w_ref.shape[1]
    tile = tile_of(width)
    heads = width // (3 * HEAD_DIM)
    sequences = n * rows // length

    def load(i):
        at = pl.ds(pl.multiple_of(i * rows, rows), rows)
        return pltpu.make_async_copy(rows_hbm.at[at, :], buf.at[lax.rem(i, 2)], load_sem.at[lax.rem(i, 2)])

    load(0).start()
    gather.start()

    def store(i):
        at = pl.ds(pl.multiple_of(i * rows, rows), rows)
        return pltpu.make_async_copy(proj.at[at, :], proj_hbm.at[at, :], store_sem.at[i])

    def project(i, carry):
        load(i).wait()

        @pl.when(i + 1 < n)
        def _():
            load(i + 1).start()

        at = pl.ds(pl.multiple_of(i * rows, rows), rows)
        for first in range(0, width, tile):
            cols = slice(first, first + tile)
            proj[at, cols] = (
                jnp.dot(buf[lax.rem(i, 2)], w_ref[:, cols], preferred_element_type=jnp.float32) + bias_ref[:, cols]
            ).astype(proj.dtype)
        store(i).start()
        return carry

    lax.fori_loop(0, n, project, 0)
    gather.forward(1)

    def one(i, carry):
        s, head = i // heads, lax.rem(i, heads)
        attend_one(
            slope_ref[head],
            proj,
            pl.multiple_of(s * length, length),
            head,
            column_ref.at[s],
            row_ref.at[s],
            mixed_ref,
            length,
        )
        return carry

    lax.fori_loop(0, sequences * heads, one, 0)
    for count in range(2, gather.bits + 1):
        gather.forward(count)
    for i in range(n):
        store(i).wait()
    for mask in range(2**gather.bits):
        gather.wait_core(mask)
    gather.finish_sends()
    gather.keep().wait()


def project_attend(attn_rows, weight, bias, slopes, labels, own, n, collective_id):
    total, depth = attn_rows.shape
    rows, width = own.shape[0], weight.shape[1]
    heads = width // (3 * HEAD_DIM)
    vmem = pl.BlockSpec(memory_space=pltpu.VMEM)
    hbm = pl.BlockSpec(memory_space=pl.ANY)
    dma = pltpu.SemaphoreType.DMA
    return pl.pallas_call(
        functools.partial(project_kernel, n, labels.shape[1]),
        out_shape=(
            jax.ShapeDtypeStruct((total, own.shape[1]), own.dtype),
            jax.ShapeDtypeStruct((total, width), jnp.bfloat16),
            jax.ShapeDtypeStruct((total, heads * HEAD_DIM), jnp.bfloat16),
        ),
        in_specs=[pl.BlockSpec(memory_space=pltpu.SMEM), vmem, hbm, vmem, vmem, vmem, vmem],
        out_specs=(hbm, hbm, vmem),
        scratch_shapes=[
            pltpu.VMEM((total, width), jnp.bfloat16),
            pltpu.VMEM((2, rows, depth), jnp.bfloat16),
            dma((2,)),
            dma((n,)),
        ]
        + gather_sems(n),
        compiler_params=pltpu.CompilerParams(
            collective_id=collective_id, has_side_effects=True, vmem_limit_bytes=VMEM_LIMIT
        ),
        cost_estimate=LINK_COST,
        name="project_attend",
    )(slopes, own, attn_rows, weight, bias, labels[:, :, None], labels[:, None, :])


def gelu_both(value):
    c, a = 0.7978845608028654, 0.044715
    square = value * value
    half = 0.5 + 0.5 * jnp.tanh(value * (c + (c * a) * square))
    active = value * half
    slope = half + (2.0 * active) * (1.0 - half) * (c + (3.0 * c * a) * square)
    return active, slope


def expand_kernel(
    n, own_ref, grad_hbm, up_ref, down_ref, bias_ref, rows_hbm, act_hbm, pre_hbm, sum_ref,
    gathered, grads, act, pre, load_sem, act_sem, pre_sem, rows_sem, *sems
):
    gather = Gather(n, own_ref, gathered, sems)
    rows, depth = own_ref.shape
    width = up_ref.shape[1]
    tile = tile_of(width)
    order = [gather.place(mask, core) for mask in (0,) for core in (0, 1)]
    for count in range(1, gather.bits + 1):
        for core in (0, 1):
            order += [gather.place(mask, core) for mask in gather.level(count)]

    def span(at):
        return pl.ds(pl.multiple_of(at * rows, rows), rows)

    def load(i):
        return pltpu.make_async_copy(grad_hbm.at[span(order[i]), :], grads.at[i % 2], load_sem.at[i % 2])

    def store(i):
        return (
            pltpu.make_async_copy(act.at[i % 2], act_hbm.at[span(order[i]), :], act_sem.at[i % 2]),
            pltpu.make_async_copy(pre.at[i % 2], pre_hbm.at[span(order[i]), :], pre_sem.at[i % 2]),
        )

    def keep_rows(i):
        return pltpu.make_async_copy(gathered.at[span(order[i]), :], rows_hbm.at[span(order[i]), :], rows_sem.at[i])

    def work(i):
        at = order[i]
        keep_rows(i).start()
        load(i).wait()
        if i + 1 < n:
            load(i + 1).start()
        if i >= 2:
            for copy in store(i - 2):
                copy.wait()

        def columns(j, carry):
            cols = pl.ds(pl.multiple_of(j * tile, tile), tile)
            before = (
                jnp.dot(gathered[span(at), :], up_ref[:, cols], preferred_element_type=jnp.float32)
                + bias_ref[:, cols]
            )
            back = lax.dot_general(grads[i % 2], down_ref[cols, :], NT, preferred_element_type=jnp.float32)
            active, slope = gelu_both(before)
            act[i % 2, :, cols] = active.astype(act.dtype)
            rounded = (back * slope).astype(pre.dtype)
            pre[i % 2, :, cols] = rounded
            sum_ref[:, cols] += jnp.sum(rounded.astype(jnp.float32), axis=0, keepdims=True)
            return carry

        lax.fori_loop(0, width // tile, columns, 0)
        for copy in store(i):
            copy.start()

    sum_ref[...] = jnp.zeros_like(sum_ref)
    load(0).start()
    gather.start()
    gather.keep().wait()
    work(0)
    gather.wait_core(0)
    work(1)
    i = 2
    for count in range(1, gather.bits + 1):
        masks = gather.level(count)
        gather.forward(count)
        for _ in masks:
            work(i)
            i += 1
        for mask in masks:
            gather.wait_core(mask)
            work(i)
            i += 1
    for last in (n - 2, n - 1):
        for copy in store(last):
            copy.wait()
    for i in range(n):
        keep_rows(i).wait()
    gather.finish_sends()


def expand(own, grad_rows, up, down, bias, n, collective_id):
    rows, depth = own.shape
    width = up.shape[1]
    total = n * rows
    vmem = pl.BlockSpec(memory_space=pltpu.VMEM)
    hbm = pl.BlockSpec(memory_space=pl.ANY)
    dma = pltpu.SemaphoreType.DMA
    return pl.pallas_call(
        functools.partial(expand_kernel, n),
        out_shape=(
            jax.ShapeDtypeStruct((total, depth), jnp.bfloat16),
            jax.ShapeDtypeStruct((total, width), jnp.bfloat16),
            jax.ShapeDtypeStruct((total, width), jnp.bfloat16),
            jax.ShapeDtypeStruct((1, width), jnp.float32),
        ),
        in_specs=[vmem, hbm, vmem, vmem, vmem],
        out_specs=(hbm, hbm, hbm, vmem),
        scratch_shapes=[
            pltpu.VMEM((total, depth), jnp.bfloat16),
            pltpu.VMEM((2, rows, depth), jnp.bfloat16),
            pltpu.VMEM((2, rows, width), jnp.bfloat16),
            pltpu.VMEM((2, rows, width), jnp.bfloat16),
            dma((2,)),
            dma((2,)),
            dma((2,)),
            dma((n,)),
        ]
        + gather_sems(n),
        compiler_params=pltpu.CompilerParams(
            collective_id=collective_id, has_side_effects=True, vmem_limit_bytes=VMEM_LIMIT
        ),
        cost_estimate=LINK_COST,
        name="expand",
    )(own, grad_rows, up, down, bias)


class Product:
    def __init__(self, left, right, out, scratch):
        self.left, self.right, self.out = left, right, out
        self.lbuf, self.rbuf, self.acc, self.obuf, self.left_sem, self.right_sem, self.out_sem = scratch
        self.depth, self.tall = self.lbuf.shape[1:]
        self.wide = self.rbuf.shape[2]
        self.inner = left.shape[0] // self.depth
        self.across = right.shape[1] // self.wide
        self.steps = (left.shape[1] // self.tall) * self.across * self.inner

    def load(self, i):
        k = lax.rem(i, self.inner)
        col = lax.rem(i // self.inner, self.across)
        row = i // (self.inner * self.across)
        rows = pl.ds(pl.multiple_of(k * self.depth, self.depth), self.depth)
        slot = lax.rem(i, 2)
        return (
            pltpu.make_async_copy(
                self.left.at[rows, pl.ds(pl.multiple_of(row * self.tall, self.tall), self.tall)],
                self.lbuf.at[slot],
                self.left_sem.at[slot],
            ),
            pltpu.make_async_copy(
                self.right.at[rows, pl.ds(pl.multiple_of(col * self.wide, self.wide), self.wide)],
                self.rbuf.at[slot],
                self.right_sem.at[slot],
            ),
        )

    def store(self, tile):
        col = lax.rem(tile, self.across)
        row = tile // self.across
        return pltpu.make_async_copy(
            self.obuf,
            self.out.at[
                pl.ds(pl.multiple_of(row * self.tall, self.tall), self.tall),
                pl.ds(pl.multiple_of(col * self.wide, self.wide), self.wide),
            ],
            self.out_sem,
        )

    def start(self):
        for copy in self.load(0):
            copy.start()

    def step(self, i, carry=0):
        for copy in self.load(i):
            copy.wait()

        @pl.when(i + 1 < self.steps)
        def _():
            for copy in self.load(i + 1):
                copy.start()

        k = lax.rem(i, self.inner)
        slot = lax.rem(i, 2)
        part = min(self.wide, 512)

        @pl.when(k == 0)
        def _():
            self.acc[...] = jnp.zeros_like(self.acc)

        for first in range(0, self.wide, part):
            cols = slice(first, first + part)
            self.acc[:, cols] += lax.dot_general(
                self.lbuf[slot], self.rbuf[slot, :, cols], TN, preferred_element_type=jnp.float32
            )

        @pl.when(k == self.inner - 1)
        def _():
            tile = i // self.inner

            @pl.when(tile > 0)
            def _():
                self.store(tile - 1).wait()

            self.obuf[...] = self.acc[...].astype(self.obuf.dtype)
            self.store(tile).start()

        return carry

    def batch(self, j, batches):
        per = -(-self.steps // batches)
        first = j * per
        lax.fori_loop(first, jnp.minimum(first + per, self.steps), self.step, 0)

    def finish(self):
        self.store(self.steps // self.inner - 1).wait()


def product_scratch(rows, tall, wide):
    dma = pltpu.SemaphoreType.DMA
    depth = min(1024, rows)
    tall, wide = min(512, tall), min(1024, wide)
    return [
        pltpu.VMEM((2, depth, tall), jnp.bfloat16),
        pltpu.VMEM((2, depth, wide), jnp.bfloat16),
        pltpu.VMEM((tall, wide), jnp.float32),
        pltpu.VMEM((tall, wide), jnp.bfloat16),
        dma((2,)),
        dma((2,)),
        dma(()),
    ]


def row_blocks(rows, each, work):
    def one(i, carry):
        work(pl.ds(pl.multiple_of(i * each, each), each))
        return carry

    lax.fori_loop(0, rows // each, one, 0)


def normal_rows(value):
    center = value - jnp.mean(value, axis=1, keepdims=True)
    factor = lax.rsqrt(jnp.mean(center * center, axis=1, keepdims=True) + 1e-05)
    return center * factor, factor


def dense_kernel(
    n, a_hbm, w_ref, input_hbm, bias_ref, gain_ref, shift_ref, out_ref, next_ref, inputs, input_sem, *scratch
):
    fetch = pltpu.make_async_copy(input_hbm, inputs, input_sem)
    fetch.start()
    Scatter(n, False, a_hbm, w_ref, out_ref, scratch).run()
    fetch.wait()

    def work(at):
        residual = inputs[at, :].astype(jnp.float32) + out_ref[at, :] + bias_ref[...]
        out_ref[at, :] = residual
        normed, _ = normal_rows(residual)
        next_ref[at, :] = (normed * gain_ref[...] + shift_ref[...]).astype(next_ref.dtype)

    row_blocks(out_ref.shape[0], 32, work)


def back_rows(grad, source, gain):
    normed, factor = normal_rows(source)
    scaled = grad * gain
    product = grad * normed
    back = factor * (
        scaled
        - jnp.mean(scaled, axis=1, keepdims=True)
        - normed * jnp.mean(scaled * normed, axis=1, keepdims=True)
    )
    return back, product


def column_sum(value):
    return jnp.sum(value, axis=0, keepdims=True)


def expand_back_kernel(
    n, a_hbm, w_ref, act_hbm, rows_hbm, residual_hbm, cotangent_hbm, gain_ref,
    out_ref, next_ref, sums_ref, grad_hbm, residual, cotangent, fetch_sem, *scratch
):
    fetches = (
        pltpu.make_async_copy(residual_hbm, residual, fetch_sem.at[0]),
        pltpu.make_async_copy(cotangent_hbm, cotangent, fetch_sem.at[1]),
    )
    for fetch in fetches:
        fetch.start()
    product = Product(act_hbm, rows_hbm, grad_hbm, scratch[:7])
    scatter = Scatter(n, True, a_hbm, w_ref, out_ref, scratch[7:])
    product.start()
    scatter.run(lambda j: product.batch(j, scatter.chunks))
    product.finish()
    for fetch in fetches:
        fetch.wait()
    sums_ref[...] = jnp.zeros_like(sums_ref)

    def work(at):
        grad = out_ref[at, :]
        other = cotangent[at, :].astype(jnp.float32)
        back, terms = back_rows(grad, residual[at, :], gain_ref[...])
        result = other + back
        out_ref[at, :] = result
        next_ref[at, :] = result.astype(next_ref.dtype)
        sums_ref[0:1, :] += column_sum(terms)
        sums_ref[1:2, :] += column_sum(grad)
        sums_ref[2:3, :] += column_sum(result)
        sums_ref[3:4, :] += column_sum(other)

    row_blocks(out_ref.shape[0], 32, work)


def comm_params(collective_id):
    return pltpu.CompilerParams(collective_id=collective_id, has_side_effects=True, vmem_limit_bytes=VMEM_LIMIT)


VMEM_SPEC = pl.BlockSpec(memory_space=pltpu.VMEM)
HBM_SPEC = pl.BlockSpec(memory_space=pl.ANY)
CHUNKS = 4


def dense(mixed, weight, inputs, bias, gain, shift, n, collective_id):
    rows, width = inputs.shape
    return pl.pallas_call(
        functools.partial(dense_kernel, n),
        out_shape=(
            jax.ShapeDtypeStruct((rows, width), jnp.float32),
            jax.ShapeDtypeStruct((rows, width), jnp.bfloat16),
        ),
        in_specs=[HBM_SPEC, VMEM_SPEC, HBM_SPEC, VMEM_SPEC, VMEM_SPEC, VMEM_SPEC],
        out_specs=(VMEM_SPEC, VMEM_SPEC),
        scratch_shapes=[pltpu.VMEM((rows, width), inputs.dtype), pltpu.SemaphoreType.DMA(())]
        + scatter_scratch(n, rows, mixed.shape[1], width, CHUNKS),
        compiler_params=comm_params(collective_id),
        cost_estimate=LINK_COST,
        name="dense",
    )(mixed, weight, inputs, bias, gain, shift)


def expand_back(grad_pre, up, activated, grad_rows, residual, cotangent, gain, n, collective_id):
    rows, width = residual.shape
    units = activated.shape[1]
    return pl.pallas_call(
        functools.partial(expand_back_kernel, n),
        out_shape=(
            jax.ShapeDtypeStruct((rows, width), jnp.float32),
            jax.ShapeDtypeStruct((rows, width), jnp.bfloat16),
            jax.ShapeDtypeStruct((8, width), jnp.float32),
            jax.ShapeDtypeStruct((units, width), jnp.bfloat16),
        ),
        in_specs=[HBM_SPEC, VMEM_SPEC, HBM_SPEC, HBM_SPEC, HBM_SPEC, HBM_SPEC, VMEM_SPEC],
        out_specs=(VMEM_SPEC, VMEM_SPEC, VMEM_SPEC, HBM_SPEC),
        scratch_shapes=[
            pltpu.VMEM((rows, width), jnp.float32),
            pltpu.VMEM((rows, width), cotangent.dtype),
            pltpu.SemaphoreType.DMA((2,)),
        ]
        + product_scratch(n * rows, units, width)
        + scatter_scratch(n, rows, units, width, CHUNKS),
        compiler_params=comm_params(collective_id),
        cost_estimate=LINK_COST,
        name="expand_back",
    )(grad_pre, up, activated, grad_rows, residual, cotangent, gain)


def dense_back_kernel(
    n, own_ref, mixed_ref, w_ref, left_hbm, right_hbm, grad_mixed_ref, grad_dense_ref, grad_up_hbm, gathered, acc, *scratch
):
    product = Product(left_hbm, right_hbm, grad_up_hbm, scratch[:7])
    gather = Gather(n, own_ref, gathered, scratch[7:])
    rows = own_ref.shape[0]

    def work(at):
        span = pl.ds(pl.multiple_of(at * rows, rows), rows)
        grad_mixed_ref[span, :] = lax.dot_general(
            gathered[span, :], w_ref[...], NT, preferred_element_type=jnp.float32
        ).astype(grad_mixed_ref.dtype)
        width = acc.shape[1]
        part = min(width, 512)
        for first in range(0, width, part):
            cols = slice(first, first + part)
            acc[:, cols] += lax.dot_general(
                mixed_ref[span, :], gathered[span, cols], TN, preferred_element_type=jnp.float32
            )

    product.start()
    gather.start()
    acc[...] = jnp.zeros_like(acc)
    product.batch(0, 1)
    for count in range(1, gather.bits + 1):
        gather.forward(count)
        if count == 1:
            gather.keep().wait()
            work(gather.place(0, 0))
            gather.wait_core(0)
            work(gather.place(0, 1))
        for core in (0, 1):
            for mask in gather.level(count):
                if core:
                    gather.wait_core(mask)
                work(gather.place(mask, core))
    grad_dense_ref[...] = acc[...].astype(grad_dense_ref.dtype)
    product.finish()
    gather.finish_sends()


def dense_back(own, mixed, weight, mlp_rows, grad_pre, n, collective_id):
    rows, width = own.shape
    total, depth = mixed.shape
    return pl.pallas_call(
        functools.partial(dense_back_kernel, n),
        out_shape=(
            jax.ShapeDtypeStruct((total, depth), jnp.bfloat16),
            jax.ShapeDtypeStruct((depth, width), jnp.bfloat16),
            jax.ShapeDtypeStruct((mlp_rows.shape[1], grad_pre.shape[1]), jnp.bfloat16),
        ),
        in_specs=[VMEM_SPEC, VMEM_SPEC, VMEM_SPEC, HBM_SPEC, HBM_SPEC],
        out_specs=(VMEM_SPEC, VMEM_SPEC, HBM_SPEC),
        scratch_shapes=[pltpu.VMEM((total, width), jnp.bfloat16), pltpu.VMEM((depth, width), jnp.float32)]
        + product_scratch(total, mlp_rows.shape[1], grad_pre.shape[1])
        + gather_sems(n),
        compiler_params=comm_params(collective_id),
        cost_estimate=LINK_COST,
        name="dense_back",
    )(own, mixed, weight, mlp_rows, grad_pre)


def attend_back_one(slope, proj_ref, grad_ref, start, head, column_ref, row_ref, out_ref, dk_ref, dv_ref, sums_ref, length):
    at = pl.multiple_of(head * 3 * HEAD_DIM, HEAD_DIM)
    own = pl.ds(pl.multiple_of(head * HEAD_DIM, HEAD_DIM), HEAD_DIM)

    def cols(which):
        return pl.ds(at + which * HEAD_DIM, HEAD_DIM)

    def take(which, first, size):
        return proj_ref[pl.ds(start + first, size), cols(which)]

    sums = None
    for first in reversed(range(0, length, BLOCK)):
        last = first + BLOCK
        q, g = take(0, first, BLOCK), grad_ref[pl.ds(start + first, BLOCK), own]
        scores = masked_scores(slope, q, take(1, 0, last), column_ref[first:last, :], row_ref[:, :last], first)
        top = jnp.max(scores, axis=1, keepdims=True)
        expo = jnp.exp2(scores - top)
        probs = expo * (1.0 / jnp.sum(expo, axis=1, keepdims=True))
        grad_probs = lax.dot_general(g, take(2, 0, last), NT, preferred_element_type=jnp.float32)
        product = probs * grad_probs
        grad_scores = (product - probs * jnp.sum(product, axis=1, keepdims=True)).astype(jnp.bfloat16)
        rounded = probs.astype(jnp.bfloat16)
        grad_queries = (jnp.dot(grad_scores, take(1, 0, last), preferred_element_type=jnp.float32) * SCALE).astype(
            out_ref.dtype
        )
        out_ref[pl.ds(start + first, BLOCK), cols(0)] = grad_queries
        here = column_sum(grad_queries.astype(jnp.float32))
        sums = here if sums is None else sums + here
        grad_keys = lax.dot_general(grad_scores, q, TN, preferred_element_type=jnp.float32)
        grad_values = lax.dot_general(rounded, g, TN, preferred_element_type=jnp.float32)
        if last == length:
            dk_ref[...] = grad_keys
            dv_ref[...] = grad_values
        else:
            dk_ref[:last, :] += grad_keys
            dv_ref[:last, :] += grad_values
    span = pl.ds(start, length)
    out_ref[span, cols(1)] = (dk_ref[...] * SCALE).astype(out_ref.dtype)
    grad_values = dv_ref[...].astype(out_ref.dtype)
    out_ref[span, cols(2)] = grad_values
    sums_ref[0:1, own] += sums
    sums_ref[1:2, own] += column_sum(grad_values.astype(jnp.float32))


def shrink_kernel(
    n, length, slope_ref, a_hbm, w_ref, residual_hbm, bias_ref, proj_hbm, grad_mixed_ref, column_ref, row_ref,
    hidden_ref, grad_proj_ref, sums_ref, out, residual, proj, dk, dv, fetch_sem, *scratch
):
    fetches = (
        pltpu.make_async_copy(proj_hbm, proj, fetch_sem.at[0]),
        pltpu.make_async_copy(residual_hbm, residual, fetch_sem.at[1]),
    )
    for fetch in fetches:
        fetch.start()
    scatter = Scatter(n, False, a_hbm, w_ref, out, scratch)
    heads = grad_proj_ref.shape[1] // (3 * HEAD_DIM)
    units = grad_proj_ref.shape[0] // length * heads
    per = -(-units // scatter.chunks)
    sums_ref[...] = jnp.zeros_like(sums_ref)

    def one(i, carry):
        s, head = i // heads, lax.rem(i, heads)
        attend_back_one(
            slope_ref[head], proj, grad_mixed_ref, pl.multiple_of(s * length, length), head, column_ref.at[s],
            row_ref.at[s], grad_proj_ref, dk, dv, sums_ref, length,
        )
        return carry

    def filler(j):
        @pl.when(j == 0)
        def _():
            fetches[0].wait()

        lax.fori_loop(j * per, jnp.minimum(j * per + per, units), one, 0)

    scatter.run(filler)
    fetches[1].wait()

    def work(at):
        hidden_ref[at, :] = (residual[at, :] + out[at, :] + bias_ref[...]).astype(hidden_ref.dtype)

    row_blocks(out.shape[0], 64, work)


def shrink(activated, down, residual, bias, slopes, proj, grad_mixed, labels, n, collective_id):
    rows, width = residual.shape
    heads_width = grad_mixed.shape[1]
    length = labels.shape[1]
    return pl.pallas_call(
        functools.partial(shrink_kernel, n, length),
        out_shape=(
            jax.ShapeDtypeStruct((rows, width), jnp.bfloat16),
            jax.ShapeDtypeStruct(proj.shape, jnp.bfloat16),
            jax.ShapeDtypeStruct((8, heads_width), jnp.float32),
        ),
        in_specs=[
            pl.BlockSpec(memory_space=pltpu.SMEM), HBM_SPEC, VMEM_SPEC, HBM_SPEC, VMEM_SPEC, HBM_SPEC, VMEM_SPEC, VMEM_SPEC,
            VMEM_SPEC,
        ],
        out_specs=(VMEM_SPEC, VMEM_SPEC, VMEM_SPEC),
        scratch_shapes=[
            pltpu.VMEM((rows, width), jnp.float32),
            pltpu.VMEM((rows, width), jnp.float32),
            pltpu.VMEM(proj.shape, jnp.bfloat16),
            pltpu.VMEM((length, HEAD_DIM), jnp.float32),
            pltpu.VMEM((length, HEAD_DIM), jnp.float32),
            pltpu.SemaphoreType.DMA((2,)),
        ]
        + scatter_scratch(n, rows, activated.shape[1], width, CHUNKS),
        compiler_params=comm_params(collective_id),
        cost_estimate=LINK_COST,
        name="shrink",
    )(slopes, activated, down, residual, bias, proj, grad_mixed, labels[:, :, None], labels[:, None, :])


def project_back_kernel(
    n, d, a_hbm, w_ref, input_hbm, grad_hbm, gain_ref, early_ref, up_sum_ref, head_sums_ref,
    out_ref, sums_ref, biases_ref, inputs, grads, fetch_sem, *scratch
):
    fetches = (
        pltpu.make_async_copy(input_hbm, inputs, fetch_sem.at[0]),
        pltpu.make_async_copy(grad_hbm, grads, fetch_sem.at[1]),
    )
    for fetch in fetches:
        fetch.start()
    early, biases, late = (Total(n, d, scratch[6 * i : 6 * i + 6]) for i in range(3))
    scatter = Scatter(n, True, a_hbm, w_ref, out_ref, scratch[18:])
    model = out_ref.shape[1]
    half, quarter = model // 2, model // 4
    heads_width = head_sums_ref.shape[1]

    def pack(i, width):
        return [(i * (model // width) + k, slice(k * width, (k + 1) * width)) for k in range(model // width)]

    def filler(j):
        for level in range(min(early.levels + 1, scatter.chunks)):

            @pl.when(j == level)
            def _():
                if level == 0:
                    biases.lines[0] = jnp.zeros(biases.lines.shape[1:], jnp.float32)
                    biases.lines[0, 0:1, :] = up_sum_ref[...]
                    biases.lines[0, 1:3, :heads_width] = head_sums_ref[0:2, :]
                    biases.spread()
                    for i in range(4):
                        for row, cols in pack(i, half):
                            early.pair[0, row : row + 1, :] = early_ref[i : i + 1, cols]
                early.step(level)

    scatter.run(filler, d)
    for level in range(scatter.chunks, early.levels + 1):
        early.step(level)
    for fetch in fetches:
        fetch.wait()
    late.pair[0] = jnp.zeros(late.pair.shape[1:], jnp.float32)

    def work(at):
        grad = out_ref[at, :]
        back, terms = back_rows(grad, inputs[at, :].astype(jnp.float32), gain_ref[...])
        out_ref[at, :] = grads[at, :] + back
        for i, value in enumerate((column_sum(terms), column_sum(grad))):
            for row, cols in pack(i, quarter):
                late.pair[0, row : row + 1, :] += value[:, cols]

    row_blocks(out_ref.shape[0], 32, work)
    late.step(0)
    biases_ref[...] = biases.finish(False)
    total = early.finish()
    for i in range(4):
        for row, cols in pack(i, half):
            sums_ref[i : i + 1, cols] = total[row : row + 1, :]
    for level in range(1, late.levels + 1):
        late.step(level)
    total = late.finish()
    for i in range(2):
        for row, cols in pack(i, quarter):
            sums_ref[4 + i : 5 + i, cols] = total[row : row + 1, :]
    sums_ref[6:8, :] = jnp.zeros((2, model), jnp.float32)


def project_back(grad_proj, weight, inputs, grad_residual, gain, early, up_sum, head_sums, n, d, collective_id):
    rows, width = inputs.shape
    units = up_sum.shape[1]
    return pl.pallas_call(
        functools.partial(project_back_kernel, n, d),
        out_shape=(
            jax.ShapeDtypeStruct((rows, width), jnp.float32),
            jax.ShapeDtypeStruct((8, width), jnp.float32),
            jax.ShapeDtypeStruct((8, units), jnp.float32),
        ),
        in_specs=[HBM_SPEC, VMEM_SPEC, HBM_SPEC, HBM_SPEC] + [VMEM_SPEC] * 4,
        out_specs=(VMEM_SPEC, VMEM_SPEC, VMEM_SPEC),
        scratch_shapes=[
            pltpu.VMEM((rows, width), inputs.dtype),
            pltpu.VMEM((rows, width), jnp.float32),
            pltpu.SemaphoreType.DMA((2,)),
        ]
        + total_scratch(n, d, 8, width // 2)
        + total_scratch(n, d, 8, units)
        + total_scratch(n, d, 8, width // 4)
        + scatter_scratch(n, rows, grad_proj.shape[1], width, CHUNKS),
        compiler_params=comm_params(collective_id),
        cost_estimate=LINK_COST,
        name="project_back",
    )(grad_proj, weight, inputs, grad_residual, gain, early, up_sum, head_sums)


HEADS = 16


def normalize(rows):
    center = rows - jnp.mean(rows, axis=1, keepdims=True)
    factor = lax.rsqrt(jnp.mean(center * center, axis=1, keepdims=True) + 1e-05)
    return center * factor


def wide(vector):
    return vector.astype(jnp.float32)[None]


def share(grad, dimension):
    return lax.psum_scatter(grad, "dp", scatter_dimension=dimension, tiled=True).astype(jnp.float32)


def on_device(
    hidden_input,
    first_gain,
    first_shift,
    qkv_weight,
    query_bias,
    value_bias,
    dense_weight,
    dense_bias,
    second_gain,
    second_shift,
    up_weight,
    up_bias,
    down_weight,
    down_bias,
    segments,
    document_lengths,
    cotangent,
    *,
    n,
    d,
):
    heads_local = query_bias.shape[0] // HEAD_DIM
    normed_first = normalize(hidden_input.astype(jnp.float32))
    attn_input = (normed_first * wide(first_gain) + wide(first_shift)).astype(jnp.bfloat16)
    attn_rows = gather_rows(attn_input, n, 1)
    project_full, dense_full, expand_full, shrink_full = (
        lax.all_gather(qkv_weight, "dp", axis=0, tiled=True),
        lax.all_gather(dense_weight, "dp", axis=1, tiled=True),
        lax.all_gather(up_weight, "dp", axis=0, tiled=True),
        lax.all_gather(down_weight, "dp", axis=1, tiled=True),
    )
    group_rows = attn_rows.shape[0]
    sequences = document_lengths.shape[0]
    length = group_rows // sequences
    heads_index = lax.axis_index("tensor") * heads_local + lax.broadcasted_iota(
        jnp.int32, (heads_local,), 0
    )
    slopes = jnp.exp2(-8.0 * (heads_index.astype(jnp.float32) + 1.0) / HEADS) * LOG2E
    position = lax.broadcasted_iota(jnp.int32, (sequences, length), 1)
    filled = jnp.sum(document_lengths, axis=1, keepdims=True)
    labels = jnp.where(position < filled, segments.reshape(sequences, length), length + position)
    query_bias32 = query_bias.astype(jnp.float32).reshape(heads_local, HEAD_DIM)
    value_bias32 = value_bias.astype(jnp.float32).reshape(heads_local, HEAD_DIM)
    proj_bias = jnp.stack((query_bias32, jnp.zeros_like(query_bias32), value_bias32), axis=1).reshape(
        heads_local * 3 * HEAD_DIM
    )
    grad_rows, proj, mixed = project_attend(
        attn_rows, project_full, proj_bias[None], slopes, labels, cotangent, n, 6
    )
    residual, mlp_input = dense(
        mixed, dense_full, hidden_input, wide(dense_bias), wide(second_gain), wide(second_shift), n, 2
    )
    mlp_rows, activated, grad_pre, sum_up_bias = expand(
        mlp_input, grad_rows, expand_full, shrink_full, wide(up_bias), n, 7
    )
    grad_residual, grad_attn_out, early_sums, grad_down = expand_back(
        grad_pre, expand_full, activated, grad_rows, residual, cotangent, wide(second_gain), n, 4
    )
    grad_down_weight = share(grad_down, 1)
    grad_mixed, grad_dense, grad_up = dense_back(grad_attn_out, mixed, dense_full, mlp_rows, grad_pre, n, 9)
    grad_down_weight, activated, grad_mixed = lax.optimization_barrier((grad_down_weight, activated, grad_mixed))
    grad_up_weight = share(grad_up, 0)
    hidden_output, grad_proj, head_sums = shrink(
        activated, shrink_full, residual, wide(down_bias), slopes, proj, grad_mixed, labels, n, 3
    )
    grad_project = jnp.einsum("td,tc->dc", attn_rows, grad_proj, preferred_element_type=jnp.float32).astype(
        jnp.bfloat16
    )
    grad_qkv_weight = share(grad_project, 0)
    grad_dense_weight = share(grad_dense, 1)
    grad_input, sums, biases = project_back(
        grad_proj, project_full, hidden_input, grad_residual, wide(first_gain), early_sums, sum_up_bias, head_sums, n, d, 5
    )
    heads_width = heads_local * HEAD_DIM
    grad_second_gain, grad_second_shift, grad_dense_bias, grad_down_bias, grad_first_gain, grad_first_shift = (
        sums[i] for i in range(6)
    )
    grad_up_bias, grad_query_bias, grad_value_bias = biases[0], biases[1, :heads_width], biases[2, :heads_width]
    return (
        hidden_output,
        grad_input,
        grad_first_gain,
        grad_first_shift,
        grad_qkv_weight,
        grad_query_bias,
        grad_value_bias,
        grad_dense_weight,
        grad_dense_bias,
        grad_second_gain,
        grad_second_shift,
        grad_up_weight,
        grad_up_bias,
        grad_down_weight,
        grad_down_bias,
    )


def solution(mesh):
    return jax.shard_map(
        functools.partial(on_device, n=mesh.shape["tensor"], d=mesh.shape["dp"]),
        mesh=mesh,
        in_specs=(
            P(("dp", "tensor"), None),
            P(),
            P(),
            P("dp", "tensor"),
            P("tensor"),
            P("tensor"),
            P("tensor", "dp"),
            P(),
            P(),
            P(),
            P("dp", "tensor"),
            P("tensor"),
            P("tensor", "dp"),
            P(),
            P("dp"),
            P("dp", None),
            P(("dp", "tensor"), None),
        ),
        out_specs=(
            P(("dp", "tensor"), None),
            P(("dp", "tensor"), None),
            P(),
            P(),
            P("dp", "tensor"),
            P("tensor"),
            P("tensor"),
            P("tensor", "dp"),
            P(),
            P(),
            P(),
            P("dp", "tensor"),
            P("tensor"),
            P("tensor", "dp"),
            P(),
        ),
        check_vma=False,
    )
```

```python
import functools
import math

import jax
import jax.numpy as jnp
from jax import lax
from jax.experimental import pallas as pl
from jax.experimental.pallas import tpu as pltpu
from jax.sharding import PartitionSpec as P

VMEM_LIMIT = 62 << 20
LINK_COST = pl.CostEstimate(flops=0, bytes_accessed=280_000_000, transcendentals=0)


def flip(index, bit):
    return index + (1 - 2 * ((index // 2**bit) % 2)) * 2**bit


def chip_bits(n):
    return n.bit_length() - 2


def column_parts(width, count):
    blocks = width // 128
    edges = [128 * (blocks * i // count) for i in range(count + 1)]
    return [(a, b - a) for a, b in zip(edges[:-1], edges[1:])]


def peer(index):
    return {"tensor": index}


def greet(me, bits, d=1):
    barrier = pltpu.get_barrier_semaphore()
    for bit in range(bits + 1):
        pl.semaphore_signal(
            barrier, inc=1, device_id=peer(flip(me, bit)), device_id_type=pl.DeviceIdType.MESH
        )
    for ahead in range(1, d):
        pl.semaphore_signal(
            barrier, inc=1, device_id=ahead_on_dp(ahead, d), device_id_type=pl.DeviceIdType.MESH
        )
    pl.semaphore_wait(barrier, bits + d)


def ahead_on_dp(ahead, d):
    return {"dp": lax.rem(lax.axis_index("dp") + ahead, d)}


def remote(src, dst, send_sem, recv_sem, target):
    return pltpu.make_async_remote_copy(
        src_ref=src,
        dst_ref=dst,
        send_sem=send_sem,
        recv_sem=recv_sem,
        device_id=peer(target),
        device_id_type=pl.DeviceIdType.MESH,
    )


class Gather:
    def __init__(self, n, own_ref, out_ref, sems):
        self.me = lax.axis_index("tensor")
        self.bits = chip_bits(n)
        self.rows, width = own_ref.shape
        self.parts = column_parts(width, self.bits)
        self.own, self.out = own_ref, out_ref
        self.own_sem, self.chip_send, self.chip_recv, self.core_send, self.core_recv = sems
        self.sends = []

    def slot(self, part, index):
        at = self.me
        for step in range(self.bits):
            if (index >> step) & 1:
                at = flip(at, 1 + (part + step) % self.bits)
        return at

    def place(self, mask, core):
        at = flip(self.me, 0) if core else self.me
        for bit in range(self.bits):
            if (mask >> bit) & 1:
                at = flip(at, 1 + bit)
        return at

    def index_of(self, part, mask):
        return sum(2 ** ((bit - part) % self.bits) for bit in range(self.bits) if (mask >> bit) & 1)

    def level(self, count):
        return [index for index in range(2**self.bits) if index.bit_count() == count]

    def block(self, part, index, core=0):
        start, size = self.parts[part]
        at = flip(self.slot(part, index), 0) if core else self.slot(part, index)
        return self.out.at[pl.ds(pl.multiple_of(at * self.rows, self.rows), self.rows), pl.ds(start, size)]

    def source(self, part, index):
        start, size = self.parts[part]
        return self.own.at[:, pl.ds(start, size)] if index == 0 else self.block(part, index)

    def send(self, part, index, step):
        arrives = index + 2**step
        copy = remote(
            self.source(part, index),
            self.block(part, index),
            self.chip_send.at[part, arrives],
            self.chip_recv.at[part, arrives],
            flip(self.me, 1 + (part + step) % self.bits),
        )
        copy.start()
        self.sends.append(copy)

    def hand_over(self, part, index):
        copy = remote(
            self.source(part, index),
            self.block(part, index),
            self.core_send.at[part, index],
            self.core_recv.at[part, index],
            flip(self.me, 0),
        )
        copy.start()
        self.sends.append(copy)

    def keep(self):
        rows = pl.ds(pl.multiple_of(self.me * self.rows, self.rows), self.rows)
        return pltpu.make_async_copy(self.own, self.out.at[rows, :], self.own_sem)

    def start(self):
        greet(self.me, self.bits)
        for step in range(self.bits):
            for part in range(self.bits):
                self.send(part, 0, step)
        for part in range(self.bits):
            self.hand_over(part, 0)
        self.keep().start()

    def forward(self, count):
        for index in self.level(count):
            for part in range(self.bits):
                arrived = self.block(part, index)
                remote(
                    arrived, arrived, self.chip_send.at[part, index], self.chip_recv.at[part, index], flip(self.me, 0)
                ).wait_recv()
                for step in range(index.bit_length(), self.bits):
                    self.send(part, index, step)
                self.hand_over(part, index)

    def wait_core(self, mask):
        for part in range(self.bits):
            index = self.index_of(part, mask)
            arrived = self.block(part, index, 1)
            remote(
                arrived, arrived, self.core_send.at[part, index], self.core_recv.at[part, index], flip(self.me, 0)
            ).wait_recv()

    def finish_sends(self):
        for copy in self.sends:
            copy.wait_send()


def gather_kernel(n, x_ref, out_ref, *sems):
    gather = Gather(n, x_ref, out_ref, sems)
    gather.start()
    for count in range(1, gather.bits + 1):
        gather.forward(count)
    for mask in range(2**gather.bits):
        gather.wait_core(mask)
    gather.finish_sends()
    gather.keep().wait()


def gather_sems(n):
    bits = chip_bits(n)
    dma = pltpu.SemaphoreType.DMA
    return [dma(())] + [dma((bits, 2**bits))] * 4


def gather_rows(x, n, collective_id):
    rows, width = x.shape
    return pl.pallas_call(
        functools.partial(gather_kernel, n),
        out_shape=jax.ShapeDtypeStruct((n * rows, width), x.dtype),
        in_specs=[pl.BlockSpec(memory_space=pltpu.VMEM)],
        out_specs=pl.BlockSpec(memory_space=pl.ANY),
        scratch_shapes=gather_sems(n),
        compiler_params=pltpu.CompilerParams(
            collective_id=collective_id, has_side_effects=True, vmem_limit_bytes=VMEM_LIMIT
        ),
        cost_estimate=LINK_COST,
        name="gather_rows",
    )(x)


class Scatter:
    def __init__(self, n, transposed, a_hbm, w_ref, out_ref, scratch):
        (self.csend, self.crecv, self.recv, self.other, self.mine, self.load_sem) = scratch[:6]
        self.core_send, self.core_recv, self.chip_send, self.chip_recv = scratch[6:]
        self.me = lax.axis_index("tensor")
        self.bits = chip_bits(n)
        self.total = 2**self.bits
        self.transposed = transposed
        self.a, self.w, self.out = a_hbm, w_ref, out_ref
        self.rows, width = out_ref.shape
        self.chunk = self.csend.shape[2]
        self.chunks = self.rows // self.chunk
        self.parts = column_parts(width, self.bits)

    def index_of(self, part, mask):
        top = self.bits - 1
        return sum(2 ** (top - (bit - part) % self.bits) for bit in range(self.bits) if (mask >> bit) & 1)

    def place(self, mask, core):
        at = flip(self.me, 0) if core else self.me
        for bit in range(self.bits):
            if (mask >> bit) & 1:
                at = flip(at, 1 + bit)
        return at

    def rows_of(self, j):
        return pl.ds(pl.multiple_of(j * self.chunk, self.chunk), self.chunk)

    def loads(self, j, core):
        into = self.other if core else self.mine
        copies = []
        for mask in range(self.total):
            start = pl.multiple_of(self.place(mask, core) * self.rows + j * self.chunk, self.chunk)
            copies.append(
                pltpu.make_async_copy(
                    self.a.at[pl.ds(start, self.chunk), :],
                    into.at[lax.rem(j, 2), pl.ds(mask * self.chunk, self.chunk), :],
                    self.load_sem.at[core, lax.rem(j, 2), mask],
                )
            )
        return copies

    def core_copy(self, j, part):
        start, size = self.parts[part]
        return remote(
            self.csend.at[lax.rem(j, 2), :, :, pl.ds(start, size)],
            self.crecv.at[:, self.rows_of(j), pl.ds(start, size)],
            self.core_send.at[part, j],
            self.core_recv.at[part, j],
            flip(self.me, 0),
        )

    def chip_copy(self, j, part, step):
        half = self.total >> (step + 1)
        first = sum(self.total >> (s + 1) for s in range(step))
        start, size = self.parts[part]
        return remote(
            self.crecv.at[pl.ds(half, half), self.rows_of(j), pl.ds(start, size)],
            self.recv.at[pl.ds(first, half), self.rows_of(j), pl.ds(start, size)],
            self.chip_send.at[part, step, j],
            self.chip_recv.at[part, step, j],
            flip(self.me, 1 + (part + step) % self.bits),
        )

    def tiles(self, part, lhs, put):
        start, size = self.parts[part]
        tile = 256 if size % 256 == 0 and start % 256 == 0 else 128

        def one(i, carry):
            cols = pl.ds(pl.multiple_of(start + i * tile, tile), tile)
            if self.transposed:
                value = lax.dot_general(
                    lhs[...], self.w[cols, :], (((1,), (1,)), ((), ())), preferred_element_type=jnp.float32
                )
            else:
                value = jnp.dot(lhs[...], self.w[:, cols], preferred_element_type=jnp.float32)
            put(cols, value)
            return carry

        lax.fori_loop(0, size // tile, one, 0)

    def piece(self, value, mask):
        return value[mask * self.chunk : (mask + 1) * self.chunk, :]

    def stage_core(self, j):
        for copy in self.loads(j, 1):
            copy.wait()

        @pl.when(j >= 2)
        def _():
            for part in range(self.bits):
                self.core_copy(j - 2, part).wait_send()

        for part in range(self.bits):

            def put(cols, value):
                for mask in range(self.total):
                    self.csend[lax.rem(j, 2), self.index_of(part, mask), :, cols] = self.piece(value, mask).astype(
                        self.csend.dtype
                    )

            self.tiles(part, self.other.at[lax.rem(j, 2)], put)
            self.core_copy(j, part).start()

    def stage_first(self, j):
        for copy in self.loads(j, 0):
            copy.wait()
        for part in range(self.bits):
            self.core_copy(j, part).wait_recv()

            def put(cols, value):
                for mask in range(self.total):
                    index = self.index_of(part, mask)
                    got = self.piece(value, mask) + self.crecv[index, self.rows_of(j), cols].astype(jnp.float32)
                    if index:
                        self.crecv[index, self.rows_of(j), cols] = got.astype(self.crecv.dtype)
                    else:
                        self.out[self.rows_of(j), cols] = got

            self.tiles(part, self.mine.at[lax.rem(j, 2)], put)
            self.chip_copy(j, part, 0).start()

    def stage_next(self, j, step):
        half = self.total >> (step + 1)
        first = sum(self.total >> (s + 1) for s in range(step))
        for part in range(self.bits):
            start, size = self.parts[part]
            cols = slice(start, start + size)
            self.chip_copy(j, part, step).wait_recv()
            for index in reversed(range(half)):
                got = self.recv[first + index, self.rows_of(j), cols].astype(jnp.float32)
                if index:
                    value = self.crecv[index, self.rows_of(j), cols].astype(jnp.float32) + got
                    self.crecv[index, self.rows_of(j), cols] = value.astype(self.crecv.dtype)
                else:
                    self.out[self.rows_of(j), cols] += got
            if step + 1 < self.bits:
                self.chip_copy(j, part, step + 1).start()

    def run(self, filler=None, after=None, d=1):
        for copy in self.loads(0, 1):
            copy.start()
        greet(self.me, self.bits, d)

        def body(u, carry):
            @pl.when(u + 1 < self.chunks)
            def _():
                for copy in self.loads(u + 1, 1):
                    copy.start()

            @pl.when(u < self.chunks)
            def _():
                for copy in self.loads(u, 0):
                    copy.start()
                self.stage_core(u)

            @pl.when((u >= 1) & (u <= self.chunks))
            def _():
                self.stage_first(u - 1)

            for step in range(self.bits):

                @pl.when((u >= 2 + step) & (u < self.chunks + 2 + step))
                def _():
                    self.stage_next(u - 2 - step, step)

            if filler is not None:

                @pl.when((u >= 1) & (u <= self.chunks))
                def _():
                    filler(u - 1)

            if after is not None:
                done = u - self.bits - 1

                @pl.when(done >= 0)
                def _():
                    after(done)

            return carry

        lax.fori_loop(0, self.chunks + self.bits + 1, body, 0)
        for part in range(self.bits):
            for j in range(self.chunks):
                if j >= self.chunks - 2:
                    self.core_copy(j, part).wait_send()
                for step in range(self.bits):
                    self.chip_copy(j, part, step).wait_send()


def scatter_scratch(n, rows, depth, width, chunks):
    bits = chip_bits(n)
    total = 2**bits
    chunk = rows // chunks
    dma = pltpu.SemaphoreType.DMA
    return [
        pltpu.VMEM((2, total, chunk, width), jnp.bfloat16),
        pltpu.VMEM((total, rows, width), jnp.bfloat16),
        pltpu.VMEM((total - 1, rows, width), jnp.bfloat16),
        pltpu.VMEM((2, total * chunk, depth), jnp.bfloat16),
        pltpu.VMEM((2, total * chunk, depth), jnp.bfloat16),
        dma((2, 2, total)),
        dma((bits, chunks)),
        dma((bits, chunks)),
        dma((bits, bits, chunks)),
        dma((bits, bits, chunks)),
    ]


HEAD_DIM = 128
LOG2E = 1.4426950408889634
SCALE = 1.0 / math.sqrt(HEAD_DIM)
BLOCK = 256
NT = (((1,), (1,)), ((), ()))
TN = (((0,), (0,)), ((), ()))


def masked_scores(slope, q, keys, query_labels, key_labels, first):
    raw = lax.dot_general(q, keys, NT, preferred_element_type=jnp.float32)
    rows, width = raw.shape
    column = lax.broadcasted_iota(jnp.int32, (1, width), 1)
    bias = column.astype(jnp.float32) * slope
    same = query_labels == key_labels
    causal = lax.broadcasted_iota(jnp.int32, (rows, width), 1) <= first + lax.broadcasted_iota(
        jnp.int32, (rows, width), 0
    )
    return jnp.where(same & causal, raw * (SCALE * LOG2E) + bias, -1e30)


class Total:
    def __init__(self, n, d, scratch):
        self.pair, self.lines, self.send, self.recv, self.line_send, self.line_recv = scratch
        self.me, self.d = lax.axis_index("tensor"), d
        self.levels = n.bit_length() - 1

    def level_copy(self, level):
        return remote(
            self.pair.at[2 * level],
            self.pair.at[2 * level + 1],
            self.send.at[level],
            self.recv.at[level],
            flip(self.me, level),
        )

    def line_copy(self, ahead):
        return pltpu.make_async_remote_copy(
            src_ref=self.lines.at[0],
            dst_ref=self.lines.at[ahead],
            send_sem=self.line_send.at[ahead],
            recv_sem=self.line_recv.at[ahead],
            device_id=ahead_on_dp(ahead, self.d),
            device_id_type=pl.DeviceIdType.MESH,
        )

    def spread(self):
        for ahead in range(1, self.d):
            self.line_copy(ahead).start()

    def step(self, level):
        if level:
            self.level_copy(level - 1).wait_recv()
            self.pair[2 * level] = self.pair[2 * level - 2] + self.pair[2 * level - 1]
        if level < self.levels:
            self.level_copy(level).start()
        else:
            self.lines[0] = self.pair[2 * level]
            self.spread()

    def finish(self, levels=True):
        for ahead in range(1, self.d):
            self.line_copy(ahead).wait_recv()
        z = lax.axis_index("dp")
        total = None
        for index in range(self.d):
            value = self.lines[lax.rem(z - index + self.d, self.d)]
            total = value if total is None else total + value
        for ahead in range(1, self.d):
            self.line_copy(ahead).wait_send()
        if levels:
            for level in range(self.levels):
                self.level_copy(level).wait_send()
        return total


def total_scratch(n, d, rows, width):
    levels = n.bit_length() - 1
    dma = pltpu.SemaphoreType.DMA
    return [
        pltpu.VMEM((2 * levels + 1, rows, width), jnp.float32),
        pltpu.VMEM((d, rows, width), jnp.float32),
        dma((levels,)),
        dma((levels,)),
        dma((d,)),
        dma((d,)),
    ]


def tile_of(width):
    return 256 if width % 256 == 0 else width


def attend_one(slope, proj_ref, start, head, column_ref, row_ref, out_ref, length):
    at = pl.multiple_of(head * 3 * HEAD_DIM, HEAD_DIM)

    def take(which, first, size):
        return proj_ref[pl.ds(start + first, size), pl.ds(at + which * HEAD_DIM, HEAD_DIM)]

    for first in range(0, length, BLOCK):
        last = first + BLOCK
        scores = masked_scores(
            slope, take(0, first, BLOCK), take(1, 0, last), column_ref[first:last, :], row_ref[:, :last], first
        )
        top = jnp.max(scores, axis=1, keepdims=True)
        expo = jnp.exp2(scores - top)
        total = jnp.sum(expo, axis=1, keepdims=True)
        mixed = jnp.dot(expo.astype(jnp.bfloat16), take(2, 0, last), preferred_element_type=jnp.float32)
        out_ref[pl.ds(start + first, BLOCK), pl.ds(pl.multiple_of(head * HEAD_DIM, HEAD_DIM), HEAD_DIM)] = (
            mixed / total
        ).astype(out_ref.dtype)


def project_kernel(
    n, length, slope_ref, own_ref, rows_hbm, w_ref, bias_ref, column_ref, row_ref, gathered, proj_hbm, mixed_ref,
    proj, buf, load_sem, store_sem, *sems
):
    gather = Gather(n, own_ref, gathered, sems)
    rows = own_ref.shape[0]
    width = w_ref.shape[1]
    tile = tile_of(width)
    heads = width // (3 * HEAD_DIM)
    sequences = n * rows // length

    def load(i):
        at = pl.ds(pl.multiple_of(i * rows, rows), rows)
        return pltpu.make_async_copy(rows_hbm.at[at, :], buf.at[lax.rem(i, 2)], load_sem.at[lax.rem(i, 2)])

    load(0).start()
    gather.start()

    def store(i):
        at = pl.ds(pl.multiple_of(i * rows, rows), rows)
        return pltpu.make_async_copy(proj.at[at, :], proj_hbm.at[at, :], store_sem.at[i])

    def project(i, carry):
        load(i).wait()

        @pl.when(i + 1 < n)
        def _():
            load(i + 1).start()

        at = pl.ds(pl.multiple_of(i * rows, rows), rows)
        for first in range(0, width, tile):
            cols = slice(first, first + tile)
            proj[at, cols] = (
                jnp.dot(buf[lax.rem(i, 2)], w_ref[:, cols], preferred_element_type=jnp.float32) + bias_ref[:, cols]
            ).astype(proj.dtype)
        store(i).start()
        return carry

    lax.fori_loop(0, n, project, 0)
    gather.forward(1)

    def one(i, carry):
        s, head = i // heads, lax.rem(i, heads)
        attend_one(
            slope_ref[head],
            proj,
            pl.multiple_of(s * length, length),
            head,
            column_ref.at[s],
            row_ref.at[s],
            mixed_ref,
            length,
        )
        return carry

    lax.fori_loop(0, sequences * heads, one, 0)
    for count in range(2, gather.bits + 1):
        gather.forward(count)
    for i in range(n):
        store(i).wait()
    for mask in range(2**gather.bits):
        gather.wait_core(mask)
    gather.finish_sends()
    gather.keep().wait()


def project_attend(attn_rows, weight, bias, slopes, labels, own, n, collective_id):
    total, depth = attn_rows.shape
    rows, width = own.shape[0], weight.shape[1]
    heads = width // (3 * HEAD_DIM)
    vmem = pl.BlockSpec(memory_space=pltpu.VMEM)
    hbm = pl.BlockSpec(memory_space=pl.ANY)
    dma = pltpu.SemaphoreType.DMA
    return pl.pallas_call(
        functools.partial(project_kernel, n, labels.shape[1]),
        out_shape=(
            jax.ShapeDtypeStruct((total, own.shape[1]), own.dtype),
            jax.ShapeDtypeStruct((total, width), jnp.bfloat16),
            jax.ShapeDtypeStruct((total, heads * HEAD_DIM), jnp.bfloat16),
        ),
        in_specs=[pl.BlockSpec(memory_space=pltpu.SMEM), vmem, hbm, vmem, vmem, vmem, vmem],
        out_specs=(hbm, hbm, vmem),
        scratch_shapes=[
            pltpu.VMEM((total, width), jnp.bfloat16),
            pltpu.VMEM((2, rows, depth), jnp.bfloat16),
            dma((2,)),
            dma((n,)),
        ]
        + gather_sems(n),
        compiler_params=pltpu.CompilerParams(
            collective_id=collective_id, has_side_effects=True, vmem_limit_bytes=VMEM_LIMIT
        ),
        cost_estimate=LINK_COST,
        name="project_attend",
    )(slopes, own, attn_rows, weight, bias, labels[:, :, None], labels[:, None, :])


def gelu_both(value):
    c, a = 0.7978845608028654, 0.044715
    square = value * value
    half = 0.5 + 0.5 * jnp.tanh(value * (c + (c * a) * square))
    active = value * half
    slope = half + (2.0 * active) * (1.0 - half) * (c + (3.0 * c * a) * square)
    return active, slope


def expand_kernel(
    n, own_ref, grad_hbm, up_ref, down_ref, bias_ref, rows_hbm, act_hbm, pre_hbm, sum_ref,
    gathered, grads, act, pre, load_sem, act_sem, pre_sem, rows_sem, *sems
):
    gather = Gather(n, own_ref, gathered, sems)
    rows, depth = own_ref.shape
    width = up_ref.shape[1]
    tile = tile_of(width)
    order = [gather.place(mask, core) for mask in (0,) for core in (0, 1)]
    for count in range(1, gather.bits + 1):
        for core in (0, 1):
            order += [gather.place(mask, core) for mask in gather.level(count)]

    def span(at):
        return pl.ds(pl.multiple_of(at * rows, rows), rows)

    def load(i):
        return pltpu.make_async_copy(grad_hbm.at[span(order[i]), :], grads.at[i % 2], load_sem.at[i % 2])

    def store(i):
        return (
            pltpu.make_async_copy(act.at[i % 2], act_hbm.at[span(order[i]), :], act_sem.at[i % 2]),
            pltpu.make_async_copy(pre.at[i % 2], pre_hbm.at[span(order[i]), :], pre_sem.at[i % 2]),
        )

    def keep_rows(i):
        return pltpu.make_async_copy(gathered.at[span(order[i]), :], rows_hbm.at[span(order[i]), :], rows_sem.at[i])

    def work(i):
        at = order[i]
        keep_rows(i).start()
        load(i).wait()
        if i + 1 < n:
            load(i + 1).start()
        if i >= 2:
            for copy in store(i - 2):
                copy.wait()

        def columns(j, carry):
            cols = pl.ds(pl.multiple_of(j * tile, tile), tile)
            before = (
                jnp.dot(gathered[span(at), :], up_ref[:, cols], preferred_element_type=jnp.float32)
                + bias_ref[:, cols]
            )
            back = lax.dot_general(grads[i % 2], down_ref[cols, :], NT, preferred_element_type=jnp.float32)
            active, slope = gelu_both(before)
            act[i % 2, :, cols] = active.astype(act.dtype)
            rounded = (back * slope).astype(pre.dtype)
            pre[i % 2, :, cols] = rounded
            sum_ref[:, cols] += jnp.sum(rounded.astype(jnp.float32), axis=0, keepdims=True)
            return carry

        lax.fori_loop(0, width // tile, columns, 0)
        for copy in store(i):
            copy.start()

    sum_ref[...] = jnp.zeros_like(sum_ref)
    load(0).start()
    gather.start()
    gather.keep().wait()
    work(0)
    gather.wait_core(0)
    work(1)
    i = 2
    for count in range(1, gather.bits + 1):
        masks = gather.level(count)
        gather.forward(count)
        for _ in masks:
            work(i)
            i += 1
        for mask in masks:
            gather.wait_core(mask)
            work(i)
            i += 1
    for last in (n - 2, n - 1):
        for copy in store(last):
            copy.wait()
    for i in range(n):
        keep_rows(i).wait()
    gather.finish_sends()


def expand(own, grad_rows, up, down, bias, n, collective_id):
    rows, depth = own.shape
    width = up.shape[1]
    total = n * rows
    vmem = pl.BlockSpec(memory_space=pltpu.VMEM)
    hbm = pl.BlockSpec(memory_space=pl.ANY)
    dma = pltpu.SemaphoreType.DMA
    return pl.pallas_call(
        functools.partial(expand_kernel, n),
        out_shape=(
            jax.ShapeDtypeStruct((total, depth), jnp.bfloat16),
            jax.ShapeDtypeStruct((total, width), jnp.bfloat16),
            jax.ShapeDtypeStruct((total, width), jnp.bfloat16),
            jax.ShapeDtypeStruct((1, width), jnp.float32),
        ),
        in_specs=[vmem, hbm, vmem, vmem, vmem],
        out_specs=(hbm, hbm, hbm, vmem),
        scratch_shapes=[
            pltpu.VMEM((total, depth), jnp.bfloat16),
            pltpu.VMEM((2, rows, depth), jnp.bfloat16),
            pltpu.VMEM((2, rows, width), jnp.bfloat16),
            pltpu.VMEM((2, rows, width), jnp.bfloat16),
            dma((2,)),
            dma((2,)),
            dma((2,)),
            dma((n,)),
        ]
        + gather_sems(n),
        compiler_params=pltpu.CompilerParams(
            collective_id=collective_id, has_side_effects=True, vmem_limit_bytes=VMEM_LIMIT
        ),
        cost_estimate=LINK_COST,
        name="expand",
    )(own, grad_rows, up, down, bias)


class Product:
    def __init__(self, left, right, out, scratch):
        self.left, self.right, self.out = left, right, out
        self.lbuf, self.rbuf, self.acc, self.obuf, self.left_sem, self.right_sem, self.out_sem = scratch
        self.depth, self.tall = self.lbuf.shape[1:]
        self.wide = self.rbuf.shape[2]
        self.inner = left.shape[0] // self.depth
        self.across = right.shape[1] // self.wide
        self.steps = (left.shape[1] // self.tall) * self.across * self.inner

    def load(self, i):
        k = lax.rem(i, self.inner)
        col = lax.rem(i // self.inner, self.across)
        row = i // (self.inner * self.across)
        rows = pl.ds(pl.multiple_of(k * self.depth, self.depth), self.depth)
        slot = lax.rem(i, 2)
        return (
            pltpu.make_async_copy(
                self.left.at[rows, pl.ds(pl.multiple_of(row * self.tall, self.tall), self.tall)],
                self.lbuf.at[slot],
                self.left_sem.at[slot],
            ),
            pltpu.make_async_copy(
                self.right.at[rows, pl.ds(pl.multiple_of(col * self.wide, self.wide), self.wide)],
                self.rbuf.at[slot],
                self.right_sem.at[slot],
            ),
        )

    def store(self, tile):
        col = lax.rem(tile, self.across)
        row = tile // self.across
        return pltpu.make_async_copy(
            self.obuf,
            self.out.at[
                pl.ds(pl.multiple_of(row * self.tall, self.tall), self.tall),
                pl.ds(pl.multiple_of(col * self.wide, self.wide), self.wide),
            ],
            self.out_sem,
        )

    def start(self):
        for copy in self.load(0):
            copy.start()

    def step(self, i, carry=0):
        for copy in self.load(i):
            copy.wait()

        @pl.when(i + 1 < self.steps)
        def _():
            for copy in self.load(i + 1):
                copy.start()

        k = lax.rem(i, self.inner)
        slot = lax.rem(i, 2)
        part = next(size for size in (512, 384, self.wide) if self.wide % size == 0)

        @pl.when(k == 0)
        def _():
            self.acc[...] = jnp.zeros_like(self.acc)

        for first in range(0, self.wide, part):
            cols = slice(first, first + part)
            self.acc[:, cols] += lax.dot_general(
                self.lbuf[slot], self.rbuf[slot, :, cols], TN, preferred_element_type=jnp.float32
            )

        @pl.when(k == self.inner - 1)
        def _():
            tile = i // self.inner

            @pl.when(tile > 0)
            def _():
                self.store(tile - 1).wait()

            self.obuf[...] = self.acc[...].astype(self.obuf.dtype)
            self.store(tile).start()

        return carry

    def batch(self, j, batches):
        per = -(-self.steps // batches)
        first = j * per
        lax.fori_loop(first, jnp.minimum(first + per, self.steps), self.step, 0)

    def finish(self):
        self.store(self.steps // self.inner - 1).wait()


def product_scratch(rows, tall, wide):
    dma = pltpu.SemaphoreType.DMA
    depth = min(1024, rows)
    tall, wide = min(512, tall), min(1024, wide)
    return [
        pltpu.VMEM((2, depth, tall), jnp.bfloat16),
        pltpu.VMEM((2, depth, wide), jnp.bfloat16),
        pltpu.VMEM((tall, wide), jnp.float32),
        pltpu.VMEM((tall, wide), jnp.bfloat16),
        dma((2,)),
        dma((2,)),
        dma(()),
    ]


def row_blocks(first, rows, each, work):
    def one(i, carry):
        work(pl.ds(pl.multiple_of(first + i * each, each), each))
        return carry

    lax.fori_loop(0, rows // each, one, 0)


def after_chunk(scatter, fetches, work):
    def after(j):
        @pl.when(j == 0)
        def _():
            for fetch in fetches:
                fetch.wait()

        row_blocks(j * scatter.chunk, scatter.chunk, 32, work)

    return after


def normal_rows(value):
    center = value - jnp.mean(value, axis=1, keepdims=True)
    factor = lax.rsqrt(jnp.mean(center * center, axis=1, keepdims=True) + 1e-05)
    return center * factor, factor


def dense_kernel(
    n, a_hbm, w_ref, input_hbm, bias_ref, gain_ref, shift_ref, out_ref, next_ref, inputs, input_sem, *scratch
):
    fetch = pltpu.make_async_copy(input_hbm, inputs, input_sem)
    fetch.start()
    scatter = Scatter(n, False, a_hbm, w_ref, out_ref, scratch)

    def work(at):
        residual = inputs[at, :].astype(jnp.float32) + out_ref[at, :] + bias_ref[...]
        out_ref[at, :] = residual
        normed, _ = normal_rows(residual)
        next_ref[at, :] = (normed * gain_ref[...] + shift_ref[...]).astype(next_ref.dtype)

    scatter.run(after=after_chunk(scatter, (fetch,), work))


def back_rows(grad, source, gain):
    normed, factor = normal_rows(source)
    scaled = grad * gain
    product = grad * normed
    back = factor * (
        scaled
        - jnp.mean(scaled, axis=1, keepdims=True)
        - normed * jnp.mean(scaled * normed, axis=1, keepdims=True)
    )
    return back, product


def column_sum(value):
    return jnp.sum(value, axis=0, keepdims=True)


def expand_back_kernel(
    n, a_hbm, w_ref, act_hbm, rows_hbm, residual_hbm, cotangent_hbm, gain_ref,
    out_ref, next_ref, sums_ref, grad_hbm, residual, cotangent, fetch_sem, *scratch
):
    fetches = (
        pltpu.make_async_copy(residual_hbm, residual, fetch_sem.at[0]),
        pltpu.make_async_copy(cotangent_hbm, cotangent, fetch_sem.at[1]),
    )
    for fetch in fetches:
        fetch.start()
    product = Product(act_hbm, rows_hbm, grad_hbm, scratch[:7])
    scatter = Scatter(n, True, a_hbm, w_ref, out_ref, scratch[7:])
    product.start()
    sums_ref[...] = jnp.zeros_like(sums_ref)

    def work(at):
        grad = out_ref[at, :]
        other = cotangent[at, :].astype(jnp.float32)
        back, terms = back_rows(grad, residual[at, :], gain_ref[...])
        result = other + back
        out_ref[at, :] = result
        next_ref[at, :] = result.astype(next_ref.dtype)
        sums_ref[0:1, :] += column_sum(terms)
        sums_ref[1:2, :] += column_sum(grad)
        sums_ref[2:3, :] += column_sum(result)
        sums_ref[3:4, :] += column_sum(other)

    scatter.run(lambda j: product.batch(j, scatter.chunks), after_chunk(scatter, fetches, work))
    product.finish()


def comm_params(collective_id):
    return pltpu.CompilerParams(collective_id=collective_id, has_side_effects=True, vmem_limit_bytes=VMEM_LIMIT)


VMEM_SPEC = pl.BlockSpec(memory_space=pltpu.VMEM)
HBM_SPEC = pl.BlockSpec(memory_space=pl.ANY)
CHUNKS = 4


def dense(mixed, weight, inputs, bias, gain, shift, n, collective_id):
    rows, width = inputs.shape
    return pl.pallas_call(
        functools.partial(dense_kernel, n),
        out_shape=(
            jax.ShapeDtypeStruct((rows, width), jnp.float32),
            jax.ShapeDtypeStruct((rows, width), jnp.bfloat16),
        ),
        in_specs=[HBM_SPEC, VMEM_SPEC, HBM_SPEC, VMEM_SPEC, VMEM_SPEC, VMEM_SPEC],
        out_specs=(VMEM_SPEC, VMEM_SPEC),
        scratch_shapes=[pltpu.VMEM((rows, width), inputs.dtype), pltpu.SemaphoreType.DMA(())]
        + scatter_scratch(n, rows, mixed.shape[1], width, CHUNKS),
        compiler_params=comm_params(collective_id),
        cost_estimate=LINK_COST,
        name="dense",
    )(mixed, weight, inputs, bias, gain, shift)


def expand_back(grad_pre, up, activated, grad_rows, residual, cotangent, gain, n, collective_id):
    rows, width = residual.shape
    units = activated.shape[1]
    return pl.pallas_call(
        functools.partial(expand_back_kernel, n),
        out_shape=(
            jax.ShapeDtypeStruct((rows, width), jnp.float32),
            jax.ShapeDtypeStruct((rows, width), jnp.bfloat16),
            jax.ShapeDtypeStruct((8, width), jnp.float32),
            jax.ShapeDtypeStruct((units, width), jnp.bfloat16),
        ),
        in_specs=[HBM_SPEC, VMEM_SPEC, HBM_SPEC, HBM_SPEC, HBM_SPEC, HBM_SPEC, VMEM_SPEC],
        out_specs=(VMEM_SPEC, VMEM_SPEC, VMEM_SPEC, HBM_SPEC),
        scratch_shapes=[
            pltpu.VMEM((rows, width), jnp.float32),
            pltpu.VMEM((rows, width), cotangent.dtype),
            pltpu.SemaphoreType.DMA((2,)),
        ]
        + product_scratch(n * rows, units, width)
        + scatter_scratch(n, rows, units, width, CHUNKS),
        compiler_params=comm_params(collective_id),
        cost_estimate=LINK_COST,
        name="expand_back",
    )(grad_pre, up, activated, grad_rows, residual, cotangent, gain)


def attend_back_one(slope, proj_ref, grad_ref, start, head, column_ref, row_ref, out_ref, dk_ref, dv_ref, sums_ref, length):
    at = pl.multiple_of(head * 3 * HEAD_DIM, HEAD_DIM)
    own = pl.ds(pl.multiple_of(head * HEAD_DIM, HEAD_DIM), HEAD_DIM)

    def cols(which):
        return pl.ds(at + which * HEAD_DIM, HEAD_DIM)

    def take(which, first, size):
        return proj_ref[pl.ds(start + first, size), cols(which)]

    sums = None
    for first in reversed(range(0, length, BLOCK)):
        last = first + BLOCK
        q, g = take(0, first, BLOCK), grad_ref[pl.ds(start + first, BLOCK), own]
        scores = masked_scores(slope, q, take(1, 0, last), column_ref[first:last, :], row_ref[:, :last], first)
        top = jnp.max(scores, axis=1, keepdims=True)
        expo = jnp.exp2(scores - top)
        probs = expo * (1.0 / jnp.sum(expo, axis=1, keepdims=True))
        grad_probs = lax.dot_general(g, take(2, 0, last), NT, preferred_element_type=jnp.float32)
        product = probs * grad_probs
        grad_scores = (product - probs * jnp.sum(product, axis=1, keepdims=True)).astype(jnp.bfloat16)
        rounded = probs.astype(jnp.bfloat16)
        grad_queries = (jnp.dot(grad_scores, take(1, 0, last), preferred_element_type=jnp.float32) * SCALE).astype(
            out_ref.dtype
        )
        out_ref[pl.ds(start + first, BLOCK), cols(0)] = grad_queries
        here = column_sum(grad_queries.astype(jnp.float32))
        sums = here if sums is None else sums + here
        grad_keys = lax.dot_general(grad_scores, q, TN, preferred_element_type=jnp.float32)
        grad_values = lax.dot_general(rounded, g, TN, preferred_element_type=jnp.float32)
        if last == length:
            dk_ref[...] = grad_keys
            dv_ref[...] = grad_values
        else:
            dk_ref[:last, :] += grad_keys
            dv_ref[:last, :] += grad_values
    span = pl.ds(start, length)
    out_ref[span, cols(1)] = (dk_ref[...] * SCALE).astype(out_ref.dtype)
    grad_values = dv_ref[...].astype(out_ref.dtype)
    out_ref[span, cols(2)] = grad_values
    sums_ref[0:1, own] += sums
    sums_ref[1:2, own] += column_sum(grad_values.astype(jnp.float32))


def dense_back_kernel(
    n, length, slope_ref, own_ref, mixed_ref, w_ref, left_hbm, right_hbm, proj_hbm, column_ref, row_ref,
    grad_proj_ref, sums_ref, grad_dense_ref, grad_up_hbm, gathered, acc, grad_mixed, proj, dk, dv, fetch_sem, *scratch
):
    fetch = pltpu.make_async_copy(proj_hbm, proj, fetch_sem)
    fetch.start()
    product = Product(left_hbm, right_hbm, grad_up_hbm, scratch[:7])
    gather = Gather(n, own_ref, gathered, scratch[7:])
    rows = own_ref.shape[0]
    heads = sums_ref.shape[1] // HEAD_DIM
    chips = max(1, length // (2 * rows))
    sequences = max(1, 2 * rows // length)

    def work(at):
        span = pl.ds(pl.multiple_of(at * rows, rows), rows)
        grad_mixed[span, :] = lax.dot_general(
            gathered[span, :], w_ref[...], NT, preferred_element_type=jnp.float32
        ).astype(grad_mixed.dtype)
        width = acc.shape[1]
        part = min(width, 512)
        for first in range(0, width, part):
            cols = slice(first, first + part)
            acc[:, cols] += lax.dot_general(
                mixed_ref[span, :], gathered[span, cols], TN, preferred_element_type=jnp.float32
            )

    def attend(mask):
        first = (gather.place(mask, 0) // 2 // chips) * sequences

        def one(i, carry):
            s, head = first + i // heads, lax.rem(i, heads)
            attend_back_one(
                slope_ref[head], proj, grad_mixed, pl.multiple_of(s * length, length), head, column_ref.at[s],
                row_ref.at[s], grad_proj_ref, dk, dv, sums_ref, length,
            )
            return carry

        lax.fori_loop(0, sequences * heads, one, 0)

    arrived = {}

    def pair(mask):
        if mask == 0:
            gather.keep().wait()
        work(gather.place(mask, 0))
        gather.wait_core(mask)
        work(gather.place(mask, 1))
        group = arrived.setdefault(mask // chips, [])
        group.append(mask)
        if len(group) == chips:
            attend(mask)

    product.start()
    gather.start()
    acc[...] = jnp.zeros_like(acc)
    sums_ref[...] = jnp.zeros_like(sums_ref)
    product.batch(0, 1)
    fetch.wait()
    pair(0)
    for count in range(1, gather.bits + 1):
        gather.forward(count)
        for mask in gather.level(count):
            pair(mask)
    grad_dense_ref[...] = acc[...].astype(grad_dense_ref.dtype)
    product.finish()
    gather.finish_sends()


def dense_back(own, mixed, weight, mlp_rows, grad_pre, proj, slopes, labels, n, collective_id):
    rows, width = own.shape
    total, depth = mixed.shape
    length = labels.shape[1]
    return pl.pallas_call(
        functools.partial(dense_back_kernel, n, length),
        out_shape=(
            jax.ShapeDtypeStruct(proj.shape, jnp.bfloat16),
            jax.ShapeDtypeStruct((8, depth), jnp.float32),
            jax.ShapeDtypeStruct((depth, width), jnp.bfloat16),
            jax.ShapeDtypeStruct((mlp_rows.shape[1], grad_pre.shape[1]), jnp.bfloat16),
        ),
        in_specs=[pl.BlockSpec(memory_space=pltpu.SMEM), VMEM_SPEC, VMEM_SPEC, VMEM_SPEC]
        + [HBM_SPEC] * 3
        + [VMEM_SPEC] * 2,
        out_specs=(VMEM_SPEC, VMEM_SPEC, VMEM_SPEC, HBM_SPEC),
        scratch_shapes=[
            pltpu.VMEM((total, width), jnp.bfloat16),
            pltpu.VMEM((depth, width), jnp.float32),
            pltpu.VMEM((total, depth), jnp.bfloat16),
            pltpu.VMEM(proj.shape, jnp.bfloat16),
            pltpu.VMEM((length, HEAD_DIM), jnp.float32),
            pltpu.VMEM((length, HEAD_DIM), jnp.float32),
            pltpu.SemaphoreType.DMA(()),
        ]
        + product_scratch(total, mlp_rows.shape[1], grad_pre.shape[1])
        + gather_sems(n),
        compiler_params=comm_params(collective_id),
        cost_estimate=LINK_COST,
        name="dense_back",
    )(slopes, own, mixed, weight, mlp_rows, grad_pre, proj, labels[:, :, None], labels[:, None, :])


def shrink_kernel(
    n, d, a_hbm, w_ref, residual_hbm, bias_ref, early_ref, up_sum_ref, head_sums_ref,
    hidden_ref, sums_ref, biases_ref, out, residual, fetch_sem, *scratch
):
    fetch = pltpu.make_async_copy(residual_hbm, residual, fetch_sem)
    fetch.start()
    flat, biases = Total(n, d, scratch[:6]), Total(n, d, scratch[6:12])
    scatter = Scatter(n, False, a_hbm, w_ref, out, scratch[12:])
    heads_width = head_sums_ref.shape[1]

    def filler(j):
        for level in range(min(flat.levels + 1, scatter.chunks)):

            @pl.when(j == level)
            def _():
                if level == 0:
                    biases.lines[0] = jnp.zeros(biases.lines.shape[1:], jnp.float32)
                    biases.lines[0, 0:1, :] = up_sum_ref[...]
                    biases.lines[0, 1:3, :heads_width] = head_sums_ref[0:2, :]
                    biases.spread()
                    flat.pair[0] = early_ref[...]
                flat.step(level)

    def work(at):
        hidden_ref[at, :] = (residual[at, :] + out[at, :] + bias_ref[...]).astype(hidden_ref.dtype)

    scatter.run(filler, after_chunk(scatter, (fetch,), work), d)
    for level in range(scatter.chunks, flat.levels + 1):
        flat.step(level)
    biases_ref[...] = biases.finish(False)
    sums_ref[...] = flat.finish()


def shrink(activated, down, residual, bias, sums, up_sum, head_sums, n, d, collective_id):
    rows, width = residual.shape
    units = up_sum.shape[1]
    return pl.pallas_call(
        functools.partial(shrink_kernel, n, d),
        out_shape=(
            jax.ShapeDtypeStruct((rows, width), jnp.bfloat16),
            jax.ShapeDtypeStruct((8, width), jnp.float32),
            jax.ShapeDtypeStruct((8, units), jnp.float32),
        ),
        in_specs=[HBM_SPEC, VMEM_SPEC, HBM_SPEC] + [VMEM_SPEC] * 4,
        out_specs=(VMEM_SPEC, VMEM_SPEC, VMEM_SPEC),
        scratch_shapes=[
            pltpu.VMEM((rows, width), jnp.float32),
            pltpu.VMEM((rows, width), jnp.float32),
            pltpu.SemaphoreType.DMA(()),
        ]
        + total_scratch(n, d, 8, width)
        + total_scratch(n, d, 8, units)
        + scatter_scratch(n, rows, activated.shape[1], width, CHUNKS),
        compiler_params=comm_params(collective_id),
        cost_estimate=LINK_COST,
        name="shrink",
    )(activated, down, residual, bias, sums, up_sum, head_sums)


def project_back_kernel(
    n, a_hbm, w_ref, input_hbm, grad_hbm, gain_ref, early_ref, left_hbm,
    out_ref, sums_ref, weight_hbm, inputs, grads, fetch_sem, *scratch
):
    fetches = (
        pltpu.make_async_copy(input_hbm, inputs, fetch_sem.at[0]),
        pltpu.make_async_copy(grad_hbm, grads, fetch_sem.at[1]),
    )
    for fetch in fetches:
        fetch.start()
    product = Product(left_hbm, a_hbm, weight_hbm, scratch[:7])
    scatter = Scatter(n, True, a_hbm, w_ref, out_ref, scratch[7:])
    product.start()
    sums_ref[...] = early_ref[...]

    def work(at):
        grad = out_ref[at, :]
        back, terms = back_rows(grad, inputs[at, :].astype(jnp.float32), gain_ref[...])
        out_ref[at, :] = grads[at, :] + back
        sums_ref[4:5, :] += column_sum(terms)
        sums_ref[5:6, :] += column_sum(grad)

    scatter.run(lambda j: product.batch(j, scatter.chunks), after_chunk(scatter, fetches, work))
    product.finish()


def project_back(grad_proj, weight, inputs, grad_residual, gain, early, attn_rows, n, collective_id):
    rows, width = inputs.shape
    columns = grad_proj.shape[1]
    return pl.pallas_call(
        functools.partial(project_back_kernel, n),
        out_shape=(
            jax.ShapeDtypeStruct((rows, width), jnp.float32),
            jax.ShapeDtypeStruct((8, width), jnp.float32),
            jax.ShapeDtypeStruct((width, columns), jnp.bfloat16),
        ),
        in_specs=[HBM_SPEC, VMEM_SPEC, HBM_SPEC, HBM_SPEC, VMEM_SPEC, VMEM_SPEC, HBM_SPEC],
        out_specs=(VMEM_SPEC, VMEM_SPEC, HBM_SPEC),
        scratch_shapes=[
            pltpu.VMEM((rows, width), inputs.dtype),
            pltpu.VMEM((rows, width), jnp.float32),
            pltpu.SemaphoreType.DMA((2,)),
        ]
        + product_scratch(n * rows, width, columns)
        + scatter_scratch(n, rows, columns, width, CHUNKS),
        compiler_params=comm_params(collective_id),
        cost_estimate=LINK_COST,
        name="project_back",
    )(grad_proj, weight, inputs, grad_residual, gain, early, attn_rows)


HEADS = 16


def normalize(rows):
    center = rows - jnp.mean(rows, axis=1, keepdims=True)
    factor = lax.rsqrt(jnp.mean(center * center, axis=1, keepdims=True) + 1e-05)
    return center * factor


def wide(vector):
    return vector.astype(jnp.float32)[None]


def share(grad, dimension):
    return lax.psum_scatter(grad, "dp", scatter_dimension=dimension, tiled=True).astype(jnp.float32)


def on_device(
    hidden_input,
    first_gain,
    first_shift,
    qkv_weight,
    query_bias,
    value_bias,
    dense_weight,
    dense_bias,
    second_gain,
    second_shift,
    up_weight,
    up_bias,
    down_weight,
    down_bias,
    segments,
    document_lengths,
    cotangent,
    *,
    n,
    d,
):
    heads_local = query_bias.shape[0] // HEAD_DIM
    normed_first = normalize(hidden_input.astype(jnp.float32))
    attn_input = (normed_first * wide(first_gain) + wide(first_shift)).astype(jnp.bfloat16)
    attn_rows = gather_rows(attn_input, n, 1)
    project_full, dense_full, expand_full, shrink_full = (
        lax.all_gather(qkv_weight, "dp", axis=0, tiled=True),
        lax.all_gather(dense_weight, "dp", axis=1, tiled=True),
        lax.all_gather(up_weight, "dp", axis=0, tiled=True),
        lax.all_gather(down_weight, "dp", axis=1, tiled=True),
    )
    group_rows = attn_rows.shape[0]
    sequences = document_lengths.shape[0]
    length = group_rows // sequences
    heads_index = lax.axis_index("tensor") * heads_local + lax.broadcasted_iota(
        jnp.int32, (heads_local,), 0
    )
    slopes = jnp.exp2(-8.0 * (heads_index.astype(jnp.float32) + 1.0) / HEADS) * LOG2E
    position = lax.broadcasted_iota(jnp.int32, (sequences, length), 1)
    filled = jnp.sum(document_lengths, axis=1, keepdims=True)
    labels = jnp.where(position < filled, segments.reshape(sequences, length), length + position)
    query_bias32 = query_bias.astype(jnp.float32).reshape(heads_local, HEAD_DIM)
    value_bias32 = value_bias.astype(jnp.float32).reshape(heads_local, HEAD_DIM)
    proj_bias = jnp.stack((query_bias32, jnp.zeros_like(query_bias32), value_bias32), axis=1).reshape(
        heads_local * 3 * HEAD_DIM
    )
    grad_rows, proj, mixed = project_attend(
        attn_rows, project_full, proj_bias[None], slopes, labels, cotangent, n, 6
    )
    residual, mlp_input = dense(
        mixed, dense_full, hidden_input, wide(dense_bias), wide(second_gain), wide(second_shift), n, 2
    )
    mlp_rows, activated, grad_pre, sum_up_bias = expand(
        mlp_input, grad_rows, expand_full, shrink_full, wide(up_bias), n, 7
    )
    grad_residual, grad_attn_out, early_sums, grad_down = expand_back(
        grad_pre, expand_full, activated, grad_rows, residual, cotangent, wide(second_gain), n, 4
    )
    grad_down_weight = share(grad_down, 1)
    grad_proj, head_sums, grad_dense, grad_up = dense_back(
        grad_attn_out, mixed, dense_full, mlp_rows, grad_pre, proj, slopes, labels, n, 9
    )
    grad_down_weight, grad_proj = lax.optimization_barrier((grad_down_weight, grad_proj))
    grad_up_weight = share(grad_up, 0)
    grad_dense_weight = share(grad_dense, 1)
    grad_input, sums, grad_project = project_back(
        grad_proj, project_full, hidden_input, grad_residual, wide(first_gain), early_sums, attn_rows, n, 5
    )
    grad_qkv_weight = share(grad_project, 0)
    hidden_output, sums, biases = shrink(
        activated, shrink_full, residual, wide(down_bias), sums, sum_up_bias, head_sums, n, d, 3
    )
    heads_width = heads_local * HEAD_DIM
    grad_second_gain, grad_second_shift, grad_dense_bias, grad_down_bias, grad_first_gain, grad_first_shift = (
        sums[i] for i in range(6)
    )
    grad_up_bias, grad_query_bias, grad_value_bias = biases[0], biases[1, :heads_width], biases[2, :heads_width]
    return (
        hidden_output,
        grad_input,
        grad_first_gain,
        grad_first_shift,
        grad_qkv_weight,
        grad_query_bias,
        grad_value_bias,
        grad_dense_weight,
        grad_dense_bias,
        grad_second_gain,
        grad_second_shift,
        grad_up_weight,
        grad_up_bias,
        grad_down_weight,
        grad_down_bias,
    )


def solution(mesh):
    return jax.shard_map(
        functools.partial(on_device, n=mesh.shape["tensor"], d=mesh.shape["dp"]),
        mesh=mesh,
        in_specs=(
            P(("dp", "tensor"), None),
            P(),
            P(),
            P("dp", "tensor"),
            P("tensor"),
            P("tensor"),
            P("tensor", "dp"),
            P(),
            P(),
            P(),
            P("dp", "tensor"),
            P("tensor"),
            P("tensor", "dp"),
            P(),
            P("dp"),
            P("dp", None),
            P(("dp", "tensor"), None),
        ),
        out_specs=(
            P(("dp", "tensor"), None),
            P(("dp", "tensor"), None),
            P(),
            P(),
            P("dp", "tensor"),
            P("tensor"),
            P("tensor"),
            P("tensor", "dp"),
            P(),
            P(),
            P(),
            P("dp", "tensor"),
            P("tensor"),
            P("tensor", "dp"),
            P(),
        ),
        check_vma=False,
    )
```

```python
import functools
import math

import jax
import jax.numpy as jnp
from jax import lax
from jax.experimental import pallas as pl
from jax.experimental.pallas import tpu as pltpu
from jax.sharding import PartitionSpec as P

VMEM_LIMIT = 62 << 20
LINK_COST = pl.CostEstimate(flops=0, bytes_accessed=280_000_000, transcendentals=0)


def flip(index, bit):
    return index + (1 - 2 * ((index // 2**bit) % 2)) * 2**bit


def look_up(table, i):
    if isinstance(i, int):
        return table[i]
    value = table[0]
    for k in range(1, len(table)):
        value = value + (i >= k).astype(jnp.int32) * (table[k] - table[k - 1])
    return value


def parity(i):
    return i % 2 if isinstance(i, int) else lax.rem(i, 2)


def chip_bits(n):
    return n.bit_length() - 2


def column_parts(width, count):
    blocks = width // 128
    edges = [128 * (blocks * i // count) for i in range(count + 1)]
    return [(a, b - a) for a, b in zip(edges[:-1], edges[1:])]


def peer(index):
    return {"tensor": index}


def greet(me, bits, d=1):
    barrier = pltpu.get_barrier_semaphore()
    for bit in range(bits + 1):
        pl.semaphore_signal(
            barrier, inc=1, device_id=peer(flip(me, bit)), device_id_type=pl.DeviceIdType.MESH
        )
    for ahead in range(1, d):
        pl.semaphore_signal(
            barrier, inc=1, device_id=ahead_on_dp(ahead, d), device_id_type=pl.DeviceIdType.MESH
        )
    pl.semaphore_wait(barrier, bits + d)


def ahead_on_dp(ahead, d):
    return {"dp": lax.rem(lax.axis_index("dp") + ahead, d)}


def remote(src, dst, send_sem, recv_sem, target):
    return pltpu.make_async_remote_copy(
        src_ref=src,
        dst_ref=dst,
        send_sem=send_sem,
        recv_sem=recv_sem,
        device_id=peer(target),
        device_id_type=pl.DeviceIdType.MESH,
    )


class Gather:
    def __init__(self, n, own_ref, out_ref, sems):
        self.me = lax.axis_index("tensor")
        self.bits = chip_bits(n)
        self.rows, width = own_ref.shape
        self.parts = column_parts(width, self.bits)
        self.own, self.out = own_ref, out_ref
        self.own_sem, self.chip_send, self.chip_recv, self.core_send, self.core_recv = sems

    def slot(self, part, index):
        at = self.me
        for step in range(self.bits):
            if (index >> step) & 1:
                at = flip(at, 1 + (part + step) % self.bits)
        return at

    def place(self, mask, core):
        at = flip(self.me, 0) if core else self.me
        for bit in range(self.bits):
            if (mask >> bit) & 1:
                at = flip(at, 1 + bit)
        return at

    def away(self, codes, t):
        code, at = look_up(codes, t), self.me
        for bit in range(self.bits + 1):
            at = at + (code // 2**bit) % 2 * (1 - 2 * ((self.me // 2**bit) % 2)) * 2**bit
        return at

    def index_of(self, part, mask):
        return sum(2 ** ((bit - part) % self.bits) for bit in range(self.bits) if (mask >> bit) & 1)

    def level(self, count):
        return [index for index in range(2**self.bits) if index.bit_count() == count]

    def block(self, part, index, core=0):
        start, size = self.parts[part]
        at = flip(self.slot(part, index), 0) if core else self.slot(part, index)
        return self.out.at[pl.ds(pl.multiple_of(at * self.rows, self.rows), self.rows), pl.ds(start, size)]

    def source(self, part, index):
        start, size = self.parts[part]
        return self.own.at[:, pl.ds(start, size)] if index == 0 else self.block(part, index)

    def chip_copy(self, part, index, step):
        arrives = index + 2**step
        return remote(
            self.source(part, index),
            self.block(part, index),
            self.chip_send.at[part, arrives],
            self.chip_recv.at[part, arrives],
            flip(self.me, 1 + (part + step) % self.bits),
        )

    def core_copy(self, part, index):
        return remote(
            self.source(part, index),
            self.block(part, index),
            self.core_send.at[part, index],
            self.core_recv.at[part, index],
            flip(self.me, 0),
        )

    def keep(self):
        rows = pl.ds(pl.multiple_of(self.me * self.rows, self.rows), self.rows)
        return pltpu.make_async_copy(self.own, self.out.at[rows, :], self.own_sem)

    def start(self):
        greet(self.me, self.bits)
        for step in range(self.bits):
            for part in range(self.bits):
                self.chip_copy(part, 0, step).start()
        for part in range(self.bits):
            self.core_copy(part, 0).start()
        self.keep().start()

    def forward(self, count):
        for index in self.level(count):
            for part in range(self.bits):
                arrived = self.block(part, index)
                remote(
                    arrived, arrived, self.chip_send.at[part, index], self.chip_recv.at[part, index], flip(self.me, 0)
                ).wait_recv()
                for step in range(index.bit_length(), self.bits):
                    self.chip_copy(part, index, step).start()
                self.core_copy(part, index).start()

    def wait_core(self, mask):
        for part in range(self.bits):
            index = self.index_of(part, mask)
            arrived = self.block(part, index, 1)
            remote(
                arrived, arrived, self.core_send.at[part, index], self.core_recv.at[part, index], flip(self.me, 0)
            ).wait_recv()

    def finish_sends(self):
        for part in range(self.bits):
            for index in range(2**self.bits):
                for step in range(index.bit_length(), self.bits):
                    self.chip_copy(part, index, step).wait_send()
                self.core_copy(part, index).wait_send()


def gather_kernel(n, x_ref, gain_ref, shift_ref, out_ref, own, *sems):
    def work(at):
        normed, _ = normal_rows(x_ref[at, :].astype(jnp.float32))
        own[at, :] = (normed * gain_ref[...] + shift_ref[...]).astype(own.dtype)

    row_blocks(0, own.shape[0], 32, work)
    gather = Gather(n, own, out_ref, sems)
    gather.start()
    for count in range(1, gather.bits + 1):
        gather.forward(count)
    for mask in range(2**gather.bits):
        gather.wait_core(mask)
    gather.finish_sends()
    gather.keep().wait()


def gather_sems(n):
    bits = chip_bits(n)
    dma = pltpu.SemaphoreType.DMA
    return [dma(())] + [dma((bits, 2**bits))] * 4


def gather_rows(x, gain, shift, n, collective_id):
    rows, width = x.shape
    return pl.pallas_call(
        functools.partial(gather_kernel, n),
        out_shape=jax.ShapeDtypeStruct((n * rows, width), x.dtype),
        in_specs=[pl.BlockSpec(memory_space=pltpu.VMEM)] * 3,
        out_specs=pl.BlockSpec(memory_space=pl.ANY),
        scratch_shapes=[pltpu.VMEM((rows, width), x.dtype)] + gather_sems(n),
        compiler_params=pltpu.CompilerParams(
            collective_id=collective_id, has_side_effects=True, vmem_limit_bytes=VMEM_LIMIT
        ),
        cost_estimate=LINK_COST,
        name="gather_rows",
    )(x, gain, shift)


class Scatter:
    def __init__(self, n, transposed, a_hbm, w_ref, out_ref, scratch):
        (self.csend, self.crecv, self.recv, self.other, self.mine, self.load_sem) = scratch[:6]
        self.core_send, self.core_recv, self.chip_send, self.chip_recv = scratch[6:]
        self.me = lax.axis_index("tensor")
        self.bits = chip_bits(n)
        self.total = 2**self.bits
        self.transposed = transposed
        self.a, self.w, self.out = a_hbm, w_ref, out_ref
        self.rows, width = out_ref.shape
        self.chunk = self.csend.shape[2]
        self.chunks = self.rows // self.chunk
        self.parts = column_parts(width, self.bits)

    def index_of(self, part, mask):
        top = self.bits - 1
        return sum(2 ** (top - (bit - part) % self.bits) for bit in range(self.bits) if (mask >> bit) & 1)

    def place(self, mask, core):
        at = flip(self.me, 0) if core else self.me
        for bit in range(self.bits):
            if (mask >> bit) & 1:
                at = flip(at, 1 + bit)
        return at

    def rows_of(self, j):
        return pl.ds(pl.multiple_of(j * self.chunk, self.chunk), self.chunk)

    def loads(self, j, core):
        into = self.other if core else self.mine
        copies = []
        for mask in range(self.total):
            start = pl.multiple_of(self.place(mask, core) * self.rows + j * self.chunk, self.chunk)
            copies.append(
                pltpu.make_async_copy(
                    self.a.at[pl.ds(start, self.chunk), :],
                    into.at[lax.rem(j, 2), pl.ds(mask * self.chunk, self.chunk), :],
                    self.load_sem.at[core, lax.rem(j, 2), mask],
                )
            )
        return copies

    def core_copy(self, j, part):
        start, size = self.parts[part]
        return remote(
            self.csend.at[lax.rem(j, 2), :, :, pl.ds(start, size)],
            self.crecv.at[:, self.rows_of(j), pl.ds(start, size)],
            self.core_send.at[part, j],
            self.core_recv.at[part, j],
            flip(self.me, 0),
        )

    def chip_copy(self, j, part, step):
        half = self.total >> (step + 1)
        first = sum(self.total >> (s + 1) for s in range(step))
        start, size = self.parts[part]
        return remote(
            self.crecv.at[pl.ds(half, half), self.rows_of(j), pl.ds(start, size)],
            self.recv.at[pl.ds(first, half), self.rows_of(j), pl.ds(start, size)],
            self.chip_send.at[part, step, j],
            self.chip_recv.at[part, step, j],
            flip(self.me, 1 + (part + step) % self.bits),
        )

    def tiles(self, part, lhs, put):
        start, size = self.parts[part]
        tile = 256 if size % 256 == 0 and start % 256 == 0 else 128

        def one(i, carry):
            cols = pl.ds(pl.multiple_of(start + i * tile, tile), tile)
            if self.transposed:
                value = lax.dot_general(
                    lhs[...], self.w[cols, :], (((1,), (1,)), ((), ())), preferred_element_type=jnp.float32
                )
            else:
                value = jnp.dot(lhs[...], self.w[:, cols], preferred_element_type=jnp.float32)
            put(cols, value)
            return carry

        lax.fori_loop(0, size // tile, one, 0)

    def piece(self, value, mask):
        return value[mask * self.chunk : (mask + 1) * self.chunk, :]

    def stage_core(self, j):
        for copy in self.loads(j, 1):
            copy.wait()

        @pl.when(j >= 2)
        def _():
            for part in range(self.bits):
                self.core_copy(j - 2, part).wait_send()

        for part in range(self.bits):

            def put(cols, value):
                for mask in range(self.total):
                    self.csend[lax.rem(j, 2), self.index_of(part, mask), :, cols] = self.piece(value, mask).astype(
                        self.csend.dtype
                    )

            self.tiles(part, self.other.at[lax.rem(j, 2)], put)
            self.core_copy(j, part).start()

    def stage_first(self, j):
        for copy in self.loads(j, 0):
            copy.wait()
        for part in range(self.bits):
            self.core_copy(j, part).wait_recv()

            def put(cols, value):
                for mask in range(self.total):
                    index = self.index_of(part, mask)
                    got = self.piece(value, mask) + self.crecv[index, self.rows_of(j), cols].astype(jnp.float32)
                    if index:
                        self.crecv[index, self.rows_of(j), cols] = got.astype(self.crecv.dtype)
                    else:
                        self.out[self.rows_of(j), cols] = got

            self.tiles(part, self.mine.at[lax.rem(j, 2)], put)
            self.chip_copy(j, part, 0).start()

    def stage_next(self, j, step):
        half = self.total >> (step + 1)
        first = sum(self.total >> (s + 1) for s in range(step))
        for part in range(self.bits):
            start, size = self.parts[part]
            cols = slice(start, start + size)
            self.chip_copy(j, part, step).wait_recv()
            for index in reversed(range(half)):
                got = self.recv[first + index, self.rows_of(j), cols].astype(jnp.float32)
                if index:
                    value = self.crecv[index, self.rows_of(j), cols].astype(jnp.float32) + got
                    self.crecv[index, self.rows_of(j), cols] = value.astype(self.crecv.dtype)
                else:
                    self.out[self.rows_of(j), cols] += got
            if step + 1 < self.bits:
                self.chip_copy(j, part, step + 1).start()

    def run(self, filler=None, after=None, d=1):
        for copy in self.loads(0, 1):
            copy.start()
        greet(self.me, self.bits, d)

        def body(u, carry):
            @pl.when(u + 1 < self.chunks)
            def _():
                for copy in self.loads(u + 1, 1):
                    copy.start()

            @pl.when(u < self.chunks)
            def _():
                for copy in self.loads(u, 0):
                    copy.start()
                self.stage_core(u)

            @pl.when((u >= 1) & (u <= self.chunks))
            def _():
                self.stage_first(u - 1)

            for step in range(self.bits):

                @pl.when((u >= 2 + step) & (u < self.chunks + 2 + step))
                def _():
                    self.stage_next(u - 2 - step, step)

            if filler is not None:

                @pl.when((u >= 1) & (u <= self.chunks))
                def _():
                    filler(u - 1)

            if after is not None:
                done = u - self.bits - 1

                @pl.when(done >= 0)
                def _():
                    after(done)

            return carry

        lax.fori_loop(0, self.chunks + self.bits + 1, body, 0)
        for part in range(self.bits):
            for j in range(self.chunks):
                if j >= self.chunks - 2:
                    self.core_copy(j, part).wait_send()
                for step in range(self.bits):
                    self.chip_copy(j, part, step).wait_send()


def scatter_scratch(n, rows, depth, width, chunks):
    bits = chip_bits(n)
    total = 2**bits
    chunk = rows // chunks
    dma = pltpu.SemaphoreType.DMA
    return [
        pltpu.VMEM((2, total, chunk, width), jnp.bfloat16),
        pltpu.VMEM((total, rows, width), jnp.bfloat16),
        pltpu.VMEM((total - 1, rows, width), jnp.bfloat16),
        pltpu.VMEM((2, total * chunk, depth), jnp.bfloat16),
        pltpu.VMEM((2, total * chunk, depth), jnp.bfloat16),
        dma((2, 2, total)),
        dma((bits, chunks)),
        dma((bits, chunks)),
        dma((bits, bits, chunks)),
        dma((bits, bits, chunks)),
    ]


HEAD_DIM = 128
LOG2E = 1.4426950408889634
SCALE = 1.0 / math.sqrt(HEAD_DIM)
BLOCK = 256
NT = (((1,), (1,)), ((), ()))
TN = (((0,), (0,)), ((), ()))


def as_column(row):
    width = row.shape[1]
    here = lax.broadcasted_iota(jnp.int32, (width, width), 0) == lax.broadcasted_iota(jnp.int32, (width, width), 1)
    return jnp.sum(jnp.where(here, row, 0.0), axis=1, keepdims=True)


def masked_scores(slope, q, keys, query_labels, key_labels, first):
    raw = lax.dot_general(q, keys, NT, preferred_element_type=jnp.float32)
    rows, width = raw.shape
    column = lax.broadcasted_iota(jnp.int32, (1, width), 1)
    bias = column.astype(jnp.float32) * slope
    same = query_labels == key_labels
    causal = lax.broadcasted_iota(jnp.int32, (rows, width), 1) <= first + lax.broadcasted_iota(
        jnp.int32, (rows, width), 0
    )
    return jnp.where(same & causal, raw * (SCALE * LOG2E) + bias, -1e30)


class Total:
    def __init__(self, n, d, scratch):
        self.pair, self.lines, self.send, self.recv, self.line_send, self.line_recv = scratch
        self.me, self.d = lax.axis_index("tensor"), d
        self.levels = n.bit_length() - 1

    def level_copy(self, level):
        return remote(
            self.pair.at[2 * level],
            self.pair.at[2 * level + 1],
            self.send.at[level],
            self.recv.at[level],
            flip(self.me, level),
        )

    def line_copy(self, ahead):
        return pltpu.make_async_remote_copy(
            src_ref=self.lines.at[0],
            dst_ref=self.lines.at[ahead],
            send_sem=self.line_send.at[ahead],
            recv_sem=self.line_recv.at[ahead],
            device_id=ahead_on_dp(ahead, self.d),
            device_id_type=pl.DeviceIdType.MESH,
        )

    def spread(self):
        for ahead in range(1, self.d):
            self.line_copy(ahead).start()

    def step(self, level):
        if level:
            self.level_copy(level - 1).wait_recv()
            self.pair[2 * level] = self.pair[2 * level - 2] + self.pair[2 * level - 1]
        if level < self.levels:
            self.level_copy(level).start()
        else:
            self.lines[0] = self.pair[2 * level]
            self.spread()

    def finish(self, levels=True):
        for ahead in range(1, self.d):
            self.line_copy(ahead).wait_recv()
        z = lax.axis_index("dp")
        total = None
        for index in range(self.d):
            value = self.lines[lax.rem(z - index + self.d, self.d)]
            total = value if total is None else total + value
        for ahead in range(1, self.d):
            self.line_copy(ahead).wait_send()
        if levels:
            for level in range(self.levels):
                self.level_copy(level).wait_send()
        return total


def total_scratch(n, d, rows, width):
    levels = n.bit_length() - 1
    dma = pltpu.SemaphoreType.DMA
    return [
        pltpu.VMEM((2 * levels + 1, rows, width), jnp.float32),
        pltpu.VMEM((d, rows, width), jnp.float32),
        dma((levels,)),
        dma((levels,)),
        dma((d,)),
        dma((d,)),
    ]


def tile_of(width):
    return 256 if width % 256 == 0 else width


def attend_one(slope, proj_ref, start, head, row_ref, out_ref, length):
    at = pl.multiple_of(head * 3 * HEAD_DIM, HEAD_DIM)

    def take(which, first, size):
        return proj_ref[pl.ds(start + first, size), pl.ds(at + which * HEAD_DIM, HEAD_DIM)]

    for first in range(0, length, BLOCK):
        last = first + BLOCK
        scores = masked_scores(
            slope, take(0, first, BLOCK), take(1, 0, last), as_column(row_ref[:, first:last]), row_ref[:, :last], first
        )
        top = jnp.max(scores, axis=1, keepdims=True)
        expo = jnp.exp2(scores - top)
        total = jnp.sum(expo, axis=1, keepdims=True)
        mixed = jnp.dot(expo.astype(jnp.bfloat16), take(2, 0, last), preferred_element_type=jnp.float32)
        out_ref[pl.ds(start + first, BLOCK), pl.ds(pl.multiple_of(head * HEAD_DIM, HEAD_DIM), HEAD_DIM)] = (
            mixed / total
        ).astype(out_ref.dtype)


def project_kernel(
    n, length, slope_ref, own_ref, rows_hbm, w_ref, bias_ref, row_ref, gathered, proj_hbm, mixed_ref,
    proj, buf, load_sem, store_sem, *sems
):
    gather = Gather(n, own_ref, gathered, sems)
    rows = own_ref.shape[0]
    width = w_ref.shape[1]
    tile = tile_of(width)
    heads = width // (3 * HEAD_DIM)
    sequences = n * rows // length

    def load(i):
        at = pl.ds(pl.multiple_of(i * rows, rows), rows)
        return pltpu.make_async_copy(rows_hbm.at[at, :], buf.at[lax.rem(i, 2)], load_sem.at[lax.rem(i, 2)])

    load(0).start()
    gather.start()

    def store(i):
        at = pl.ds(pl.multiple_of(i * rows, rows), rows)
        return pltpu.make_async_copy(proj.at[at, :], proj_hbm.at[at, :], store_sem.at[i])

    def project(i, carry):
        load(i).wait()

        @pl.when(i + 1 < n)
        def _():
            load(i + 1).start()

        at = pl.ds(pl.multiple_of(i * rows, rows), rows)
        for first in range(0, width, tile):
            cols = slice(first, first + tile)
            proj[at, cols] = (
                jnp.dot(buf[lax.rem(i, 2)], w_ref[:, cols], preferred_element_type=jnp.float32) + bias_ref[:, cols]
            ).astype(proj.dtype)
        store(i).start()
        return carry

    lax.fori_loop(0, n, project, 0)
    gather.forward(1)

    def one(i, carry):
        s, head = i // heads, lax.rem(i, heads)
        attend_one(
            slope_ref[head],
            proj,
            pl.multiple_of(s * length, length),
            head,
            row_ref.at[s],
            mixed_ref,
            length,
        )
        return carry

    lax.fori_loop(0, sequences * heads, one, 0)
    for count in range(2, gather.bits + 1):
        gather.forward(count)
    for i in range(n):
        store(i).wait()
    for mask in range(2**gather.bits):
        gather.wait_core(mask)
    gather.finish_sends()
    gather.keep().wait()


def project_attend(attn_rows, weight, bias, slopes, labels, own, n, collective_id):
    total, depth = attn_rows.shape
    rows, width = own.shape[0], weight.shape[1]
    heads = width // (3 * HEAD_DIM)
    vmem = pl.BlockSpec(memory_space=pltpu.VMEM)
    hbm = pl.BlockSpec(memory_space=pl.ANY)
    dma = pltpu.SemaphoreType.DMA
    return pl.pallas_call(
        functools.partial(project_kernel, n, labels.shape[1]),
        out_shape=(
            jax.ShapeDtypeStruct((total, own.shape[1]), own.dtype),
            jax.ShapeDtypeStruct((total, width), jnp.bfloat16),
            jax.ShapeDtypeStruct((total, heads * HEAD_DIM), jnp.bfloat16),
        ),
        in_specs=[pl.BlockSpec(memory_space=pltpu.SMEM), vmem, hbm, vmem, vmem, vmem],
        out_specs=(hbm, hbm, vmem),
        scratch_shapes=[
            pltpu.VMEM((total, width), jnp.bfloat16),
            pltpu.VMEM((2, rows, depth), jnp.bfloat16),
            dma((2,)),
            dma((n,)),
        ]
        + gather_sems(n),
        compiler_params=pltpu.CompilerParams(
            collective_id=collective_id, has_side_effects=True, vmem_limit_bytes=VMEM_LIMIT
        ),
        cost_estimate=LINK_COST,
        name="project_attend",
    )(slopes, own, attn_rows, weight, bias, labels[:, None, :])


def gelu_both(value):
    c, a = 0.7978845608028654, 0.044715
    square = value * value
    half = 0.5 + 0.5 * jnp.tanh(value * (c + (c * a) * square))
    active = value * half
    slope = half + (2.0 * active) * (1.0 - half) * (c + (3.0 * c * a) * square)
    return active, slope


def expand_kernel(
    n, own_ref, grad_hbm, up_ref, down_ref, bias_ref, rows_hbm, act_hbm, pre_hbm, sum_ref,
    gathered, grads, backs, act, pre, load_sem, act_sem, pre_sem, rows_sem, *sems
):
    gather = Gather(n, own_ref, gathered, sems)
    rows, depth = own_ref.shape
    width = up_ref.shape[1]
    tile = tile_of(width)
    levels = [gather.level(count) for count in range(gather.bits + 1)]
    codes = [2 * mask + core for masks in levels for core in (0, 1) for mask in masks]

    def span(i):
        return pl.ds(pl.multiple_of(gather.away(codes, i) * rows, rows), rows)

    def load(i):
        return pltpu.make_async_copy(grad_hbm.at[span(i), :], grads.at[parity(i)], load_sem.at[parity(i)])

    def store(i):
        slot = parity(i)
        return (
            pltpu.make_async_copy(act.at[slot], act_hbm.at[span(i), :], act_sem.at[slot]),
            pltpu.make_async_copy(pre.at[slot], pre_hbm.at[span(i), :], pre_sem.at[slot]),
        )

    def keep_rows(i):
        return pltpu.make_async_copy(gathered.at[span(i), :], rows_hbm.at[span(i), :], rows_sem.at[i])

    def cols_of(j):
        return pl.ds(pl.multiple_of(j * tile, tile), tile)

    def back(i, carry):
        load(i).wait()

        @pl.when(i + 1 < n)
        def _():
            load(i + 1).start()

        def columns(j, carry):
            value = lax.dot_general(
                grads[parity(i)], down_ref[cols_of(j), :], NT, preferred_element_type=jnp.float32
            )
            backs[i, :, cols_of(j)] = value.astype(backs.dtype)
            return carry

        lax.fori_loop(0, width // tile, columns, 0)
        return carry

    def work(i, carry):
        first = 0
        for count, masks in enumerate(levels):
            if count:
                pl.when(i == first)(functools.partial(gather.forward, count))
            for k, mask in enumerate(masks):
                pl.when(i == first + len(masks) + k)(functools.partial(gather.wait_core, mask))
            first += 2 * len(masks)
        keep_rows(i).start()

        @pl.when(i >= 2)
        def _():
            for copy in store(i - 2):
                copy.wait()

        here, slot = span(i), parity(i)

        def columns(j, carry):
            cols = cols_of(j)
            before = jnp.dot(gathered[here, :], up_ref[:, cols], preferred_element_type=jnp.float32) + bias_ref[:, cols]
            active, slope = gelu_both(before)
            act[slot, :, cols] = active.astype(act.dtype)
            rounded = (backs[i, :, cols].astype(jnp.float32) * slope).astype(pre.dtype)
            pre[slot, :, cols] = rounded
            sum_ref[:, cols] += jnp.sum(rounded.astype(jnp.float32), axis=0, keepdims=True)
            return carry

        lax.fori_loop(0, width // tile, columns, 0)
        for copy in store(i):
            copy.start()
        return carry

    sum_ref[...] = jnp.zeros_like(sum_ref)
    load(0).start()
    gather.start()
    lax.fori_loop(0, n, back, 0)
    gather.keep().wait()
    lax.fori_loop(0, n, work, 0)
    for last in (n - 2, n - 1):
        for copy in store(last):
            copy.wait()
    for i in range(n):
        keep_rows(i).wait()
    gather.finish_sends()


def expand(own, grad_rows, up, down, bias, n, collective_id):
    rows, depth = own.shape
    width = up.shape[1]
    total = n * rows
    vmem = pl.BlockSpec(memory_space=pltpu.VMEM)
    hbm = pl.BlockSpec(memory_space=pl.ANY)
    dma = pltpu.SemaphoreType.DMA
    return pl.pallas_call(
        functools.partial(expand_kernel, n),
        out_shape=(
            jax.ShapeDtypeStruct((total, depth), jnp.bfloat16),
            jax.ShapeDtypeStruct((total, width), jnp.bfloat16),
            jax.ShapeDtypeStruct((total, width), jnp.bfloat16),
            jax.ShapeDtypeStruct((1, width), jnp.float32),
        ),
        in_specs=[vmem, hbm, vmem, vmem, vmem],
        out_specs=(hbm, hbm, hbm, vmem),
        scratch_shapes=[
            pltpu.VMEM((total, depth), jnp.bfloat16),
            pltpu.VMEM((2, rows, depth), jnp.bfloat16),
            pltpu.VMEM((n, rows, width), jnp.bfloat16),
            pltpu.VMEM((2, rows, width), jnp.bfloat16),
            pltpu.VMEM((2, rows, width), jnp.bfloat16),
            dma((2,)),
            dma((2,)),
            dma((2,)),
            dma((n,)),
        ]
        + gather_sems(n),
        compiler_params=pltpu.CompilerParams(
            collective_id=collective_id, has_side_effects=True, vmem_limit_bytes=VMEM_LIMIT
        ),
        cost_estimate=LINK_COST,
        name="expand",
    )(own, grad_rows, up, down, bias)


class Product:
    def __init__(self, left, right, out, scratch):
        self.left, self.right, self.out = left, right, out
        self.lbuf, self.rbuf, self.acc, self.obuf, self.left_sem, self.right_sem, self.out_sem = scratch
        self.depth, self.tall = self.lbuf.shape[1:]
        self.wide = self.rbuf.shape[2]
        self.inner = left.shape[0] // self.depth
        self.across = right.shape[1] // self.wide
        self.steps = (left.shape[1] // self.tall) * self.across * self.inner

    def load(self, i):
        k = lax.rem(i, self.inner)
        col = lax.rem(i // self.inner, self.across)
        row = i // (self.inner * self.across)
        rows = pl.ds(pl.multiple_of(k * self.depth, self.depth), self.depth)
        slot = lax.rem(i, 2)
        return (
            pltpu.make_async_copy(
                self.left.at[rows, pl.ds(pl.multiple_of(row * self.tall, self.tall), self.tall)],
                self.lbuf.at[slot],
                self.left_sem.at[slot],
            ),
            pltpu.make_async_copy(
                self.right.at[rows, pl.ds(pl.multiple_of(col * self.wide, self.wide), self.wide)],
                self.rbuf.at[slot],
                self.right_sem.at[slot],
            ),
        )

    def store(self, tile):
        col = lax.rem(tile, self.across)
        row = tile // self.across
        return pltpu.make_async_copy(
            self.obuf,
            self.out.at[
                pl.ds(pl.multiple_of(row * self.tall, self.tall), self.tall),
                pl.ds(pl.multiple_of(col * self.wide, self.wide), self.wide),
            ],
            self.out_sem,
        )

    def start(self):
        for copy in self.load(0):
            copy.start()

    def step(self, i, carry=0):
        for copy in self.load(i):
            copy.wait()

        @pl.when(i + 1 < self.steps)
        def _():
            for copy in self.load(i + 1):
                copy.start()

        k = lax.rem(i, self.inner)
        slot = lax.rem(i, 2)
        part = next(size for size in (512, 384, self.wide) if self.wide % size == 0)

        @pl.when(k == 0)
        def _():
            self.acc[...] = jnp.zeros_like(self.acc)

        for first in range(0, self.wide, part):
            cols = slice(first, first + part)
            self.acc[:, cols] += lax.dot_general(
                self.lbuf[slot], self.rbuf[slot, :, cols], TN, preferred_element_type=jnp.float32
            )

        @pl.when(k == self.inner - 1)
        def _():
            tile = i // self.inner

            @pl.when(tile > 0)
            def _():
                self.store(tile - 1).wait()

            self.obuf[...] = self.acc[...].astype(self.obuf.dtype)
            self.store(tile).start()

        return carry

    def batch(self, j, batches):
        per = -(-self.steps // batches)
        first = j * per
        lax.fori_loop(first, jnp.minimum(first + per, self.steps), self.step, 0)

    def finish(self):
        self.store(self.steps // self.inner - 1).wait()


def product_scratch(rows, tall, wide):
    dma = pltpu.SemaphoreType.DMA
    depth = min(1024, rows)
    tall, wide = min(512, tall), min(1024, wide)
    return [
        pltpu.VMEM((2, depth, tall), jnp.bfloat16),
        pltpu.VMEM((2, depth, wide), jnp.bfloat16),
        pltpu.VMEM((tall, wide), jnp.float32),
        pltpu.VMEM((tall, wide), jnp.bfloat16),
        dma((2,)),
        dma((2,)),
        dma(()),
    ]


def row_blocks(first, rows, each, work):
    def one(i, carry):
        work(pl.ds(pl.multiple_of(first + i * each, each), each))
        return carry

    lax.fori_loop(0, rows // each, one, 0)


def after_chunk(scatter, fetches, work):
    def after(j):
        @pl.when(j == 0)
        def _():
            for fetch in fetches:
                fetch.wait()

        row_blocks(j * scatter.chunk, scatter.chunk, 32, work)

    return after


def normal_rows(value):
    center = value - jnp.mean(value, axis=1, keepdims=True)
    factor = lax.rsqrt(jnp.mean(center * center, axis=1, keepdims=True) + 1e-05)
    return center * factor, factor


def dense_kernel(
    n, a_hbm, w_ref, input_hbm, bias_ref, gain_ref, shift_ref, out_ref, next_ref, inputs, input_sem, *scratch
):
    fetch = pltpu.make_async_copy(input_hbm, inputs, input_sem)
    fetch.start()
    scatter = Scatter(n, False, a_hbm, w_ref, out_ref, scratch)

    def work(at):
        residual = inputs[at, :].astype(jnp.float32) + out_ref[at, :] + bias_ref[...]
        out_ref[at, :] = residual
        normed, _ = normal_rows(residual)
        next_ref[at, :] = (normed * gain_ref[...] + shift_ref[...]).astype(next_ref.dtype)

    scatter.run(after=after_chunk(scatter, (fetch,), work))


def back_rows(grad, source, gain):
    normed, factor = normal_rows(source)
    scaled = grad * gain
    product = grad * normed
    back = factor * (
        scaled
        - jnp.mean(scaled, axis=1, keepdims=True)
        - normed * jnp.mean(scaled * normed, axis=1, keepdims=True)
    )
    return back, product


def column_sum(value):
    return jnp.sum(value, axis=0, keepdims=True)


def expand_back_kernel(
    n, a_hbm, w_ref, act_hbm, rows_hbm, residual_hbm, cotangent_hbm, gain_ref,
    out_ref, next_ref, sums_ref, grad_hbm, residual, cotangent, fetch_sem, *scratch
):
    fetches = (
        pltpu.make_async_copy(residual_hbm, residual, fetch_sem.at[0]),
        pltpu.make_async_copy(cotangent_hbm, cotangent, fetch_sem.at[1]),
    )
    for fetch in fetches:
        fetch.start()
    product = Product(act_hbm, rows_hbm, grad_hbm, scratch[:7])
    scatter = Scatter(n, True, a_hbm, w_ref, out_ref, scratch[7:])
    product.start()
    sums_ref[...] = jnp.zeros_like(sums_ref)

    def work(at):
        grad = out_ref[at, :]
        other = cotangent[at, :].astype(jnp.float32)
        back, terms = back_rows(grad, residual[at, :], gain_ref[...])
        result = other + back
        out_ref[at, :] = result
        next_ref[at, :] = result.astype(next_ref.dtype)
        sums_ref[0:1, :] += column_sum(terms)
        sums_ref[1:2, :] += column_sum(grad)
        sums_ref[2:3, :] += column_sum(result)
        sums_ref[3:4, :] += column_sum(other)

    scatter.run(lambda j: product.batch(j, scatter.chunks), after_chunk(scatter, fetches, work))
    product.finish()


def comm_params(collective_id):
    return pltpu.CompilerParams(collective_id=collective_id, has_side_effects=True, vmem_limit_bytes=VMEM_LIMIT)


VMEM_SPEC = pl.BlockSpec(memory_space=pltpu.VMEM)
HBM_SPEC = pl.BlockSpec(memory_space=pl.ANY)
CHUNKS = 4


def dense(mixed, weight, inputs, bias, gain, shift, n, collective_id):
    rows, width = inputs.shape
    return pl.pallas_call(
        functools.partial(dense_kernel, n),
        out_shape=(
            jax.ShapeDtypeStruct((rows, width), jnp.float32),
            jax.ShapeDtypeStruct((rows, width), jnp.bfloat16),
        ),
        in_specs=[HBM_SPEC, VMEM_SPEC, HBM_SPEC, VMEM_SPEC, VMEM_SPEC, VMEM_SPEC],
        out_specs=(VMEM_SPEC, VMEM_SPEC),
        scratch_shapes=[pltpu.VMEM((rows, width), inputs.dtype), pltpu.SemaphoreType.DMA(())]
        + scatter_scratch(n, rows, mixed.shape[1], width, CHUNKS),
        compiler_params=comm_params(collective_id),
        cost_estimate=LINK_COST,
        name="dense",
    )(mixed, weight, inputs, bias, gain, shift)


def expand_back(grad_pre, up, activated, grad_rows, residual, cotangent, gain, n, collective_id):
    rows, width = residual.shape
    units = activated.shape[1]
    return pl.pallas_call(
        functools.partial(expand_back_kernel, n),
        out_shape=(
            jax.ShapeDtypeStruct((rows, width), jnp.float32),
            jax.ShapeDtypeStruct((rows, width), jnp.bfloat16),
            jax.ShapeDtypeStruct((8, width), jnp.float32),
            jax.ShapeDtypeStruct((units, width), jnp.bfloat16),
        ),
        in_specs=[HBM_SPEC, VMEM_SPEC, HBM_SPEC, HBM_SPEC, HBM_SPEC, HBM_SPEC, VMEM_SPEC],
        out_specs=(VMEM_SPEC, VMEM_SPEC, VMEM_SPEC, HBM_SPEC),
        scratch_shapes=[
            pltpu.VMEM((rows, width), jnp.float32),
            pltpu.VMEM((rows, width), cotangent.dtype),
            pltpu.SemaphoreType.DMA((2,)),
        ]
        + product_scratch(n * rows, units, width)
        + scatter_scratch(n, rows, units, width, CHUNKS),
        compiler_params=comm_params(collective_id),
        cost_estimate=LINK_COST,
        name="expand_back",
    )(grad_pre, up, activated, grad_rows, residual, cotangent, gain)


def attend_back_one(slope, proj_ref, grad_ref, start, head, row_ref, out_ref, dk_ref, dv_ref, sums_ref, length):
    at = pl.multiple_of(head * 3 * HEAD_DIM, HEAD_DIM)
    own = pl.ds(pl.multiple_of(head * HEAD_DIM, HEAD_DIM), HEAD_DIM)

    def cols(which):
        return pl.ds(at + which * HEAD_DIM, HEAD_DIM)

    def take(which, first, size):
        return proj_ref[pl.ds(start + first, size), cols(which)]

    sums = None
    for first in reversed(range(0, length, BLOCK)):
        last = first + BLOCK
        q, g = take(0, first, BLOCK), grad_ref[pl.ds(start + first, BLOCK), own]
        scores = masked_scores(slope, q, take(1, 0, last), as_column(row_ref[:, first:last]), row_ref[:, :last], first)
        top = jnp.max(scores, axis=1, keepdims=True)
        expo = jnp.exp2(scores - top)
        probs = expo * (1.0 / jnp.sum(expo, axis=1, keepdims=True))
        grad_probs = lax.dot_general(g, take(2, 0, last), NT, preferred_element_type=jnp.float32)
        product = probs * grad_probs
        grad_scores = (product - probs * jnp.sum(product, axis=1, keepdims=True)).astype(jnp.bfloat16)
        rounded = probs.astype(jnp.bfloat16)
        grad_queries = (jnp.dot(grad_scores, take(1, 0, last), preferred_element_type=jnp.float32) * SCALE).astype(
            out_ref.dtype
        )
        out_ref[pl.ds(start + first, BLOCK), cols(0)] = grad_queries
        here = column_sum(grad_queries.astype(jnp.float32))
        sums = here if sums is None else sums + here
        grad_keys = lax.dot_general(grad_scores, q, TN, preferred_element_type=jnp.float32)
        grad_values = lax.dot_general(rounded, g, TN, preferred_element_type=jnp.float32)
        if last == length:
            dk_ref[...] = grad_keys
            dv_ref[...] = grad_values
        else:
            dk_ref[:last, :] += grad_keys
            dv_ref[:last, :] += grad_values
    span = pl.ds(start, length)
    out_ref[span, cols(1)] = (dk_ref[...] * SCALE).astype(out_ref.dtype)
    grad_values = dv_ref[...].astype(out_ref.dtype)
    out_ref[span, cols(2)] = grad_values
    sums_ref[0:1, own] += sums
    sums_ref[1:2, own] += column_sum(grad_values.astype(jnp.float32))


def dense_back_kernel(
    n, length, slope_ref, own_ref, mixed_ref, w_ref, left_hbm, right_hbm, proj_hbm, row_ref,
    grad_proj_ref, sums_ref, grad_dense_ref, grad_up_hbm, gathered, acc, grad_mixed, proj, dk, dv, fetch_sem, *scratch
):
    fetch = pltpu.make_async_copy(proj_hbm, proj, fetch_sem)
    fetch.start()
    product = Product(left_hbm, right_hbm, grad_up_hbm, scratch[:7])
    gather = Gather(n, own_ref, gathered, scratch[7:])
    rows = own_ref.shape[0]
    heads = sums_ref.shape[1] // HEAD_DIM
    chips = max(1, length // (2 * rows))
    sequences = max(1, 2 * rows // length)

    def work(at):
        span = pl.ds(pl.multiple_of(at * rows, rows), rows)
        grad_mixed[span, :] = lax.dot_general(
            gathered[span, :], w_ref[...], NT, preferred_element_type=jnp.float32
        ).astype(grad_mixed.dtype)
        width = acc.shape[1]
        part = min(width, 512)
        for first in range(0, width, part):
            cols = slice(first, first + part)
            acc[:, cols] += lax.dot_general(
                mixed_ref[span, :], gathered[span, cols], TN, preferred_element_type=jnp.float32
            )

    order = [mask for count in range(gather.bits + 1) for mask in gather.level(count)]
    codes = [2 * mask + core for mask in order for core in (0, 1)]
    complete = [
        int(core == 1 and all(other // chips != mask // chips for other in order[k + 1 :]))
        for k, mask in enumerate(order)
        for core in (0, 1)
    ]

    def step(t, carry):
        for k, mask in enumerate(order):
            if k and mask.bit_count() > order[k - 1].bit_count():
                pl.when(t == 2 * k)(functools.partial(gather.forward, mask.bit_count()))
            pl.when(t == 2 * k + 1)(functools.partial(gather.wait_core, mask))
        at = gather.away(codes, t)
        work(at)

        @pl.when(look_up(complete, t) == 1)
        def _():
            first = (at // 2 // chips) * sequences

            def one(i, carry):
                s, head = first + i // heads, lax.rem(i, heads)
                attend_back_one(
                    slope_ref[head], proj, grad_mixed, pl.multiple_of(s * length, length), head, row_ref.at[s],
                    grad_proj_ref, dk, dv, sums_ref, length,
                )
                return carry

            lax.fori_loop(0, sequences * heads, one, 0)

        return carry

    product.start()
    gather.start()
    acc[...] = jnp.zeros_like(acc)
    sums_ref[...] = jnp.zeros_like(sums_ref)
    product.batch(0, 1)
    fetch.wait()
    gather.keep().wait()
    lax.fori_loop(0, 2 * len(order), step, 0)
    grad_dense_ref[...] = acc[...].astype(grad_dense_ref.dtype)
    product.finish()
    gather.finish_sends()


def dense_back(own, mixed, weight, mlp_rows, grad_pre, proj, slopes, labels, n, collective_id):
    rows, width = own.shape
    total, depth = mixed.shape
    length = labels.shape[1]
    return pl.pallas_call(
        functools.partial(dense_back_kernel, n, length),
        out_shape=(
            jax.ShapeDtypeStruct(proj.shape, jnp.bfloat16),
            jax.ShapeDtypeStruct((8, depth), jnp.float32),
            jax.ShapeDtypeStruct((depth, width), jnp.bfloat16),
            jax.ShapeDtypeStruct((mlp_rows.shape[1], grad_pre.shape[1]), jnp.bfloat16),
        ),
        in_specs=[pl.BlockSpec(memory_space=pltpu.SMEM), VMEM_SPEC, VMEM_SPEC, VMEM_SPEC]
        + [HBM_SPEC] * 3
        + [VMEM_SPEC],
        out_specs=(VMEM_SPEC, VMEM_SPEC, VMEM_SPEC, HBM_SPEC),
        scratch_shapes=[
            pltpu.VMEM((total, width), jnp.bfloat16),
            pltpu.VMEM((depth, width), jnp.float32),
            pltpu.VMEM((total, depth), jnp.bfloat16),
            pltpu.VMEM(proj.shape, jnp.bfloat16),
            pltpu.VMEM((length, HEAD_DIM), jnp.float32),
            pltpu.VMEM((length, HEAD_DIM), jnp.float32),
            pltpu.SemaphoreType.DMA(()),
        ]
        + product_scratch(total, mlp_rows.shape[1], grad_pre.shape[1])
        + gather_sems(n),
        compiler_params=comm_params(collective_id),
        cost_estimate=LINK_COST,
        name="dense_back",
    )(slopes, own, mixed, weight, mlp_rows, grad_pre, proj, labels[:, None, :])


def shrink_kernel(
    n, d, a_hbm, w_ref, residual_hbm, bias_ref, early_ref, up_sum_ref, head_sums_ref,
    hidden_ref, sums_ref, biases_ref, out, residual, fetch_sem, *scratch
):
    fetch = pltpu.make_async_copy(residual_hbm, residual, fetch_sem)
    fetch.start()
    flat, biases = Total(n, d, scratch[:6]), Total(n, d, scratch[6:12])
    scatter = Scatter(n, False, a_hbm, w_ref, out, scratch[12:])
    heads_width = head_sums_ref.shape[1]

    def filler(j):
        for level in range(min(flat.levels + 1, scatter.chunks)):

            @pl.when(j == level)
            def _():
                if level == 0:
                    biases.lines[0] = jnp.zeros(biases.lines.shape[1:], jnp.float32)
                    biases.lines[0, 0:1, :] = up_sum_ref[...]
                    biases.lines[0, 1:3, :heads_width] = head_sums_ref[0:2, :]
                    biases.spread()
                    flat.pair[0] = early_ref[...]
                flat.step(level)

    def work(at):
        hidden_ref[at, :] = (residual[at, :] + out[at, :] + bias_ref[...]).astype(hidden_ref.dtype)

    scatter.run(filler, after_chunk(scatter, (fetch,), work), d)
    for level in range(scatter.chunks, flat.levels + 1):
        flat.step(level)
    biases_ref[...] = biases.finish(False)
    sums_ref[...] = flat.finish()


def shrink(activated, down, residual, bias, sums, up_sum, head_sums, n, d, collective_id):
    rows, width = residual.shape
    units = up_sum.shape[1]
    return pl.pallas_call(
        functools.partial(shrink_kernel, n, d),
        out_shape=(
            jax.ShapeDtypeStruct((rows, width), jnp.bfloat16),
            jax.ShapeDtypeStruct((8, width), jnp.float32),
            jax.ShapeDtypeStruct((8, units), jnp.float32),
        ),
        in_specs=[HBM_SPEC, VMEM_SPEC, HBM_SPEC] + [VMEM_SPEC] * 4,
        out_specs=(VMEM_SPEC, VMEM_SPEC, VMEM_SPEC),
        scratch_shapes=[
            pltpu.VMEM((rows, width), jnp.float32),
            pltpu.VMEM((rows, width), jnp.float32),
            pltpu.SemaphoreType.DMA(()),
        ]
        + total_scratch(n, d, 8, width)
        + total_scratch(n, d, 8, units)
        + scatter_scratch(n, rows, activated.shape[1], width, CHUNKS),
        compiler_params=comm_params(collective_id),
        cost_estimate=LINK_COST,
        name="shrink",
    )(activated, down, residual, bias, sums, up_sum, head_sums)


def project_back_kernel(
    n, a_hbm, w_ref, input_hbm, grad_hbm, gain_ref, early_ref, left_hbm,
    out_ref, sums_ref, weight_hbm, inputs, grads, fetch_sem, *scratch
):
    fetches = (
        pltpu.make_async_copy(input_hbm, inputs, fetch_sem.at[0]),
        pltpu.make_async_copy(grad_hbm, grads, fetch_sem.at[1]),
    )
    for fetch in fetches:
        fetch.start()
    product = Product(left_hbm, a_hbm, weight_hbm, scratch[:7])
    scatter = Scatter(n, True, a_hbm, w_ref, out_ref, scratch[7:])
    product.start()
    sums_ref[...] = early_ref[...]

    def work(at):
        grad = out_ref[at, :]
        back, terms = back_rows(grad, inputs[at, :].astype(jnp.float32), gain_ref[...])
        out_ref[at, :] = grads[at, :] + back
        sums_ref[4:5, :] += column_sum(terms)
        sums_ref[5:6, :] += column_sum(grad)

    scatter.run(lambda j: product.batch(j, scatter.chunks), after_chunk(scatter, fetches, work))
    product.finish()


def project_back(grad_proj, weight, inputs, grad_residual, gain, early, attn_rows, n, collective_id):
    rows, width = inputs.shape
    columns = grad_proj.shape[1]
    return pl.pallas_call(
        functools.partial(project_back_kernel, n),
        out_shape=(
            jax.ShapeDtypeStruct((rows, width), jnp.float32),
            jax.ShapeDtypeStruct((8, width), jnp.float32),
            jax.ShapeDtypeStruct((width, columns), jnp.bfloat16),
        ),
        in_specs=[HBM_SPEC, VMEM_SPEC, HBM_SPEC, HBM_SPEC, VMEM_SPEC, VMEM_SPEC, HBM_SPEC],
        out_specs=(VMEM_SPEC, VMEM_SPEC, HBM_SPEC),
        scratch_shapes=[
            pltpu.VMEM((rows, width), inputs.dtype),
            pltpu.VMEM((rows, width), jnp.float32),
            pltpu.SemaphoreType.DMA((2,)),
        ]
        + product_scratch(n * rows, width, columns)
        + scatter_scratch(n, rows, columns, width, CHUNKS),
        compiler_params=comm_params(collective_id),
        cost_estimate=LINK_COST,
        name="project_back",
    )(grad_proj, weight, inputs, grad_residual, gain, early, attn_rows)


HEADS = 16


def wide(vector):
    return vector.astype(jnp.float32)[None]


def share(grad, dimension):
    return lax.psum_scatter(grad, "dp", scatter_dimension=dimension, tiled=True)


def finish_kernel(heads_width, *refs):
    ins, outs = refs[:8], refs[8:]
    for source, target in zip(ins[:6], outs[:6]):
        target[...] = source[...].astype(target.dtype)

    @pl.when(pl.program_id(0) == 0)
    def _():
        sums, biases = ins[6:]
        for i in range(6):
            outs[6 + i][...] = sums[i : i + 1, :]
        outs[12][...] = biases[0:1, :]
        outs[13][...] = biases[1:2, :heads_width]
        outs[14][...] = biases[2:3, :heads_width]


def finish(hidden_output, grad_input, weights, sums, biases, heads_width):
    steps = 8

    def rows_block(x):
        return pl.BlockSpec((x.shape[0] // steps, x.shape[1]), lambda i: (i, 0))

    def whole_block(shape):
        return pl.BlockSpec(shape, lambda i: (0, 0))

    large = (hidden_output, grad_input) + weights
    small = [(1, sums.shape[1])] * 6 + [(1, biases.shape[1]), (1, heads_width), (1, heads_width)]
    results = pl.pallas_call(
        functools.partial(finish_kernel, heads_width),
        grid=(steps,),
        out_shape=[jax.ShapeDtypeStruct(hidden_output.shape, hidden_output.dtype)]
        + [jax.ShapeDtypeStruct(x.shape, jnp.float32) for x in large[1:]]
        + [jax.ShapeDtypeStruct(shape, jnp.float32) for shape in small],
        in_specs=[rows_block(x) for x in large] + [whole_block(sums.shape), whole_block(biases.shape)],
        out_specs=[rows_block(x) for x in large] + [whole_block(shape) for shape in small],
        name="finish",
    )(*large, sums, biases)
    return results[:6], [x.reshape(-1) for x in results[6:]]


def on_device(
    hidden_input,
    first_gain,
    first_shift,
    qkv_weight,
    query_bias,
    value_bias,
    dense_weight,
    dense_bias,
    second_gain,
    second_shift,
    up_weight,
    up_bias,
    down_weight,
    down_bias,
    segments,
    document_lengths,
    cotangent,
    *,
    n,
    d,
):
    heads_local = query_bias.shape[0] // HEAD_DIM
    attn_rows = gather_rows(hidden_input, wide(first_gain), wide(first_shift), n, 1)
    project_full, dense_full, expand_full, shrink_full = (
        lax.all_gather(qkv_weight, "dp", axis=0, tiled=True),
        lax.all_gather(dense_weight, "dp", axis=1, tiled=True),
        lax.all_gather(up_weight, "dp", axis=0, tiled=True),
        lax.all_gather(down_weight, "dp", axis=1, tiled=True),
    )
    group_rows = attn_rows.shape[0]
    sequences = document_lengths.shape[0]
    length = group_rows // sequences
    heads_index = lax.axis_index("tensor") * heads_local + lax.broadcasted_iota(
        jnp.int32, (heads_local,), 0
    )
    slopes = jnp.exp2(-8.0 * (heads_index.astype(jnp.float32) + 1.0) / HEADS) * LOG2E
    position = lax.broadcasted_iota(jnp.int32, (sequences, length), 1)
    filled = jnp.sum(document_lengths, axis=1, keepdims=True)
    labels = jnp.where(position < filled, segments.reshape(sequences, length), length + position).astype(jnp.float32)
    query_bias32 = query_bias.astype(jnp.float32).reshape(heads_local, HEAD_DIM)
    value_bias32 = value_bias.astype(jnp.float32).reshape(heads_local, HEAD_DIM)
    proj_bias = jnp.stack((query_bias32, jnp.zeros_like(query_bias32), value_bias32), axis=1).reshape(
        heads_local * 3 * HEAD_DIM
    )
    grad_rows, proj, mixed = project_attend(
        attn_rows, project_full, proj_bias[None], slopes, labels, cotangent, n, 6
    )
    residual, mlp_input = dense(
        mixed, dense_full, hidden_input, wide(dense_bias), wide(second_gain), wide(second_shift), n, 2
    )
    mlp_rows, activated, grad_pre, sum_up_bias = expand(
        mlp_input, grad_rows, expand_full, shrink_full, wide(up_bias), n, 7
    )
    grad_residual, grad_attn_out, early_sums, grad_down = expand_back(
        grad_pre, expand_full, activated, grad_rows, residual, cotangent, wide(second_gain), n, 4
    )
    grad_down_weight = share(grad_down, 1)
    grad_proj, head_sums, grad_dense, grad_up = dense_back(
        grad_attn_out, mixed, dense_full, mlp_rows, grad_pre, proj, slopes, labels, n, 9
    )
    grad_down_weight, grad_proj = lax.optimization_barrier((grad_down_weight, grad_proj))
    grad_up_weight = share(grad_up, 0)
    grad_dense_weight = share(grad_dense, 1)
    grad_input, sums, grad_project = project_back(
        grad_proj, project_full, hidden_input, grad_residual, wide(first_gain), early_sums, attn_rows, n, 5
    )
    grad_qkv_weight = share(grad_project, 0)
    hidden_output, sums, biases = shrink(
        activated, shrink_full, residual, wide(down_bias), sums, sum_up_bias, head_sums, n, d, 3
    )
    heads_width = heads_local * HEAD_DIM
    large, small = finish(
        hidden_output,
        grad_input,
        (grad_qkv_weight, grad_dense_weight, grad_up_weight, grad_down_weight),
        sums,
        biases,
        heads_width,
    )
    hidden_output, grad_input, grad_qkv_weight, grad_dense_weight, grad_up_weight, grad_down_weight = large
    grad_second_gain, grad_second_shift, grad_dense_bias, grad_down_bias, grad_first_gain, grad_first_shift = small[:6]
    grad_up_bias, grad_query_bias, grad_value_bias = small[6:]
    return (
        hidden_output,
        grad_input,
        grad_first_gain,
        grad_first_shift,
        grad_qkv_weight,
        grad_query_bias,
        grad_value_bias,
        grad_dense_weight,
        grad_dense_bias,
        grad_second_gain,
        grad_second_shift,
        grad_up_weight,
        grad_up_bias,
        grad_down_weight,
        grad_down_bias,
    )


def solution(mesh):
    return jax.shard_map(
        functools.partial(on_device, n=mesh.shape["tensor"], d=mesh.shape["dp"]),
        mesh=mesh,
        in_specs=(
            P(("dp", "tensor"), None),
            P(),
            P(),
            P("dp", "tensor"),
            P("tensor"),
            P("tensor"),
            P("tensor", "dp"),
            P(),
            P(),
            P(),
            P("dp", "tensor"),
            P("tensor"),
            P("tensor", "dp"),
            P(),
            P("dp"),
            P("dp", None),
            P(("dp", "tensor"), None),
        ),
        out_specs=(
            P(("dp", "tensor"), None),
            P(("dp", "tensor"), None),
            P(),
            P(),
            P("dp", "tensor"),
            P("tensor"),
            P("tensor"),
            P("tensor", "dp"),
            P(),
            P(),
            P(),
            P("dp", "tensor"),
            P("tensor"),
            P("tensor", "dp"),
            P(),
        ),
        check_vma=False,
    )
```

```python
import functools
import math

import jax
import jax.numpy as jnp
from jax import lax
from jax.experimental import pallas as pl
from jax.experimental.pallas import tpu as pltpu
from jax.sharding import PartitionSpec as P

VMEM_LIMIT = 62 << 20
LINK_COST = pl.CostEstimate(flops=0, bytes_accessed=280_000_000, transcendentals=0)


def flip(index, bit):
    return index + (1 - 2 * ((index // 2**bit) % 2)) * 2**bit


def look_up(table, i):
    if isinstance(i, int):
        return table[i]
    value = table[0]
    for k in range(1, len(table)):
        value = value + (i >= k).astype(jnp.int32) * (table[k] - table[k - 1])
    return value


def parity(i):
    return i % 2 if isinstance(i, int) else lax.rem(i, 2)


def chip_bits(n):
    return n.bit_length() - 2


def column_parts(width, count):
    blocks = width // 128
    edges = [128 * (blocks * i // count) for i in range(count + 1)]
    return [(a, b - a) for a, b in zip(edges[:-1], edges[1:])]


def peer(index):
    return {"tensor": index}


def greet(me, bits, d=1, meanwhile=None):
    barrier = pltpu.get_barrier_semaphore()
    for bit in range(bits + 1):
        pl.semaphore_signal(
            barrier, inc=1, device_id=peer(flip(me, bit)), device_id_type=pl.DeviceIdType.MESH
        )
    for ahead in range(1, d):
        pl.semaphore_signal(
            barrier, inc=1, device_id=ahead_on_dp(ahead, d), device_id_type=pl.DeviceIdType.MESH
        )
    if meanwhile is not None:
        meanwhile()
    pl.semaphore_wait(barrier, bits + d)


def ahead_on_dp(ahead, d):
    return {"dp": lax.rem(lax.axis_index("dp") + ahead, d)}


def remote(src, dst, send_sem, recv_sem, target):
    return pltpu.make_async_remote_copy(
        src_ref=src,
        dst_ref=dst,
        send_sem=send_sem,
        recv_sem=recv_sem,
        device_id=peer(target),
        device_id_type=pl.DeviceIdType.MESH,
    )


class Gather:
    def __init__(self, n, own_ref, out_ref, sems):
        self.me = lax.axis_index("tensor")
        self.bits = chip_bits(n)
        self.rows, width = own_ref.shape
        self.parts = column_parts(width, self.bits)
        self.own, self.out = own_ref, out_ref
        self.own_sem, self.chip_send, self.chip_recv, self.core_send, self.core_recv = sems

    def slot(self, part, index):
        at = self.me
        for step in range(self.bits):
            if (index >> step) & 1:
                at = flip(at, 1 + (part + step) % self.bits)
        return at

    def place(self, mask, core):
        at = flip(self.me, 0) if core else self.me
        for bit in range(self.bits):
            if (mask >> bit) & 1:
                at = flip(at, 1 + bit)
        return at

    def away(self, codes, t):
        code, at = look_up(codes, t), self.me
        for bit in range(self.bits + 1):
            at = at + (code // 2**bit) % 2 * (1 - 2 * ((self.me // 2**bit) % 2)) * 2**bit
        return at

    def index_of(self, part, mask):
        return sum(2 ** ((bit - part) % self.bits) for bit in range(self.bits) if (mask >> bit) & 1)

    def level(self, count):
        return [index for index in range(2**self.bits) if index.bit_count() == count]

    def block(self, part, index, core=0):
        start, size = self.parts[part]
        at = flip(self.slot(part, index), 0) if core else self.slot(part, index)
        return self.out.at[pl.ds(pl.multiple_of(at * self.rows, self.rows), self.rows), pl.ds(start, size)]

    def source(self, part, index):
        start, size = self.parts[part]
        return self.own.at[:, pl.ds(start, size)] if index == 0 else self.block(part, index)

    def chip_copy(self, part, index, step):
        arrives = index + 2**step
        return remote(
            self.source(part, index),
            self.block(part, index),
            self.chip_send.at[part, arrives],
            self.chip_recv.at[part, arrives],
            flip(self.me, 1 + (part + step) % self.bits),
        )

    def core_copy(self, part, index):
        return remote(
            self.source(part, index),
            self.block(part, index),
            self.core_send.at[part, index],
            self.core_recv.at[part, index],
            flip(self.me, 0),
        )

    def keep(self):
        rows = pl.ds(pl.multiple_of(self.me * self.rows, self.rows), self.rows)
        return pltpu.make_async_copy(self.own, self.out.at[rows, :], self.own_sem)

    def start(self, meanwhile=None):
        greet(self.me, self.bits, meanwhile=meanwhile)
        for step in range(self.bits):
            for part in range(self.bits):
                self.chip_copy(part, 0, step).start()
        for part in range(self.bits):
            self.core_copy(part, 0).start()
        self.keep().start()

    def forward(self, count):
        for index in self.level(count):
            for part in range(self.bits):
                arrived = self.block(part, index)
                remote(
                    arrived, arrived, self.chip_send.at[part, index], self.chip_recv.at[part, index], flip(self.me, 0)
                ).wait_recv()
                for step in range(index.bit_length(), self.bits):
                    self.chip_copy(part, index, step).start()
                self.core_copy(part, index).start()

    def wait_core(self, mask):
        for part in range(self.bits):
            index = self.index_of(part, mask)
            arrived = self.block(part, index, 1)
            remote(
                arrived, arrived, self.core_send.at[part, index], self.core_recv.at[part, index], flip(self.me, 0)
            ).wait_recv()

    def finish_sends(self):
        for part in range(self.bits):
            for index in range(2**self.bits):
                for step in range(index.bit_length(), self.bits):
                    self.chip_copy(part, index, step).wait_send()
                self.core_copy(part, index).wait_send()


def gather_kernel(n, x_ref, *refs):
    flat_refs, (out_ref, vectors_ref, own, *sems) = refs[:9], refs[9:]

    def put(row, start, ref):
        size = ref.shape[0]
        vectors_ref[row, :, start : start + size] = ref[...].astype(jnp.float32).reshape(1, size)

    put(FIRST_GAIN, 0, flat_refs[FIRST_GAIN])
    put(FIRST_SHIFT, 0, flat_refs[FIRST_SHIFT])

    def work(at):
        normed, _ = normal_rows(x_ref[at, :].astype(jnp.float32))
        own[at, :] = (normed * vectors_ref[FIRST_GAIN] + vectors_ref[FIRST_SHIFT]).astype(own.dtype)

    gather = Gather(n, own, out_ref, sems)
    gather.start(lambda: row_blocks(0, own.shape[0], 32, work))
    for row in range(FIRST_SHIFT + 1, UP_BIAS):
        put(row, 0, flat_refs[row])
    vectors_ref[UP_BIAS] = jnp.zeros(vectors_ref.shape[1:], jnp.float32)
    vectors_ref[HEAD_BIASES] = jnp.zeros(vectors_ref.shape[1:], jnp.float32)
    put(UP_BIAS, 0, flat_refs[UP_BIAS])
    put(HEAD_BIASES, 0, flat_refs[7])
    put(HEAD_BIASES, flat_refs[7].shape[0], flat_refs[8])
    for count in range(1, gather.bits + 1):
        gather.forward(count)
    for mask in range(2**gather.bits):
        gather.wait_core(mask)
    gather.finish_sends()
    gather.keep().wait()


def gather_sems(n):
    bits = chip_bits(n)
    dma = pltpu.SemaphoreType.DMA
    return [dma(())] + [dma((bits, 2**bits))] * 4


def gather_rows(x, vectors, n, collective_id):
    rows, width = x.shape
    return pl.pallas_call(
        functools.partial(gather_kernel, n),
        out_shape=(
            jax.ShapeDtypeStruct((n * rows, width), x.dtype),
            jax.ShapeDtypeStruct((8, 1, width), jnp.float32),
        ),
        in_specs=[VMEM_SPEC] * 10,
        out_specs=(HBM_SPEC, VMEM_SPEC),
        scratch_shapes=[pltpu.VMEM((rows, width), x.dtype)] + gather_sems(n),
        compiler_params=pltpu.CompilerParams(
            collective_id=collective_id, has_side_effects=True, vmem_limit_bytes=VMEM_LIMIT
        ),
        cost_estimate=LINK_COST,
        name="gather_rows",
    )(x, *vectors)


class Scatter:
    def __init__(self, n, transposed, a_hbm, w_ref, out_ref, scratch):
        (self.csend, self.crecv, self.recv, self.other, self.mine, self.load_sem) = scratch[:6]
        self.core_send, self.core_recv, self.chip_send, self.chip_recv = scratch[6:]
        self.me = lax.axis_index("tensor")
        self.bits = chip_bits(n)
        self.total = 2**self.bits
        self.transposed = transposed
        self.a, self.w, self.out = a_hbm, w_ref, out_ref
        self.rows, width = out_ref.shape
        self.chunk = self.csend.shape[2]
        self.chunks = self.rows // self.chunk
        self.parts = column_parts(width, self.bits)

    def index_of(self, part, mask):
        top = self.bits - 1
        return sum(2 ** (top - (bit - part) % self.bits) for bit in range(self.bits) if (mask >> bit) & 1)

    def place(self, mask, core):
        at = flip(self.me, 0) if core else self.me
        for bit in range(self.bits):
            if (mask >> bit) & 1:
                at = flip(at, 1 + bit)
        return at

    def rows_of(self, j):
        return pl.ds(pl.multiple_of(j * self.chunk, self.chunk), self.chunk)

    def loads(self, j, core):
        into = self.other if core else self.mine
        copies = []
        for mask in range(self.total):
            start = pl.multiple_of(self.place(mask, core) * self.rows + j * self.chunk, self.chunk)
            copies.append(
                pltpu.make_async_copy(
                    self.a.at[pl.ds(start, self.chunk), :],
                    into.at[lax.rem(j, 2), pl.ds(mask * self.chunk, self.chunk), :],
                    self.load_sem.at[core, lax.rem(j, 2), mask],
                )
            )
        return copies

    def core_copy(self, j, part):
        start, size = self.parts[part]
        return remote(
            self.csend.at[lax.rem(j, 2), :, :, pl.ds(start, size)],
            self.crecv.at[:, self.rows_of(j), pl.ds(start, size)],
            self.core_send.at[part, j],
            self.core_recv.at[part, j],
            flip(self.me, 0),
        )

    def chip_copy(self, j, part, step):
        half = self.total >> (step + 1)
        first = sum(self.total >> (s + 1) for s in range(step))
        start, size = self.parts[part]
        return remote(
            self.crecv.at[pl.ds(half, half), self.rows_of(j), pl.ds(start, size)],
            self.recv.at[pl.ds(first, half), self.rows_of(j), pl.ds(start, size)],
            self.chip_send.at[part, step, j],
            self.chip_recv.at[part, step, j],
            flip(self.me, 1 + (part + step) % self.bits),
        )

    def tiles(self, part, lhs, put):
        start, size = self.parts[part]
        tile = 256 if size % 256 == 0 and start % 256 == 0 else 128

        def one(i, carry):
            cols = pl.ds(pl.multiple_of(start + i * tile, tile), tile)
            if self.transposed:
                value = lax.dot_general(
                    lhs[...], self.w[cols, :], (((1,), (1,)), ((), ())), preferred_element_type=jnp.float32
                )
            else:
                value = jnp.dot(lhs[...], self.w[:, cols], preferred_element_type=jnp.float32)
            put(cols, value)
            return carry

        lax.fori_loop(0, size // tile, one, 0)

    def piece(self, value, mask):
        return value[mask * self.chunk : (mask + 1) * self.chunk, :]

    def stage_core(self, j):
        for copy in self.loads(j, 1):
            copy.wait()

        @pl.when(j >= 2)
        def _():
            for part in range(self.bits):
                self.core_copy(j - 2, part).wait_send()

        for part in range(self.bits):

            def put(cols, value):
                for mask in range(self.total):
                    self.csend[lax.rem(j, 2), self.index_of(part, mask), :, cols] = self.piece(value, mask).astype(
                        self.csend.dtype
                    )

            self.tiles(part, self.other.at[lax.rem(j, 2)], put)
            self.core_copy(j, part).start()

    def stage_first(self, j):
        for copy in self.loads(j, 0):
            copy.wait()
        for part in range(self.bits):
            self.core_copy(j, part).wait_recv()

            def put(cols, value):
                for mask in range(self.total):
                    index = self.index_of(part, mask)
                    got = self.piece(value, mask) + self.crecv[index, self.rows_of(j), cols].astype(jnp.float32)
                    if index:
                        self.crecv[index, self.rows_of(j), cols] = got.astype(self.crecv.dtype)
                    else:
                        self.out[self.rows_of(j), cols] = got

            self.tiles(part, self.mine.at[lax.rem(j, 2)], put)
            self.chip_copy(j, part, 0).start()

    def stage_next(self, j, step):
        half = self.total >> (step + 1)
        first = sum(self.total >> (s + 1) for s in range(step))
        for part in range(self.bits):
            start, size = self.parts[part]
            cols = slice(start, start + size)
            self.chip_copy(j, part, step).wait_recv()
            for index in reversed(range(half)):
                got = self.recv[first + index, self.rows_of(j), cols].astype(jnp.float32)
                if index:
                    value = self.crecv[index, self.rows_of(j), cols].astype(jnp.float32) + got
                    self.crecv[index, self.rows_of(j), cols] = value.astype(self.crecv.dtype)
                else:
                    self.out[self.rows_of(j), cols] += got
            if step + 1 < self.bits:
                self.chip_copy(j, part, step + 1).start()

    def run(self, filler=None, after=None, d=1):
        for copy in self.loads(0, 1):
            copy.start()
        greet(self.me, self.bits, d)

        def body(u, carry):
            @pl.when(u + 1 < self.chunks)
            def _():
                for copy in self.loads(u + 1, 1):
                    copy.start()

            @pl.when(u < self.chunks)
            def _():
                for copy in self.loads(u, 0):
                    copy.start()
                self.stage_core(u)

            @pl.when((u >= 1) & (u <= self.chunks))
            def _():
                self.stage_first(u - 1)

            for step in range(self.bits):

                @pl.when((u >= 2 + step) & (u < self.chunks + 2 + step))
                def _():
                    self.stage_next(u - 2 - step, step)

            if filler is not None:

                @pl.when((u >= 1) & (u <= self.chunks))
                def _():
                    filler(u - 1)

            if after is not None:
                done = u - self.bits - 1

                @pl.when(done >= 0)
                def _():
                    after(done)

            return carry

        lax.fori_loop(0, self.chunks + self.bits + 1, body, 0)
        for part in range(self.bits):
            for j in range(self.chunks):
                if j >= self.chunks - 2:
                    self.core_copy(j, part).wait_send()
                for step in range(self.bits):
                    self.chip_copy(j, part, step).wait_send()


def scatter_scratch(n, rows, depth, width, chunks):
    bits = chip_bits(n)
    total = 2**bits
    chunk = rows // chunks
    dma = pltpu.SemaphoreType.DMA
    return [
        pltpu.VMEM((2, total, chunk, width), jnp.bfloat16),
        pltpu.VMEM((total, rows, width), jnp.bfloat16),
        pltpu.VMEM((total - 1, rows, width), jnp.bfloat16),
        pltpu.VMEM((2, total * chunk, depth), jnp.bfloat16),
        pltpu.VMEM((2, total * chunk, depth), jnp.bfloat16),
        dma((2, 2, total)),
        dma((bits, chunks)),
        dma((bits, chunks)),
        dma((bits, bits, chunks)),
        dma((bits, bits, chunks)),
    ]


HEAD_DIM = 128
HEADS = 16
FIRST_GAIN, FIRST_SHIFT, DENSE_BIAS, SECOND_GAIN, SECOND_SHIFT, DOWN_BIAS, UP_BIAS, HEAD_BIASES = range(8)
LOG2E = 1.4426950408889634
SCALE = 1.0 / math.sqrt(HEAD_DIM)
BLOCK = 256
NT = (((1,), (1,)), ((), ()))
TN = (((0,), (0,)), ((), ()))


def as_column(row):
    width = row.shape[1]
    here = lax.broadcasted_iota(jnp.int32, (width, width), 0) == lax.broadcasted_iota(jnp.int32, (width, width), 1)
    return jnp.sum(jnp.where(here, row, 0.0), axis=1, keepdims=True)


def masked_scores(slope, q, keys, query_labels, key_labels, first):
    raw = lax.dot_general(q, keys, NT, preferred_element_type=jnp.float32)
    rows, width = raw.shape
    column = lax.broadcasted_iota(jnp.int32, (1, width), 1)
    bias = column.astype(jnp.float32) * slope
    same = query_labels == key_labels
    causal = lax.broadcasted_iota(jnp.int32, (rows, width), 1) <= first + lax.broadcasted_iota(
        jnp.int32, (rows, width), 0
    )
    return jnp.where(same & causal, raw * (SCALE * LOG2E) + bias, -1e30)


class Total:
    def __init__(self, n, d, scratch):
        self.pair, self.lines, self.send, self.recv, self.line_send, self.line_recv = scratch
        self.me, self.d = lax.axis_index("tensor"), d
        self.levels = n.bit_length() - 1

    def level_copy(self, level):
        return remote(
            self.pair.at[2 * level],
            self.pair.at[2 * level + 1],
            self.send.at[level],
            self.recv.at[level],
            flip(self.me, level),
        )

    def line_copy(self, ahead):
        return pltpu.make_async_remote_copy(
            src_ref=self.lines.at[0],
            dst_ref=self.lines.at[ahead],
            send_sem=self.line_send.at[ahead],
            recv_sem=self.line_recv.at[ahead],
            device_id=ahead_on_dp(ahead, self.d),
            device_id_type=pl.DeviceIdType.MESH,
        )

    def spread(self):
        for ahead in range(1, self.d):
            self.line_copy(ahead).start()

    def step(self, level):
        if level:
            self.level_copy(level - 1).wait_recv()
            self.pair[2 * level] = self.pair[2 * level - 2] + self.pair[2 * level - 1]
        if level < self.levels:
            self.level_copy(level).start()
        else:
            self.lines[0] = self.pair[2 * level]
            self.spread()

    def finish(self, levels=True):
        for ahead in range(1, self.d):
            self.line_copy(ahead).wait_recv()
        z = lax.axis_index("dp")
        total = None
        for index in range(self.d):
            value = self.lines[lax.rem(z - index + self.d, self.d)]
            total = value if total is None else total + value
        for ahead in range(1, self.d):
            self.line_copy(ahead).wait_send()
        if levels:
            for level in range(self.levels):
                self.level_copy(level).wait_send()
        return total


def total_scratch(n, d, rows, width):
    levels = n.bit_length() - 1
    dma = pltpu.SemaphoreType.DMA
    return [
        pltpu.VMEM((2 * levels + 1, rows, width), jnp.float32),
        pltpu.VMEM((d, rows, width), jnp.float32),
        dma((levels,)),
        dma((levels,)),
        dma((d,)),
        dma((d,)),
    ]


def tile_of(width):
    return 256 if width % 256 == 0 else width


def attend_one(slope, proj_ref, start, head, row_ref, out_ref, length):
    at = pl.multiple_of(head * 3 * HEAD_DIM, HEAD_DIM)

    def take(which, first, size):
        return proj_ref[pl.ds(start + first, size), pl.ds(at + which * HEAD_DIM, HEAD_DIM)]

    for first in range(0, length, BLOCK):
        last = first + BLOCK
        scores = masked_scores(
            slope, take(0, first, BLOCK), take(1, 0, last), as_column(row_ref[:, first:last]), row_ref[:, :last], first
        )
        top = jnp.max(scores, axis=1, keepdims=True)
        expo = jnp.exp2(scores - top)
        total = jnp.sum(expo, axis=1, keepdims=True)
        mixed = jnp.dot(expo.astype(jnp.bfloat16), take(2, 0, last), preferred_element_type=jnp.float32)
        out_ref[pl.ds(start + first, BLOCK), pl.ds(pl.multiple_of(head * HEAD_DIM, HEAD_DIM), HEAD_DIM)] = (
            mixed / total
        ).astype(out_ref.dtype)


def project_kernel(
    n, length, slope_ref, own_ref, rows_hbm, w_ref, vectors_ref, row_ref, gathered, proj_hbm, mixed_ref,
    proj, buf, bias, load_sem, store_sem, *sems
):
    gather = Gather(n, own_ref, gathered, sems)
    rows = own_ref.shape[0]
    width = w_ref.shape[1]
    tile = tile_of(width)
    heads = width // (3 * HEAD_DIM)
    sequences = n * rows // length

    def load(i):
        at = pl.ds(pl.multiple_of(i * rows, rows), rows)
        return pltpu.make_async_copy(rows_hbm.at[at, :], buf.at[lax.rem(i, 2)], load_sem.at[lax.rem(i, 2)])

    load(0).start()
    bias[...] = jnp.zeros_like(bias)
    for head in range(heads):
        for which, first in ((0, 0), (2, heads * HEAD_DIM)):
            at = (3 * head + which) * HEAD_DIM
            bias[:, at : at + HEAD_DIM] = vectors_ref[HEAD_BIASES, :, first + head * HEAD_DIM : first + (head + 1) * HEAD_DIM]
    gather.start()

    def store(i):
        at = pl.ds(pl.multiple_of(i * rows, rows), rows)
        return pltpu.make_async_copy(proj.at[at, :], proj_hbm.at[at, :], store_sem.at[i])

    def project(i, carry):
        load(i).wait()

        @pl.when(i + 1 < n)
        def _():
            load(i + 1).start()

        at = pl.ds(pl.multiple_of(i * rows, rows), rows)
        for first in range(0, width, tile):
            cols = slice(first, first + tile)
            proj[at, cols] = (
                jnp.dot(buf[lax.rem(i, 2)], w_ref[:, cols], preferred_element_type=jnp.float32) + bias[:, cols]
            ).astype(proj.dtype)
        store(i).start()
        return carry

    lax.fori_loop(0, n, project, 0)
    gather.forward(1)

    def one(i, carry):
        s, head = i // heads, lax.rem(i, heads)
        attend_one(
            slope_ref[head],
            proj,
            pl.multiple_of(s * length, length),
            head,
            row_ref.at[s],
            mixed_ref,
            length,
        )
        return carry

    lax.fori_loop(0, sequences * heads, one, 0)
    for count in range(2, gather.bits + 1):
        gather.forward(count)
    for i in range(n):
        store(i).wait()
    for mask in range(2**gather.bits):
        gather.wait_core(mask)
    gather.finish_sends()
    gather.keep().wait()


def project_attend(attn_rows, weight, vectors, slopes, labels, own, n, collective_id):
    total, depth = attn_rows.shape
    rows, width = own.shape[0], weight.shape[1]
    heads = width // (3 * HEAD_DIM)
    vmem = pl.BlockSpec(memory_space=pltpu.VMEM)
    hbm = pl.BlockSpec(memory_space=pl.ANY)
    dma = pltpu.SemaphoreType.DMA
    return pl.pallas_call(
        functools.partial(project_kernel, n, labels.shape[1]),
        out_shape=(
            jax.ShapeDtypeStruct((total, own.shape[1]), own.dtype),
            jax.ShapeDtypeStruct((total, width), jnp.bfloat16),
            jax.ShapeDtypeStruct((total, heads * HEAD_DIM), jnp.bfloat16),
        ),
        in_specs=[pl.BlockSpec(memory_space=pltpu.SMEM), vmem, hbm, vmem, vmem, vmem],
        out_specs=(hbm, hbm, vmem),
        scratch_shapes=[
            pltpu.VMEM((total, width), jnp.bfloat16),
            pltpu.VMEM((2, rows, depth), jnp.bfloat16),
            pltpu.VMEM((1, width), jnp.float32),
            dma((2,)),
            dma((n,)),
        ]
        + gather_sems(n),
        compiler_params=pltpu.CompilerParams(
            collective_id=collective_id, has_side_effects=True, vmem_limit_bytes=VMEM_LIMIT
        ),
        cost_estimate=LINK_COST,
        name="project_attend",
    )(slopes, own, attn_rows, weight, vectors, labels[:, None, :])


def gelu_both(value):
    c, a = 0.7978845608028654, 0.044715
    square = value * value
    half = 0.5 + 0.5 * jnp.tanh(value * (c + (c * a) * square))
    active = value * half
    slope = half + (2.0 * active) * (1.0 - half) * (c + (3.0 * c * a) * square)
    return active, slope


def expand_kernel(
    n, own_ref, grad_hbm, up_ref, down_ref, vectors_ref, rows_hbm, act_hbm, pre_hbm, sum_ref,
    gathered, grads, backs, act, pre, load_sem, act_sem, pre_sem, rows_sem, *sems
):
    gather = Gather(n, own_ref, gathered, sems)
    rows, depth = own_ref.shape
    width = up_ref.shape[1]
    tile = tile_of(width)
    levels = [gather.level(count) for count in range(gather.bits + 1)]
    codes = [2 * mask + core for masks in levels for core in (0, 1) for mask in masks]

    def span(i):
        return pl.ds(pl.multiple_of(gather.away(codes, i) * rows, rows), rows)

    def load(i):
        return pltpu.make_async_copy(grad_hbm.at[span(i), :], grads.at[parity(i)], load_sem.at[parity(i)])

    def store(i):
        slot = parity(i)
        return (
            pltpu.make_async_copy(act.at[slot], act_hbm.at[span(i), :], act_sem.at[slot]),
            pltpu.make_async_copy(pre.at[slot], pre_hbm.at[span(i), :], pre_sem.at[slot]),
        )

    def keep_rows(i):
        return pltpu.make_async_copy(gathered.at[span(i), :], rows_hbm.at[span(i), :], rows_sem.at[i])

    def cols_of(j):
        return pl.ds(pl.multiple_of(j * tile, tile), tile)

    def back(i, carry):
        load(i).wait()

        @pl.when(i + 1 < n)
        def _():
            load(i + 1).start()

        def columns(j, carry):
            value = lax.dot_general(
                grads[parity(i)], down_ref[cols_of(j), :], NT, preferred_element_type=jnp.float32
            )
            backs[i, :, cols_of(j)] = value.astype(backs.dtype)
            return carry

        lax.fori_loop(0, width // tile, columns, 0)
        return carry

    def work(i, carry):
        first = 0
        for count, masks in enumerate(levels):
            if count:
                pl.when(i == first)(functools.partial(gather.forward, count))
            for k, mask in enumerate(masks):
                pl.when(i == first + len(masks) + k)(functools.partial(gather.wait_core, mask))
            first += 2 * len(masks)
        keep_rows(i).start()

        @pl.when(i >= 2)
        def _():
            for copy in store(i - 2):
                copy.wait()

        here, slot = span(i), parity(i)

        def columns(j, carry):
            cols = cols_of(j)
            before = jnp.dot(gathered[here, :], up_ref[:, cols], preferred_element_type=jnp.float32)
            before = before + vectors_ref[UP_BIAS, :, cols]
            active, slope = gelu_both(before)
            act[slot, :, cols] = active.astype(act.dtype)
            rounded = (backs[i, :, cols].astype(jnp.float32) * slope).astype(pre.dtype)
            pre[slot, :, cols] = rounded
            sum_ref[:, cols] += jnp.sum(rounded.astype(jnp.float32), axis=0, keepdims=True)
            return carry

        lax.fori_loop(0, width // tile, columns, 0)
        for copy in store(i):
            copy.start()
        return carry

    sum_ref[...] = jnp.zeros_like(sum_ref)
    load(0).start()
    gather.start()
    lax.fori_loop(0, n, back, 0)
    gather.keep().wait()
    lax.fori_loop(0, n, work, 0)
    for last in (n - 2, n - 1):
        for copy in store(last):
            copy.wait()
    for i in range(n):
        keep_rows(i).wait()
    gather.finish_sends()


def expand(own, grad_rows, up, down, vectors, n, collective_id):
    rows, depth = own.shape
    width = up.shape[1]
    total = n * rows
    vmem = pl.BlockSpec(memory_space=pltpu.VMEM)
    hbm = pl.BlockSpec(memory_space=pl.ANY)
    dma = pltpu.SemaphoreType.DMA
    return pl.pallas_call(
        functools.partial(expand_kernel, n),
        out_shape=(
            jax.ShapeDtypeStruct((total, depth), jnp.bfloat16),
            jax.ShapeDtypeStruct((total, width), jnp.bfloat16),
            jax.ShapeDtypeStruct((total, width), jnp.bfloat16),
            jax.ShapeDtypeStruct((1, width), jnp.float32),
        ),
        in_specs=[vmem, hbm, vmem, vmem, vmem],
        out_specs=(hbm, hbm, hbm, vmem),
        scratch_shapes=[
            pltpu.VMEM((total, depth), jnp.bfloat16),
            pltpu.VMEM((2, rows, depth), jnp.bfloat16),
            pltpu.VMEM((n, rows, width), jnp.bfloat16),
            pltpu.VMEM((2, rows, width), jnp.bfloat16),
            pltpu.VMEM((2, rows, width), jnp.bfloat16),
            dma((2,)),
            dma((2,)),
            dma((2,)),
            dma((n,)),
        ]
        + gather_sems(n),
        compiler_params=pltpu.CompilerParams(
            collective_id=collective_id, has_side_effects=True, vmem_limit_bytes=VMEM_LIMIT
        ),
        cost_estimate=LINK_COST,
        name="expand",
    )(own, grad_rows, up, down, vectors)


class Product:
    def __init__(self, left, right, out, scratch):
        self.left, self.right, self.out = left, right, out
        self.lbuf, self.rbuf, self.acc, self.obuf, self.left_sem, self.right_sem, self.out_sem = scratch
        self.depth, self.tall = self.lbuf.shape[1:]
        self.wide = self.rbuf.shape[2]
        self.inner = left.shape[0] // self.depth
        self.across = right.shape[1] // self.wide
        self.steps = (left.shape[1] // self.tall) * self.across * self.inner

    def load(self, i):
        k = lax.rem(i, self.inner)
        col = lax.rem(i // self.inner, self.across)
        row = i // (self.inner * self.across)
        rows = pl.ds(pl.multiple_of(k * self.depth, self.depth), self.depth)
        slot = lax.rem(i, 2)
        return (
            pltpu.make_async_copy(
                self.left.at[rows, pl.ds(pl.multiple_of(row * self.tall, self.tall), self.tall)],
                self.lbuf.at[slot],
                self.left_sem.at[slot],
            ),
            pltpu.make_async_copy(
                self.right.at[rows, pl.ds(pl.multiple_of(col * self.wide, self.wide), self.wide)],
                self.rbuf.at[slot],
                self.right_sem.at[slot],
            ),
        )

    def store(self, tile):
        col = lax.rem(tile, self.across)
        row = tile // self.across
        return pltpu.make_async_copy(
            self.obuf,
            self.out.at[
                pl.ds(pl.multiple_of(row * self.tall, self.tall), self.tall),
                pl.ds(pl.multiple_of(col * self.wide, self.wide), self.wide),
            ],
            self.out_sem,
        )

    def start(self):
        for copy in self.load(0):
            copy.start()

    def step(self, i, carry=0):
        for copy in self.load(i):
            copy.wait()

        @pl.when(i + 1 < self.steps)
        def _():
            for copy in self.load(i + 1):
                copy.start()

        k = lax.rem(i, self.inner)
        slot = lax.rem(i, 2)
        part = next(size for size in (512, 384, self.wide) if self.wide % size == 0)

        @pl.when(k == 0)
        def _():
            self.acc[...] = jnp.zeros_like(self.acc)

        for first in range(0, self.wide, part):
            cols = slice(first, first + part)
            self.acc[:, cols] += lax.dot_general(
                self.lbuf[slot], self.rbuf[slot, :, cols], TN, preferred_element_type=jnp.float32
            )

        @pl.when(k == self.inner - 1)
        def _():
            tile = i // self.inner

            @pl.when(tile > 0)
            def _():
                self.store(tile - 1).wait()

            self.obuf[...] = self.acc[...].astype(self.obuf.dtype)
            self.store(tile).start()

        return carry

    def batch(self, j, batches):
        per = -(-self.steps // batches)
        first = j * per
        lax.fori_loop(first, jnp.minimum(first + per, self.steps), self.step, 0)

    def finish(self):
        self.store(self.steps // self.inner - 1).wait()


def product_scratch(rows, tall, wide):
    dma = pltpu.SemaphoreType.DMA
    depth = min(1024, rows)
    tall, wide = min(512, tall), min(1024, wide)
    return [
        pltpu.VMEM((2, depth, tall), jnp.bfloat16),
        pltpu.VMEM((2, depth, wide), jnp.bfloat16),
        pltpu.VMEM((tall, wide), jnp.float32),
        pltpu.VMEM((tall, wide), jnp.bfloat16),
        dma((2,)),
        dma((2,)),
        dma(()),
    ]


def row_blocks(first, rows, each, work):
    def one(i, carry):
        work(pl.ds(pl.multiple_of(first + i * each, each), each))
        return carry

    lax.fori_loop(0, rows // each, one, 0)


def after_chunk(scatter, fetches, work):
    def after(j):
        @pl.when(j == 0)
        def _():
            for fetch in fetches:
                fetch.wait()

        row_blocks(j * scatter.chunk, scatter.chunk, 32, work)

    return after


def normal_rows(value):
    center = value - jnp.mean(value, axis=1, keepdims=True)
    factor = lax.rsqrt(jnp.mean(center * center, axis=1, keepdims=True) + 1e-05)
    return center * factor, factor


def dense_kernel(
    n, a_hbm, w_ref, input_hbm, vectors_ref, out_ref, next_ref, inputs, input_sem, *scratch
):
    fetch = pltpu.make_async_copy(input_hbm, inputs, input_sem)
    fetch.start()
    scatter = Scatter(n, False, a_hbm, w_ref, out_ref, scratch)

    def work(at):
        residual = inputs[at, :].astype(jnp.float32) + out_ref[at, :] + vectors_ref[DENSE_BIAS]
        out_ref[at, :] = residual
        normed, _ = normal_rows(residual)
        next_ref[at, :] = (normed * vectors_ref[SECOND_GAIN] + vectors_ref[SECOND_SHIFT]).astype(next_ref.dtype)

    scatter.run(after=after_chunk(scatter, (fetch,), work))


def back_rows(grad, source, gain):
    normed, factor = normal_rows(source)
    scaled = grad * gain
    product = grad * normed
    back = factor * (
        scaled
        - jnp.mean(scaled, axis=1, keepdims=True)
        - normed * jnp.mean(scaled * normed, axis=1, keepdims=True)
    )
    return back, product


def column_sum(value):
    return jnp.sum(value, axis=0, keepdims=True)


def expand_back_kernel(
    n, a_hbm, w_ref, act_hbm, rows_hbm, residual_hbm, cotangent_hbm, vectors_ref,
    out_ref, next_ref, sums_ref, grad_hbm, residual, cotangent, fetch_sem, *scratch
):
    fetches = (
        pltpu.make_async_copy(residual_hbm, residual, fetch_sem.at[0]),
        pltpu.make_async_copy(cotangent_hbm, cotangent, fetch_sem.at[1]),
    )
    for fetch in fetches:
        fetch.start()
    product = Product(act_hbm, rows_hbm, grad_hbm, scratch[:7])
    scatter = Scatter(n, True, a_hbm, w_ref, out_ref, scratch[7:])
    product.start()
    sums_ref[...] = jnp.zeros_like(sums_ref)

    def work(at):
        grad = out_ref[at, :]
        other = cotangent[at, :].astype(jnp.float32)
        back, terms = back_rows(grad, residual[at, :], vectors_ref[SECOND_GAIN])
        result = other + back
        out_ref[at, :] = result
        next_ref[at, :] = result.astype(next_ref.dtype)
        sums_ref[0:1, :] += column_sum(terms)
        sums_ref[1:2, :] += column_sum(grad)
        sums_ref[2:3, :] += column_sum(result)
        sums_ref[3:4, :] += column_sum(other)

    scatter.run(lambda j: product.batch(j, scatter.chunks), after_chunk(scatter, fetches, work))
    product.finish()


def comm_params(collective_id):
    return pltpu.CompilerParams(collective_id=collective_id, has_side_effects=True, vmem_limit_bytes=VMEM_LIMIT)


VMEM_SPEC = pl.BlockSpec(memory_space=pltpu.VMEM)
HBM_SPEC = pl.BlockSpec(memory_space=pl.ANY)
CHUNKS = 8


def dense(mixed, weight, inputs, vectors, n, collective_id):
    rows, width = inputs.shape
    return pl.pallas_call(
        functools.partial(dense_kernel, n),
        out_shape=(
            jax.ShapeDtypeStruct((rows, width), jnp.float32),
            jax.ShapeDtypeStruct((rows, width), jnp.bfloat16),
        ),
        in_specs=[HBM_SPEC, VMEM_SPEC, HBM_SPEC, VMEM_SPEC],
        out_specs=(VMEM_SPEC, VMEM_SPEC),
        scratch_shapes=[pltpu.VMEM((rows, width), inputs.dtype), pltpu.SemaphoreType.DMA(())]
        + scatter_scratch(n, rows, mixed.shape[1], width, CHUNKS),
        compiler_params=comm_params(collective_id),
        cost_estimate=LINK_COST,
        name="dense",
    )(mixed, weight, inputs, vectors)


def expand_back(grad_pre, up, activated, grad_rows, residual, cotangent, vectors, n, collective_id):
    rows, width = residual.shape
    units = activated.shape[1]
    return pl.pallas_call(
        functools.partial(expand_back_kernel, n),
        out_shape=(
            jax.ShapeDtypeStruct((rows, width), jnp.float32),
            jax.ShapeDtypeStruct((rows, width), jnp.bfloat16),
            jax.ShapeDtypeStruct((8, width), jnp.float32),
            jax.ShapeDtypeStruct((units, width), jnp.bfloat16),
        ),
        in_specs=[HBM_SPEC, VMEM_SPEC, HBM_SPEC, HBM_SPEC, HBM_SPEC, HBM_SPEC, VMEM_SPEC],
        out_specs=(VMEM_SPEC, VMEM_SPEC, VMEM_SPEC, HBM_SPEC),
        scratch_shapes=[
            pltpu.VMEM((rows, width), jnp.float32),
            pltpu.VMEM((rows, width), cotangent.dtype),
            pltpu.SemaphoreType.DMA((2,)),
        ]
        + product_scratch(n * rows, units, width)
        + scatter_scratch(n, rows, units, width, CHUNKS),
        compiler_params=comm_params(collective_id),
        cost_estimate=LINK_COST,
        name="expand_back",
    )(grad_pre, up, activated, grad_rows, residual, cotangent, vectors)


def attend_back_one(slope, proj_ref, grad_ref, start, head, row_ref, out_ref, dk_ref, dv_ref, sums_ref, length):
    at = pl.multiple_of(head * 3 * HEAD_DIM, HEAD_DIM)
    own = pl.ds(pl.multiple_of(head * HEAD_DIM, HEAD_DIM), HEAD_DIM)

    def cols(which):
        return pl.ds(at + which * HEAD_DIM, HEAD_DIM)

    def take(which, first, size):
        return proj_ref[pl.ds(start + first, size), cols(which)]

    sums = None
    for first in reversed(range(0, length, BLOCK)):
        last = first + BLOCK
        q, g = take(0, first, BLOCK), grad_ref[pl.ds(start + first, BLOCK), own]
        scores = masked_scores(slope, q, take(1, 0, last), as_column(row_ref[:, first:last]), row_ref[:, :last], first)
        top = jnp.max(scores, axis=1, keepdims=True)
        expo = jnp.exp2(scores - top)
        probs = expo * (1.0 / jnp.sum(expo, axis=1, keepdims=True))
        grad_probs = lax.dot_general(g, take(2, 0, last), NT, preferred_element_type=jnp.float32)
        product = probs * grad_probs
        grad_scores = (product - probs * jnp.sum(product, axis=1, keepdims=True)).astype(jnp.bfloat16)
        rounded = probs.astype(jnp.bfloat16)
        grad_queries = (jnp.dot(grad_scores, take(1, 0, last), preferred_element_type=jnp.float32) * SCALE).astype(
            out_ref.dtype
        )
        out_ref[pl.ds(start + first, BLOCK), cols(0)] = grad_queries
        here = column_sum(grad_queries.astype(jnp.float32))
        sums = here if sums is None else sums + here
        grad_keys = lax.dot_general(grad_scores, q, TN, preferred_element_type=jnp.float32)
        grad_values = lax.dot_general(rounded, g, TN, preferred_element_type=jnp.float32)
        if last == length:
            dk_ref[...] = grad_keys
            dv_ref[...] = grad_values
        else:
            dk_ref[:last, :] += grad_keys
            dv_ref[:last, :] += grad_values
    span = pl.ds(start, length)
    out_ref[span, cols(1)] = (dk_ref[...] * SCALE).astype(out_ref.dtype)
    grad_values = dv_ref[...].astype(out_ref.dtype)
    out_ref[span, cols(2)] = grad_values
    sums_ref[0:1, own] += sums
    sums_ref[1:2, own] += column_sum(grad_values.astype(jnp.float32))


def dense_back_kernel(
    n, length, slope_ref, own_ref, mixed_ref, w_ref, left_hbm, right_hbm, proj_hbm, row_ref,
    grad_proj_ref, sums_ref, grad_dense_ref, grad_up_hbm, gathered, acc, grad_mixed, proj, dk, dv, fetch_sem, *scratch
):
    fetch = pltpu.make_async_copy(proj_hbm, proj, fetch_sem)
    fetch.start()
    product = Product(left_hbm, right_hbm, grad_up_hbm, scratch[:7])
    gather = Gather(n, own_ref, gathered, scratch[7:])
    rows = own_ref.shape[0]
    heads = sums_ref.shape[1] // HEAD_DIM
    chips = max(1, length // (2 * rows))
    sequences = max(1, 2 * rows // length)

    def work(at):
        span = pl.ds(pl.multiple_of(at * rows, rows), rows)
        grad_mixed[span, :] = lax.dot_general(
            gathered[span, :], w_ref[...], NT, preferred_element_type=jnp.float32
        ).astype(grad_mixed.dtype)
        width = acc.shape[1]
        part = min(width, 512)
        for first in range(0, width, part):
            cols = slice(first, first + part)
            acc[:, cols] += lax.dot_general(
                mixed_ref[span, :], gathered[span, cols], TN, preferred_element_type=jnp.float32
            )

    order = [mask for count in range(gather.bits + 1) for mask in gather.level(count)]
    codes = [2 * mask + core for mask in order for core in (0, 1)]
    complete = [
        int(core == 1 and all(other // chips != mask // chips for other in order[k + 1 :]))
        for k, mask in enumerate(order)
        for core in (0, 1)
    ]

    def step(t, carry):
        for k, mask in enumerate(order):
            if k and mask.bit_count() > order[k - 1].bit_count():
                pl.when(t == 2 * k)(functools.partial(gather.forward, mask.bit_count()))
            pl.when(t == 2 * k + 1)(functools.partial(gather.wait_core, mask))
        at = gather.away(codes, t)
        work(at)

        @pl.when(look_up(complete, t) == 1)
        def _():
            first = (at // 2 // chips) * sequences

            def one(i, carry):
                s, head = first + i // heads, lax.rem(i, heads)
                attend_back_one(
                    slope_ref[head], proj, grad_mixed, pl.multiple_of(s * length, length), head, row_ref.at[s],
                    grad_proj_ref, dk, dv, sums_ref, length,
                )
                return carry

            lax.fori_loop(0, sequences * heads, one, 0)

        return carry

    product.start()
    gather.start()
    acc[...] = jnp.zeros_like(acc)
    sums_ref[...] = jnp.zeros_like(sums_ref)
    product.batch(0, 1)
    fetch.wait()
    gather.keep().wait()
    lax.fori_loop(0, 2 * len(order), step, 0)
    grad_dense_ref[...] = acc[...].astype(grad_dense_ref.dtype)
    product.finish()
    gather.finish_sends()


def dense_back(own, mixed, weight, mlp_rows, grad_pre, proj, slopes, labels, n, collective_id):
    rows, width = own.shape
    total, depth = mixed.shape
    length = labels.shape[1]
    return pl.pallas_call(
        functools.partial(dense_back_kernel, n, length),
        out_shape=(
            jax.ShapeDtypeStruct(proj.shape, jnp.bfloat16),
            jax.ShapeDtypeStruct((8, depth), jnp.float32),
            jax.ShapeDtypeStruct((depth, width), jnp.bfloat16),
            jax.ShapeDtypeStruct((mlp_rows.shape[1], grad_pre.shape[1]), jnp.bfloat16),
        ),
        in_specs=[pl.BlockSpec(memory_space=pltpu.SMEM), VMEM_SPEC, VMEM_SPEC, VMEM_SPEC]
        + [HBM_SPEC] * 3
        + [VMEM_SPEC],
        out_specs=(VMEM_SPEC, VMEM_SPEC, VMEM_SPEC, HBM_SPEC),
        scratch_shapes=[
            pltpu.VMEM((total, width), jnp.bfloat16),
            pltpu.VMEM((depth, width), jnp.float32),
            pltpu.VMEM((total, depth), jnp.bfloat16),
            pltpu.VMEM(proj.shape, jnp.bfloat16),
            pltpu.VMEM((length, HEAD_DIM), jnp.float32),
            pltpu.VMEM((length, HEAD_DIM), jnp.float32),
            pltpu.SemaphoreType.DMA(()),
        ]
        + product_scratch(total, mlp_rows.shape[1], grad_pre.shape[1])
        + gather_sems(n),
        compiler_params=comm_params(collective_id),
        cost_estimate=LINK_COST,
        name="dense_back",
    )(slopes, own, mixed, weight, mlp_rows, grad_pre, proj, labels[:, None, :])


def shrink_kernel(
    n, d, a_hbm, w_ref, residual_hbm, vectors_ref, early_ref, up_sum_ref, head_sums_ref,
    hidden_ref, sums_ref, biases_ref, out, residual, fetch_sem, *scratch
):
    fetch = pltpu.make_async_copy(residual_hbm, residual, fetch_sem)
    fetch.start()
    flat, biases = Total(n, d, scratch[:6]), Total(n, d, scratch[6:12])
    scatter = Scatter(n, False, a_hbm, w_ref, out, scratch[12:])
    heads_width = head_sums_ref.shape[1]

    def filler(j):
        for level in range(min(flat.levels + 1, scatter.chunks)):

            @pl.when(j == level)
            def _():
                if level == 0:
                    biases.lines[0] = jnp.zeros(biases.lines.shape[1:], jnp.float32)
                    biases.lines[0, 0:1, :] = up_sum_ref[...]
                    biases.lines[0, 1:3, :heads_width] = head_sums_ref[0:2, :]
                    biases.spread()
                    flat.pair[0] = early_ref[...]
                flat.step(level)

    def work(at):
        hidden_ref[at, :] = (residual[at, :] + out[at, :] + vectors_ref[DOWN_BIAS]).astype(hidden_ref.dtype)

    scatter.run(filler, after_chunk(scatter, (fetch,), work), d)
    for level in range(scatter.chunks, flat.levels + 1):
        flat.step(level)
    biases_ref[...] = biases.finish(False)
    sums_ref[...] = flat.finish()


def shrink(activated, down, residual, vectors, sums, up_sum, head_sums, n, d, collective_id):
    rows, width = residual.shape
    units = up_sum.shape[1]
    return pl.pallas_call(
        functools.partial(shrink_kernel, n, d),
        out_shape=(
            jax.ShapeDtypeStruct((rows, width), jnp.bfloat16),
            jax.ShapeDtypeStruct((8, width), jnp.float32),
            jax.ShapeDtypeStruct((8, units), jnp.float32),
        ),
        in_specs=[HBM_SPEC, VMEM_SPEC, HBM_SPEC] + [VMEM_SPEC] * 4,
        out_specs=(VMEM_SPEC, VMEM_SPEC, VMEM_SPEC),
        scratch_shapes=[
            pltpu.VMEM((rows, width), jnp.float32),
            pltpu.VMEM((rows, width), jnp.float32),
            pltpu.SemaphoreType.DMA(()),
        ]
        + total_scratch(n, d, 8, width)
        + total_scratch(n, d, 8, units)
        + scatter_scratch(n, rows, activated.shape[1], width, CHUNKS),
        compiler_params=comm_params(collective_id),
        cost_estimate=LINK_COST,
        name="shrink",
    )(activated, down, residual, vectors, sums, up_sum, head_sums)


def project_back_kernel(
    n, a_hbm, w_ref, input_hbm, grad_hbm, vectors_ref, early_ref, left_hbm,
    out_ref, sums_ref, weight_hbm, inputs, grads, fetch_sem, *scratch
):
    fetches = (
        pltpu.make_async_copy(input_hbm, inputs, fetch_sem.at[0]),
        pltpu.make_async_copy(grad_hbm, grads, fetch_sem.at[1]),
    )
    for fetch in fetches:
        fetch.start()
    product = Product(left_hbm, a_hbm, weight_hbm, scratch[:7])
    scatter = Scatter(n, True, a_hbm, w_ref, out_ref, scratch[7:])
    product.start()
    sums_ref[...] = early_ref[...]

    def work(at):
        grad = out_ref[at, :]
        back, terms = back_rows(grad, inputs[at, :].astype(jnp.float32), vectors_ref[FIRST_GAIN])
        out_ref[at, :] = grads[at, :] + back
        sums_ref[4:5, :] += column_sum(terms)
        sums_ref[5:6, :] += column_sum(grad)

    scatter.run(lambda j: product.batch(j, scatter.chunks), after_chunk(scatter, fetches, work))
    product.finish()


def project_back(grad_proj, weight, inputs, grad_residual, vectors, early, attn_rows, n, collective_id):
    rows, width = inputs.shape
    columns = grad_proj.shape[1]
    return pl.pallas_call(
        functools.partial(project_back_kernel, n),
        out_shape=(
            jax.ShapeDtypeStruct((rows, width), jnp.float32),
            jax.ShapeDtypeStruct((8, width), jnp.float32),
            jax.ShapeDtypeStruct((width, columns), jnp.bfloat16),
        ),
        in_specs=[HBM_SPEC, VMEM_SPEC, HBM_SPEC, HBM_SPEC, VMEM_SPEC, VMEM_SPEC, HBM_SPEC],
        out_specs=(VMEM_SPEC, VMEM_SPEC, HBM_SPEC),
        scratch_shapes=[
            pltpu.VMEM((rows, width), inputs.dtype),
            pltpu.VMEM((rows, width), jnp.float32),
            pltpu.SemaphoreType.DMA((2,)),
        ]
        + product_scratch(n * rows, width, columns)
        + scatter_scratch(n, rows, columns, width, CHUNKS),
        compiler_params=comm_params(collective_id),
        cost_estimate=LINK_COST,
        name="project_back",
    )(grad_proj, weight, inputs, grad_residual, vectors, early, attn_rows)


def share(grad, dimension):
    return lax.psum_scatter(grad, "dp", scatter_dimension=dimension, tiled=True)


def finish_kernel(heads_width, *refs):
    ins, outs = refs[:8], refs[8:]
    for source, target in zip(ins[:6], outs[:6]):
        target[...] = source[...].astype(target.dtype)

    @pl.when(pl.program_id(0) == 0)
    def _():
        sums, biases = ins[6:]
        for i in range(6):
            outs[6 + i][...] = sums[i : i + 1, :]
        outs[12][...] = biases[0:1, :]
        outs[13][...] = biases[1:2, :heads_width]
        outs[14][...] = biases[2:3, :heads_width]


def finish(hidden_output, grad_input, weights, sums, biases, heads_width):
    steps = 2

    def rows_block(x):
        return pl.BlockSpec((x.shape[0] // steps, x.shape[1]), lambda i: (i, 0))

    def whole_block(shape):
        return pl.BlockSpec(shape, lambda i: (0, 0))

    large = (hidden_output, grad_input) + weights
    small = [(1, sums.shape[1])] * 6 + [(1, biases.shape[1]), (1, heads_width), (1, heads_width)]
    results = pl.pallas_call(
        functools.partial(finish_kernel, heads_width),
        grid=(steps,),
        out_shape=[jax.ShapeDtypeStruct(hidden_output.shape, hidden_output.dtype)]
        + [jax.ShapeDtypeStruct(x.shape, jnp.float32) for x in large[1:]]
        + [jax.ShapeDtypeStruct(shape, jnp.float32) for shape in small],
        in_specs=[rows_block(x) for x in large] + [whole_block(sums.shape), whole_block(biases.shape)],
        out_specs=[rows_block(x) for x in large] + [whole_block(shape) for shape in small],
        name="finish",
    )(*large, sums, biases)
    return results[:6], [x.reshape(-1) for x in results[6:]]


def on_device(
    hidden_input,
    first_gain,
    first_shift,
    qkv_weight,
    query_bias,
    value_bias,
    dense_weight,
    dense_bias,
    second_gain,
    second_shift,
    up_weight,
    up_bias,
    down_weight,
    down_bias,
    segments,
    document_lengths,
    cotangent,
    *,
    n,
    d,
):
    heads_local = query_bias.shape[0] // HEAD_DIM
    attn_rows, vectors = gather_rows(
        hidden_input,
        (
            first_gain,
            first_shift,
            dense_bias,
            second_gain,
            second_shift,
            down_bias,
            up_bias,
            query_bias,
            value_bias,
        ),
        n,
        1,
    )
    project_full, dense_full, expand_full, shrink_full = (
        lax.all_gather(qkv_weight, "dp", axis=0, tiled=True),
        lax.all_gather(dense_weight, "dp", axis=1, tiled=True),
        lax.all_gather(up_weight, "dp", axis=0, tiled=True),
        lax.all_gather(down_weight, "dp", axis=1, tiled=True),
    )
    group_rows = attn_rows.shape[0]
    sequences = document_lengths.shape[0]
    length = group_rows // sequences
    heads_index = lax.axis_index("tensor") * heads_local + lax.broadcasted_iota(
        jnp.int32, (heads_local,), 0
    )
    slopes = jnp.exp2(-8.0 * (heads_index.astype(jnp.float32) + 1.0) / HEADS) * LOG2E
    position = lax.broadcasted_iota(jnp.int32, (sequences, length), 1)
    filled = jnp.sum(document_lengths, axis=1, keepdims=True)
    labels = jnp.where(position < filled, segments.reshape(sequences, length), length + position).astype(jnp.float32)
    grad_rows, proj, mixed = project_attend(
        attn_rows, project_full, vectors, slopes, labels, cotangent, n, 6
    )
    residual, mlp_input = dense(
        mixed, dense_full, hidden_input, vectors, n, 2
    )
    mlp_rows, activated, grad_pre, sum_up_bias = expand(
        mlp_input, grad_rows, expand_full, shrink_full, vectors, n, 7
    )
    grad_residual, grad_attn_out, early_sums, grad_down = expand_back(
        grad_pre, expand_full, activated, grad_rows, residual, cotangent, vectors, n, 4
    )
    grad_down_weight = share(grad_down, 1)
    grad_proj, head_sums, grad_dense, grad_up = dense_back(
        grad_attn_out, mixed, dense_full, mlp_rows, grad_pre, proj, slopes, labels, n, 9
    )
    grad_down_weight, grad_proj = lax.optimization_barrier((grad_down_weight, grad_proj))
    grad_up_weight = share(grad_up, 0)
    grad_dense_weight = share(grad_dense, 1)
    grad_input, sums, grad_project = project_back(
        grad_proj, project_full, hidden_input, grad_residual, vectors, early_sums, attn_rows, n, 5
    )
    grad_qkv_weight = share(grad_project, 0)
    hidden_output, sums, biases = shrink(
        activated, shrink_full, residual, vectors, sums, sum_up_bias, head_sums, n, d, 3
    )
    heads_width = heads_local * HEAD_DIM
    large, small = finish(
        hidden_output,
        grad_input,
        (grad_qkv_weight, grad_dense_weight, grad_up_weight, grad_down_weight),
        sums,
        biases,
        heads_width,
    )
    hidden_output, grad_input, grad_qkv_weight, grad_dense_weight, grad_up_weight, grad_down_weight = large
    grad_second_gain, grad_second_shift, grad_dense_bias, grad_down_bias, grad_first_gain, grad_first_shift = small[:6]
    grad_up_bias, grad_query_bias, grad_value_bias = small[6:]
    return (
        hidden_output,
        grad_input,
        grad_first_gain,
        grad_first_shift,
        grad_qkv_weight,
        grad_query_bias,
        grad_value_bias,
        grad_dense_weight,
        grad_dense_bias,
        grad_second_gain,
        grad_second_shift,
        grad_up_weight,
        grad_up_bias,
        grad_down_weight,
        grad_down_bias,
    )


def solution(mesh):
    return jax.shard_map(
        functools.partial(on_device, n=mesh.shape["tensor"], d=mesh.shape["dp"]),
        mesh=mesh,
        in_specs=(
            P(("dp", "tensor"), None),
            P(),
            P(),
            P("dp", "tensor"),
            P("tensor"),
            P("tensor"),
            P("tensor", "dp"),
            P(),
            P(),
            P(),
            P("dp", "tensor"),
            P("tensor"),
            P("tensor", "dp"),
            P(),
            P("dp"),
            P("dp", None),
            P(("dp", "tensor"), None),
        ),
        out_specs=(
            P(("dp", "tensor"), None),
            P(("dp", "tensor"), None),
            P(),
            P(),
            P("dp", "tensor"),
            P("tensor"),
            P("tensor"),
            P("tensor", "dp"),
            P(),
            P(),
            P(),
            P("dp", "tensor"),
            P("tensor"),
            P("tensor", "dp"),
            P(),
        ),
        check_vma=False,
    )
```

```python
import functools
import math

import jax
import jax.numpy as jnp
from jax import lax
from jax.experimental import pallas as pl
from jax.experimental.pallas import tpu as pltpu
from jax.sharding import PartitionSpec as P

VMEM_LIMIT = 62 << 20
LINK_COST = pl.CostEstimate(flops=0, bytes_accessed=280_000_000, transcendentals=0)


def flip(index, bit):
    return index + (1 - 2 * ((index // 2**bit) % 2)) * 2**bit


def look_up(table, i):
    if isinstance(i, int):
        return table[i]
    value = table[0]
    for k in range(1, len(table)):
        value = value + (i >= k).astype(jnp.int32) * (table[k] - table[k - 1])
    return value


def parity(i):
    return i % 2 if isinstance(i, int) else lax.rem(i, 2)


def chip_bits(n):
    return n.bit_length() - 2


def column_parts(width, count):
    blocks = width // 128
    edges = [128 * (blocks * i // count) for i in range(count + 1)]
    return [(a, b - a) for a, b in zip(edges[:-1], edges[1:])]


def peer(index):
    return {"tensor": index}


def greet(me, bits, d=1, meanwhile=None):
    barrier = pltpu.get_barrier_semaphore()
    for bit in range(bits + 1):
        pl.semaphore_signal(
            barrier, inc=1, device_id=peer(flip(me, bit)), device_id_type=pl.DeviceIdType.MESH
        )
    for ahead in range(1, d):
        pl.semaphore_signal(
            barrier, inc=1, device_id=ahead_on_dp(ahead, d), device_id_type=pl.DeviceIdType.MESH
        )
    if meanwhile is not None:
        meanwhile()
    pl.semaphore_wait(barrier, bits + d)


def ahead_on_dp(ahead, d):
    return {"dp": lax.rem(lax.axis_index("dp") + ahead, d)}


def remote(src, dst, send_sem, recv_sem, target):
    return pltpu.make_async_remote_copy(
        src_ref=src,
        dst_ref=dst,
        send_sem=send_sem,
        recv_sem=recv_sem,
        device_id=peer(target),
        device_id_type=pl.DeviceIdType.MESH,
    )


class Gather:
    def __init__(self, n, own_ref, out_ref, sems):
        self.me = lax.axis_index("tensor")
        self.bits = chip_bits(n)
        self.rows, width = own_ref.shape
        self.parts = column_parts(width, self.bits)
        self.own, self.out = own_ref, out_ref
        self.own_sem, self.chip_send, self.chip_recv, self.core_send, self.core_recv = sems

    def slot(self, part, index):
        at = self.me
        for step in range(self.bits):
            if (index >> step) & 1:
                at = flip(at, 1 + (part + step) % self.bits)
        return at

    def place(self, mask, core):
        at = flip(self.me, 0) if core else self.me
        for bit in range(self.bits):
            if (mask >> bit) & 1:
                at = flip(at, 1 + bit)
        return at

    def away(self, codes, t):
        code, at = look_up(codes, t), self.me
        for bit in range(self.bits + 1):
            at = at + (code // 2**bit) % 2 * (1 - 2 * ((self.me // 2**bit) % 2)) * 2**bit
        return at

    def index_of(self, part, mask):
        return sum(2 ** ((bit - part) % self.bits) for bit in range(self.bits) if (mask >> bit) & 1)

    def level(self, count):
        return [index for index in range(2**self.bits) if index.bit_count() == count]

    def block(self, part, index, core=0):
        start, size = self.parts[part]
        at = flip(self.slot(part, index), 0) if core else self.slot(part, index)
        return self.out.at[pl.ds(pl.multiple_of(at * self.rows, self.rows), self.rows), pl.ds(start, size)]

    def source(self, part, index):
        start, size = self.parts[part]
        return self.own.at[:, pl.ds(start, size)] if index == 0 else self.block(part, index)

    def chip_copy(self, part, index, step):
        arrives = index + 2**step
        return remote(
            self.source(part, index),
            self.block(part, index),
            self.chip_send.at[part, arrives],
            self.chip_recv.at[part, arrives],
            flip(self.me, 1 + (part + step) % self.bits),
        )

    def core_copy(self, part, index):
        return remote(
            self.source(part, index),
            self.block(part, index),
            self.core_send.at[part, index],
            self.core_recv.at[part, index],
            flip(self.me, 0),
        )

    def keep(self):
        rows = pl.ds(pl.multiple_of(self.me * self.rows, self.rows), self.rows)
        return pltpu.make_async_copy(self.own, self.out.at[rows, :], self.own_sem)

    def start(self, meanwhile=None, d=1):
        greet(self.me, self.bits, d, meanwhile)
        for step in range(self.bits):
            for part in range(self.bits):
                self.chip_copy(part, 0, step).start()
        for part in range(self.bits):
            self.core_copy(part, 0).start()
        self.keep().start()

    def forward(self, count):
        for index in self.level(count):
            for part in range(self.bits):
                arrived = self.block(part, index)
                remote(
                    arrived, arrived, self.chip_send.at[part, index], self.chip_recv.at[part, index], flip(self.me, 0)
                ).wait_recv()
                for step in range(index.bit_length(), self.bits):
                    self.chip_copy(part, index, step).start()
                self.core_copy(part, index).start()

    def wait_core(self, mask):
        for part in range(self.bits):
            index = self.index_of(part, mask)
            arrived = self.block(part, index, 1)
            remote(
                arrived, arrived, self.core_send.at[part, index], self.core_recv.at[part, index], flip(self.me, 0)
            ).wait_recv()

    def finish_sends(self):
        for part in range(self.bits):
            for index in range(2**self.bits):
                for step in range(index.bit_length(), self.bits):
                    self.chip_copy(part, index, step).wait_send()
                self.core_copy(part, index).wait_send()


class Spread:
    def __init__(self, d, shard, full, sems):
        self.d, self.shard, self.full = d, shard, full
        self.own_sem, self.send_sem, self.recv_sem = sems
        self.z = lax.axis_index("dp")

    def columns(self, z):
        width = self.shard.shape[1]
        return self.full.at[:, pl.ds(pl.multiple_of(z * width, width), width)]

    def copy(self, ahead):
        return pltpu.make_async_remote_copy(
            src_ref=self.shard,
            dst_ref=self.columns(self.z),
            send_sem=self.send_sem.at[ahead],
            recv_sem=self.recv_sem.at[ahead],
            device_id=ahead_on_dp(ahead, self.d),
            device_id_type=pl.DeviceIdType.MESH,
        )

    def keep(self):
        return pltpu.make_async_copy(self.shard, self.columns(self.z), self.own_sem)

    def start(self):
        for ahead in range(1, self.d):
            self.copy(ahead).start()
        self.keep().start()

    def finish(self):
        for ahead in range(1, self.d):
            arrived = self.columns(lax.rem(self.z + self.d - ahead, self.d))
            pltpu.make_async_remote_copy(
                src_ref=self.shard,
                dst_ref=arrived,
                send_sem=self.send_sem.at[ahead],
                recv_sem=self.recv_sem.at[ahead],
                device_id=ahead_on_dp(ahead, self.d),
                device_id_type=pl.DeviceIdType.MESH,
            ).wait_recv()
            self.copy(ahead).wait_send()
        self.keep().wait()


def gather_kernel(n, d, x_ref, *refs):
    flat_refs, (shard_ref, out_ref, vectors_ref, full_ref, own, *sems) = refs[:9], refs[9:]
    spread = Spread(d, shard_ref, full_ref, sems[:3])
    sems = sems[3:]

    def put(row, start, ref):
        size = ref.shape[0]
        vectors_ref[row, :, start : start + size] = ref[...].astype(jnp.float32).reshape(1, size)

    put(FIRST_GAIN, 0, flat_refs[FIRST_GAIN])
    put(FIRST_SHIFT, 0, flat_refs[FIRST_SHIFT])

    def work(at):
        normed, _ = normal_rows(x_ref[at, :].astype(jnp.float32))
        own[at, :] = (normed * vectors_ref[FIRST_GAIN] + vectors_ref[FIRST_SHIFT]).astype(own.dtype)

    gather = Gather(n, own, out_ref, sems)
    gather.start(lambda: row_blocks(0, own.shape[0], 32, work), d)
    spread.start()
    for row in range(FIRST_SHIFT + 1, UP_BIAS):
        put(row, 0, flat_refs[row])
    vectors_ref[UP_BIAS] = jnp.zeros(vectors_ref.shape[1:], jnp.float32)
    vectors_ref[HEAD_BIASES] = jnp.zeros(vectors_ref.shape[1:], jnp.float32)
    put(UP_BIAS, 0, flat_refs[UP_BIAS])
    put(HEAD_BIASES, 0, flat_refs[7])
    put(HEAD_BIASES, flat_refs[7].shape[0], flat_refs[8])
    for count in range(1, gather.bits + 1):
        gather.forward(count)
    for mask in range(2**gather.bits):
        gather.wait_core(mask)
    gather.finish_sends()
    spread.finish()
    gather.keep().wait()


def gather_sems(n):
    bits = chip_bits(n)
    dma = pltpu.SemaphoreType.DMA
    return [dma(())] + [dma((bits, 2**bits))] * 4


def gather_rows(x, vectors, shard, n, d, collective_id):
    rows, width = x.shape
    return pl.pallas_call(
        functools.partial(gather_kernel, n, d),
        out_shape=(
            jax.ShapeDtypeStruct((n * rows, width), x.dtype),
            jax.ShapeDtypeStruct((8, 1, width), jnp.float32),
            jax.ShapeDtypeStruct((shard.shape[0], d * shard.shape[1]), shard.dtype),
        ),
        in_specs=[VMEM_SPEC] * 11,
        out_specs=(HBM_SPEC, VMEM_SPEC, HBM_SPEC),
        scratch_shapes=[
            pltpu.VMEM((rows, width), x.dtype),
            pltpu.SemaphoreType.DMA(()),
            pltpu.SemaphoreType.DMA((d,)),
            pltpu.SemaphoreType.DMA((d,)),
        ]
        + gather_sems(n),
        compiler_params=pltpu.CompilerParams(
            collective_id=collective_id, has_side_effects=True, vmem_limit_bytes=VMEM_LIMIT
        ),
        cost_estimate=LINK_COST,
        name="gather_rows",
    )(x, *vectors, shard)


class Scatter:
    def __init__(self, n, transposed, a_hbm, w_ref, out_ref, scratch):
        (self.csend, self.crecv, self.recv, self.other, self.mine, self.load_sem) = scratch[:6]
        self.core_send, self.core_recv, self.chip_send, self.chip_recv = scratch[6:]
        self.me = lax.axis_index("tensor")
        self.bits = chip_bits(n)
        self.total = 2**self.bits
        self.transposed = transposed
        self.a, self.w, self.out = a_hbm, w_ref, out_ref
        self.rows, width = out_ref.shape
        self.chunk = self.csend.shape[2]
        self.chunks = self.rows // self.chunk
        self.parts = column_parts(width, self.bits)

    def index_of(self, part, mask):
        top = self.bits - 1
        return sum(2 ** (top - (bit - part) % self.bits) for bit in range(self.bits) if (mask >> bit) & 1)

    def place(self, mask, core):
        at = flip(self.me, 0) if core else self.me
        for bit in range(self.bits):
            if (mask >> bit) & 1:
                at = flip(at, 1 + bit)
        return at

    def rows_of(self, j):
        return pl.ds(pl.multiple_of(j * self.chunk, self.chunk), self.chunk)

    def loads(self, j, core):
        into = self.other if core else self.mine
        copies = []
        for mask in range(self.total):
            start = pl.multiple_of(self.place(mask, core) * self.rows + j * self.chunk, self.chunk)
            copies.append(
                pltpu.make_async_copy(
                    self.a.at[pl.ds(start, self.chunk), :],
                    into.at[lax.rem(j, 2), pl.ds(mask * self.chunk, self.chunk), :],
                    self.load_sem.at[core, lax.rem(j, 2), mask],
                )
            )
        return copies

    def core_copy(self, j, part):
        start, size = self.parts[part]
        return remote(
            self.csend.at[lax.rem(j, 2), :, :, pl.ds(start, size)],
            self.crecv.at[:, self.rows_of(j), pl.ds(start, size)],
            self.core_send.at[part, j],
            self.core_recv.at[part, j],
            flip(self.me, 0),
        )

    def chip_copy(self, j, part, step):
        half = self.total >> (step + 1)
        first = sum(self.total >> (s + 1) for s in range(step))
        start, size = self.parts[part]
        return remote(
            self.crecv.at[pl.ds(half, half), self.rows_of(j), pl.ds(start, size)],
            self.recv.at[pl.ds(first, half), self.rows_of(j), pl.ds(start, size)],
            self.chip_send.at[part, step, j],
            self.chip_recv.at[part, step, j],
            flip(self.me, 1 + (part + step) % self.bits),
        )

    def tiles(self, part, lhs, put):
        start, size = self.parts[part]
        tile = 256 if size % 256 == 0 and start % 256 == 0 else 128

        def one(i, carry):
            cols = pl.ds(pl.multiple_of(start + i * tile, tile), tile)
            if self.transposed:
                value = lax.dot_general(
                    lhs[...], self.w[cols, :], (((1,), (1,)), ((), ())), preferred_element_type=jnp.float32
                )
            else:
                value = jnp.dot(lhs[...], self.w[:, cols], preferred_element_type=jnp.float32)
            put(cols, value)
            return carry

        lax.fori_loop(0, size // tile, one, 0)

    def piece(self, value, mask):
        return value[mask * self.chunk : (mask + 1) * self.chunk, :]

    def stage_core(self, j):
        for copy in self.loads(j, 1):
            copy.wait()

        @pl.when(j >= 2)
        def _():
            for part in range(self.bits):
                self.core_copy(j - 2, part).wait_send()

        for part in range(self.bits):

            def put(cols, value):
                for mask in range(self.total):
                    self.csend[lax.rem(j, 2), self.index_of(part, mask), :, cols] = self.piece(value, mask).astype(
                        self.csend.dtype
                    )

            self.tiles(part, self.other.at[lax.rem(j, 2)], put)
            self.core_copy(j, part).start()

    def stage_first(self, j):
        for copy in self.loads(j, 0):
            copy.wait()
        for part in range(self.bits):
            self.core_copy(j, part).wait_recv()

            def put(cols, value):
                for mask in range(self.total):
                    index = self.index_of(part, mask)
                    got = self.piece(value, mask) + self.crecv[index, self.rows_of(j), cols].astype(jnp.float32)
                    if index:
                        self.crecv[index, self.rows_of(j), cols] = got.astype(self.crecv.dtype)
                    else:
                        self.out[self.rows_of(j), cols] = got

            self.tiles(part, self.mine.at[lax.rem(j, 2)], put)
            self.chip_copy(j, part, 0).start()

    def stage_next(self, j, step):
        half = self.total >> (step + 1)
        first = sum(self.total >> (s + 1) for s in range(step))
        for part in range(self.bits):
            start, size = self.parts[part]
            cols = slice(start, start + size)
            self.chip_copy(j, part, step).wait_recv()
            for index in reversed(range(half)):
                got = self.recv[first + index, self.rows_of(j), cols].astype(jnp.float32)
                if index:
                    value = self.crecv[index, self.rows_of(j), cols].astype(jnp.float32) + got
                    self.crecv[index, self.rows_of(j), cols] = value.astype(self.crecv.dtype)
                else:
                    self.out[self.rows_of(j), cols] += got
            if step + 1 < self.bits:
                self.chip_copy(j, part, step + 1).start()

    def run(self, filler=None, after=None, d=1):
        for copy in self.loads(0, 1):
            copy.start()
        greet(self.me, self.bits, d)

        def body(u, carry):
            @pl.when(u + 1 < self.chunks)
            def _():
                for copy in self.loads(u + 1, 1):
                    copy.start()

            @pl.when(u < self.chunks)
            def _():
                for copy in self.loads(u, 0):
                    copy.start()
                self.stage_core(u)

            @pl.when((u >= 1) & (u <= self.chunks))
            def _():
                self.stage_first(u - 1)

            for step in range(self.bits):

                @pl.when((u >= 2 + step) & (u < self.chunks + 2 + step))
                def _():
                    self.stage_next(u - 2 - step, step)

            if filler is not None:

                @pl.when((u >= 1) & (u <= self.chunks))
                def _():
                    filler(u - 1)

            if after is not None:
                done = u - self.bits - 1

                @pl.when(done >= 0)
                def _():
                    after(done)

            return carry

        lax.fori_loop(0, self.chunks + self.bits + 1, body, 0)
        for part in range(self.bits):
            for j in range(self.chunks):
                if j >= self.chunks - 2:
                    self.core_copy(j, part).wait_send()
                for step in range(self.bits):
                    self.chip_copy(j, part, step).wait_send()


def scatter_scratch(n, rows, depth, width, chunks):
    bits = chip_bits(n)
    total = 2**bits
    chunk = rows // chunks
    dma = pltpu.SemaphoreType.DMA
    return [
        pltpu.VMEM((2, total, chunk, width), jnp.bfloat16),
        pltpu.VMEM((total, rows, width), jnp.bfloat16),
        pltpu.VMEM((total - 1, rows, width), jnp.bfloat16),
        pltpu.VMEM((2, total * chunk, depth), jnp.bfloat16),
        pltpu.VMEM((2, total * chunk, depth), jnp.bfloat16),
        dma((2, 2, total)),
        dma((bits, chunks)),
        dma((bits, chunks)),
        dma((bits, bits, chunks)),
        dma((bits, bits, chunks)),
    ]


HEAD_DIM = 128
HEADS = 16
FIRST_GAIN, FIRST_SHIFT, DENSE_BIAS, SECOND_GAIN, SECOND_SHIFT, DOWN_BIAS, UP_BIAS, HEAD_BIASES = range(8)
LOG2E = 1.4426950408889634
SCALE = 1.0 / math.sqrt(HEAD_DIM)
BLOCK = 256
NT = (((1,), (1,)), ((), ()))
TN = (((0,), (0,)), ((), ()))


def as_column(row):
    width = row.shape[1]
    here = lax.broadcasted_iota(jnp.int32, (width, width), 0) == lax.broadcasted_iota(jnp.int32, (width, width), 1)
    return jnp.sum(jnp.where(here, row, 0.0), axis=1, keepdims=True)


def masked_scores(slope, q, keys, query_labels, key_labels, first):
    raw = lax.dot_general(q, keys, NT, preferred_element_type=jnp.float32)
    rows, width = raw.shape
    column = lax.broadcasted_iota(jnp.int32, (1, width), 1)
    bias = column.astype(jnp.float32) * slope
    same = query_labels == key_labels
    causal = lax.broadcasted_iota(jnp.int32, (rows, width), 1) <= first + lax.broadcasted_iota(
        jnp.int32, (rows, width), 0
    )
    return jnp.where(same & causal, raw * (SCALE * LOG2E) + bias, -1e30)


class Total:
    def __init__(self, n, d, scratch):
        self.pair, self.lines, self.send, self.recv, self.line_send, self.line_recv = scratch
        self.me, self.d = lax.axis_index("tensor"), d
        self.levels = n.bit_length() - 1

    def level_copy(self, level):
        return remote(
            self.pair.at[2 * level],
            self.pair.at[2 * level + 1],
            self.send.at[level],
            self.recv.at[level],
            flip(self.me, level),
        )

    def line_copy(self, ahead):
        return pltpu.make_async_remote_copy(
            src_ref=self.lines.at[0],
            dst_ref=self.lines.at[ahead],
            send_sem=self.line_send.at[ahead],
            recv_sem=self.line_recv.at[ahead],
            device_id=ahead_on_dp(ahead, self.d),
            device_id_type=pl.DeviceIdType.MESH,
        )

    def spread(self):
        for ahead in range(1, self.d):
            self.line_copy(ahead).start()

    def step(self, level):
        if level:
            self.level_copy(level - 1).wait_recv()
            self.pair[2 * level] = self.pair[2 * level - 2] + self.pair[2 * level - 1]
        if level < self.levels:
            self.level_copy(level).start()
        else:
            self.lines[0] = self.pair[2 * level]
            self.spread()

    def finish(self, levels=True):
        for ahead in range(1, self.d):
            self.line_copy(ahead).wait_recv()
        z = lax.axis_index("dp")
        total = None
        for index in range(self.d):
            value = self.lines[lax.rem(z - index + self.d, self.d)]
            total = value if total is None else total + value
        for ahead in range(1, self.d):
            self.line_copy(ahead).wait_send()
        if levels:
            for level in range(self.levels):
                self.level_copy(level).wait_send()
        return total


def total_scratch(n, d, rows, width):
    levels = n.bit_length() - 1
    dma = pltpu.SemaphoreType.DMA
    return [
        pltpu.VMEM((2 * levels + 1, rows, width), jnp.float32),
        pltpu.VMEM((d, rows, width), jnp.float32),
        dma((levels,)),
        dma((levels,)),
        dma((d,)),
        dma((d,)),
    ]


def tile_of(width):
    return 256 if width % 256 == 0 else width


def attend_one(slope, proj_ref, start, head, row_ref, out_ref, length):
    at = pl.multiple_of(head * 3 * HEAD_DIM, HEAD_DIM)

    def take(which, first, size):
        return proj_ref[pl.ds(start + first, size), pl.ds(at + which * HEAD_DIM, HEAD_DIM)]

    for first in range(0, length, BLOCK):
        last = first + BLOCK
        scores = masked_scores(
            slope, take(0, first, BLOCK), take(1, 0, last), as_column(row_ref[:, first:last]), row_ref[:, :last], first
        )
        top = jnp.max(scores, axis=1, keepdims=True)
        expo = jnp.exp2(scores - top)
        total = jnp.sum(expo, axis=1, keepdims=True)
        mixed = jnp.dot(expo.astype(jnp.bfloat16), take(2, 0, last), preferred_element_type=jnp.float32)
        out_ref[pl.ds(start + first, BLOCK), pl.ds(pl.multiple_of(head * HEAD_DIM, HEAD_DIM), HEAD_DIM)] = (
            mixed / total
        ).astype(out_ref.dtype)


def project_kernel(
    n, length, slope_ref, own_ref, rows_hbm, w_ref, vectors_ref, row_ref, gathered, proj_hbm, mixed_ref,
    proj, buf, bias, load_sem, store_sem, *sems
):
    gather = Gather(n, own_ref, gathered, sems)
    rows = own_ref.shape[0]
    width = w_ref.shape[1]
    tile = tile_of(width)
    heads = width // (3 * HEAD_DIM)
    sequences = n * rows // length

    def load(i):
        at = pl.ds(pl.multiple_of(i * rows, rows), rows)
        return pltpu.make_async_copy(rows_hbm.at[at, :], buf.at[lax.rem(i, 2)], load_sem.at[lax.rem(i, 2)])

    load(0).start()
    bias[...] = jnp.zeros_like(bias)
    for head in range(heads):
        for which, first in ((0, 0), (2, heads * HEAD_DIM)):
            at = (3 * head + which) * HEAD_DIM
            bias[:, at : at + HEAD_DIM] = vectors_ref[HEAD_BIASES, :, first + head * HEAD_DIM : first + (head + 1) * HEAD_DIM]
    gather.start()

    def store(i):
        at = pl.ds(pl.multiple_of(i * rows, rows), rows)
        return pltpu.make_async_copy(proj.at[at, :], proj_hbm.at[at, :], store_sem.at[i])

    def project(i, carry):
        load(i).wait()

        @pl.when(i + 1 < n)
        def _():
            load(i + 1).start()

        at = pl.ds(pl.multiple_of(i * rows, rows), rows)
        for first in range(0, width, tile):
            cols = slice(first, first + tile)
            proj[at, cols] = (
                jnp.dot(buf[lax.rem(i, 2)], w_ref[:, cols], preferred_element_type=jnp.float32) + bias[:, cols]
            ).astype(proj.dtype)
        store(i).start()
        return carry

    lax.fori_loop(0, n, project, 0)
    gather.forward(1)

    def one(i, carry):
        s, head = i // heads, lax.rem(i, heads)
        attend_one(
            slope_ref[head],
            proj,
            pl.multiple_of(s * length, length),
            head,
            row_ref.at[s],
            mixed_ref,
            length,
        )
        return carry

    lax.fori_loop(0, sequences * heads, one, 0)
    for count in range(2, gather.bits + 1):
        gather.forward(count)
    for i in range(n):
        store(i).wait()
    for mask in range(2**gather.bits):
        gather.wait_core(mask)
    gather.finish_sends()
    gather.keep().wait()


def project_attend(attn_rows, weight, vectors, slopes, labels, own, n, collective_id):
    total, depth = attn_rows.shape
    rows, width = own.shape[0], weight.shape[1]
    heads = width // (3 * HEAD_DIM)
    vmem = pl.BlockSpec(memory_space=pltpu.VMEM)
    hbm = pl.BlockSpec(memory_space=pl.ANY)
    dma = pltpu.SemaphoreType.DMA
    return pl.pallas_call(
        functools.partial(project_kernel, n, labels.shape[1]),
        out_shape=(
            jax.ShapeDtypeStruct((total, own.shape[1]), own.dtype),
            jax.ShapeDtypeStruct((total, width), jnp.bfloat16),
            jax.ShapeDtypeStruct((total, heads * HEAD_DIM), jnp.bfloat16),
        ),
        in_specs=[pl.BlockSpec(memory_space=pltpu.SMEM), vmem, hbm, vmem, vmem, vmem],
        out_specs=(hbm, hbm, vmem),
        scratch_shapes=[
            pltpu.VMEM((total, width), jnp.bfloat16),
            pltpu.VMEM((2, rows, depth), jnp.bfloat16),
            pltpu.VMEM((1, width), jnp.float32),
            dma((2,)),
            dma((n,)),
        ]
        + gather_sems(n),
        compiler_params=pltpu.CompilerParams(
            collective_id=collective_id, has_side_effects=True, vmem_limit_bytes=VMEM_LIMIT
        ),
        cost_estimate=LINK_COST,
        name="project_attend",
    )(slopes, own, attn_rows, weight, vectors, labels[:, None, :])


def gelu_both(value):
    c, a = 0.7978845608028654, 0.044715
    square = value * value
    half = 0.5 + 0.5 * jnp.tanh(value * (c + (c * a) * square))
    active = value * half
    slope = half + (2.0 * active) * (1.0 - half) * (c + (3.0 * c * a) * square)
    return active, slope


def expand_kernel(
    n, own_ref, grad_hbm, up_ref, down_ref, vectors_ref, rows_hbm, act_hbm, pre_hbm, sum_ref,
    gathered, grads, backs, act, pre, load_sem, act_sem, pre_sem, rows_sem, *sems
):
    gather = Gather(n, own_ref, gathered, sems)
    rows, depth = own_ref.shape
    width = up_ref.shape[1]
    tile = tile_of(width)
    levels = [gather.level(count) for count in range(gather.bits + 1)]
    codes = [2 * mask + core for masks in levels for core in (0, 1) for mask in masks]

    def span(i):
        return pl.ds(pl.multiple_of(gather.away(codes, i) * rows, rows), rows)

    def load(i):
        return pltpu.make_async_copy(grad_hbm.at[span(i), :], grads.at[parity(i)], load_sem.at[parity(i)])

    def store(i):
        slot = parity(i)
        return (
            pltpu.make_async_copy(act.at[slot], act_hbm.at[span(i), :], act_sem.at[slot]),
            pltpu.make_async_copy(pre.at[slot], pre_hbm.at[span(i), :], pre_sem.at[slot]),
        )

    def keep_rows(i):
        return pltpu.make_async_copy(gathered.at[span(i), :], rows_hbm.at[span(i), :], rows_sem.at[i])

    def cols_of(j):
        return pl.ds(pl.multiple_of(j * tile, tile), tile)

    def back(i, carry):
        load(i).wait()

        @pl.when(i + 1 < n)
        def _():
            load(i + 1).start()

        def columns(j, carry):
            value = lax.dot_general(
                grads[parity(i)], down_ref[cols_of(j), :], NT, preferred_element_type=jnp.float32
            )
            backs[i, :, cols_of(j)] = value.astype(backs.dtype)
            return carry

        lax.fori_loop(0, width // tile, columns, 0)
        return carry

    def work(i, carry):
        first = 0
        for count, masks in enumerate(levels):
            if count:
                pl.when(i == first)(functools.partial(gather.forward, count))
            for k, mask in enumerate(masks):
                pl.when(i == first + len(masks) + k)(functools.partial(gather.wait_core, mask))
            first += 2 * len(masks)
        keep_rows(i).start()

        @pl.when(i >= 2)
        def _():
            for copy in store(i - 2):
                copy.wait()

        here, slot = span(i), parity(i)

        def columns(j, carry):
            cols = cols_of(j)
            before = jnp.dot(gathered[here, :], up_ref[:, cols], preferred_element_type=jnp.float32)
            before = before + vectors_ref[UP_BIAS, :, cols]
            active, slope = gelu_both(before)
            act[slot, :, cols] = active.astype(act.dtype)
            rounded = (backs[i, :, cols].astype(jnp.float32) * slope).astype(pre.dtype)
            pre[slot, :, cols] = rounded
            sum_ref[:, cols] += jnp.sum(rounded.astype(jnp.float32), axis=0, keepdims=True)
            return carry

        lax.fori_loop(0, width // tile, columns, 0)
        for copy in store(i):
            copy.start()
        return carry

    sum_ref[...] = jnp.zeros_like(sum_ref)
    load(0).start()
    gather.start()
    lax.fori_loop(0, n, back, 0)
    gather.keep().wait()
    lax.fori_loop(0, n, work, 0)
    for last in (n - 2, n - 1):
        for copy in store(last):
            copy.wait()
    for i in range(n):
        keep_rows(i).wait()
    gather.finish_sends()


def expand(own, grad_rows, up, down, vectors, n, collective_id):
    rows, depth = own.shape
    width = up.shape[1]
    total = n * rows
    vmem = pl.BlockSpec(memory_space=pltpu.VMEM)
    hbm = pl.BlockSpec(memory_space=pl.ANY)
    dma = pltpu.SemaphoreType.DMA
    return pl.pallas_call(
        functools.partial(expand_kernel, n),
        out_shape=(
            jax.ShapeDtypeStruct((total, depth), jnp.bfloat16),
            jax.ShapeDtypeStruct((total, width), jnp.bfloat16),
            jax.ShapeDtypeStruct((total, width), jnp.bfloat16),
            jax.ShapeDtypeStruct((1, width), jnp.float32),
        ),
        in_specs=[vmem, hbm, vmem, vmem, vmem],
        out_specs=(hbm, hbm, hbm, vmem),
        scratch_shapes=[
            pltpu.VMEM((total, depth), jnp.bfloat16),
            pltpu.VMEM((2, rows, depth), jnp.bfloat16),
            pltpu.VMEM((n, rows, width), jnp.bfloat16),
            pltpu.VMEM((2, rows, width), jnp.bfloat16),
            pltpu.VMEM((2, rows, width), jnp.bfloat16),
            dma((2,)),
            dma((2,)),
            dma((2,)),
            dma((n,)),
        ]
        + gather_sems(n),
        compiler_params=pltpu.CompilerParams(
            collective_id=collective_id, has_side_effects=True, vmem_limit_bytes=VMEM_LIMIT
        ),
        cost_estimate=LINK_COST,
        name="expand",
    )(own, grad_rows, up, down, vectors)


class Product:
    def __init__(self, left, right, out, scratch):
        self.left, self.right, self.out = left, right, out
        self.lbuf, self.rbuf, self.acc, self.obuf, self.left_sem, self.right_sem, self.out_sem = scratch
        self.depth, self.tall = self.lbuf.shape[1:]
        self.wide = self.rbuf.shape[2]
        self.inner = left.shape[0] // self.depth
        self.across = right.shape[1] // self.wide
        self.steps = (left.shape[1] // self.tall) * self.across * self.inner

    def load(self, i):
        k = lax.rem(i, self.inner)
        col = lax.rem(i // self.inner, self.across)
        row = i // (self.inner * self.across)
        rows = pl.ds(pl.multiple_of(k * self.depth, self.depth), self.depth)
        slot = lax.rem(i, 2)
        return (
            pltpu.make_async_copy(
                self.left.at[rows, pl.ds(pl.multiple_of(row * self.tall, self.tall), self.tall)],
                self.lbuf.at[slot],
                self.left_sem.at[slot],
            ),
            pltpu.make_async_copy(
                self.right.at[rows, pl.ds(pl.multiple_of(col * self.wide, self.wide), self.wide)],
                self.rbuf.at[slot],
                self.right_sem.at[slot],
            ),
        )

    def store(self, tile):
        col = lax.rem(tile, self.across)
        row = tile // self.across
        return pltpu.make_async_copy(
            self.obuf,
            self.out.at[
                pl.ds(pl.multiple_of(row * self.tall, self.tall), self.tall),
                pl.ds(pl.multiple_of(col * self.wide, self.wide), self.wide),
            ],
            self.out_sem,
        )

    def start(self):
        for copy in self.load(0):
            copy.start()

    def step(self, i, carry=0):
        for copy in self.load(i):
            copy.wait()

        @pl.when(i + 1 < self.steps)
        def _():
            for copy in self.load(i + 1):
                copy.start()

        k = lax.rem(i, self.inner)
        slot = lax.rem(i, 2)
        part = next(size for size in (512, 384, self.wide) if self.wide % size == 0)

        @pl.when(k == 0)
        def _():
            self.acc[...] = jnp.zeros_like(self.acc)

        for first in range(0, self.wide, part):
            cols = slice(first, first + part)
            self.acc[:, cols] += lax.dot_general(
                self.lbuf[slot], self.rbuf[slot, :, cols], TN, preferred_element_type=jnp.float32
            )

        @pl.when(k == self.inner - 1)
        def _():
            tile = i // self.inner

            @pl.when(tile > 0)
            def _():
                self.store(tile - 1).wait()

            self.obuf[...] = self.acc[...].astype(self.obuf.dtype)
            self.store(tile).start()

        return carry

    def batch(self, j, batches):
        per = -(-self.steps // batches)
        first = j * per
        lax.fori_loop(first, jnp.minimum(first + per, self.steps), self.step, 0)

    def finish(self):
        self.store(self.steps // self.inner - 1).wait()


def product_scratch(rows, tall, wide):
    dma = pltpu.SemaphoreType.DMA
    depth = min(1024, rows)
    tall, wide = min(512, tall), min(1024, wide)
    return [
        pltpu.VMEM((2, depth, tall), jnp.bfloat16),
        pltpu.VMEM((2, depth, wide), jnp.bfloat16),
        pltpu.VMEM((tall, wide), jnp.float32),
        pltpu.VMEM((tall, wide), jnp.bfloat16),
        dma((2,)),
        dma((2,)),
        dma(()),
    ]


def row_blocks(first, rows, each, work):
    def one(i, carry):
        work(pl.ds(pl.multiple_of(first + i * each, each), each))
        return carry

    lax.fori_loop(0, rows // each, one, 0)


def after_chunk(scatter, fetches, work):
    def after(j):
        @pl.when(j == 0)
        def _():
            for fetch in fetches:
                fetch.wait()

        row_blocks(j * scatter.chunk, scatter.chunk, 32, work)

    return after


def normal_rows(value):
    center = value - jnp.mean(value, axis=1, keepdims=True)
    factor = lax.rsqrt(jnp.mean(center * center, axis=1, keepdims=True) + 1e-05)
    return center * factor, factor


def dense_kernel(
    n, a_hbm, w_ref, input_hbm, vectors_ref, out_ref, next_ref, inputs, input_sem, *scratch
):
    fetch = pltpu.make_async_copy(input_hbm, inputs, input_sem)
    fetch.start()
    scatter = Scatter(n, False, a_hbm, w_ref, out_ref, scratch)

    def work(at):
        residual = inputs[at, :].astype(jnp.float32) + out_ref[at, :] + vectors_ref[DENSE_BIAS]
        out_ref[at, :] = residual
        normed, _ = normal_rows(residual)
        next_ref[at, :] = (normed * vectors_ref[SECOND_GAIN] + vectors_ref[SECOND_SHIFT]).astype(next_ref.dtype)

    scatter.run(after=after_chunk(scatter, (fetch,), work))


def back_rows(grad, source, gain):
    normed, factor = normal_rows(source)
    scaled = grad * gain
    product = grad * normed
    back = factor * (
        scaled
        - jnp.mean(scaled, axis=1, keepdims=True)
        - normed * jnp.mean(scaled * normed, axis=1, keepdims=True)
    )
    return back, product


def column_sum(value):
    return jnp.sum(value, axis=0, keepdims=True)


def expand_back_kernel(
    n, a_hbm, w_ref, act_hbm, rows_hbm, residual_hbm, cotangent_hbm, vectors_ref,
    out_ref, next_ref, sums_ref, grad_hbm, residual, cotangent, fetch_sem, *scratch
):
    fetches = (
        pltpu.make_async_copy(residual_hbm, residual, fetch_sem.at[0]),
        pltpu.make_async_copy(cotangent_hbm, cotangent, fetch_sem.at[1]),
    )
    for fetch in fetches:
        fetch.start()
    product = Product(act_hbm, rows_hbm, grad_hbm, scratch[:7])
    scatter = Scatter(n, True, a_hbm, w_ref, out_ref, scratch[7:])
    product.start()
    sums_ref[...] = jnp.zeros_like(sums_ref)

    def work(at):
        grad = out_ref[at, :]
        other = cotangent[at, :].astype(jnp.float32)
        back, terms = back_rows(grad, residual[at, :], vectors_ref[SECOND_GAIN])
        result = other + back
        out_ref[at, :] = result
        next_ref[at, :] = result.astype(next_ref.dtype)
        sums_ref[0:1, :] += column_sum(terms)
        sums_ref[1:2, :] += column_sum(grad)
        sums_ref[2:3, :] += column_sum(result)
        sums_ref[3:4, :] += column_sum(other)

    scatter.run(lambda j: product.batch(j, scatter.chunks), after_chunk(scatter, fetches, work))
    product.finish()


def comm_params(collective_id):
    return pltpu.CompilerParams(collective_id=collective_id, has_side_effects=True, vmem_limit_bytes=VMEM_LIMIT)


VMEM_SPEC = pl.BlockSpec(memory_space=pltpu.VMEM)
HBM_SPEC = pl.BlockSpec(memory_space=pl.ANY)
CHUNKS = 8
FILLED_CHUNKS = 4


def dense(mixed, weight, inputs, vectors, n, collective_id):
    rows, width = inputs.shape
    return pl.pallas_call(
        functools.partial(dense_kernel, n),
        out_shape=(
            jax.ShapeDtypeStruct((rows, width), jnp.float32),
            jax.ShapeDtypeStruct((rows, width), jnp.bfloat16),
        ),
        in_specs=[HBM_SPEC, VMEM_SPEC, HBM_SPEC, VMEM_SPEC],
        out_specs=(VMEM_SPEC, VMEM_SPEC),
        scratch_shapes=[pltpu.VMEM((rows, width), inputs.dtype), pltpu.SemaphoreType.DMA(())]
        + scatter_scratch(n, rows, mixed.shape[1], width, CHUNKS),
        compiler_params=comm_params(collective_id),
        cost_estimate=LINK_COST,
        name="dense",
    )(mixed, weight, inputs, vectors)


def expand_back(grad_pre, up, activated, grad_rows, residual, cotangent, vectors, n, collective_id):
    rows, width = residual.shape
    units = activated.shape[1]
    return pl.pallas_call(
        functools.partial(expand_back_kernel, n),
        out_shape=(
            jax.ShapeDtypeStruct((rows, width), jnp.float32),
            jax.ShapeDtypeStruct((rows, width), jnp.bfloat16),
            jax.ShapeDtypeStruct((8, width), jnp.float32),
            jax.ShapeDtypeStruct((units, width), jnp.bfloat16),
        ),
        in_specs=[HBM_SPEC, VMEM_SPEC, HBM_SPEC, HBM_SPEC, HBM_SPEC, HBM_SPEC, VMEM_SPEC],
        out_specs=(VMEM_SPEC, VMEM_SPEC, VMEM_SPEC, HBM_SPEC),
        scratch_shapes=[
            pltpu.VMEM((rows, width), jnp.float32),
            pltpu.VMEM((rows, width), cotangent.dtype),
            pltpu.SemaphoreType.DMA((2,)),
        ]
        + product_scratch(n * rows, units, width)
        + scatter_scratch(n, rows, units, width, FILLED_CHUNKS),
        compiler_params=comm_params(collective_id),
        cost_estimate=LINK_COST,
        name="expand_back",
    )(grad_pre, up, activated, grad_rows, residual, cotangent, vectors)


def attend_back_one(slope, proj_ref, grad_ref, start, head, row_ref, out_ref, dk_ref, dv_ref, sums_ref, length):
    at = pl.multiple_of(head * 3 * HEAD_DIM, HEAD_DIM)
    own = pl.ds(pl.multiple_of(head * HEAD_DIM, HEAD_DIM), HEAD_DIM)

    def cols(which):
        return pl.ds(at + which * HEAD_DIM, HEAD_DIM)

    def take(which, first, size):
        return proj_ref[pl.ds(start + first, size), cols(which)]

    sums = None
    for first in reversed(range(0, length, BLOCK)):
        last = first + BLOCK
        q, g = take(0, first, BLOCK), grad_ref[pl.ds(start + first, BLOCK), own]
        scores = masked_scores(slope, q, take(1, 0, last), as_column(row_ref[:, first:last]), row_ref[:, :last], first)
        top = jnp.max(scores, axis=1, keepdims=True)
        expo = jnp.exp2(scores - top)
        probs = expo * (1.0 / jnp.sum(expo, axis=1, keepdims=True))
        grad_probs = lax.dot_general(g, take(2, 0, last), NT, preferred_element_type=jnp.float32)
        product = probs * grad_probs
        grad_scores = (product - probs * jnp.sum(product, axis=1, keepdims=True)).astype(jnp.bfloat16)
        rounded = probs.astype(jnp.bfloat16)
        grad_queries = (jnp.dot(grad_scores, take(1, 0, last), preferred_element_type=jnp.float32) * SCALE).astype(
            out_ref.dtype
        )
        out_ref[pl.ds(start + first, BLOCK), cols(0)] = grad_queries
        here = column_sum(grad_queries.astype(jnp.float32))
        sums = here if sums is None else sums + here
        grad_keys = lax.dot_general(grad_scores, q, TN, preferred_element_type=jnp.float32)
        grad_values = lax.dot_general(rounded, g, TN, preferred_element_type=jnp.float32)
        if last == length:
            dk_ref[...] = grad_keys
            dv_ref[...] = grad_values
        else:
            dk_ref[:last, :] += grad_keys
            dv_ref[:last, :] += grad_values
    span = pl.ds(start, length)
    out_ref[span, cols(1)] = (dk_ref[...] * SCALE).astype(out_ref.dtype)
    grad_values = dv_ref[...].astype(out_ref.dtype)
    out_ref[span, cols(2)] = grad_values
    sums_ref[0:1, own] += sums
    sums_ref[1:2, own] += column_sum(grad_values.astype(jnp.float32))


def dense_back_kernel(
    n, length, slope_ref, own_ref, mixed_ref, w_ref, left_hbm, right_hbm, proj_hbm, row_ref,
    grad_proj_ref, sums_ref, grad_dense_ref, grad_up_hbm, gathered, acc, grad_mixed, proj, dk, dv, fetch_sem, *scratch
):
    fetch = pltpu.make_async_copy(proj_hbm, proj, fetch_sem)
    fetch.start()
    product = Product(left_hbm, right_hbm, grad_up_hbm, scratch[:7])
    gather = Gather(n, own_ref, gathered, scratch[7:])
    rows = own_ref.shape[0]
    heads = sums_ref.shape[1] // HEAD_DIM
    chips = max(1, length // (2 * rows))
    sequences = max(1, 2 * rows // length)

    def work(at):
        span = pl.ds(pl.multiple_of(at * rows, rows), rows)
        grad_mixed[span, :] = lax.dot_general(
            gathered[span, :], w_ref[...], NT, preferred_element_type=jnp.float32
        ).astype(grad_mixed.dtype)
        width = acc.shape[1]
        part = min(width, 512)
        for first in range(0, width, part):
            cols = slice(first, first + part)
            acc[:, cols] += lax.dot_general(
                mixed_ref[span, :], gathered[span, cols], TN, preferred_element_type=jnp.float32
            )

    order = [mask for count in range(gather.bits + 1) for mask in gather.level(count)]
    codes = [2 * mask + core for mask in order for core in (0, 1)]
    complete = [
        int(core == 1 and all(other // chips != mask // chips for other in order[k + 1 :]))
        for k, mask in enumerate(order)
        for core in (0, 1)
    ]

    def step(t, carry):
        for k, mask in enumerate(order):
            if k and mask.bit_count() > order[k - 1].bit_count():
                pl.when(t == 2 * k)(functools.partial(gather.forward, mask.bit_count()))
            pl.when(t == 2 * k + 1)(functools.partial(gather.wait_core, mask))
        at = gather.away(codes, t)
        work(at)

        @pl.when(look_up(complete, t) == 1)
        def _():
            first = (at // 2 // chips) * sequences

            def one(i, carry):
                s, head = first + i // heads, lax.rem(i, heads)
                attend_back_one(
                    slope_ref[head], proj, grad_mixed, pl.multiple_of(s * length, length), head, row_ref.at[s],
                    grad_proj_ref, dk, dv, sums_ref, length,
                )
                return carry

            lax.fori_loop(0, sequences * heads, one, 0)

        return carry

    product.start()
    gather.start()
    acc[...] = jnp.zeros_like(acc)
    sums_ref[...] = jnp.zeros_like(sums_ref)
    product.batch(0, 1)
    fetch.wait()
    gather.keep().wait()
    lax.fori_loop(0, 2 * len(order), step, 0)
    grad_dense_ref[...] = acc[...].astype(grad_dense_ref.dtype)
    product.finish()
    gather.finish_sends()


def dense_back(own, mixed, weight, mlp_rows, grad_pre, proj, slopes, labels, n, collective_id):
    rows, width = own.shape
    total, depth = mixed.shape
    length = labels.shape[1]
    return pl.pallas_call(
        functools.partial(dense_back_kernel, n, length),
        out_shape=(
            jax.ShapeDtypeStruct(proj.shape, jnp.bfloat16),
            jax.ShapeDtypeStruct((8, depth), jnp.float32),
            jax.ShapeDtypeStruct((depth, width), jnp.bfloat16),
            jax.ShapeDtypeStruct((mlp_rows.shape[1], grad_pre.shape[1]), jnp.bfloat16),
        ),
        in_specs=[pl.BlockSpec(memory_space=pltpu.SMEM), VMEM_SPEC, VMEM_SPEC, VMEM_SPEC]
        + [HBM_SPEC] * 3
        + [VMEM_SPEC],
        out_specs=(VMEM_SPEC, VMEM_SPEC, VMEM_SPEC, HBM_SPEC),
        scratch_shapes=[
            pltpu.VMEM((total, width), jnp.bfloat16),
            pltpu.VMEM((depth, width), jnp.float32),
            pltpu.VMEM((total, depth), jnp.bfloat16),
            pltpu.VMEM(proj.shape, jnp.bfloat16),
            pltpu.VMEM((length, HEAD_DIM), jnp.float32),
            pltpu.VMEM((length, HEAD_DIM), jnp.float32),
            pltpu.SemaphoreType.DMA(()),
        ]
        + product_scratch(total, mlp_rows.shape[1], grad_pre.shape[1])
        + gather_sems(n),
        compiler_params=comm_params(collective_id),
        cost_estimate=LINK_COST,
        name="dense_back",
    )(slopes, own, mixed, weight, mlp_rows, grad_pre, proj, labels[:, None, :])


def shrink_kernel(
    n, d, a_hbm, w_ref, residual_hbm, vectors_ref, early_ref, up_sum_ref, head_sums_ref,
    hidden_ref, sums_ref, biases_ref, out, residual, fetch_sem, *scratch
):
    fetch = pltpu.make_async_copy(residual_hbm, residual, fetch_sem)
    fetch.start()
    flat, biases = Total(n, d, scratch[:6]), Total(n, d, scratch[6:12])
    scatter = Scatter(n, False, a_hbm, w_ref, out, scratch[12:])
    heads_width = head_sums_ref.shape[1]

    def filler(j):
        for level in range(min(flat.levels + 1, scatter.chunks)):

            @pl.when(j == level)
            def _():
                if level == 0:
                    biases.lines[0] = jnp.zeros(biases.lines.shape[1:], jnp.float32)
                    biases.lines[0, 0:1, :] = up_sum_ref[...]
                    biases.lines[0, 1:3, :heads_width] = head_sums_ref[0:2, :]
                    biases.spread()
                    flat.pair[0] = early_ref[...]
                flat.step(level)

    def work(at):
        hidden_ref[at, :] = (residual[at, :] + out[at, :] + vectors_ref[DOWN_BIAS]).astype(hidden_ref.dtype)

    scatter.run(filler, after_chunk(scatter, (fetch,), work), d)
    for level in range(scatter.chunks, flat.levels + 1):
        flat.step(level)
    biases_ref[...] = biases.finish(False)
    sums_ref[...] = flat.finish()


def shrink(activated, down, residual, vectors, sums, up_sum, head_sums, n, d, collective_id):
    rows, width = residual.shape
    units = up_sum.shape[1]
    return pl.pallas_call(
        functools.partial(shrink_kernel, n, d),
        out_shape=(
            jax.ShapeDtypeStruct((rows, width), jnp.bfloat16),
            jax.ShapeDtypeStruct((8, width), jnp.float32),
            jax.ShapeDtypeStruct((8, units), jnp.float32),
        ),
        in_specs=[HBM_SPEC, VMEM_SPEC, HBM_SPEC] + [VMEM_SPEC] * 4,
        out_specs=(VMEM_SPEC, VMEM_SPEC, VMEM_SPEC),
        scratch_shapes=[
            pltpu.VMEM((rows, width), jnp.float32),
            pltpu.VMEM((rows, width), jnp.float32),
            pltpu.SemaphoreType.DMA(()),
        ]
        + total_scratch(n, d, 8, width)
        + total_scratch(n, d, 8, units)
        + scatter_scratch(n, rows, activated.shape[1], width, CHUNKS),
        compiler_params=comm_params(collective_id),
        cost_estimate=LINK_COST,
        name="shrink",
    )(activated, down, residual, vectors, sums, up_sum, head_sums)


def project_back_kernel(
    n, a_hbm, w_ref, input_hbm, grad_hbm, vectors_ref, early_ref, left_hbm,
    out_ref, sums_ref, weight_hbm, inputs, grads, fetch_sem, *scratch
):
    fetches = (
        pltpu.make_async_copy(input_hbm, inputs, fetch_sem.at[0]),
        pltpu.make_async_copy(grad_hbm, grads, fetch_sem.at[1]),
    )
    for fetch in fetches:
        fetch.start()
    product = Product(left_hbm, a_hbm, weight_hbm, scratch[:7])
    scatter = Scatter(n, True, a_hbm, w_ref, out_ref, scratch[7:])
    product.start()
    sums_ref[...] = early_ref[...]

    def work(at):
        grad = out_ref[at, :]
        back, terms = back_rows(grad, inputs[at, :].astype(jnp.float32), vectors_ref[FIRST_GAIN])
        out_ref[at, :] = grads[at, :] + back
        sums_ref[4:5, :] += column_sum(terms)
        sums_ref[5:6, :] += column_sum(grad)

    scatter.run(lambda j: product.batch(j, scatter.chunks), after_chunk(scatter, fetches, work))
    product.finish()


def project_back(grad_proj, weight, inputs, grad_residual, vectors, early, attn_rows, n, collective_id):
    rows, width = inputs.shape
    columns = grad_proj.shape[1]
    return pl.pallas_call(
        functools.partial(project_back_kernel, n),
        out_shape=(
            jax.ShapeDtypeStruct((rows, width), jnp.float32),
            jax.ShapeDtypeStruct((8, width), jnp.float32),
            jax.ShapeDtypeStruct((width, columns), jnp.bfloat16),
        ),
        in_specs=[HBM_SPEC, VMEM_SPEC, HBM_SPEC, HBM_SPEC, VMEM_SPEC, VMEM_SPEC, HBM_SPEC],
        out_specs=(VMEM_SPEC, VMEM_SPEC, HBM_SPEC),
        scratch_shapes=[
            pltpu.VMEM((rows, width), inputs.dtype),
            pltpu.VMEM((rows, width), jnp.float32),
            pltpu.SemaphoreType.DMA((2,)),
        ]
        + product_scratch(n * rows, width, columns)
        + scatter_scratch(n, rows, columns, width, CHUNKS),
        compiler_params=comm_params(collective_id),
        cost_estimate=LINK_COST,
        name="project_back",
    )(grad_proj, weight, inputs, grad_residual, vectors, early, attn_rows)


def share(grad, dimension):
    return lax.psum_scatter(grad, "dp", scatter_dimension=dimension, tiled=True)


def finish_kernel(heads_width, *refs):
    ins, outs = refs[:8], refs[8:]
    for source, target in zip(ins[:6], outs[:6]):
        target[...] = source[...].astype(target.dtype)

    @pl.when(pl.program_id(0) == 0)
    def _():
        sums, biases = ins[6:]
        for i in range(6):
            outs[6 + i][...] = sums[i : i + 1, :]
        outs[12][...] = biases[0:1, :]
        outs[13][...] = biases[1:2, :heads_width]
        outs[14][...] = biases[2:3, :heads_width]


def finish(hidden_output, grad_input, weights, sums, biases, heads_width):
    steps = 2

    def rows_block(x):
        return pl.BlockSpec((x.shape[0] // steps, x.shape[1]), lambda i: (i, 0))

    def whole_block(shape):
        return pl.BlockSpec(shape, lambda i: (0, 0))

    large = (hidden_output, grad_input) + weights
    small = [(1, sums.shape[1])] * 6 + [(1, biases.shape[1]), (1, heads_width), (1, heads_width)]
    results = pl.pallas_call(
        functools.partial(finish_kernel, heads_width),
        grid=(steps,),
        out_shape=[jax.ShapeDtypeStruct(hidden_output.shape, hidden_output.dtype)]
        + [jax.ShapeDtypeStruct(x.shape, jnp.float32) for x in large[1:]]
        + [jax.ShapeDtypeStruct(shape, jnp.float32) for shape in small],
        in_specs=[rows_block(x) for x in large] + [whole_block(sums.shape), whole_block(biases.shape)],
        out_specs=[rows_block(x) for x in large] + [whole_block(shape) for shape in small],
        name="finish",
    )(*large, sums, biases)
    return results[:6], [x.reshape(-1) for x in results[6:]]


def on_device(
    hidden_input,
    first_gain,
    first_shift,
    qkv_weight,
    query_bias,
    value_bias,
    dense_weight,
    dense_bias,
    second_gain,
    second_shift,
    up_weight,
    up_bias,
    down_weight,
    down_bias,
    segments,
    document_lengths,
    cotangent,
    *,
    n,
    d,
):
    heads_local = query_bias.shape[0] // HEAD_DIM
    attn_rows, vectors, dense_full = gather_rows(
        hidden_input,
        (
            first_gain,
            first_shift,
            dense_bias,
            second_gain,
            second_shift,
            down_bias,
            up_bias,
            query_bias,
            value_bias,
        ),
        dense_weight,
        n,
        d,
        1,
    )
    project_full, expand_full, shrink_full = (
        lax.all_gather(qkv_weight, "dp", axis=0, tiled=True),
        lax.all_gather(up_weight, "dp", axis=0, tiled=True),
        lax.all_gather(down_weight, "dp", axis=1, tiled=True),
    )
    group_rows = attn_rows.shape[0]
    sequences = document_lengths.shape[0]
    length = group_rows // sequences
    heads_index = lax.axis_index("tensor") * heads_local + lax.broadcasted_iota(
        jnp.int32, (heads_local,), 0
    )
    slopes = jnp.exp2(-8.0 * (heads_index.astype(jnp.float32) + 1.0) / HEADS) * LOG2E
    position = lax.broadcasted_iota(jnp.int32, (sequences, length), 1)
    filled = jnp.sum(document_lengths, axis=1, keepdims=True)
    labels = jnp.where(position < filled, segments.reshape(sequences, length), length + position).astype(jnp.float32)
    grad_rows, proj, mixed = project_attend(
        attn_rows, project_full, vectors, slopes, labels, cotangent, n, 6
    )
    residual, mlp_input = dense(
        mixed, dense_full, hidden_input, vectors, n, 2
    )
    mlp_rows, activated, grad_pre, sum_up_bias = expand(
        mlp_input, grad_rows, expand_full, shrink_full, vectors, n, 7
    )
    grad_residual, grad_attn_out, early_sums, grad_down = expand_back(
        grad_pre, expand_full, activated, grad_rows, residual, cotangent, vectors, n, 4
    )
    grad_down_weight = share(grad_down, 1)
    grad_proj, head_sums, grad_dense, grad_up = dense_back(
        grad_attn_out, mixed, dense_full, mlp_rows, grad_pre, proj, slopes, labels, n, 9
    )
    grad_down_weight, grad_proj = lax.optimization_barrier((grad_down_weight, grad_proj))
    grad_up_weight = share(grad_up, 0)
    grad_dense_weight = share(grad_dense, 1)
    grad_input, sums, grad_project = project_back(
        grad_proj, project_full, hidden_input, grad_residual, vectors, early_sums, attn_rows, n, 5
    )
    grad_qkv_weight = share(grad_project, 0)
    hidden_output, sums, biases = shrink(
        activated, shrink_full, residual, vectors, sums, sum_up_bias, head_sums, n, d, 3
    )
    heads_width = heads_local * HEAD_DIM
    large, small = finish(
        hidden_output,
        grad_input,
        (grad_qkv_weight, grad_dense_weight, grad_up_weight, grad_down_weight),
        sums,
        biases,
        heads_width,
    )
    hidden_output, grad_input, grad_qkv_weight, grad_dense_weight, grad_up_weight, grad_down_weight = large
    grad_second_gain, grad_second_shift, grad_dense_bias, grad_down_bias, grad_first_gain, grad_first_shift = small[:6]
    grad_up_bias, grad_query_bias, grad_value_bias = small[6:]
    return (
        hidden_output,
        grad_input,
        grad_first_gain,
        grad_first_shift,
        grad_qkv_weight,
        grad_query_bias,
        grad_value_bias,
        grad_dense_weight,
        grad_dense_bias,
        grad_second_gain,
        grad_second_shift,
        grad_up_weight,
        grad_up_bias,
        grad_down_weight,
        grad_down_bias,
    )


def solution(mesh):
    return jax.shard_map(
        functools.partial(on_device, n=mesh.shape["tensor"], d=mesh.shape["dp"]),
        mesh=mesh,
        in_specs=(
            P(("dp", "tensor"), None),
            P(),
            P(),
            P("dp", "tensor"),
            P("tensor"),
            P("tensor"),
            P("tensor", "dp"),
            P(),
            P(),
            P(),
            P("dp", "tensor"),
            P("tensor"),
            P("tensor", "dp"),
            P(),
            P("dp"),
            P("dp", None),
            P(("dp", "tensor"), None),
        ),
        out_specs=(
            P(("dp", "tensor"), None),
            P(("dp", "tensor"), None),
            P(),
            P(),
            P("dp", "tensor"),
            P("tensor"),
            P("tensor"),
            P("tensor", "dp"),
            P(),
            P(),
            P(),
            P("dp", "tensor"),
            P("tensor"),
            P("tensor", "dp"),
            P(),
        ),
        check_vma=False,
    )
```

```python
import functools
import math

import jax
import jax.numpy as jnp
from jax import lax
from jax.experimental import pallas as pl
from jax.experimental.pallas import tpu as pltpu
from jax.sharding import PartitionSpec as P

VMEM_LIMIT = 62 << 20
LINK_COST = pl.CostEstimate(flops=0, bytes_accessed=280_000_000, transcendentals=0)


def flip(index, bit):
    return index + (1 - 2 * ((index // 2**bit) % 2)) * 2**bit


def look_up(table, i):
    if isinstance(i, int):
        return table[i]
    value = table[0]
    for k in range(1, len(table)):
        value = value + (i >= k).astype(jnp.int32) * (table[k] - table[k - 1])
    return value


def parity(i):
    return i % 2 if isinstance(i, int) else lax.rem(i, 2)


def chip_bits(n):
    return n.bit_length() - 2


def column_parts(width, count):
    blocks = width // 128
    edges = [128 * (blocks * i // count) for i in range(count + 1)]
    return [(a, b - a) for a, b in zip(edges[:-1], edges[1:])]


def peer(index):
    return {"tensor": index}


def greet(me, bits, d=1, meanwhile=None):
    barrier = pltpu.get_barrier_semaphore()
    for bit in range(bits + 1):
        pl.semaphore_signal(
            barrier, inc=1, device_id=peer(flip(me, bit)), device_id_type=pl.DeviceIdType.MESH
        )
    for ahead in range(1, d):
        pl.semaphore_signal(
            barrier, inc=1, device_id=ahead_on_dp(ahead, d), device_id_type=pl.DeviceIdType.MESH
        )
    if meanwhile is not None:
        meanwhile()
    pl.semaphore_wait(barrier, bits + d)


def ahead_on_dp(ahead, d):
    return {"dp": lax.rem(lax.axis_index("dp") + ahead, d)}


def remote(src, dst, send_sem, recv_sem, target):
    return pltpu.make_async_remote_copy(
        src_ref=src,
        dst_ref=dst,
        send_sem=send_sem,
        recv_sem=recv_sem,
        device_id=peer(target),
        device_id_type=pl.DeviceIdType.MESH,
    )


class Gather:
    def __init__(self, n, own_ref, out_ref, sems):
        self.me = lax.axis_index("tensor")
        self.bits = chip_bits(n)
        self.rows, width = own_ref.shape
        self.parts = column_parts(width, self.bits)
        self.own, self.out = own_ref, out_ref
        self.own_sem, self.chip_send, self.chip_recv, self.core_send, self.core_recv = sems

    def slot(self, part, index):
        at = self.me
        for step in range(self.bits):
            if (index >> step) & 1:
                at = flip(at, 1 + (part + step) % self.bits)
        return at

    def place(self, mask, core):
        at = flip(self.me, 0) if core else self.me
        for bit in range(self.bits):
            if (mask >> bit) & 1:
                at = flip(at, 1 + bit)
        return at

    def away(self, codes, t):
        code, at = look_up(codes, t), self.me
        for bit in range(self.bits + 1):
            at = at + (code // 2**bit) % 2 * (1 - 2 * ((self.me // 2**bit) % 2)) * 2**bit
        return at

    def index_of(self, part, mask):
        return sum(2 ** ((bit - part) % self.bits) for bit in range(self.bits) if (mask >> bit) & 1)

    def level(self, count):
        return [index for index in range(2**self.bits) if index.bit_count() == count]

    def block(self, part, index, core=0):
        start, size = self.parts[part]
        at = flip(self.slot(part, index), 0) if core else self.slot(part, index)
        return self.out.at[pl.ds(pl.multiple_of(at * self.rows, self.rows), self.rows), pl.ds(start, size)]

    def source(self, part, index):
        start, size = self.parts[part]
        return self.own.at[:, pl.ds(start, size)] if index == 0 else self.block(part, index)

    def chip_copy(self, part, index, step):
        arrives = index + 2**step
        return remote(
            self.source(part, index),
            self.block(part, index),
            self.chip_send.at[part, arrives],
            self.chip_recv.at[part, arrives],
            flip(self.me, 1 + (part + step) % self.bits),
        )

    def core_copy(self, part, index):
        return remote(
            self.source(part, index),
            self.block(part, index),
            self.core_send.at[part, index],
            self.core_recv.at[part, index],
            flip(self.me, 0),
        )

    def keep(self):
        rows = pl.ds(pl.multiple_of(self.me * self.rows, self.rows), self.rows)
        return pltpu.make_async_copy(self.own, self.out.at[rows, :], self.own_sem)

    def start(self, meanwhile=None, d=1):
        greet(self.me, self.bits, d, meanwhile)
        for step in range(self.bits):
            for part in range(self.bits):
                self.chip_copy(part, 0, step).start()
        for part in range(self.bits):
            self.core_copy(part, 0).start()
        self.keep().start()

    def forward(self, count):
        for index in self.level(count):
            for part in range(self.bits):
                arrived = self.block(part, index)
                remote(
                    arrived, arrived, self.chip_send.at[part, index], self.chip_recv.at[part, index], flip(self.me, 0)
                ).wait_recv()
                for step in range(index.bit_length(), self.bits):
                    self.chip_copy(part, index, step).start()
                self.core_copy(part, index).start()

    def wait_core(self, mask):
        for part in range(self.bits):
            index = self.index_of(part, mask)
            arrived = self.block(part, index, 1)
            remote(
                arrived, arrived, self.core_send.at[part, index], self.core_recv.at[part, index], flip(self.me, 0)
            ).wait_recv()

    def finish_sends(self):
        for part in range(self.bits):
            for index in range(2**self.bits):
                for step in range(index.bit_length(), self.bits):
                    self.chip_copy(part, index, step).wait_send()
                self.core_copy(part, index).wait_send()


class Spread:
    def __init__(self, d, shard, full, sems):
        self.d, self.shard, self.full = d, shard, full
        self.own_sem, self.send_sem, self.recv_sem = sems
        self.z = lax.axis_index("dp")

    def columns(self, z):
        width = self.shard.shape[1]
        return self.full.at[:, pl.ds(pl.multiple_of(z * width, width), width)]

    def copy(self, ahead):
        return pltpu.make_async_remote_copy(
            src_ref=self.shard,
            dst_ref=self.columns(self.z),
            send_sem=self.send_sem.at[ahead],
            recv_sem=self.recv_sem.at[ahead],
            device_id=ahead_on_dp(ahead, self.d),
            device_id_type=pl.DeviceIdType.MESH,
        )

    def keep(self):
        return pltpu.make_async_copy(self.shard, self.columns(self.z), self.own_sem)

    def start(self):
        for ahead in range(1, self.d):
            self.copy(ahead).start()
        self.keep().start()

    def finish(self):
        for ahead in range(1, self.d):
            arrived = self.columns(lax.rem(self.z + self.d - ahead, self.d))
            pltpu.make_async_remote_copy(
                src_ref=self.shard,
                dst_ref=arrived,
                send_sem=self.send_sem.at[ahead],
                recv_sem=self.recv_sem.at[ahead],
                device_id=ahead_on_dp(ahead, self.d),
                device_id_type=pl.DeviceIdType.MESH,
            ).wait_recv()
            self.copy(ahead).wait_send()
        self.keep().wait()


def gather_kernel(n, d, x_ref, *refs):
    flat_refs, (shard_ref, out_ref, vectors_ref, full_ref, own, *sems) = refs[:9], refs[9:]
    spread = Spread(d, shard_ref, full_ref, sems[:3])
    sems = sems[3:]

    def put(row, start, ref):
        size = ref.shape[0]
        vectors_ref[row, :, start : start + size] = ref[...].astype(jnp.float32).reshape(1, size)

    put(FIRST_GAIN, 0, flat_refs[FIRST_GAIN])
    put(FIRST_SHIFT, 0, flat_refs[FIRST_SHIFT])

    def work(at):
        normed, _ = normal_rows(x_ref[at, :].astype(jnp.float32))
        own[at, :] = (normed * vectors_ref[FIRST_GAIN] + vectors_ref[FIRST_SHIFT]).astype(own.dtype)

    gather = Gather(n, own, out_ref, sems)
    gather.start(lambda: row_blocks(0, own.shape[0], 64, work), d)
    spread.start()
    for row in range(FIRST_SHIFT + 1, UP_BIAS):
        put(row, 0, flat_refs[row])
    vectors_ref[UP_BIAS] = jnp.zeros(vectors_ref.shape[1:], jnp.float32)
    vectors_ref[HEAD_BIASES] = jnp.zeros(vectors_ref.shape[1:], jnp.float32)
    put(UP_BIAS, 0, flat_refs[UP_BIAS])
    put(HEAD_BIASES, 0, flat_refs[7])
    put(HEAD_BIASES, flat_refs[7].shape[0], flat_refs[8])
    for count in range(1, gather.bits + 1):
        gather.forward(count)
    for mask in range(2**gather.bits):
        gather.wait_core(mask)
    gather.finish_sends()
    spread.finish()
    gather.keep().wait()


def gather_sems(n):
    bits = chip_bits(n)
    dma = pltpu.SemaphoreType.DMA
    return [dma(())] + [dma((bits, 2**bits))] * 4


def gather_rows(x, vectors, shard, n, d, collective_id):
    rows, width = x.shape
    return pl.pallas_call(
        functools.partial(gather_kernel, n, d),
        out_shape=(
            jax.ShapeDtypeStruct((n * rows, width), x.dtype),
            jax.ShapeDtypeStruct((8, 1, width), jnp.float32),
            jax.ShapeDtypeStruct((shard.shape[0], d * shard.shape[1]), shard.dtype),
        ),
        in_specs=[VMEM_SPEC] * 11,
        out_specs=(HBM_SPEC, VMEM_SPEC, HBM_SPEC),
        scratch_shapes=[
            pltpu.VMEM((rows, width), x.dtype),
            pltpu.SemaphoreType.DMA(()),
            pltpu.SemaphoreType.DMA((d,)),
            pltpu.SemaphoreType.DMA((d,)),
        ]
        + gather_sems(n),
        compiler_params=pltpu.CompilerParams(
            collective_id=collective_id, has_side_effects=True, vmem_limit_bytes=VMEM_LIMIT
        ),
        cost_estimate=LINK_COST,
        name="gather_rows",
    )(x, *vectors, shard)


class Scatter:
    def __init__(self, n, transposed, a_hbm, w_ref, out_ref, scratch):
        (self.csend, self.crecv, self.recv, self.other, self.mine, self.load_sem) = scratch[:6]
        self.core_send, self.core_recv, self.chip_send, self.chip_recv = scratch[6:]
        self.me = lax.axis_index("tensor")
        self.bits = chip_bits(n)
        self.total = 2**self.bits
        self.transposed = transposed
        self.a, self.w, self.out = a_hbm, w_ref, out_ref
        self.rows, width = out_ref.shape
        self.chunk = self.csend.shape[2]
        self.chunks = self.rows // self.chunk
        self.parts = column_parts(width, self.bits)

    def index_of(self, part, mask):
        top = self.bits - 1
        return sum(2 ** (top - (bit - part) % self.bits) for bit in range(self.bits) if (mask >> bit) & 1)

    def place(self, mask, core):
        at = flip(self.me, 0) if core else self.me
        for bit in range(self.bits):
            if (mask >> bit) & 1:
                at = flip(at, 1 + bit)
        return at

    def rows_of(self, j):
        return pl.ds(pl.multiple_of(j * self.chunk, self.chunk), self.chunk)

    def loads(self, j, core):
        into = self.other if core else self.mine
        copies = []
        for mask in range(self.total):
            start = pl.multiple_of(self.place(mask, core) * self.rows + j * self.chunk, self.chunk)
            copies.append(
                pltpu.make_async_copy(
                    self.a.at[pl.ds(start, self.chunk), :],
                    into.at[lax.rem(j, 2), pl.ds(mask * self.chunk, self.chunk), :],
                    self.load_sem.at[core, lax.rem(j, 2), mask],
                )
            )
        return copies

    def core_copy(self, j, part):
        start, size = self.parts[part]
        return remote(
            self.csend.at[lax.rem(j, 2), :, :, pl.ds(start, size)],
            self.crecv.at[:, self.rows_of(j), pl.ds(start, size)],
            self.core_send.at[part, j],
            self.core_recv.at[part, j],
            flip(self.me, 0),
        )

    def chip_copy(self, j, part, step):
        half = self.total >> (step + 1)
        first = sum(self.total >> (s + 1) for s in range(step))
        start, size = self.parts[part]
        return remote(
            self.crecv.at[pl.ds(half, half), self.rows_of(j), pl.ds(start, size)],
            self.recv.at[pl.ds(first, half), self.rows_of(j), pl.ds(start, size)],
            self.chip_send.at[part, step, j],
            self.chip_recv.at[part, step, j],
            flip(self.me, 1 + (part + step) % self.bits),
        )

    def tiles(self, part, lhs, put):
        start, size = self.parts[part]
        tile = next(tile for tile in (512, 256, 128) if size % tile == 0 and start % tile == 0)

        def one(i, carry):
            cols = pl.ds(pl.multiple_of(start + i * tile, tile), tile)
            if self.transposed:
                value = lax.dot_general(
                    lhs[...], self.w[cols, :], (((1,), (1,)), ((), ())), preferred_element_type=jnp.float32
                )
            else:
                value = jnp.dot(lhs[...], self.w[:, cols], preferred_element_type=jnp.float32)
            put(cols, value)
            return carry

        lax.fori_loop(0, size // tile, one, 0)

    def piece(self, value, mask):
        return value[mask * self.chunk : (mask + 1) * self.chunk, :]

    def stage_core(self, j):
        for copy in self.loads(j, 1):
            copy.wait()

        @pl.when(j >= 2)
        def _():
            for part in range(self.bits):
                self.core_copy(j - 2, part).wait_send()

        for part in range(self.bits):

            def put(cols, value):
                for mask in range(self.total):
                    self.csend[lax.rem(j, 2), self.index_of(part, mask), :, cols] = self.piece(value, mask).astype(
                        self.csend.dtype
                    )

            self.tiles(part, self.other.at[lax.rem(j, 2)], put)
            self.core_copy(j, part).start()

    def stage_first(self, j):
        for copy in self.loads(j, 0):
            copy.wait()
        for part in range(self.bits):
            self.core_copy(j, part).wait_recv()

            def put(cols, value):
                for mask in range(self.total):
                    index = self.index_of(part, mask)
                    got = self.piece(value, mask) + self.crecv[index, self.rows_of(j), cols].astype(jnp.float32)
                    if index:
                        self.crecv[index, self.rows_of(j), cols] = got.astype(self.crecv.dtype)
                    else:
                        self.out[self.rows_of(j), cols] = got

            self.tiles(part, self.mine.at[lax.rem(j, 2)], put)
            self.chip_copy(j, part, 0).start()

    def stage_next(self, j, step):
        half = self.total >> (step + 1)
        first = sum(self.total >> (s + 1) for s in range(step))
        for part in range(self.bits):
            start, size = self.parts[part]
            cols = slice(start, start + size)
            self.chip_copy(j, part, step).wait_recv()
            for index in reversed(range(half)):
                got = self.recv[first + index, self.rows_of(j), cols].astype(jnp.float32)
                if index:
                    value = self.crecv[index, self.rows_of(j), cols].astype(jnp.float32) + got
                    self.crecv[index, self.rows_of(j), cols] = value.astype(self.crecv.dtype)
                else:
                    self.out[self.rows_of(j), cols] += got
            if step + 1 < self.bits:
                self.chip_copy(j, part, step + 1).start()

    def run(self, filler=None, after=None, d=1):
        for copy in self.loads(0, 1):
            copy.start()
        greet(self.me, self.bits, d)

        def body(u, carry):
            @pl.when(u + 1 < self.chunks)
            def _():
                for copy in self.loads(u + 1, 1):
                    copy.start()

            @pl.when(u < self.chunks)
            def _():
                for copy in self.loads(u, 0):
                    copy.start()
                self.stage_core(u)

            @pl.when((u >= 1) & (u <= self.chunks))
            def _():
                self.stage_first(u - 1)

            for step in range(self.bits):

                @pl.when((u >= 2 + step) & (u < self.chunks + 2 + step))
                def _():
                    self.stage_next(u - 2 - step, step)

            if filler is not None:

                @pl.when((u >= 1) & (u <= self.chunks))
                def _():
                    filler(u - 1)

            if after is not None:
                done = u - self.bits - 1

                @pl.when(done >= 0)
                def _():
                    after(done)

            return carry

        lax.fori_loop(0, self.chunks + self.bits + 1, body, 0)
        for part in range(self.bits):
            for j in range(self.chunks):
                if j >= self.chunks - 2:
                    self.core_copy(j, part).wait_send()
                for step in range(self.bits):
                    self.chip_copy(j, part, step).wait_send()


def scatter_scratch(n, rows, depth, width, chunks):
    bits = chip_bits(n)
    total = 2**bits
    chunk = rows // chunks
    dma = pltpu.SemaphoreType.DMA
    return [
        pltpu.VMEM((2, total, chunk, width), jnp.bfloat16),
        pltpu.VMEM((total, rows, width), jnp.bfloat16),
        pltpu.VMEM((total - 1, rows, width), jnp.bfloat16),
        pltpu.VMEM((2, total * chunk, depth), jnp.bfloat16),
        pltpu.VMEM((2, total * chunk, depth), jnp.bfloat16),
        dma((2, 2, total)),
        dma((bits, chunks)),
        dma((bits, chunks)),
        dma((bits, bits, chunks)),
        dma((bits, bits, chunks)),
    ]


HEAD_DIM = 128
HEADS = 16
FIRST_GAIN, FIRST_SHIFT, DENSE_BIAS, SECOND_GAIN, SECOND_SHIFT, DOWN_BIAS, UP_BIAS, HEAD_BIASES = range(8)
LOG2E = 1.4426950408889634
SCALE = 1.0 / math.sqrt(HEAD_DIM)
BLOCK = 256
NT = (((1,), (1,)), ((), ()))
TN = (((0,), (0,)), ((), ()))


def as_column(row):
    width = row.shape[1]
    here = lax.broadcasted_iota(jnp.int32, (width, width), 0) == lax.broadcasted_iota(jnp.int32, (width, width), 1)
    return jnp.sum(jnp.where(here, row, 0.0), axis=1, keepdims=True)


def masked_scores(slope, q, keys, query_labels, key_labels, first):
    raw = lax.dot_general(q, keys, NT, preferred_element_type=jnp.float32)
    rows, width = raw.shape
    column = lax.broadcasted_iota(jnp.int32, (1, width), 1)
    bias = column.astype(jnp.float32) * slope
    same = query_labels == key_labels
    causal = lax.broadcasted_iota(jnp.int32, (rows, width), 1) <= first + lax.broadcasted_iota(
        jnp.int32, (rows, width), 0
    )
    return jnp.where(same & causal, raw * (SCALE * LOG2E) + bias, -1e30)


class Total:
    def __init__(self, n, d, scratch):
        self.pair, self.lines, self.send, self.recv, self.line_send, self.line_recv = scratch
        self.me, self.d = lax.axis_index("tensor"), d
        self.levels = n.bit_length() - 1

    def level_copy(self, level):
        return remote(
            self.pair.at[2 * level],
            self.pair.at[2 * level + 1],
            self.send.at[level],
            self.recv.at[level],
            flip(self.me, level),
        )

    def line_copy(self, ahead):
        return pltpu.make_async_remote_copy(
            src_ref=self.lines.at[0],
            dst_ref=self.lines.at[ahead],
            send_sem=self.line_send.at[ahead],
            recv_sem=self.line_recv.at[ahead],
            device_id=ahead_on_dp(ahead, self.d),
            device_id_type=pl.DeviceIdType.MESH,
        )

    def spread(self):
        for ahead in range(1, self.d):
            self.line_copy(ahead).start()

    def step(self, level):
        if level:
            self.level_copy(level - 1).wait_recv()
            self.pair[2 * level] = self.pair[2 * level - 2] + self.pair[2 * level - 1]
        if level < self.levels:
            self.level_copy(level).start()
        else:
            self.lines[0] = self.pair[2 * level]
            self.spread()

    def finish(self, levels=True):
        for ahead in range(1, self.d):
            self.line_copy(ahead).wait_recv()
        z = lax.axis_index("dp")
        total = None
        for index in range(self.d):
            value = self.lines[lax.rem(z - index + self.d, self.d)]
            total = value if total is None else total + value
        for ahead in range(1, self.d):
            self.line_copy(ahead).wait_send()
        if levels:
            for level in range(self.levels):
                self.level_copy(level).wait_send()
        return total


def total_scratch(n, d, rows, width):
    levels = n.bit_length() - 1
    dma = pltpu.SemaphoreType.DMA
    return [
        pltpu.VMEM((2 * levels + 1, rows, width), jnp.float32),
        pltpu.VMEM((d, rows, width), jnp.float32),
        dma((levels,)),
        dma((levels,)),
        dma((d,)),
        dma((d,)),
    ]


def tile_of(width):
    return 256 if width % 256 == 0 else width


def attend_one(slope, proj_ref, start, head, row_ref, out_ref, length):
    at = pl.multiple_of(head * 3 * HEAD_DIM, HEAD_DIM)

    def take(which, first, size):
        return proj_ref[pl.ds(start + first, size), pl.ds(at + which * HEAD_DIM, HEAD_DIM)]

    for first in range(0, length, BLOCK):
        last = first + BLOCK
        scores = masked_scores(
            slope, take(0, first, BLOCK), take(1, 0, last), as_column(row_ref[:, first:last]), row_ref[:, :last], first
        )
        top = jnp.max(scores, axis=1, keepdims=True)
        expo = jnp.exp2(scores - top)
        total = jnp.sum(expo, axis=1, keepdims=True)
        mixed = jnp.dot(expo.astype(jnp.bfloat16), take(2, 0, last), preferred_element_type=jnp.float32)
        out_ref[pl.ds(start + first, BLOCK), pl.ds(pl.multiple_of(head * HEAD_DIM, HEAD_DIM), HEAD_DIM)] = (
            mixed / total
        ).astype(out_ref.dtype)


def project_kernel(
    n, length, slope_ref, own_ref, rows_hbm, w_ref, vectors_ref, row_ref, gathered, proj_hbm, mixed_ref,
    proj, buf, bias, load_sem, store_sem, *sems
):
    gather = Gather(n, own_ref, gathered, sems)
    rows = own_ref.shape[0]
    width = w_ref.shape[1]
    tile = tile_of(width)
    heads = width // (3 * HEAD_DIM)
    sequences = n * rows // length

    def load(i):
        at = pl.ds(pl.multiple_of(i * rows, rows), rows)
        return pltpu.make_async_copy(rows_hbm.at[at, :], buf.at[lax.rem(i, 2)], load_sem.at[lax.rem(i, 2)])

    load(0).start()
    bias[...] = jnp.zeros_like(bias)
    for head in range(heads):
        for which, first in ((0, 0), (2, heads * HEAD_DIM)):
            at = (3 * head + which) * HEAD_DIM
            bias[:, at : at + HEAD_DIM] = vectors_ref[HEAD_BIASES, :, first + head * HEAD_DIM : first + (head + 1) * HEAD_DIM]
    gather.start()

    def store(i):
        at = pl.ds(pl.multiple_of(i * rows, rows), rows)
        return pltpu.make_async_copy(proj.at[at, :], proj_hbm.at[at, :], store_sem.at[i])

    def project(i, carry):
        load(i).wait()

        @pl.when(i + 1 < n)
        def _():
            load(i + 1).start()

        at = pl.ds(pl.multiple_of(i * rows, rows), rows)
        for first in range(0, width, tile):
            cols = slice(first, first + tile)
            proj[at, cols] = (
                jnp.dot(buf[lax.rem(i, 2)], w_ref[:, cols], preferred_element_type=jnp.float32) + bias[:, cols]
            ).astype(proj.dtype)
        store(i).start()
        return carry

    lax.fori_loop(0, n, project, 0)
    gather.forward(1)

    def one(i, carry):
        s, head = i // heads, lax.rem(i, heads)
        attend_one(
            slope_ref[head],
            proj,
            pl.multiple_of(s * length, length),
            head,
            row_ref.at[s],
            mixed_ref,
            length,
        )
        return carry

    lax.fori_loop(0, sequences * heads, one, 0)
    for count in range(2, gather.bits + 1):
        gather.forward(count)
    for i in range(n):
        store(i).wait()
    for mask in range(2**gather.bits):
        gather.wait_core(mask)
    gather.finish_sends()
    gather.keep().wait()


def project_attend(attn_rows, weight, vectors, slopes, labels, own, n, collective_id):
    total, depth = attn_rows.shape
    rows, width = own.shape[0], weight.shape[1]
    heads = width // (3 * HEAD_DIM)
    vmem = pl.BlockSpec(memory_space=pltpu.VMEM)
    hbm = pl.BlockSpec(memory_space=pl.ANY)
    dma = pltpu.SemaphoreType.DMA
    return pl.pallas_call(
        functools.partial(project_kernel, n, labels.shape[1]),
        out_shape=(
            jax.ShapeDtypeStruct((total, own.shape[1]), own.dtype),
            jax.ShapeDtypeStruct((total, width), jnp.bfloat16),
            jax.ShapeDtypeStruct((total, heads * HEAD_DIM), jnp.bfloat16),
        ),
        in_specs=[pl.BlockSpec(memory_space=pltpu.SMEM), vmem, hbm, vmem, vmem, vmem],
        out_specs=(hbm, hbm, vmem),
        scratch_shapes=[
            pltpu.VMEM((total, width), jnp.bfloat16),
            pltpu.VMEM((2, rows, depth), jnp.bfloat16),
            pltpu.VMEM((1, width), jnp.float32),
            dma((2,)),
            dma((n,)),
        ]
        + gather_sems(n),
        compiler_params=pltpu.CompilerParams(
            collective_id=collective_id, has_side_effects=True, vmem_limit_bytes=VMEM_LIMIT
        ),
        cost_estimate=LINK_COST,
        name="project_attend",
    )(slopes, own, attn_rows, weight, vectors, labels[:, None, :])


def gelu_both(value):
    c, a = 0.7978845608028654, 0.044715
    square = value * value
    half = 0.5 + 0.5 * jnp.tanh(value * (c + (c * a) * square))
    active = value * half
    slope = half + (2.0 * active) * (1.0 - half) * (c + (3.0 * c * a) * square)
    return active, slope


def expand_kernel(
    n, own_ref, grad_hbm, up_ref, down_ref, vectors_ref, rows_hbm, act_hbm, pre_hbm, sum_ref,
    gathered, grads, backs, act, pre, load_sem, act_sem, pre_sem, rows_sem, *sems
):
    gather = Gather(n, own_ref, gathered, sems)
    rows, depth = own_ref.shape
    width = up_ref.shape[1]
    tile = tile_of(width)
    levels = [gather.level(count) for count in range(gather.bits + 1)]
    codes = [2 * mask + core for masks in levels for core in (0, 1) for mask in masks]

    def span(i):
        return pl.ds(pl.multiple_of(gather.away(codes, i) * rows, rows), rows)

    def load(i):
        return pltpu.make_async_copy(grad_hbm.at[span(i), :], grads.at[parity(i)], load_sem.at[parity(i)])

    def store(i):
        slot = parity(i)
        return (
            pltpu.make_async_copy(act.at[slot], act_hbm.at[span(i), :], act_sem.at[slot]),
            pltpu.make_async_copy(pre.at[slot], pre_hbm.at[span(i), :], pre_sem.at[slot]),
        )

    def keep_rows(i):
        return pltpu.make_async_copy(gathered.at[span(i), :], rows_hbm.at[span(i), :], rows_sem.at[i])

    def cols_of(j):
        return pl.ds(pl.multiple_of(j * tile, tile), tile)

    def back(i, carry):
        load(i).wait()

        @pl.when(i + 1 < n)
        def _():
            load(i + 1).start()

        def columns(j, carry):
            value = lax.dot_general(
                grads[parity(i)], down_ref[cols_of(j), :], NT, preferred_element_type=jnp.float32
            )
            backs[i, :, cols_of(j)] = value.astype(backs.dtype)
            return carry

        lax.fori_loop(0, width // tile, columns, 0)
        return carry

    def work(i, carry):
        first = 0
        for count, masks in enumerate(levels):
            if count:
                pl.when(i == first)(functools.partial(gather.forward, count))
            for k, mask in enumerate(masks):
                pl.when(i == first + len(masks) + k)(functools.partial(gather.wait_core, mask))
            first += 2 * len(masks)
        keep_rows(i).start()

        @pl.when(i >= 2)
        def _():
            for copy in store(i - 2):
                copy.wait()

        here, slot = span(i), parity(i)

        def columns(j, carry):
            cols = cols_of(j)
            before = jnp.dot(gathered[here, :], up_ref[:, cols], preferred_element_type=jnp.float32)
            before = before + vectors_ref[UP_BIAS, :, cols]
            active, slope = gelu_both(before)
            act[slot, :, cols] = active.astype(act.dtype)
            rounded = (backs[i, :, cols].astype(jnp.float32) * slope).astype(pre.dtype)
            pre[slot, :, cols] = rounded
            sum_ref[:, cols] += jnp.sum(rounded.astype(jnp.float32), axis=0, keepdims=True)
            return carry

        lax.fori_loop(0, width // tile, columns, 0)
        for copy in store(i):
            copy.start()
        return carry

    sum_ref[...] = jnp.zeros_like(sum_ref)
    load(0).start()
    gather.start()
    lax.fori_loop(0, n, back, 0)
    gather.keep().wait()
    lax.fori_loop(0, n, work, 0)
    for last in (n - 2, n - 1):
        for copy in store(last):
            copy.wait()
    for i in range(n):
        keep_rows(i).wait()
    gather.finish_sends()


def expand(own, grad_rows, up, down, vectors, n, collective_id):
    rows, depth = own.shape
    width = up.shape[1]
    total = n * rows
    vmem = pl.BlockSpec(memory_space=pltpu.VMEM)
    hbm = pl.BlockSpec(memory_space=pl.ANY)
    dma = pltpu.SemaphoreType.DMA
    return pl.pallas_call(
        functools.partial(expand_kernel, n),
        out_shape=(
            jax.ShapeDtypeStruct((total, depth), jnp.bfloat16),
            jax.ShapeDtypeStruct((total, width), jnp.bfloat16),
            jax.ShapeDtypeStruct((total, width), jnp.bfloat16),
            jax.ShapeDtypeStruct((1, width), jnp.float32),
        ),
        in_specs=[vmem, hbm, vmem, vmem, vmem],
        out_specs=(hbm, hbm, hbm, vmem),
        scratch_shapes=[
            pltpu.VMEM((total, depth), jnp.bfloat16),
            pltpu.VMEM((2, rows, depth), jnp.bfloat16),
            pltpu.VMEM((n, rows, width), jnp.bfloat16),
            pltpu.VMEM((2, rows, width), jnp.bfloat16),
            pltpu.VMEM((2, rows, width), jnp.bfloat16),
            dma((2,)),
            dma((2,)),
            dma((2,)),
            dma((n,)),
        ]
        + gather_sems(n),
        compiler_params=pltpu.CompilerParams(
            collective_id=collective_id, has_side_effects=True, vmem_limit_bytes=VMEM_LIMIT
        ),
        cost_estimate=LINK_COST,
        name="expand",
    )(own, grad_rows, up, down, vectors)


class Product:
    def __init__(self, left, right, out, scratch):
        self.left, self.right, self.out = left, right, out
        self.lbuf, self.rbuf, self.acc, self.obuf, self.left_sem, self.right_sem, self.out_sem = scratch
        self.depth, self.tall = self.lbuf.shape[1:]
        self.wide = self.rbuf.shape[2]
        self.inner = left.shape[0] // self.depth
        self.across = right.shape[1] // self.wide
        self.steps = (left.shape[1] // self.tall) * self.across * self.inner

    def load(self, i):
        k = lax.rem(i, self.inner)
        col = lax.rem(i // self.inner, self.across)
        row = i // (self.inner * self.across)
        rows = pl.ds(pl.multiple_of(k * self.depth, self.depth), self.depth)
        slot = lax.rem(i, 2)
        return (
            pltpu.make_async_copy(
                self.left.at[rows, pl.ds(pl.multiple_of(row * self.tall, self.tall), self.tall)],
                self.lbuf.at[slot],
                self.left_sem.at[slot],
            ),
            pltpu.make_async_copy(
                self.right.at[rows, pl.ds(pl.multiple_of(col * self.wide, self.wide), self.wide)],
                self.rbuf.at[slot],
                self.right_sem.at[slot],
            ),
        )

    def store(self, tile):
        col = lax.rem(tile, self.across)
        row = tile // self.across
        return pltpu.make_async_copy(
            self.obuf,
            self.out.at[
                pl.ds(pl.multiple_of(row * self.tall, self.tall), self.tall),
                pl.ds(pl.multiple_of(col * self.wide, self.wide), self.wide),
            ],
            self.out_sem,
        )

    def start(self):
        for copy in self.load(0):
            copy.start()

    def step(self, i, carry=0):
        for copy in self.load(i):
            copy.wait()

        @pl.when(i + 1 < self.steps)
        def _():
            for copy in self.load(i + 1):
                copy.start()

        k = lax.rem(i, self.inner)
        slot = lax.rem(i, 2)
        part = next(size for size in (512, 384, self.wide) if self.wide % size == 0)

        @pl.when(k == 0)
        def _():
            self.acc[...] = jnp.zeros_like(self.acc)

        for first in range(0, self.wide, part):
            cols = slice(first, first + part)
            self.acc[:, cols] += lax.dot_general(
                self.lbuf[slot], self.rbuf[slot, :, cols], TN, preferred_element_type=jnp.float32
            )

        @pl.when(k == self.inner - 1)
        def _():
            tile = i // self.inner

            @pl.when(tile > 0)
            def _():
                self.store(tile - 1).wait()

            self.obuf[...] = self.acc[...].astype(self.obuf.dtype)
            self.store(tile).start()

        return carry

    def batch(self, j, batches):
        per = -(-self.steps // batches)
        first = j * per
        lax.fori_loop(first, jnp.minimum(first + per, self.steps), self.step, 0)

    def finish(self):
        self.store(self.steps // self.inner - 1).wait()


def product_scratch(rows, tall, wide):
    dma = pltpu.SemaphoreType.DMA
    depth = min(1024, rows)
    tall, wide = min(512, tall), min(1024, wide)
    return [
        pltpu.VMEM((2, depth, tall), jnp.bfloat16),
        pltpu.VMEM((2, depth, wide), jnp.bfloat16),
        pltpu.VMEM((tall, wide), jnp.float32),
        pltpu.VMEM((tall, wide), jnp.bfloat16),
        dma((2,)),
        dma((2,)),
        dma(()),
    ]


def row_blocks(first, rows, each, work):
    def one(i, carry):
        work(pl.ds(pl.multiple_of(first + i * each, each), each))
        return carry

    lax.fori_loop(0, rows // each, one, 0)


def after_chunk(scatter, fetches, work):
    def after(j):
        @pl.when(j == 0)
        def _():
            for fetch in fetches:
                fetch.wait()

        row_blocks(j * scatter.chunk, scatter.chunk, 32, work)

    return after


def normal_rows(value):
    center = value - jnp.mean(value, axis=1, keepdims=True)
    factor = lax.rsqrt(jnp.mean(center * center, axis=1, keepdims=True) + 1e-05)
    return center * factor, factor


def dense_kernel(
    n, a_hbm, w_ref, input_hbm, vectors_ref, out_ref, next_ref, inputs, input_sem, *scratch
):
    fetch = pltpu.make_async_copy(input_hbm, inputs, input_sem)
    fetch.start()
    scatter = Scatter(n, False, a_hbm, w_ref, out_ref, scratch)

    def work(at):
        residual = inputs[at, :].astype(jnp.float32) + out_ref[at, :] + vectors_ref[DENSE_BIAS]
        out_ref[at, :] = residual
        normed, _ = normal_rows(residual)
        next_ref[at, :] = (normed * vectors_ref[SECOND_GAIN] + vectors_ref[SECOND_SHIFT]).astype(next_ref.dtype)

    scatter.run(after=after_chunk(scatter, (fetch,), work))


def back_rows(grad, source, gain):
    normed, factor = normal_rows(source)
    scaled = grad * gain
    product = grad * normed
    back = factor * (
        scaled
        - jnp.mean(scaled, axis=1, keepdims=True)
        - normed * jnp.mean(scaled * normed, axis=1, keepdims=True)
    )
    return back, product


def column_sum(value):
    return jnp.sum(value, axis=0, keepdims=True)


def expand_back_kernel(
    n, a_hbm, w_ref, act_hbm, rows_hbm, residual_hbm, cotangent_hbm, vectors_ref,
    out_ref, next_ref, sums_ref, grad_hbm, residual, cotangent, fetch_sem, *scratch
):
    fetches = (
        pltpu.make_async_copy(residual_hbm, residual, fetch_sem.at[0]),
        pltpu.make_async_copy(cotangent_hbm, cotangent, fetch_sem.at[1]),
    )
    for fetch in fetches:
        fetch.start()
    product = Product(act_hbm, rows_hbm, grad_hbm, scratch[:7])
    scatter = Scatter(n, True, a_hbm, w_ref, out_ref, scratch[7:])
    product.start()
    sums_ref[...] = jnp.zeros_like(sums_ref)

    def work(at):
        grad = out_ref[at, :]
        other = cotangent[at, :].astype(jnp.float32)
        back, terms = back_rows(grad, residual[at, :], vectors_ref[SECOND_GAIN])
        result = other + back
        out_ref[at, :] = result
        next_ref[at, :] = result.astype(next_ref.dtype)
        sums_ref[0:1, :] += column_sum(terms)
        sums_ref[1:2, :] += column_sum(grad)
        sums_ref[2:3, :] += column_sum(result)
        sums_ref[3:4, :] += column_sum(other)

    scatter.run(lambda j: product.batch(j, scatter.chunks), after_chunk(scatter, fetches, work))
    product.finish()


def comm_params(collective_id):
    return pltpu.CompilerParams(collective_id=collective_id, has_side_effects=True, vmem_limit_bytes=VMEM_LIMIT)


VMEM_SPEC = pl.BlockSpec(memory_space=pltpu.VMEM)
HBM_SPEC = pl.BlockSpec(memory_space=pl.ANY)
CHUNKS = 8
FILLED_CHUNKS = 4


def dense(mixed, weight, inputs, vectors, n, collective_id):
    rows, width = inputs.shape
    return pl.pallas_call(
        functools.partial(dense_kernel, n),
        out_shape=(
            jax.ShapeDtypeStruct((rows, width), jnp.float32),
            jax.ShapeDtypeStruct((rows, width), jnp.bfloat16),
        ),
        in_specs=[HBM_SPEC, VMEM_SPEC, HBM_SPEC, VMEM_SPEC],
        out_specs=(VMEM_SPEC, VMEM_SPEC),
        scratch_shapes=[pltpu.VMEM((rows, width), inputs.dtype), pltpu.SemaphoreType.DMA(())]
        + scatter_scratch(n, rows, mixed.shape[1], width, CHUNKS),
        compiler_params=comm_params(collective_id),
        cost_estimate=LINK_COST,
        name="dense",
    )(mixed, weight, inputs, vectors)


def expand_back(grad_pre, up, activated, grad_rows, residual, cotangent, vectors, n, collective_id):
    rows, width = residual.shape
    units = activated.shape[1]
    return pl.pallas_call(
        functools.partial(expand_back_kernel, n),
        out_shape=(
            jax.ShapeDtypeStruct((rows, width), jnp.float32),
            jax.ShapeDtypeStruct((rows, width), jnp.bfloat16),
            jax.ShapeDtypeStruct((8, width), jnp.float32),
            jax.ShapeDtypeStruct((units, width), jnp.bfloat16),
        ),
        in_specs=[HBM_SPEC, VMEM_SPEC, HBM_SPEC, HBM_SPEC, HBM_SPEC, HBM_SPEC, VMEM_SPEC],
        out_specs=(VMEM_SPEC, VMEM_SPEC, VMEM_SPEC, HBM_SPEC),
        scratch_shapes=[
            pltpu.VMEM((rows, width), jnp.float32),
            pltpu.VMEM((rows, width), cotangent.dtype),
            pltpu.SemaphoreType.DMA((2,)),
        ]
        + product_scratch(n * rows, units, width)
        + scatter_scratch(n, rows, units, width, FILLED_CHUNKS),
        compiler_params=comm_params(collective_id),
        cost_estimate=LINK_COST,
        name="expand_back",
    )(grad_pre, up, activated, grad_rows, residual, cotangent, vectors)


def attend_back_one(slope, proj_ref, grad_ref, start, head, row_ref, out_ref, dk_ref, dv_ref, sums_ref, length):
    at = pl.multiple_of(head * 3 * HEAD_DIM, HEAD_DIM)
    own = pl.ds(pl.multiple_of(head * HEAD_DIM, HEAD_DIM), HEAD_DIM)

    def cols(which):
        return pl.ds(at + which * HEAD_DIM, HEAD_DIM)

    def take(which, first, size):
        return proj_ref[pl.ds(start + first, size), cols(which)]

    sums = None
    for first in reversed(range(0, length, BLOCK)):
        last = first + BLOCK
        q, g = take(0, first, BLOCK), grad_ref[pl.ds(start + first, BLOCK), own]
        scores = masked_scores(slope, q, take(1, 0, last), as_column(row_ref[:, first:last]), row_ref[:, :last], first)
        top = jnp.max(scores, axis=1, keepdims=True)
        expo = jnp.exp2(scores - top)
        probs = expo * (1.0 / jnp.sum(expo, axis=1, keepdims=True))
        grad_probs = lax.dot_general(g, take(2, 0, last), NT, preferred_element_type=jnp.float32)
        product = probs * grad_probs
        grad_scores = (product - probs * jnp.sum(product, axis=1, keepdims=True)).astype(jnp.bfloat16)
        rounded = probs.astype(jnp.bfloat16)
        grad_queries = (jnp.dot(grad_scores, take(1, 0, last), preferred_element_type=jnp.float32) * SCALE).astype(
            out_ref.dtype
        )
        out_ref[pl.ds(start + first, BLOCK), cols(0)] = grad_queries
        here = column_sum(grad_queries.astype(jnp.float32))
        sums = here if sums is None else sums + here
        grad_keys = lax.dot_general(grad_scores, q, TN, preferred_element_type=jnp.float32)
        grad_values = lax.dot_general(rounded, g, TN, preferred_element_type=jnp.float32)
        if last == length:
            dk_ref[...] = grad_keys
            dv_ref[...] = grad_values
        else:
            dk_ref[:last, :] += grad_keys
            dv_ref[:last, :] += grad_values
    span = pl.ds(start, length)
    out_ref[span, cols(1)] = (dk_ref[...] * SCALE).astype(out_ref.dtype)
    grad_values = dv_ref[...].astype(out_ref.dtype)
    out_ref[span, cols(2)] = grad_values
    sums_ref[0:1, own] += sums
    sums_ref[1:2, own] += column_sum(grad_values.astype(jnp.float32))


def dense_back_kernel(
    n, length, slope_ref, own_ref, mixed_ref, w_ref, left_hbm, right_hbm, proj_hbm, row_ref,
    grad_proj_ref, sums_ref, grad_dense_ref, grad_up_hbm, gathered, acc, grad_mixed, proj, dk, dv, fetch_sem, *scratch
):
    fetch = pltpu.make_async_copy(proj_hbm, proj, fetch_sem)
    fetch.start()
    product = Product(left_hbm, right_hbm, grad_up_hbm, scratch[:7])
    gather = Gather(n, own_ref, gathered, scratch[7:])
    rows = own_ref.shape[0]
    heads = sums_ref.shape[1] // HEAD_DIM
    chips = max(1, length // (2 * rows))
    sequences = max(1, 2 * rows // length)

    def work(at):
        span = pl.ds(pl.multiple_of(at * rows, rows), rows)
        grad_mixed[span, :] = lax.dot_general(
            gathered[span, :], w_ref[...], NT, preferred_element_type=jnp.float32
        ).astype(grad_mixed.dtype)
        width = acc.shape[1]
        part = min(width, 512)
        for first in range(0, width, part):
            cols = slice(first, first + part)
            acc[:, cols] += lax.dot_general(
                mixed_ref[span, :], gathered[span, cols], TN, preferred_element_type=jnp.float32
            )

    order = [mask for count in range(gather.bits + 1) for mask in gather.level(count)]
    codes = [2 * mask + core for mask in order for core in (0, 1)]
    complete = [
        int(core == 1 and all(other // chips != mask // chips for other in order[k + 1 :]))
        for k, mask in enumerate(order)
        for core in (0, 1)
    ]

    def step(t, carry):
        for k, mask in enumerate(order):
            if k and mask.bit_count() > order[k - 1].bit_count():
                pl.when(t == 2 * k)(functools.partial(gather.forward, mask.bit_count()))
            pl.when(t == 2 * k + 1)(functools.partial(gather.wait_core, mask))
        at = gather.away(codes, t)
        work(at)

        @pl.when(look_up(complete, t) == 1)
        def _():
            first = (at // 2 // chips) * sequences

            def one(i, carry):
                s, head = first + i // heads, lax.rem(i, heads)
                attend_back_one(
                    slope_ref[head], proj, grad_mixed, pl.multiple_of(s * length, length), head, row_ref.at[s],
                    grad_proj_ref, dk, dv, sums_ref, length,
                )
                return carry

            lax.fori_loop(0, sequences * heads, one, 0)

        return carry

    product.start()
    gather.start()
    acc[...] = jnp.zeros_like(acc)
    sums_ref[...] = jnp.zeros_like(sums_ref)
    product.batch(0, 1)
    fetch.wait()
    gather.keep().wait()
    lax.fori_loop(0, 2 * len(order), step, 0)
    grad_dense_ref[...] = acc[...].astype(grad_dense_ref.dtype)
    product.finish()
    gather.finish_sends()


def dense_back(own, mixed, weight, mlp_rows, grad_pre, proj, slopes, labels, n, collective_id):
    rows, width = own.shape
    total, depth = mixed.shape
    length = labels.shape[1]
    return pl.pallas_call(
        functools.partial(dense_back_kernel, n, length),
        out_shape=(
            jax.ShapeDtypeStruct(proj.shape, jnp.bfloat16),
            jax.ShapeDtypeStruct((8, depth), jnp.float32),
            jax.ShapeDtypeStruct((depth, width), jnp.bfloat16),
            jax.ShapeDtypeStruct((mlp_rows.shape[1], grad_pre.shape[1]), jnp.bfloat16),
        ),
        in_specs=[pl.BlockSpec(memory_space=pltpu.SMEM), VMEM_SPEC, VMEM_SPEC, VMEM_SPEC]
        + [HBM_SPEC] * 3
        + [VMEM_SPEC],
        out_specs=(VMEM_SPEC, VMEM_SPEC, VMEM_SPEC, HBM_SPEC),
        scratch_shapes=[
            pltpu.VMEM((total, width), jnp.bfloat16),
            pltpu.VMEM((depth, width), jnp.float32),
            pltpu.VMEM((total, depth), jnp.bfloat16),
            pltpu.VMEM(proj.shape, jnp.bfloat16),
            pltpu.VMEM((length, HEAD_DIM), jnp.float32),
            pltpu.VMEM((length, HEAD_DIM), jnp.float32),
            pltpu.SemaphoreType.DMA(()),
        ]
        + product_scratch(total, mlp_rows.shape[1], grad_pre.shape[1])
        + gather_sems(n),
        compiler_params=comm_params(collective_id),
        cost_estimate=LINK_COST,
        name="dense_back",
    )(slopes, own, mixed, weight, mlp_rows, grad_pre, proj, labels[:, None, :])


def shrink_kernel(
    n, d, a_hbm, w_ref, residual_hbm, vectors_ref, early_ref, up_sum_ref, head_sums_ref,
    hidden_ref, sums_ref, biases_ref, out, residual, fetch_sem, *scratch
):
    fetch = pltpu.make_async_copy(residual_hbm, residual, fetch_sem)
    fetch.start()
    flat, biases = Total(n, d, scratch[:6]), Total(n, d, scratch[6:12])
    scatter = Scatter(n, False, a_hbm, w_ref, out, scratch[12:])
    heads_width = head_sums_ref.shape[1]

    def filler(j):
        for level in range(min(flat.levels + 1, scatter.chunks)):

            @pl.when(j == level)
            def _():
                if level == 0:
                    biases.lines[0] = jnp.zeros(biases.lines.shape[1:], jnp.float32)
                    biases.lines[0, 0:1, :] = up_sum_ref[...]
                    biases.lines[0, 1:3, :heads_width] = head_sums_ref[0:2, :]
                    biases.spread()
                    flat.pair[0] = early_ref[...]
                flat.step(level)

    def work(at):
        hidden_ref[at, :] = (residual[at, :] + out[at, :] + vectors_ref[DOWN_BIAS]).astype(hidden_ref.dtype)

    scatter.run(filler, after_chunk(scatter, (fetch,), work), d)
    for level in range(scatter.chunks, flat.levels + 1):
        flat.step(level)
    biases_ref[...] = biases.finish(False)
    sums_ref[...] = flat.finish()


def shrink(activated, down, residual, vectors, sums, up_sum, head_sums, n, d, collective_id):
    rows, width = residual.shape
    units = up_sum.shape[1]
    return pl.pallas_call(
        functools.partial(shrink_kernel, n, d),
        out_shape=(
            jax.ShapeDtypeStruct((rows, width), jnp.bfloat16),
            jax.ShapeDtypeStruct((8, width), jnp.float32),
            jax.ShapeDtypeStruct((8, units), jnp.float32),
        ),
        in_specs=[HBM_SPEC, VMEM_SPEC, HBM_SPEC] + [VMEM_SPEC] * 4,
        out_specs=(VMEM_SPEC, VMEM_SPEC, VMEM_SPEC),
        scratch_shapes=[
            pltpu.VMEM((rows, width), jnp.float32),
            pltpu.VMEM((rows, width), jnp.float32),
            pltpu.SemaphoreType.DMA(()),
        ]
        + total_scratch(n, d, 8, width)
        + total_scratch(n, d, 8, units)
        + scatter_scratch(n, rows, activated.shape[1], width, CHUNKS),
        compiler_params=comm_params(collective_id),
        cost_estimate=LINK_COST,
        name="shrink",
    )(activated, down, residual, vectors, sums, up_sum, head_sums)


def project_back_kernel(
    n, a_hbm, w_ref, input_hbm, grad_hbm, vectors_ref, early_ref, left_hbm,
    out_ref, sums_ref, weight_hbm, inputs, grads, fetch_sem, *scratch
):
    fetches = (
        pltpu.make_async_copy(input_hbm, inputs, fetch_sem.at[0]),
        pltpu.make_async_copy(grad_hbm, grads, fetch_sem.at[1]),
    )
    for fetch in fetches:
        fetch.start()
    product = Product(left_hbm, a_hbm, weight_hbm, scratch[:7])
    scatter = Scatter(n, True, a_hbm, w_ref, out_ref, scratch[7:])
    product.start()
    sums_ref[...] = early_ref[...]

    def work(at):
        grad = out_ref[at, :]
        back, terms = back_rows(grad, inputs[at, :].astype(jnp.float32), vectors_ref[FIRST_GAIN])
        out_ref[at, :] = grads[at, :] + back
        sums_ref[4:5, :] += column_sum(terms)
        sums_ref[5:6, :] += column_sum(grad)

    scatter.run(lambda j: product.batch(j, scatter.chunks), after_chunk(scatter, fetches, work))
    product.finish()


def project_back(grad_proj, weight, inputs, grad_residual, vectors, early, attn_rows, n, collective_id):
    rows, width = inputs.shape
    columns = grad_proj.shape[1]
    return pl.pallas_call(
        functools.partial(project_back_kernel, n),
        out_shape=(
            jax.ShapeDtypeStruct((rows, width), jnp.float32),
            jax.ShapeDtypeStruct((8, width), jnp.float32),
            jax.ShapeDtypeStruct((width, columns), jnp.bfloat16),
        ),
        in_specs=[HBM_SPEC, VMEM_SPEC, HBM_SPEC, HBM_SPEC, VMEM_SPEC, VMEM_SPEC, HBM_SPEC],
        out_specs=(VMEM_SPEC, VMEM_SPEC, HBM_SPEC),
        scratch_shapes=[
            pltpu.VMEM((rows, width), inputs.dtype),
            pltpu.VMEM((rows, width), jnp.float32),
            pltpu.SemaphoreType.DMA((2,)),
        ]
        + product_scratch(n * rows, width, columns)
        + scatter_scratch(n, rows, columns, width, CHUNKS),
        compiler_params=comm_params(collective_id),
        cost_estimate=LINK_COST,
        name="project_back",
    )(grad_proj, weight, inputs, grad_residual, vectors, early, attn_rows)


def share(grad, dimension):
    return lax.psum_scatter(grad, "dp", scatter_dimension=dimension, tiled=True)


def finish_kernel(heads_width, *refs):
    ins, outs = refs[:8], refs[8:]
    for source, target in zip(ins[:6], outs[:6]):
        target[...] = source[...].astype(target.dtype)

    @pl.when(pl.program_id(0) == 0)
    def _():
        sums, biases = ins[6:]
        for i in range(6):
            outs[6 + i][...] = sums[i : i + 1, :]
        outs[12][...] = biases[0:1, :]
        outs[13][...] = biases[1:2, :heads_width]
        outs[14][...] = biases[2:3, :heads_width]


def finish(hidden_output, grad_input, weights, sums, biases, heads_width):
    steps = 2

    def rows_block(x):
        return pl.BlockSpec((x.shape[0] // steps, x.shape[1]), lambda i: (i, 0))

    def whole_block(shape):
        return pl.BlockSpec(shape, lambda i: (0, 0))

    large = (hidden_output, grad_input) + weights
    small = [(1, sums.shape[1])] * 6 + [(1, biases.shape[1]), (1, heads_width), (1, heads_width)]
    results = pl.pallas_call(
        functools.partial(finish_kernel, heads_width),
        grid=(steps,),
        out_shape=[jax.ShapeDtypeStruct(hidden_output.shape, hidden_output.dtype)]
        + [jax.ShapeDtypeStruct(x.shape, jnp.float32) for x in large[1:]]
        + [jax.ShapeDtypeStruct(shape, jnp.float32) for shape in small],
        in_specs=[rows_block(x) for x in large] + [whole_block(sums.shape), whole_block(biases.shape)],
        out_specs=[rows_block(x) for x in large] + [whole_block(shape) for shape in small],
        name="finish",
    )(*large, sums, biases)
    return results[:6], [x.reshape(-1) for x in results[6:]]


def on_device(
    hidden_input,
    first_gain,
    first_shift,
    qkv_weight,
    query_bias,
    value_bias,
    dense_weight,
    dense_bias,
    second_gain,
    second_shift,
    up_weight,
    up_bias,
    down_weight,
    down_bias,
    segments,
    document_lengths,
    cotangent,
    *,
    n,
    d,
):
    heads_local = query_bias.shape[0] // HEAD_DIM
    attn_rows, vectors, dense_full = gather_rows(
        hidden_input,
        (
            first_gain,
            first_shift,
            dense_bias,
            second_gain,
            second_shift,
            down_bias,
            up_bias,
            query_bias,
            value_bias,
        ),
        dense_weight,
        n,
        d,
        1,
    )
    project_full, expand_full, shrink_full = (
        lax.all_gather(qkv_weight, "dp", axis=0, tiled=True),
        lax.all_gather(up_weight, "dp", axis=0, tiled=True),
        lax.all_gather(down_weight, "dp", axis=1, tiled=True),
    )
    group_rows = attn_rows.shape[0]
    sequences = document_lengths.shape[0]
    length = group_rows // sequences
    heads_index = lax.axis_index("tensor") * heads_local + lax.broadcasted_iota(
        jnp.int32, (heads_local,), 0
    )
    slopes = jnp.exp2(-8.0 * (heads_index.astype(jnp.float32) + 1.0) / HEADS) * LOG2E
    position = lax.broadcasted_iota(jnp.int32, (sequences, length), 1)
    filled = jnp.sum(document_lengths, axis=1, keepdims=True)
    labels = jnp.where(position < filled, segments.reshape(sequences, length), length + position).astype(jnp.float32)
    grad_rows, proj, mixed = project_attend(
        attn_rows, project_full, vectors, slopes, labels, cotangent, n, 6
    )
    residual, mlp_input = dense(
        mixed, dense_full, hidden_input, vectors, n, 2
    )
    mlp_rows, activated, grad_pre, sum_up_bias = expand(
        mlp_input, grad_rows, expand_full, shrink_full, vectors, n, 7
    )
    grad_residual, grad_attn_out, early_sums, grad_down = expand_back(
        grad_pre, expand_full, activated, grad_rows, residual, cotangent, vectors, n, 4
    )
    grad_down_weight = share(grad_down, 1)
    grad_proj, head_sums, grad_dense, grad_up = dense_back(
        grad_attn_out, mixed, dense_full, mlp_rows, grad_pre, proj, slopes, labels, n, 9
    )
    grad_down_weight, grad_proj = lax.optimization_barrier((grad_down_weight, grad_proj))
    grad_up_weight = share(grad_up, 0)
    grad_dense_weight = share(grad_dense, 1)
    grad_input, sums, grad_project = project_back(
        grad_proj, project_full, hidden_input, grad_residual, vectors, early_sums, attn_rows, n, 5
    )
    grad_qkv_weight = share(grad_project, 0)
    hidden_output, sums, biases = shrink(
        activated, shrink_full, residual, vectors, sums, sum_up_bias, head_sums, n, d, 3
    )
    heads_width = heads_local * HEAD_DIM
    large, small = finish(
        hidden_output,
        grad_input,
        (grad_qkv_weight, grad_dense_weight, grad_up_weight, grad_down_weight),
        sums,
        biases,
        heads_width,
    )
    hidden_output, grad_input, grad_qkv_weight, grad_dense_weight, grad_up_weight, grad_down_weight = large
    grad_second_gain, grad_second_shift, grad_dense_bias, grad_down_bias, grad_first_gain, grad_first_shift = small[:6]
    grad_up_bias, grad_query_bias, grad_value_bias = small[6:]
    return (
        hidden_output,
        grad_input,
        grad_first_gain,
        grad_first_shift,
        grad_qkv_weight,
        grad_query_bias,
        grad_value_bias,
        grad_dense_weight,
        grad_dense_bias,
        grad_second_gain,
        grad_second_shift,
        grad_up_weight,
        grad_up_bias,
        grad_down_weight,
        grad_down_bias,
    )


def solution(mesh):
    return jax.shard_map(
        functools.partial(on_device, n=mesh.shape["tensor"], d=mesh.shape["dp"]),
        mesh=mesh,
        in_specs=(
            P(("dp", "tensor"), None),
            P(),
            P(),
            P("dp", "tensor"),
            P("tensor"),
            P("tensor"),
            P("tensor", "dp"),
            P(),
            P(),
            P(),
            P("dp", "tensor"),
            P("tensor"),
            P("tensor", "dp"),
            P(),
            P("dp"),
            P("dp", None),
            P(("dp", "tensor"), None),
        ),
        out_specs=(
            P(("dp", "tensor"), None),
            P(("dp", "tensor"), None),
            P(),
            P(),
            P("dp", "tensor"),
            P("tensor"),
            P("tensor"),
            P("tensor", "dp"),
            P(),
            P(),
            P(),
            P("dp", "tensor"),
            P("tensor"),
            P("tensor", "dp"),
            P(),
        ),
        check_vma=False,
    )
```
